32 devices in a mesh: exp: 8 (over z, y), fsdp: 4 (over x, core).
Axes of the slice: x: 2, y: 2, z: 4, core: 2. Of those that a mesh axis runs over, the one named last changes fastest.
Arguments:
- tokens: bfloat16 [4096, 2048], P(('exp', 'fsdp')), may hold values from -6 to 6
- lengths: int32 [32, 4], P(('exp', 'fsdp')), may hold values from 1 to 64, 128 in all within a row
- routes: int32 [4096, 8], P(('exp', 'fsdp')), may hold values from 0 to 31, all different within a row; in each aligned block of 128 rows (0 to 127, 128 to 255, ...) at most 64 rows name the same one
- attn_gain: bfloat16 [2048], P('fsdp'), may hold values from 0.099609375 to 1.8984375
- w_query: bfloat16 [2048, 4096], P('fsdp'), may hold values from -0.125 to 0.125
- key_weight: bfloat16 [2048, 512], P('fsdp'), may hold values from -0.125 to 0.125
- value_weight: bfloat16 [2048, 512], P('fsdp'), may hold values from -0.125 to 0.125
- q_gain: bfloat16 [128], P('fsdp'), may hold values from 0.5 to 2
- k_gain: bfloat16 [128], P('fsdp'), may hold values from 0.5 to 2
- w_out: bfloat16 [4096, 2048], P('fsdp'), may hold values from -0.75 to 0.75
- mlp_gain: bfloat16 [2048], P('fsdp'), may hold values from 0.099609375 to 1.8984375
- w_router: bfloat16 [2048, 32], P('fsdp'), may hold values from -4 to 4
- expert_gate: bfloat16 [32, 2048, 768], P(('exp', 'fsdp')), may hold values from -0.125 to 0.125
- expert_up: bfloat16 [32, 2048, 768], P(('exp', 'fsdp')), may hold values from -0.125 to 0.125
- expert_down: bfloat16 [32, 768, 2048], P(('exp', 'fsdp')), may hold values from -0.875 to 0.875
- cotangent: bfloat16 [4096, 2048], P(('exp', 'fsdp')), may hold values from -6 to 6
Outputs:
- layer_out: bfloat16 [4096, 2048], P(('exp', 'fsdp'))
- grad_tokens: bfloat16 [4096, 2048], P(('exp', 'fsdp'))
- grad_attn_gain: float32 [2048], P('fsdp')
- grad_query: float32 [2048, 4096], P('fsdp')
- grad_key: float32 [2048, 512], P('fsdp')
- grad_value: float32 [2048, 512], P('fsdp')
- grad_q_gain: float32 [128], P('fsdp')
- grad_k_gain: float32 [128], P('fsdp')
- grad_out_proj: float32 [4096, 2048], P('fsdp')
- grad_mlp_gain: float32 [2048], P('fsdp')
- grad_router: float32 [2048, 32], P('fsdp')
- grad_expert_gate: float32 [32, 2048, 768], P(('exp', 'fsdp'))
- grad_expert_up: float32 [32, 2048, 768], P(('exp', 'fsdp'))
- grad_expert_down: float32 [32, 768, 2048], P(('exp', 'fsdp'))
The draws below stay inside these ranges and needn't reach their ends.
Inputs may be any that keep to these rules, and one draw needn't show every extreme that they name: `lengths`: each row packs the sequences of one device; they sum to 128, and the longest is 64. `routes`: each token names 8 different experts. Among the tokens of one device no expert is named more than 64 times, a bound that some block reaches.
All inputs are finite; a program needn't handle non-finite values.
Results may differ from the reference program's by a relative error of at most 0.023.
Values may be sent and summed in bfloat16 or wider, within the bound.
A program may use at most 320 MiB of HBM per device.

```python
import math
import jax
import jax.numpy as jnp
import numpy as np
from jax import lax

MODEL_WIDTH = 2048
QUERY_HEADS = 32
KEY_VALUE_HEADS = 4
HEAD_WIDTH = 128
FF = 768
TOPK = 8
TOK_DEV = 128
SEQS_DEV = 4
EXPERTS = 32
TOKENS = 4096
SEQ_MAX = 64
CAP = 64
N_EXP = 8
N_FSDP = 4
DEVICES = 32


def draw_q_gain(key, part):
    inner = jax.random.fold_in(key, 11)
    values = jax.random.uniform(inner, (HEAD_WIDTH,), jnp.float32, 0.6, 1.6)
    return values.astype(jnp.bfloat16)


def draw_k_gain(key, part):
    inner = jax.random.fold_in(key, 23)
    values = jax.random.uniform(inner, (HEAD_WIDTH,), jnp.float32, 0.6, 1.6)
    return values.astype(jnp.bfloat16)


def draw_w_router(key, part):
    inner = jax.random.fold_in(key, 37)
    base = jax.random.truncated_normal(inner, -4.0, 4.0, (MODEL_WIDTH, EXPERTS), jnp.float32) * MODEL_WIDTH ** (-0.5)
    return base.astype(jnp.bfloat16)


def with_spikes(values, own_key, source, target, shards_of, factor):
    owner, partner = [(jnp.arange(values.shape[dim]) // (values.shape[dim] // shards_of)).reshape([-1 if axis == dim else 1 for axis in range(values.ndim)]) for dim in (source, target)]
    chosen = jax.random.permutation(own_key, shards_of)[partner]
    strong = (owner == chosen) | (owner == (partner + shards_of // 2) % shards_of)
    return jnp.where(strong, factor * values, values)


def block_scale(own_key, dims, shards, smallest, largest):
    loudness, own = 1.0, jax.random.fold_in(own_key, 6)
    for dim, parts in shards:
        heights = jnp.exp(jax.random.uniform(jax.random.fold_in(own, dim), (parts,), jnp.float32, smallest / len(shards), largest / len(shards)))
        loudness = loudness * jnp.repeat(heights, dims[dim] // parts).reshape([-1 if axis == dim else 1 for axis in range(len(dims))])
    return loudness


def split_up(count, total, most, slope):
    loads = [(1 << 20) // math.isqrt(standing ** slope) + 1 for standing in range(2, count + 1)]
    spare, counts = total - most - (count - 1), [1] * (count - 1)
    while spare > 0:
        free = [i for i in range(count - 1) if counts[i] < most]
        mass, remaining = sum([loads[i] for i in free]), spare
        for i in free:
            addition = min(most - counts[i], max(1, remaining * loads[i] // mass), spare)
            counts[i] = counts[i] + addition
            spare = spare - addition
    return np.array([most] + counts)


def uneven_parts(rng, number_of, total, reach, skew):
    if number_of == 2:
        one = jax.random.randint(rng, (), max(1, total - reach), min(reach, total - 1) + 1)
        return jnp.stack([one, total - one])
    sizes = jnp.asarray(split_up(number_of, total, reach, skew), jnp.int32)
    pairs = (number_of - 1) // 2
    giver, receiver = sizes[1:1 + 2 * pairs:2], sizes[2:2 + 2 * pairs:2]
    room = jnp.minimum(giver - 1, reach - receiver)
    passed = jax.random.randint(jax.random.fold_in(rng, 1), (pairs,), 0, 1 << 20) % (room + 1)
    sizes = sizes.at[1:1 + 2 * pairs:2].set(giver - passed).at[2:2 + 2 * pairs:2].set(receiver + passed)
    return sizes[jax.random.permutation(jax.random.fold_in(rng, 2), number_of)]


def deal_out(stream_key, own, number, rows, amount, top, bound, lean):
    sequence = jax.random.permutation(stream_key, amount)
    crowded, usual = portions_of(amount, rows * top, bound, lean, True), portions_of(amount, rows * top, bound, lean, False)
    places = jnp.arange(amount)

    def named(sizes, offset_by):
        used = int((sizes > 0).sum())
        fixed = max(1, used // 4)
        shifted = fixed + (places - fixed + offset_by * (used - fixed)) % max(1, amount - fixed)
        return jnp.zeros((amount,), jnp.int32).at[sequence[jnp.where(places < fixed, places, shifted)]].set(jnp.asarray(sizes, jnp.int32))

    sizes = jnp.where(number % 4 == 0, named(crowded, number // 4), named(usual, number - number // 4 - 1))
    mixed = jax.random.permutation(jax.random.fold_in(own, 3), amount)
    donor, receiver = mixed[0:amount // 2 * 2:2], mixed[1:amount // 2 * 2:2]
    margin = jnp.minimum(sizes[donor] - 1, bound - sizes[receiver]) // 2
    margin = jnp.where((donor == sequence[0]) | (receiver == sequence[0]) | (sizes[receiver] == 0), 0, jnp.maximum(margin, 0))
    shifted = jax.random.randint(jax.random.fold_in(own, 4), (amount // 2,), 0, 1 << 20) % (margin + 1)
    sizes = sizes.at[donor].add(-shifted).at[receiver].add(shifted)
    labels = jnp.searchsorted(jnp.cumsum(sizes), jnp.arange(rows * top), side="right").astype(jnp.int32)
    grid = labels.reshape(top, rows).T
    grid = grid[jax.random.permutation(jax.random.fold_in(own, 1), rows)]
    offset_by = jax.random.randint(jax.random.fold_in(own, 2), (rows, 1), 0, top)
    return jnp.take_along_axis(grid, (jnp.arange(top)[None, :] + offset_by) % top, axis=1)


def portions_of(count, total, bound, lean, full):
    loads = [(1 << 20) // math.isqrt(grade ** lean) + 1 for grade in range(1, count + 1)]
    largest = bound if full else min(bound, max(-(-total // count), total * loads[0] // sum(loads)))
    least = 1 if total - largest >= count - 1 else 0
    counts, spare = [largest] + [least] * (count - 1), total - largest - least * (count - 1)
    while spare > 0:
        candidates = [i for i in range(1, count) if counts[i] < largest] or [i for i in range(1, count) if counts[i] < bound]
        mass, left = sum([loads[i] for i in candidates]), spare
        for i in candidates:
            addition = min(bound - counts[i], max(1, left * loads[i] // mass), spare)
            counts[i] = counts[i] + addition
            spare = spare - addition
    return np.array(counts)


def normal_values(own_key, dims, deviation, limit, shards=(), kind=jnp.bfloat16):
    drawn = jax.random.normal(own_key, dims, jnp.float32) * deviation
    if len(shards) > 0:
        drawn = block_scale(own_key, dims, shards, -0.22, 0.18) * drawn
    return jnp.clip(drawn, min=-limit, max=limit).astype(kind)


def noise_with(rng, dims, spread, reach, shards, heavy, kind=jnp.bfloat16):
    drawn = spread * jax.random.normal(rng, dims, jnp.float32)
    if shards:
        drawn = drawn * block_scale(rng, dims, shards, -0.22, 0.18)
    return jnp.clip(with_spikes(drawn, jax.random.fold_in(rng, 3), *heavy), -reach, reach).astype(kind)


def setup_inputs(seed: int = 0) -> dict:
    arg_keys = jax.random.split(jax.random.key(seed), 17)
    tokens = noise_with(arg_keys[0], (TOKENS, MODEL_WIDTH), 1.0, 6.0, ((0, 32),), (0, 1, 32, 2.75))
    lengths = jax.vmap(lambda own: uneven_parts(own, SEQS_DEV, TOK_DEV, SEQ_MAX, 2))(jax.random.split(arg_keys[1], DEVICES)).reshape((DEVICES, SEQS_DEV)).astype(jnp.int32)
    routes_keys = jax.random.split(jax.random.fold_in(arg_keys[2], 1), TOKENS // TOK_DEV)
    routes_turns = jax.random.permutation(jax.random.fold_in(arg_keys[2], 3), TOKENS // TOK_DEV)
    routes = jax.vmap(lambda own, number: deal_out(jax.random.fold_in(arg_keys[2], 2), own, number, TOK_DEV, EXPERTS, TOPK, CAP, 2))(routes_keys, routes_turns).reshape((TOKENS, TOPK))
    attn_gain = jnp.clip(1.0 + 0.18 * jax.random.normal(arg_keys[3], (MODEL_WIDTH,), jnp.float32), 0.099609375, 1.8984375).astype(jnp.bfloat16)
    w_query = normal_values(arg_keys[4], (MODEL_WIDTH, QUERY_HEADS * HEAD_WIDTH), MODEL_WIDTH ** -0.5, 0.125, ((0, 4),))
    key_weight = normal_values(arg_keys[5], (MODEL_WIDTH, KEY_VALUE_HEADS * HEAD_WIDTH), MODEL_WIDTH ** -0.5, 0.125, ((0, 4),))
    value_weight = normal_values(arg_keys[6], (MODEL_WIDTH, KEY_VALUE_HEADS * HEAD_WIDTH), MODEL_WIDTH ** -0.5, 0.125, ((0, 4),))
    q_gain = draw_q_gain(jax.random.fold_in(arg_keys[16], 71), 0)
    k_gain = draw_k_gain(jax.random.fold_in(arg_keys[16], 71), 0)
    w_out = normal_values(arg_keys[9], (QUERY_HEADS * HEAD_WIDTH, MODEL_WIDTH), (QUERY_HEADS * HEAD_WIDTH // 64) ** -0.5, 0.75, ((0, 4),))
    mlp_gain = jnp.clip(1.0 + 0.18 * jax.random.normal(arg_keys[10], (MODEL_WIDTH,), jnp.float32), 0.099609375, 1.8984375).astype(jnp.bfloat16)
    w_router = draw_w_router(jax.random.fold_in(arg_keys[16], 71), 0)
    expert_gate = normal_values(arg_keys[12], (EXPERTS, MODEL_WIDTH, FF), MODEL_WIDTH ** -0.5, 0.125, ((0, 32),))
    expert_up = normal_values(arg_keys[13], (EXPERTS, MODEL_WIDTH, FF), MODEL_WIDTH ** -0.5, 0.125, ((0, 32),))
    expert_down = normal_values(arg_keys[14], (EXPERTS, FF, MODEL_WIDTH), (FF // 16) ** -0.5, 0.875, ((0, 32),))
    cotangent = normal_values(arg_keys[15], (TOKENS, MODEL_WIDTH), 1.0, 6.0, ((0, 32),))
    return dict(tokens=tokens, lengths=lengths, routes=routes, attn_gain=attn_gain, w_query=w_query, key_weight=key_weight, value_weight=value_weight, q_gain=q_gain, k_gain=k_gain, w_out=w_out, mlp_gain=mlp_gain, w_router=w_router, expert_gate=expert_gate, expert_up=expert_up, expert_down=expert_down, cotangent=cotangent)


EPSILON = 1e-06
THETA = 1000000.0
MASKED = -1e+30
HIGH = lax.Precision.HIGHEST

@jax.custom_vjp
def lower_precision(v):
    return lax.optimization_barrier(v.astype(jnp.bfloat16)).astype(jnp.float32)

@jax.custom_vjp
def lower_backward(v):
    return v

def low_keep(v):
    return (lower_precision(v), None)

def low_pass(kept, grad):
    return (grad,)

def back_keep(v):
    return (v, None)

def back_low(kept, grad):
    return (lower_precision(grad),)
lower_precision.defvjp(low_keep, low_pass)
lower_backward.defvjp(back_keep, back_low)

def matrix_product(left, right):
    return jnp.dot(left, right, precision=HIGH)

def rms_scale(values):
    return lax.rsqrt(lax.optimization_barrier(jnp.mean(values * values, axis=-1, keepdims=True)) + EPSILON)

def seq_layout(length_row, token_count):
    ends = jnp.cumsum(length_row).astype(jnp.int32)
    starts = (ends - length_row).astype(jnp.int32)
    places = jnp.arange(token_count, dtype=jnp.int32)
    member = (places[:, None] >= starts[None, :]) & (places[:, None] < ends[None, :])
    numbers = jnp.arange(length_row.shape[0], dtype=jnp.int32)
    segment = lax.optimization_barrier(jnp.sum(jnp.where(member, numbers[None, :], 0), axis=1))
    position = places - lax.optimization_barrier(jnp.sum(jnp.where(member, starts[None, :], 0), axis=1))
    allowed = (segment[:, None] == segment[None, :]) & (places[None, :] <= places[:, None])
    return (position, allowed)

def rotary_tables(position, head_size):
    half = head_size // 2
    index = jnp.arange(head_size, dtype=jnp.int32) % half
    inverse = jnp.exp(index.astype(jnp.float32) * (-2.0 * math.log(THETA) / head_size))
    angles = position.astype(jnp.float32)[:, None] * inverse[None, :]
    return (jnp.cos(angles)[:, None, :], jnp.sin(angles)[:, None, :])

def rotate(values, cosine, sine):
    half = values.shape[-1] // 2
    turned = jnp.concatenate([-values[..., half:], values[..., :half]], axis=-1)
    return values * cosine + turned * sine

def slot_table(route_rows, experts, capacity):
    flat = route_rows.reshape(-1)
    onehot = (flat[:, None] == jnp.arange(experts, dtype=jnp.int32)[None, :]).astype(jnp.int32)
    ranks = jnp.cumsum(onehot, axis=0) - 1
    rank = lax.optimization_barrier(jnp.sum(ranks * onehot, axis=1))
    return (flat * capacity + rank).astype(jnp.int32)

def layer_device(params, inputs, length_row, route_rows):
    attn_gain, w_query, key_weight, value_weight, q_gain, k_gain, w_out, mlp_gain, w_router, expert_gate, expert_up, expert_down = params
    token_count = inputs.shape[0]
    head_group = QUERY_HEADS // KEY_VALUE_HEADS
    position, allowed = seq_layout(length_row, token_count)
    cosine, sine = rotary_tables(position, HEAD_WIDTH)
    hidden_state = lower_precision(inputs * rms_scale(inputs) * attn_gain)
    query_rows = lower_backward(matrix_product(hidden_state, w_query)).reshape(token_count, QUERY_HEADS, HEAD_WIDTH)
    key = lower_backward(matrix_product(hidden_state, key_weight)).reshape(token_count, KEY_VALUE_HEADS, HEAD_WIDTH)
    value_rows = lower_precision(lower_backward(matrix_product(hidden_state, value_weight))).reshape(token_count, KEY_VALUE_HEADS, HEAD_WIDTH)
    query_rows = lower_precision(rotate(query_rows * rms_scale(query_rows) * q_gain, cosine, sine))
    key = lower_precision(rotate(key * rms_scale(key) * k_gain, cosine, sine))
    query_rows = query_rows.reshape(token_count, KEY_VALUE_HEADS, head_group, HEAD_WIDTH)
    scores = lower_backward(jnp.einsum('qkgd,pkd->kgqp', query_rows, key, precision=HIGH) * HEAD_WIDTH ** (-0.5))
    scores = jnp.where(allowed[None, None], scores, MASKED)
    top = lax.optimization_barrier(jnp.max(scores, axis=-1, keepdims=True))
    raised = jnp.exp(scores - top)
    probs = lower_precision(raised / lax.optimization_barrier(jnp.sum(raised, axis=-1, keepdims=True)))
    attended = jnp.einsum('kgqp,pkd->qkgd', probs, value_rows, precision=HIGH).reshape(token_count, QUERY_HEADS * HEAD_WIDTH)
    attended = lower_precision(lower_backward(attended))
    middle = inputs + lower_backward(matrix_product(attended, w_out))
    normed = lower_precision(middle * rms_scale(middle) * mlp_gain)
    logits = lower_backward(matrix_product(normed, w_router))
    picked = jnp.take_along_axis(logits, route_rows, axis=1)
    peak = lax.optimization_barrier(jnp.max(picked, axis=1, keepdims=True))
    lifted = jnp.exp(picked - peak)
    gates = lifted / lax.optimization_barrier(jnp.sum(lifted, axis=1, keepdims=True))
    slots = slot_table(route_rows, EXPERTS, CAP)
    rows = lower_backward(jnp.repeat(normed, TOPK, axis=0))
    packed = jnp.zeros((EXPERTS * CAP, MODEL_WIDTH), jnp.float32).at[slots].set(rows).reshape(EXPERTS, CAP, MODEL_WIDTH)
    gate_pre = lower_backward(jnp.einsum('ecd,edf->ecf', packed, expert_gate, precision=HIGH))
    up_pre = lower_backward(jnp.einsum('ecd,edf->ecf', packed, expert_up, precision=HIGH))
    active = lower_precision(gate_pre * jax.nn.sigmoid(gate_pre) * up_pre)
    produced = jnp.einsum('ecf,efd->ecd', active, expert_down, precision=HIGH)
    produced = lower_precision(lower_backward(produced)).reshape(EXPERTS * CAP, MODEL_WIDTH)
    returned = produced[slots].reshape(token_count, TOPK, MODEL_WIDTH)
    mixed = lax.optimization_barrier(jnp.sum(gates[:, :, None] * returned, axis=1))
    return middle + mixed

def reference(tokens, lengths, routes, attn_gain, w_query, key_weight, value_weight, q_gain, k_gain, w_out, mlp_gain, w_router, expert_gate, expert_up, expert_down, cotangent):
    groups = N_EXP * N_FSDP
    params = tuple((item.astype(jnp.float32) for item in (attn_gain, w_query, key_weight, value_weight, q_gain, k_gain, w_out, mlp_gain, w_router, expert_gate, expert_up, expert_down)))
    inputs = tokens.astype(jnp.float32).reshape(groups, TOK_DEV, MODEL_WIDTH)
    route_rows = routes.reshape(groups, TOK_DEV, TOPK)

    def forward(weights, values):

        def one_group(item):
            return layer_device(weights, item[0], item[1], item[2])
        return lax.map(jax.checkpoint(one_group), (values, lengths, route_rows))
    outputs, pullback = jax.vjp(forward, params, inputs)
    grads, input_grad = pullback(cotangent.astype(jnp.float32).reshape(groups, TOK_DEV, MODEL_WIDTH))
    return (outputs.reshape(TOKENS, MODEL_WIDTH).astype(jnp.bfloat16), input_grad.reshape(TOKENS, MODEL_WIDTH).astype(jnp.bfloat16), grads[0], grads[1], grads[2], grads[3], grads[4], grads[5], grads[6], grads[7], grads[8], grads[9], grads[10], grads[11])
```

```python
import math

import jax
import jax.numpy as jnp
from jax import lax
from jax.sharding import PartitionSpec as P

MODEL_WIDTH = 2048
QUERY_HEADS = 32
KEY_VALUE_HEADS = 4
HEAD_WIDTH = 128


EPSILON = 1e-06
THETA = 1000000.0
MASKED = -1e30
BOTH = ("exp", "fsdp")


def matrix_product(left, right):
    return jnp.dot(left, right, preferred_element_type=jnp.float32)


def left_trans(left, right):
    return lax.dot_general(
        left, right, (((0,), (0,)), ((), ())), preferred_element_type=jnp.float32
    )


def right_transposed(left, right):
    return lax.dot_general(
        left, right, (((1,), (1,)), ((), ())), preferred_element_type=jnp.float32
    )


def contract(spec, left, right):
    return jnp.einsum(spec, left, right, preferred_element_type=jnp.float32)


def rms_scale(values):
    return lax.rsqrt(jnp.mean(values * values, axis=-1, keepdims=True) + EPSILON)


def rms_back(grad_hat, values, scale):
    normal = values * scale
    return scale * (grad_hat - normal * jnp.mean(grad_hat * normal, axis=-1, keepdims=True))


def seq_layout(length_row, token_count):
    ends = jnp.cumsum(length_row)
    starts = ends - length_row
    places = jnp.arange(token_count, dtype=jnp.int32)
    member = (places[:, None] >= starts[None, :]) & (places[:, None] < ends[None, :])
    numbers = jnp.arange(length_row.shape[0], dtype=jnp.int32)
    segment = jnp.sum(jnp.where(member, numbers[None, :], 0), axis=1)
    position = places - jnp.sum(jnp.where(member, starts[None, :], 0), axis=1)
    allowed = (segment[:, None] == segment[None, :]) & (places[None, :] <= places[:, None])
    return (position, allowed)


def rotary_tables(position, head_size):
    half = head_size // 2
    index = jnp.arange(head_size, dtype=jnp.int32) % half
    inverse = jnp.exp(index.astype(jnp.float32) * (-2.0 * math.log(THETA) / head_size))
    angles = position.astype(jnp.float32)[..., None] * inverse
    return (jnp.cos(angles)[..., None, :], jnp.sin(angles)[..., None, :])


def rotate(values, cosine, sine):
    half = values.shape[-1] // 2
    turned = jnp.concatenate([-values[..., half:], values[..., :half]], axis=-1)
    return values * cosine + turned * sine


def rotate_back(grads, cosine, sine):
    half = grads.shape[-1] // 2
    moved = grads * sine
    return grads * cosine + jnp.concatenate([moved[..., half:], -moved[..., :half]], axis=-1)


def slot_table(route_rows, experts, capacity):
    flat = route_rows.reshape(-1)
    onehot = (flat[:, None] == jnp.arange(experts, dtype=jnp.int32)[None, :]).astype(jnp.int32)
    ranks = jnp.cumsum(onehot, axis=0) - 1
    rank = jnp.sum(ranks * onehot, axis=1)
    return flat * capacity + rank


def exchange(buffer):
    return lax.all_to_all(buffer, BOTH, split_axis=0, concat_axis=0, tiled=True)


def two_halves(values):
    high = values.astype(jnp.bfloat16)
    low = (values - high.astype(jnp.float32)).astype(jnp.bfloat16)
    return high, low


def expert_forward(arrived, gate_w, up_w):
    gate_pre = matrix_product(arrived, gate_w)
    up_pre = matrix_product(arrived, up_w)
    sigma = jax.nn.sigmoid(gate_pre)
    active = (gate_pre * sigma * up_pre).astype(jnp.bfloat16)
    return gate_pre, up_pre, sigma, active


def expert_back(arrived, out_rows, hidden, gate_w, up_w, down_w):
    gate_pre, up_pre, sigma, active = hidden
    active_grad = right_transposed(out_rows, down_w)
    gate_pre_grad = (active_grad * up_pre * (sigma * (1.0 + gate_pre * (1.0 - sigma)))).astype(
        jnp.bfloat16
    )
    up_pre_grad = (active_grad * (gate_pre * sigma)).astype(jnp.bfloat16)
    rows_back = right_transposed(gate_pre_grad, gate_w) + right_transposed(up_pre_grad, up_w)
    return (
        rows_back.astype(jnp.bfloat16),
        left_trans(arrived, gate_pre_grad),
        left_trans(arrived, up_pre_grad),
        left_trans(active, out_rows),
    )


def gates_of(logits, routes, experts):
    picked = jnp.take_along_axis(logits, routes, axis=1)
    peak = jnp.max(picked, axis=1, keepdims=True)
    lifted = jnp.exp(picked - peak)
    return lifted / jnp.sum(lifted, axis=1, keepdims=True)


def moe_gathered(normed, router, routes, capacity, cotangent, weights):
    gate_w, up_w, down_w = weights
    token_count = normed.shape[0]
    experts = router.shape[1]
    mine = lax.axis_index("exp") * lax.axis_size("fsdp") + lax.axis_index("fsdp")
    all_routes = lax.all_gather(routes, BOTH, axis=0, tiled=True)
    all_grads = lax.all_gather(cotangent, BOTH, axis=0, tiled=True)
    columns = jnp.arange(experts, dtype=jnp.int32)
    named = jnp.any(all_routes[:, :, None] == columns[None, None, :], axis=1)
    own = jnp.any(all_routes == mine, axis=1).reshape(experts, token_count)
    before = jnp.tril(jnp.ones((token_count, token_count), jnp.bfloat16), -1)
    rank = right_transposed(own.astype(jnp.bfloat16), before).astype(jnp.int32)
    places = jnp.arange(capacity, dtype=jnp.int32)
    select = (own[:, None, :] & (rank[:, None, :] == places[None, :, None])).astype(jnp.bfloat16)
    grad_rows = contract(
        "bcj,bjd->bcd", select, all_grads.reshape(experts, token_count, MODEL_WIDTH)
    ).astype(jnp.bfloat16)
    grad_rows = grad_rows.reshape(experts * capacity, MODEL_WIDTH)

    all_normed = lax.all_gather(normed, BOTH, axis=0, tiled=True)
    logits = matrix_product(all_normed, router)
    masked = jnp.where(named, logits, MASKED)
    peak = jnp.max(masked, axis=1, keepdims=True)
    lifted = jnp.exp(masked - peak)
    own_gate = jnp.sum(jnp.where(columns[None, :] == mine, lifted, 0.0), axis=1) / jnp.sum(
        lifted, axis=1
    )
    row_gate = jnp.sum(
        jnp.where(select > 0, own_gate.reshape(experts, 1, token_count), 0.0), axis=2
    ).reshape(experts * capacity, 1)
    arrived = (
        contract("bcj,bjd->bcd", select, all_normed.reshape(experts, token_count, MODEL_WIDTH))
        .astype(jnp.bfloat16)
        .reshape(experts * capacity, MODEL_WIDTH)
    )
    hidden = expert_forward(arrived, gate_w, up_w)
    out_rows = (row_gate * grad_rows.astype(jnp.float32)).astype(jnp.bfloat16)
    rows_back, gate_w_grad, up_w_grad, down_grad = expert_back(
        arrived, out_rows, hidden, gate_w, up_w, down_w
    )
    produced = matrix_product(hidden[3], down_w).astype(jnp.bfloat16)
    row_grad = jnp.sum(produced.astype(jnp.float32) * grad_rows.astype(jnp.float32), axis=1)
    weighted = (row_gate * produced.astype(jnp.float32)).astype(jnp.bfloat16)

    def spread(rows):
        rows = rows.reshape(experts, capacity, rows.shape[1])
        return (
            contract("bcj,bcd->bjd", select, rows)
            .astype(jnp.bfloat16)
            .reshape(experts * token_count, rows.shape[2])
        )

    own_grad = jnp.sum(
        jnp.where(select > 0, row_grad.reshape(experts, capacity, 1), 0.0), axis=1
    ).reshape(experts * token_count, 1)
    placed = jnp.where(columns[None, :] == mine, own_grad, 0.0)
    high, low = two_halves(placed)
    back = lax.psum_scatter(
        jnp.concatenate([spread(rows_back), high, low], axis=1),
        BOTH,
        scatter_dimension=0,
        tiled=True,
    )
    mixed = lax.psum_scatter(spread(weighted), BOTH, scatter_dimension=0, tiled=True)
    summed = back[:, :MODEL_WIDTH].astype(jnp.float32)
    high = back[:, MODEL_WIDTH : MODEL_WIDTH + experts].astype(jnp.float32)
    low = back[:, MODEL_WIDTH + experts :].astype(jnp.float32)
    gate_grad = jnp.take_along_axis(high + low, routes, axis=1)
    gates = gates_of(matrix_product(normed, router), routes, experts)
    return mixed.astype(jnp.float32), summed, gates, gate_grad, gate_w_grad, up_w_grad, down_grad


def moe_exchanged(normed, router, routes, capacity, cotangent, weights):
    gate_w, up_w, down_w = weights
    token_count, topk = routes.shape
    experts = router.shape[1]
    gates = gates_of(matrix_product(normed, router), routes, experts)
    slots = slot_table(routes, experts, capacity)

    def send(rows):
        packed = jnp.zeros((experts * capacity, MODEL_WIDTH), jnp.bfloat16).at[slots].set(rows)
        return exchange(packed.reshape(experts, capacity, MODEL_WIDTH)).reshape(
            experts * capacity, MODEL_WIDTH
        )

    def bring(rows):
        rows = exchange(rows.reshape(experts, capacity, MODEL_WIDTH))
        return rows.reshape(experts * capacity, MODEL_WIDTH)[slots].reshape(
            token_count, topk, MODEL_WIDTH
        )

    arrived = send(jnp.repeat(normed, topk, axis=0))
    hidden = expert_forward(arrived, gate_w, up_w)
    scaled = (gates[:, :, None] * cotangent.astype(jnp.float32)[:, None, :]).astype(jnp.bfloat16)
    out_rows = send(scaled.reshape(token_count * topk, MODEL_WIDTH))
    rows_back, gate_w_grad, up_w_grad, down_grad = expert_back(
        arrived, out_rows, hidden, gate_w, up_w, down_w
    )
    returned = bring(matrix_product(hidden[3], down_w).astype(jnp.bfloat16))
    mixed = jnp.einsum("tk,tkd->td", gates, returned.astype(jnp.float32))
    gate_grad = jnp.einsum("td,tkd->tk", cotangent, returned, preferred_element_type=jnp.float32)
    summed = jnp.sum(bring(rows_back), axis=1, dtype=jnp.float32)
    return mixed, summed, gates, gate_grad, gate_w_grad, up_w_grad, down_grad


def local(
    tokens,
    lengths,
    routes,
    attn_gain,
    w_query,
    key_weight,
    value_weight,
    q_gain,
    k_gain,
    w_out,
    mlp_gain,
    w_router,
    expert_gate,
    expert_up,
    expert_down,
    cotangent,
):
    shards, members = lax.axis_size("fsdp"), lax.axis_size("exp")
    experts = shards * members
    token_count, topk = routes.shape
    capacity = 2 * token_count * topk // experts
    group = shards * token_count
    depth = w_query.shape[0]
    heads = QUERY_HEADS // shards
    kv_heads = max(1, KEY_VALUE_HEADS // shards)
    copies = shards * kv_heads // KEY_VALUE_HEADS
    head_group = heads // kv_heads
    wide, narrow = heads * HEAD_WIDTH, kv_heads * HEAD_WIDTH
    place = lax.axis_index("fsdp")

    gathered = lax.all_gather(
        jnp.concatenate([w_router.reshape(-1), attn_gain, mlp_gain, q_gain, k_gain]), "fsdp"
    )
    cuts, start = [], 0
    for leaf in (w_router, attn_gain, mlp_gain, q_gain, k_gain):
        cuts.append(gathered[:, start : start + leaf.size])
        start += leaf.size
    router = cuts[0].reshape(MODEL_WIDTH, experts)
    gain_attn, gain_mlp, gain_query, gain_key = [
        cut.reshape(-1).astype(jnp.float32) for cut in cuts[1:]
    ]
    all_lengths = lax.all_gather(lengths[0], "fsdp")

    def by_shard(weight):
        weight = weight.reshape(depth, KEY_VALUE_HEADS, HEAD_WIDTH)
        return jnp.repeat(weight, copies, axis=1).reshape(depth, shards, narrow)

    joined = jnp.concatenate(
        [w_query.reshape(depth, shards, wide), by_shard(key_weight), by_shard(value_weight)], axis=2
    ).transpose(1, 0, 2)

    inputs = tokens.astype(jnp.float32)
    scale_one = rms_scale(inputs)
    first_normed = (inputs * scale_one * gain_attn).astype(jnp.bfloat16)
    hidden = lax.all_to_all(first_normed, "fsdp", split_axis=1, concat_axis=0, tiled=True)
    partial = contract("gk,nkc->ngc", hidden, joined).astype(jnp.bfloat16)
    raw = lax.psum_scatter(partial, "fsdp", scatter_dimension=0, tiled=True)[0].astype(jnp.float32)
    raw = raw.reshape(shards, token_count, wide + 2 * narrow)
    query_raw = raw[:, :, :wide].reshape(shards, token_count, heads, HEAD_WIDTH)
    key_raw = raw[:, :, wide : wide + narrow].reshape(shards, token_count, kv_heads, HEAD_WIDTH)
    value = (
        raw[:, :, wide + narrow :]
        .astype(jnp.bfloat16)
        .reshape(shards, token_count, kv_heads, HEAD_WIDTH)
    )
    position, allowed = jax.vmap(lambda row: seq_layout(row, token_count))(all_lengths)
    cosine, sine = rotary_tables(position, HEAD_WIDTH)
    query_scale = rms_scale(query_raw)
    query_hat = query_raw * query_scale
    key_scale = rms_scale(key_raw)
    key_hat = key_raw * key_scale
    query = (
        rotate(query_hat * gain_query, cosine, sine)
        .astype(jnp.bfloat16)
        .reshape(shards, token_count, kv_heads, head_group, HEAD_WIDTH)
    )
    key = rotate(key_hat * gain_key, cosine, sine).astype(jnp.bfloat16)
    scores = contract("bqkgd,bpkd->bkgqp", query, key) * HEAD_WIDTH ** (-0.5)
    scores = jnp.where(allowed[:, None, None], scores, MASKED)
    top = jnp.max(scores, axis=-1, keepdims=True)
    raised = jnp.exp(scores - top)
    probs = raised / jnp.sum(raised, axis=-1, keepdims=True)
    probs_low = probs.astype(jnp.bfloat16)
    attended = contract("bkgqp,bpkd->bqkgd", probs_low, value).astype(jnp.bfloat16)
    attended = attended.reshape(group, wide)
    mixed_heads = lax.psum_scatter(
        matrix_product(attended, w_out).astype(jnp.bfloat16), "fsdp", scatter_dimension=0, tiled=True
    )
    middle = inputs + mixed_heads.astype(jnp.float32)
    scale_two = rms_scale(middle)
    normed = (middle * scale_two * gain_mlp).astype(jnp.bfloat16)

    moe = moe_gathered if capacity * experts * 2 >= token_count * experts else moe_exchanged
    mixed, summed, gates, gate_grad, gate_w_grad, up_w_grad, down_grad = moe(
        normed,
        router,
        routes,
        capacity,
        cotangent,
        (expert_gate[0], expert_up[0], expert_down[0]),
    )
    layer_out = (middle + mixed).astype(jnp.bfloat16)

    upstream = cotangent.astype(jnp.float32)
    picked_grad = gates * (gate_grad - jnp.sum(gates * gate_grad, axis=1, keepdims=True))
    onehot = routes[:, :, None] == jnp.arange(experts, dtype=jnp.int32)[None, None, :]
    logit_grad = jnp.sum(jnp.where(onehot, picked_grad[:, :, None], 0.0), axis=1).astype(
        jnp.bfloat16
    )
    normed_grad = summed + right_transposed(logit_grad, router)
    mlp_gain_grad = jnp.sum(normed_grad * middle * scale_two, axis=0)
    router_grad = left_trans(normed, logit_grad)
    middle_grad = upstream + rms_back(normed_grad * gain_mlp, middle, scale_two)
    branch_grad = lax.all_gather(middle_grad.astype(jnp.bfloat16), "fsdp", axis=0, tiled=True)
    out_w_grad = left_trans(attended, branch_grad)
    attended_grad = (
        right_transposed(branch_grad, w_out)
        .astype(jnp.bfloat16)
        .reshape(shards, token_count, kv_heads, head_group, HEAD_WIDTH)
    )
    prob_grad = contract("bqkgd,bpkd->bkgqp", attended_grad, value)
    value_grad = contract("bkgqp,bqkgd->bpkd", probs_low, attended_grad)
    balance = jnp.sum(probs * prob_grad, axis=-1, keepdims=True)
    score_grad = (probs * (prob_grad - balance)).astype(jnp.bfloat16)
    query_norm_grad = contract("bkgqp,bpkd->bqkgd", score_grad, key) * HEAD_WIDTH ** (-0.5)
    query_norm_grad = query_norm_grad.reshape(shards, token_count, heads, HEAD_WIDTH)
    key_norm_grad = contract("bkgqp,bqkgd->bpkd", score_grad, query) * HEAD_WIDTH ** (-0.5)
    query_norm_grad = rotate_back(query_norm_grad, cosine, sine)
    key_norm_grad = rotate_back(key_norm_grad, cosine, sine)
    q_gain_grad = jnp.sum(query_norm_grad * query_hat, axis=(0, 1, 2))
    k_gain_grad = jnp.sum(key_norm_grad * key_hat, axis=(0, 1, 2))
    query_grad = rms_back(query_norm_grad * gain_query, query_raw, query_scale)
    key_grad = rms_back(key_norm_grad * gain_key, key_raw, key_scale)
    head_grads = jnp.concatenate(
        [
            query_grad.reshape(group, wide),
            key_grad.reshape(group, narrow),
            value_grad.reshape(group, narrow),
        ],
        axis=1,
    ).astype(jnp.bfloat16)
    head_grads = lax.all_gather(head_grads, "fsdp")
    hidden_grad = contract("ngc,nkc->gk", head_grads, joined).astype(jnp.bfloat16)
    first_grad = lax.all_to_all(
        hidden_grad, "fsdp", split_axis=0, concat_axis=1, tiled=True
    ).astype(jnp.float32)
    attn_gain_grad = jnp.sum(first_grad * inputs * scale_one, axis=0)
    input_grad = (middle_grad + rms_back(first_grad * gain_attn, inputs, scale_one)).astype(
        jnp.bfloat16
    )
    joined_grad = contract("gk,ngc->nkc", hidden, head_grads).astype(jnp.bfloat16)

    out_sum = lax.psum(out_w_grad.astype(jnp.bfloat16), "exp").astype(jnp.float32)
    joined_sum = lax.psum(joined_grad, "exp").astype(jnp.float32)
    vectors = jnp.concatenate(
        [router_grad.reshape(-1), attn_gain_grad, mlp_gain_grad, q_gain_grad, k_gain_grad]
    )
    vectors = lax.psum(vectors, BOTH)
    sums, start = [], 0
    for leaf in (w_router, attn_gain, mlp_gain, q_gain, k_gain):
        sums.append(
            lax.dynamic_slice_in_dim(vectors, start + place * leaf.size, leaf.size).reshape(
                leaf.shape
            )
        )
        start += leaf.size * shards

    def gather_heads(part):
        return part.transpose(1, 0, 2).reshape(depth, KEY_VALUE_HEADS, copies, HEAD_WIDTH).sum(
            axis=2
        ).reshape(depth, KEY_VALUE_HEADS * HEAD_WIDTH)

    return (
        layer_out,
        input_grad,
        sums[1],
        joined_sum[:, :, :wide].transpose(1, 0, 2).reshape(depth, QUERY_HEADS * HEAD_WIDTH),
        gather_heads(joined_sum[:, :, wide : wide + narrow]),
        gather_heads(joined_sum[:, :, wide + narrow :]),
        sums[3],
        sums[4],
        out_sum,
        sums[2],
        sums[0],
        gate_w_grad[None],
        up_w_grad[None],
        down_grad[None],
    )


def solution(mesh):
    in_specs = (
        P(("exp", "fsdp"), None),
        P(("exp", "fsdp"), None),
        P(("exp", "fsdp"), None),
        P("fsdp"),
        P("fsdp", None),
        P("fsdp", None),
        P("fsdp", None),
        P("fsdp"),
        P("fsdp"),
        P("fsdp", None),
        P("fsdp"),
        P("fsdp", None),
        P(("exp", "fsdp"), None, None),
        P(("exp", "fsdp"), None, None),
        P(("exp", "fsdp"), None, None),
        P(("exp", "fsdp"), None),
    )
    out_specs = (
        P(("exp", "fsdp"), None),
        P(("exp", "fsdp"), None),
        P("fsdp"),
        P("fsdp", None),
        P("fsdp", None),
        P("fsdp", None),
        P("fsdp"),
        P("fsdp"),
        P("fsdp", None),
        P("fsdp"),
        P("fsdp", None),
        P(("exp", "fsdp"), None, None),
        P(("exp", "fsdp"), None, None),
        P(("exp", "fsdp"), None, None),
    )
    return jax.shard_map(local, mesh=mesh, in_specs=in_specs, out_specs=out_specs, check_vma=False)
```

```python
import math

import jax
import jax.numpy as jnp
from jax import lax
from jax.experimental import pallas as pl
from jax.experimental.pallas import tpu as pltpu
from jax.sharding import PartitionSpec as P

MODEL_WIDTH = 2048
QUERY_HEADS = 32
KEY_VALUE_HEADS = 4
HEAD_WIDTH = 128


EPSILON = 1e-06
THETA = 1000000.0
MASKED = -1e30
BOTH = ("exp", "fsdp")
MESH = pl.DeviceIdType.MESH


def matrix_product(left, right):
    return jnp.dot(left, right, preferred_element_type=jnp.float32)


def left_trans(left, right):
    return lax.dot_general(
        left, right, (((0,), (0,)), ((), ())), preferred_element_type=jnp.float32
    )


def right_transposed(left, right):
    return lax.dot_general(
        left, right, (((1,), (1,)), ((), ())), preferred_element_type=jnp.float32
    )


def contract(spec, left, right):
    return jnp.einsum(spec, left, right, preferred_element_type=jnp.float32)


def rms_scale(values):
    return lax.rsqrt(jnp.mean(values * values, axis=-1, keepdims=True) + EPSILON)


def rms_back(grad_hat, values, scale):
    normal = values * scale
    return scale * (grad_hat - normal * jnp.mean(grad_hat * normal, axis=-1, keepdims=True))


def seq_layout(length_row, token_count):
    ends = jnp.cumsum(length_row)
    starts = ends - length_row
    places = jnp.arange(token_count, dtype=jnp.int32)
    member = (places[:, None] >= starts[None, :]) & (places[:, None] < ends[None, :])
    numbers = jnp.arange(length_row.shape[0], dtype=jnp.int32)
    segment = jnp.sum(jnp.where(member, numbers[None, :], 0), axis=1)
    position = places - jnp.sum(jnp.where(member, starts[None, :], 0), axis=1)
    allowed = (segment[:, None] == segment[None, :]) & (places[None, :] <= places[:, None])
    return (position, allowed)


def rotary_tables(position, head_size):
    half = head_size // 2
    index = jnp.arange(head_size, dtype=jnp.int32) % half
    inverse = jnp.exp(index.astype(jnp.float32) * (-2.0 * math.log(THETA) / head_size))
    angles = position.astype(jnp.float32)[..., None] * inverse
    return (jnp.cos(angles)[..., None, :], jnp.sin(angles)[..., None, :])


def rotate(values, cosine, sine):
    half = values.shape[-1] // 2
    turned = jnp.concatenate([-values[..., half:], values[..., :half]], axis=-1)
    return values * cosine + turned * sine


def rotate_back(grads, cosine, sine):
    half = grads.shape[-1] // 2
    moved = grads * sine
    return grads * cosine + jnp.concatenate([moved[..., half:], -moved[..., :half]], axis=-1)


def slot_table(route_rows, experts, capacity):
    flat = route_rows.reshape(-1)
    onehot = (flat[:, None] == jnp.arange(experts, dtype=jnp.int32)[None, :]).astype(jnp.int32)
    ranks = jnp.cumsum(onehot, axis=0) - 1
    rank = jnp.sum(ranks * onehot, axis=1)
    return flat * capacity + rank


def exchange(buffer):
    return lax.all_to_all(buffer, BOTH, split_axis=0, concat_axis=0, tiled=True)


def two_halves(values):
    high = values.astype(jnp.bfloat16)
    low = (values - high.astype(jnp.float32)).astype(jnp.bfloat16)
    return high, low


def expert_forward(arrived, gate_w, up_w):
    gate_pre = matrix_product(arrived, gate_w)
    up_pre = matrix_product(arrived, up_w)
    sigma = jax.nn.sigmoid(gate_pre)
    active = (gate_pre * sigma * up_pre).astype(jnp.bfloat16)
    return gate_pre, up_pre, sigma, active


def expert_back(out_rows, hidden, gate_w, up_w, down_w):
    gate_pre, up_pre, sigma, _ = hidden
    active_grad = right_transposed(out_rows, down_w)
    gate_pre_grad = (active_grad * up_pre * (sigma * (1.0 + gate_pre * (1.0 - sigma)))).astype(
        jnp.bfloat16
    )
    up_pre_grad = (active_grad * (gate_pre * sigma)).astype(jnp.bfloat16)
    rows_back = right_transposed(gate_pre_grad, gate_w) + right_transposed(up_pre_grad, up_w)
    return rows_back.astype(jnp.bfloat16), gate_pre_grad, up_pre_grad


def gates_of(logits, routes, experts):
    picked = jnp.take_along_axis(logits, routes, axis=1)
    peak = jnp.max(picked, axis=1, keepdims=True)
    lifted = jnp.exp(picked - peak)
    return lifted / jnp.sum(lifted, axis=1, keepdims=True)


def spot():
    member, shard = lax.axis_index("exp"), lax.axis_index("fsdp")
    return member // 2, member % 2, shard // 2, shard % 2

def where_is(z, y, x, c):
    return (z * 2 + y, x * 2 + c)

def number(z, y, x, c):
    return z * 8 + y * 4 + x * 2 + c

def greet(peers):
    barrier = pltpu.get_barrier_semaphore()
    for peer in peers:
        pl.semaphore_signal(barrier, inc=1, device_id=peer, device_id_type=MESH)
    pl.semaphore_wait(barrier, len(peers))

def gather_kernel(x_ref, select_ref, out_ref, held, arrive, to_z, to_y, to_x, to_core):
    z, y, x, c = spot()
    half = x_ref.shape[0] // 2
    y_peer, x_peer, core_peer = (
        where_is(z, 1 - y, x, c), where_is(z, y, 1 - x, c), where_is(z, y, x, 1 - c))
    z_peers = [where_is((z + k) % 4, y, x, c) for k in range(1, 4)]
    greet([y_peer, x_peer, core_peer] + z_peers)

    def copy(block, part, sem, peer):
        view = held.at[block, pl.ds(part * half, half)]
        return pltpu.make_async_remote_copy(
            src_ref=view, dst_ref=view, send_sem=sem, recv_sem=arrive.at[block, part],
            device_id=peer, device_id_type=MESH)

    def arrived(block, part):
        copy(block, part, to_core.at[0, 0, 0], core_peer).wait_recv()

    def pick(block):
        out_ref[block] = jnp.dot(
            select_ref[block], held[block], preferred_element_type=jnp.float32
        ).astype(out_ref.dtype)

    mine = number(z, y, x, c)
    held[mine] = x_ref[...]
    for k in range(1, 4):
        for part in range(2):
            copy(mine, part, to_z.at[k - 1, part], z_peers[k - 1]).start()

    def first(k):
        return number((z + k) % 4, y, x, c)

    def second_y(k):
        return number((z + k) % 4, 1 - y, x, c)

    def second_x(k):
        return number((z + k) % 4, y, 1 - x, c)

    def third(k):
        return number((z + k) % 4, 1 - y, 1 - x, c)

    def forward_first(k):
        block = first(k)
        copy(block, 0, to_y.at[0, k], y_peer).start()
        copy(block, 1, to_x.at[0, k], x_peer).start()
        copy(block, 0, to_x.at[1, k], x_peer).start()
        copy(block, 1, to_y.at[1, k], y_peer).start()
        copy(block, 0, to_core.at[0, 0, k], core_peer).start()
        copy(block, 1, to_core.at[0, 1, k], core_peer).start()

    forward_first(0)
    pick(mine)

    @pl.loop(1, 4)
    def _(k):
        arrived(first(k), 0)
        arrived(first(k), 1)
        forward_first(k)
        pick(first(k))

    @pl.loop(0, 4)
    def _(k):
        arrived(second_y(k), 0)
        copy(second_y(k), 0, to_x.at[2, k], x_peer).start()
        copy(second_y(k), 0, to_core.at[1, 0, k], core_peer).start()
        arrived(second_x(k), 1)
        copy(second_x(k), 1, to_y.at[2, k], y_peer).start()
        copy(second_x(k), 1, to_core.at[2, 1, k], core_peer).start()
        block = number((z + k) % 4, y, x, 1 - c)
        arrived(block, 0)
        arrived(block, 1)
        pick(block)

    @pl.loop(0, 4)
    def _(k):
        arrived(second_x(k), 0)
        copy(second_x(k), 0, to_core.at[2, 0, k], core_peer).start()
        arrived(second_y(k), 1)
        copy(second_y(k), 1, to_core.at[1, 1, k], core_peer).start()
        pick(second_x(k))
        pick(second_y(k))

    @pl.loop(0, 4)
    def _(k):
        arrived(third(k), 0)
        copy(third(k), 0, to_core.at[3, 0, k], core_peer).start()
        arrived(third(k), 1)
        copy(third(k), 1, to_core.at[3, 1, k], core_peer).start()
        pick(third(k))
        for (yy, xx) in ((1 - y, x), (y, 1 - x)):
            block = number((z + k) % 4, yy, xx, 1 - c)
            arrived(block, 0)
            arrived(block, 1)
            pick(block)

    @pl.loop(0, 4)
    def _(k):
        block = number((z + k) % 4, 1 - y, 1 - x, 1 - c)
        arrived(block, 0)
        arrived(block, 1)
        pick(block)

    for k in range(1, 4):
        for part in range(2):
            copy(mine, part, to_z.at[k - 1, part], z_peers[k - 1]).wait_send()

    @pl.loop(0, 4)
    def _(k):
        for i in range(3):
            copy(mine, 0, to_y.at[i, k], y_peer).wait_send()
            copy(mine, 0, to_x.at[i, k], x_peer).wait_send()
        for i in range(4):
            for part in range(2):
                copy(mine, part, to_core.at[i, part, k], core_peer).wait_send()


def gather_pick(rows, select, collective_id):
    count, width = rows.shape
    blocks, kept = select.shape[:2]
    return pl.pallas_call(
        gather_kernel,
        out_shape=jax.ShapeDtypeStruct((blocks, kept, width), rows.dtype),
        in_specs=[pl.BlockSpec(memory_space=pltpu.VMEM)] * 2,
        out_specs=pl.BlockSpec(memory_space=pltpu.VMEM),
        scratch_shapes=[
            pltpu.VMEM((blocks, count, width), rows.dtype),
            pltpu.SemaphoreType.DMA((blocks, 2)),
            pltpu.SemaphoreType.DMA((3, 2)),
            pltpu.SemaphoreType.DMA((3, 4)),
            pltpu.SemaphoreType.DMA((3, 4)),
            pltpu.SemaphoreType.DMA((4, 2, 4)),
        ],
        compiler_params=pltpu.CompilerParams(
            collective_id=collective_id, has_side_effects=True, vmem_limit_bytes=56 << 20),
    )(rows, select)


def scatter_kernel(spread_ref, rows_ref, extra_ref, out_ref, extra_out, outgoing, core_in, total,
                   x_in, y_in, z_in, core_sent, core_got, x_sent, x_got, y_sent, y_got, z_sent, z_got):
    z, y, x, c = spot()
    width = rows_ref.shape[2]
    half = out_ref.shape[0] // 2
    y_peer, x_peer, core_peer = (
        where_is(z, 1 - y, x, c), where_is(z, y, 1 - x, c), where_is(z, y, x, 1 - c))
    greet([y_peer, x_peer, core_peer] + [where_is((z + k) % 4, y, x, c) for k in range(1, 4)])
    groups = ((1, 1), (0, 1), (1, 0), (0, 0))

    def part(block, place):
        place[:, pl.ds(0, width)] = jnp.dot(
            spread_ref[block], rows_ref[block], preferred_element_type=jnp.float32
        ).astype(place.dtype)
        place[:, pl.ds(width, 128)] = jnp.dot(
            spread_ref[block], extra_ref[block], preferred_element_type=jnp.float32
        ).astype(place.dtype)

    def block_of(group, k, core):
        other_y, other_x = groups[group]
        return number((z + k) % 4, 1 - y if other_y else y, 1 - x if other_x else x, core)

    def across(group, k):
        return pltpu.make_async_remote_copy(
            src_ref=outgoing.at[group, k], dst_ref=core_in.at[group, k],
            send_sem=core_sent.at[group, k], recv_sem=core_got.at[group, k],
            device_id=core_peer, device_id_type=MESH)

    def along(group, k, side, sent, got, target, slot, peer):
        return pltpu.make_async_remote_copy(
            src_ref=total.at[group, k, pl.ds(side * half, half)], dst_ref=target.at[slot, k],
            send_sem=sent.at[slot, k], recv_sem=got.at[slot, k],
            device_id=peer, device_id_type=MESH)

    def x_copy(group, k, side, slot):
        return along(group, k, side, x_sent, x_got, x_in, slot, x_peer)

    def y_copy(group, k, side, slot):
        return along(group, k, side, y_sent, y_got, y_in, slot, y_peer)

    def z_copy(k, side):
        return pltpu.make_async_remote_copy(
            src_ref=total.at[3, k, pl.ds(side * half, half)], dst_ref=z_in.at[k, side],
            send_sem=z_sent.at[k, side], recv_sem=z_got.at[k, side],
            device_id=where_is((z + k) % 4, y, x, c), device_id_type=MESH)

    def add(group, k, side, source):
        rows = pl.ds(side * half, half)
        total[group, k, rows] = (
            total[group, k, rows].astype(jnp.float32) + source.astype(jnp.float32)
        ).astype(total.dtype)

    order = (1, 2, 3, 0)
    for group in range(4):
        @pl.loop(0, 4)
        def _(i):
            k = (i + 1) % 4
            part(block_of(group, k, 1 - c), outgoing.at[group, k])
            across(group, k).start()
        @pl.loop(0, 4)
        def _(i):
            k = (i + 1) % 4
            part(block_of(group, k, c), total.at[group, k])
            across(group, k).wait_recv()
            total[group, k] = (
                total[group, k].astype(jnp.float32) + core_in[group, k].astype(jnp.float32)
            ).astype(total.dtype)
            if group == 0:
                x_copy(0, k, 0, 0).start()
                y_copy(0, k, 1, 0).start()
            if group == 1:
                x_copy(1, k, 0, 1).start()
            if group == 2:
                y_copy(2, k, 1, 1).start()

    @pl.loop(0, 4)
    def _(i):
        k = (i + 1) % 4
        x_copy(0, k, 0, 0).wait_recv()
        add(2, k, 0, x_in[0, k])
        y_copy(2, k, 0, 2).start()
        y_copy(0, k, 1, 0).wait_recv()
        add(1, k, 1, y_in[0, k])
        x_copy(1, k, 1, 2).start()

    @pl.loop(0, 4)
    def _(i):
        k = (i + 1) % 4
        x_copy(1, k, 0, 1).wait_recv()
        add(3, k, 0, x_in[1, k])
        y_copy(2, k, 1, 1).wait_recv()
        add(3, k, 1, y_in[1, k])

    @pl.loop(0, 4)
    def _(i):
        k = (i + 1) % 4
        y_copy(2, k, 0, 2).wait_recv()
        add(3, k, 0, y_in[2, k])
        x_copy(1, k, 1, 2).wait_recv()
        add(3, k, 1, x_in[2, k])

        @pl.when(i < 3)
        def _():
            z_copy(k, 0).start()
            z_copy(k, 1).start()

    for k in range(1, 4):
        for side in range(2):
            z_copy(k, side).wait_recv()
    for side in range(2):
        rows = pl.ds(side * half, half)
        sums = total[3, 0, rows].astype(jnp.float32)
        for k in range(1, 4):
            sums = sums + z_in[k, side].astype(jnp.float32)
        out_ref[rows] = sums[:, :width]
        extra_out[rows] = sums[:, width:]

    for k in range(1, 4):
        for side in range(2):
            z_copy(k, side).wait_send()

    @pl.loop(0, 4)
    def _(k):
        for group in range(4):
            across(group, k).wait_send()
        x_copy(0, k, 0, 0).wait_send()
        x_copy(1, k, 0, 1).wait_send()
        x_copy(1, k, 1, 2).wait_send()
        y_copy(0, k, 1, 0).wait_send()
        y_copy(2, k, 1, 1).wait_send()
        y_copy(2, k, 0, 2).wait_send()


def spread_scatter(spread, rows, extra, collective_id):
    blocks, count, kept = spread.shape
    width = rows.shape[2]
    wide = width + 128
    low = rows.dtype
    return pl.pallas_call(
        scatter_kernel,
        out_shape=(jax.ShapeDtypeStruct((count, width), jnp.float32),
                   jax.ShapeDtypeStruct((count, 128), jnp.float32)),
        in_specs=[pl.BlockSpec(memory_space=pltpu.VMEM)] * 3,
        out_specs=(pl.BlockSpec(memory_space=pltpu.VMEM), pl.BlockSpec(memory_space=pltpu.VMEM)),
        scratch_shapes=[
            pltpu.VMEM((4, 4, count, wide), low),
            pltpu.VMEM((4, 4, count, wide), low),
            pltpu.VMEM((4, 4, count, wide), low),
            pltpu.VMEM((3, 4, count // 2, wide), low),
            pltpu.VMEM((3, 4, count // 2, wide), low),
            pltpu.VMEM((4, 2, count // 2, wide), low),
            pltpu.SemaphoreType.DMA((4, 4)), pltpu.SemaphoreType.DMA((4, 4)),
            pltpu.SemaphoreType.DMA((3, 4)), pltpu.SemaphoreType.DMA((3, 4)),
            pltpu.SemaphoreType.DMA((3, 4)), pltpu.SemaphoreType.DMA((3, 4)),
            pltpu.SemaphoreType.DMA((4, 2)), pltpu.SemaphoreType.DMA((4, 2)),
        ],
        compiler_params=pltpu.CompilerParams(
            collective_id=collective_id, has_side_effects=True, vmem_limit_bytes=60 << 20),
    )(spread, rows, extra)


def reduce_kernel(part_ref, out_ref, held, y_in, z_in, final, gathered, y_sent, y_got, z_sent, z_got,
                  back_sent, back_got, side_sent, side_got):
    z, y, x, c = spot()
    y_peer = where_is(z, 1 - y, x, c)
    greet([y_peer] + [where_is((z + k) % 4, y, x, c) for k in range(1, 4)])

    def y_copy(k):
        spot_z = (z + k) % 4
        return pltpu.make_async_remote_copy(
            src_ref=part_ref.at[1 - y, spot_z], dst_ref=y_in.at[k],
            send_sem=y_sent.at[k], recv_sem=y_got.at[k], device_id=y_peer, device_id_type=MESH)

    def z_copy(k):
        return pltpu.make_async_remote_copy(
            src_ref=held.at[k], dst_ref=z_in.at[k],
            send_sem=z_sent.at[k], recv_sem=z_got.at[k],
            device_id=where_is((z + k) % 4, y, x, c), device_id_type=MESH)

    def back_copy(k):
        return pltpu.make_async_remote_copy(
            src_ref=gathered.at[0, 0], dst_ref=gathered.at[0, (4 - k) % 4],
            send_sem=back_sent.at[k], recv_sem=back_got.at[(4 - k) % 4],
            device_id=where_is((z + k) % 4, y, x, c), device_id_type=MESH)

    def back_arrived(k):
        return pltpu.make_async_remote_copy(
            src_ref=gathered.at[0, 0], dst_ref=gathered.at[0, k],
            send_sem=back_sent.at[k], recv_sem=back_got.at[k],
            device_id=where_is((z + k) % 4, y, x, c), device_id_type=MESH)

    def side_copy(k):
        return pltpu.make_async_remote_copy(
            src_ref=gathered.at[0, k], dst_ref=gathered.at[1, k],
            send_sem=side_sent.at[k], recv_sem=side_got.at[k], device_id=y_peer, device_id_type=MESH)

    @pl.loop(0, 4)
    def _(i):
        y_copy((i + 1) % 4).start()

    @pl.loop(0, 4)
    def _(i):
        k = (i + 1) % 4
        y_copy(k).wait_recv()
        held[k] = (part_ref[y, (z + k) % 4].astype(jnp.float32) + y_in[k].astype(jnp.float32)).astype(held.dtype)
        @pl.when(i < 3)
        def _():
            z_copy(k).start()

    for k in range(1, 4):
        z_copy(k).wait_recv()
    sums = held[0].astype(jnp.float32)
    for k in range(1, 4):
        sums = sums + z_in[k].astype(jnp.float32)
    gathered[0, 0] = sums.astype(gathered.dtype)
    for k in range(1, 4):
        back_copy(k).start()
    side_copy(0).start()
    out_ref[y, z] = gathered[0, 0].astype(out_ref.dtype)

    @pl.loop(1, 4)
    def _(k):
        back_arrived(k).wait_recv()
        side_copy(k).start()
        out_ref[y, (z + k) % 4] = gathered[0, k].astype(out_ref.dtype)

    @pl.loop(0, 4)
    def _(k):
        side_copy(k).wait_recv()
        out_ref[1 - y, (z + k) % 4] = gathered[1, k].astype(out_ref.dtype)

    @pl.loop(0, 4)
    def _(k):
        y_copy(k).wait_send()
        side_copy(k).wait_send()
    for k in range(1, 4):
        z_copy(k).wait_send()
        back_copy(k).wait_send()


def reduce_over_members(parts, collective_id):
    shape = parts.shape[2:]
    low = parts.dtype
    return pl.pallas_call(
        reduce_kernel,
        out_shape=jax.ShapeDtypeStruct(parts.shape, jnp.bfloat16),
        in_specs=[pl.BlockSpec(memory_space=pltpu.VMEM)],
        out_specs=pl.BlockSpec(memory_space=pltpu.VMEM),
        scratch_shapes=[
            pltpu.VMEM((4, *shape), low),
            pltpu.VMEM((4, *shape), low),
            pltpu.VMEM((4, *shape), low),
            pltpu.VMEM((8, 128), low),
            pltpu.VMEM((2, 4, *shape), low),
        ] + [pltpu.SemaphoreType.DMA((4,)) for _ in range(8)],
        compiler_params=pltpu.CompilerParams(
            collective_id=collective_id, has_side_effects=True, vmem_limit_bytes=60 << 20),
    )(parts)


def moe_gathered(normed, router, routes, capacity, cotangent, weights):
    gate_w, up_w, down_w = weights
    token_count = normed.shape[0]
    experts = router.shape[1]
    mine = lax.axis_index("exp") * lax.axis_size("fsdp") + lax.axis_index("fsdp")
    all_routes = lax.all_gather(routes, BOTH, axis=0, tiled=True)
    all_grads = lax.all_gather(cotangent, BOTH, axis=0, tiled=True)
    columns = jnp.arange(experts, dtype=jnp.int32)
    named = jnp.any(all_routes[:, :, None] == columns[None, None, :], axis=1)
    own = jnp.any(all_routes == mine, axis=1).reshape(experts, token_count)
    before = jnp.tril(jnp.ones((token_count, token_count), jnp.bfloat16), -1)
    rank = right_transposed(own.astype(jnp.bfloat16), before).astype(jnp.int32)
    places = jnp.arange(capacity, dtype=jnp.int32)
    select = (own[:, None, :] & (rank[:, None, :] == places[None, :, None])).astype(jnp.bfloat16)
    spread = (own[:, :, None] & (rank[:, :, None] == places[None, None, :])).astype(jnp.bfloat16)
    grad_rows = contract(
        "bcj,bjd->bcd", select, all_grads.reshape(experts, token_count, MODEL_WIDTH)
    ).astype(jnp.bfloat16)
    grad_rows = grad_rows.reshape(experts * capacity, MODEL_WIDTH)
    named_rows = contract(
        "bcj,bje->bce", select, named.astype(jnp.bfloat16).reshape(experts, token_count, experts)
    ).reshape(experts * capacity, experts)

    arrived = gather_pick(normed, select, 1).reshape(experts * capacity, MODEL_WIDTH)
    masked = jnp.where(named_rows > 0, matrix_product(arrived, router), MASKED)
    peak = jnp.max(masked, axis=1, keepdims=True)
    lifted = jnp.exp(masked - peak)
    row_gate = jnp.sum(
        jnp.where(columns[None, :] == mine, lifted, 0.0), axis=1, keepdims=True
    ) / jnp.sum(lifted, axis=1, keepdims=True)
    hidden = expert_forward(arrived, gate_w, up_w)
    active = hidden[3]
    out_rows = (row_gate * grad_rows.astype(jnp.float32)).astype(jnp.bfloat16)
    rows_back, gate_pre_grad, up_pre_grad = expert_back(out_rows, hidden, gate_w, up_w, down_w)
    produced = matrix_product(active, down_w).astype(jnp.bfloat16)
    row_grad = jnp.sum(
        produced.astype(jnp.float32) * grad_rows.astype(jnp.float32), axis=1, keepdims=True
    )
    weighted = (row_gate * produced.astype(jnp.float32)).astype(jnp.bfloat16)
    high, low = two_halves(row_grad)
    lanes = jnp.arange(128, dtype=jnp.int32)[None, :]
    zero = jnp.zeros((), jnp.bfloat16)
    extra = jnp.where(lanes == mine, high, jnp.where(lanes == experts + mine, low, zero))
    summed, back = spread_scatter(
        spread,
        rows_back.reshape(experts, capacity, MODEL_WIDTH),
        extra.reshape(experts, capacity, 128),
        2,
    )
    full = (
        contract("bjc,bcd->bjd", spread, weighted.reshape(experts, capacity, MODEL_WIDTH))
        .astype(jnp.bfloat16)
        .reshape(experts * token_count, MODEL_WIDTH)
    )
    summed, back, full, arrived, gate_pre_grad, up_pre_grad, active, out_rows = (
        lax.optimization_barrier(
            (summed, back, full, arrived, gate_pre_grad, up_pre_grad, active, out_rows)
        )
    )
    mixed = lax.psum_scatter(full, BOTH, scatter_dimension=0, tiled=True)
    weight_grads = (
        left_trans(arrived, gate_pre_grad),
        left_trans(arrived, up_pre_grad),
        left_trans(active, out_rows),
    )
    gate_grad = jnp.take_along_axis(
        back[:, :experts] + back[:, experts : 2 * experts], routes, axis=1
    )
    gates = gates_of(matrix_product(normed, router), routes, experts)
    return mixed.astype(jnp.float32), summed, gates, gate_grad, *weight_grads


def moe_exchanged(normed, router, routes, capacity, cotangent, weights):
    gate_w, up_w, down_w = weights
    token_count, topk = routes.shape
    experts = router.shape[1]
    gates = gates_of(matrix_product(normed, router), routes, experts)
    slots = slot_table(routes, experts, capacity)

    def send(rows):
        packed = jnp.zeros((experts * capacity, MODEL_WIDTH), jnp.bfloat16).at[slots].set(rows)
        return exchange(packed.reshape(experts, capacity, MODEL_WIDTH)).reshape(
            experts * capacity, MODEL_WIDTH
        )

    def bring(rows):
        rows = exchange(rows.reshape(experts, capacity, MODEL_WIDTH))
        return rows.reshape(experts * capacity, MODEL_WIDTH)[slots].reshape(
            token_count, topk, MODEL_WIDTH
        )

    arrived = send(jnp.repeat(normed, topk, axis=0))
    hidden = expert_forward(arrived, gate_w, up_w)
    scaled = (gates[:, :, None] * cotangent.astype(jnp.float32)[:, None, :]).astype(jnp.bfloat16)
    out_rows = send(scaled.reshape(token_count * topk, MODEL_WIDTH))
    rows_back, gate_pre_grad, up_pre_grad = expert_back(out_rows, hidden, gate_w, up_w, down_w)
    gate_w_grad = left_trans(arrived, gate_pre_grad)
    up_w_grad = left_trans(arrived, up_pre_grad)
    down_grad = left_trans(hidden[3], out_rows)
    returned = bring(matrix_product(hidden[3], down_w).astype(jnp.bfloat16))
    mixed = jnp.einsum("tk,tkd->td", gates, returned.astype(jnp.float32))
    gate_grad = jnp.einsum("td,tkd->tk", cotangent, returned, preferred_element_type=jnp.float32)
    summed = jnp.sum(bring(rows_back), axis=1, dtype=jnp.float32)
    return mixed, summed, gates, gate_grad, gate_w_grad, up_w_grad, down_grad


def local(
    tokens,
    lengths,
    routes,
    attn_gain,
    w_query,
    key_weight,
    value_weight,
    q_gain,
    k_gain,
    w_out,
    mlp_gain,
    w_router,
    expert_gate,
    expert_up,
    expert_down,
    cotangent,
):
    shards, members = lax.axis_size("fsdp"), lax.axis_size("exp")
    experts = shards * members
    token_count, topk = routes.shape
    capacity = 2 * token_count * topk // experts
    group = shards * token_count
    depth = w_query.shape[0]
    heads = QUERY_HEADS // shards
    kv_heads = max(1, KEY_VALUE_HEADS // shards)
    copies = shards * kv_heads // KEY_VALUE_HEADS
    head_group = heads // kv_heads
    wide, narrow = heads * HEAD_WIDTH, kv_heads * HEAD_WIDTH
    place = lax.axis_index("fsdp")

    gathered = lax.all_gather(
        jnp.concatenate([w_router.reshape(-1), attn_gain, mlp_gain, q_gain, k_gain]), "fsdp"
    )
    cuts, start = [], 0
    for leaf in (w_router, attn_gain, mlp_gain, q_gain, k_gain):
        cuts.append(gathered[:, start : start + leaf.size])
        start += leaf.size
    router = cuts[0].reshape(MODEL_WIDTH, experts)
    gain_attn, gain_mlp, gain_query, gain_key = [
        cut.reshape(-1).astype(jnp.float32) for cut in cuts[1:]
    ]
    all_lengths = lax.all_gather(lengths[0], "fsdp")

    def by_shard(weight):
        weight = weight.reshape(depth, KEY_VALUE_HEADS, HEAD_WIDTH)
        return jnp.repeat(weight, copies, axis=1).reshape(depth, shards, narrow)

    joined = jnp.concatenate(
        [w_query.reshape(depth, shards, wide), by_shard(key_weight), by_shard(value_weight)], axis=2
    ).transpose(1, 0, 2)

    inputs = tokens.astype(jnp.float32)
    scale_one = rms_scale(inputs)
    first_normed = (inputs * scale_one * gain_attn).astype(jnp.bfloat16)
    hidden = lax.all_to_all(first_normed, "fsdp", split_axis=1, concat_axis=0, tiled=True)
    partial = contract("gk,nkc->ngc", hidden, joined).astype(jnp.bfloat16)
    raw = lax.psum_scatter(partial, "fsdp", scatter_dimension=0, tiled=True)[0].astype(jnp.float32)
    raw = raw.reshape(shards, token_count, wide + 2 * narrow)
    query_raw = raw[:, :, :wide].reshape(shards, token_count, heads, HEAD_WIDTH)
    key_raw = raw[:, :, wide : wide + narrow].reshape(shards, token_count, kv_heads, HEAD_WIDTH)
    value = (
        raw[:, :, wide + narrow :]
        .astype(jnp.bfloat16)
        .reshape(shards, token_count, kv_heads, HEAD_WIDTH)
    )
    position, allowed = jax.vmap(lambda row: seq_layout(row, token_count))(all_lengths)
    cosine, sine = rotary_tables(position, HEAD_WIDTH)
    query_scale = rms_scale(query_raw)
    query_hat = query_raw * query_scale
    key_scale = rms_scale(key_raw)
    key_hat = key_raw * key_scale
    query = (
        rotate(query_hat * gain_query, cosine, sine)
        .astype(jnp.bfloat16)
        .reshape(shards, token_count, kv_heads, head_group, HEAD_WIDTH)
    )
    key = rotate(key_hat * gain_key, cosine, sine).astype(jnp.bfloat16)
    scores = contract("bqkgd,bpkd->bkgqp", query, key) * HEAD_WIDTH ** (-0.5)
    scores = jnp.where(allowed[:, None, None], scores, MASKED)
    top = jnp.max(scores, axis=-1, keepdims=True)
    raised = jnp.exp(scores - top)
    probs = raised / jnp.sum(raised, axis=-1, keepdims=True)
    probs_low = probs.astype(jnp.bfloat16)
    attended = contract("bkgqp,bpkd->bqkgd", probs_low, value).astype(jnp.bfloat16)
    attended = attended.reshape(group, wide)
    mixed_heads = lax.psum_scatter(
        matrix_product(attended, w_out).astype(jnp.bfloat16), "fsdp", scatter_dimension=0, tiled=True
    )
    middle = inputs + mixed_heads.astype(jnp.float32)
    scale_two = rms_scale(middle)
    normed = (middle * scale_two * gain_mlp).astype(jnp.bfloat16)

    dense = (members, shards) == (8, 4) and 2 * capacity >= token_count
    moe = moe_gathered if dense else moe_exchanged
    mixed, summed, gates, gate_grad, gate_w_grad, up_w_grad, down_grad = moe(
        normed,
        router,
        routes,
        capacity,
        cotangent,
        (expert_gate[0], expert_up[0], expert_down[0]),
    )
    layer_out = (middle + mixed).astype(jnp.bfloat16)

    upstream = cotangent.astype(jnp.float32)
    picked_grad = gates * (gate_grad - jnp.sum(gates * gate_grad, axis=1, keepdims=True))
    onehot = routes[:, :, None] == jnp.arange(experts, dtype=jnp.int32)[None, None, :]
    logit_grad = jnp.sum(jnp.where(onehot, picked_grad[:, :, None], 0.0), axis=1).astype(
        jnp.bfloat16
    )
    normed_grad = summed + right_transposed(logit_grad, router)
    mlp_gain_grad = jnp.sum(normed_grad * middle * scale_two, axis=0)
    router_grad = left_trans(normed, logit_grad)
    middle_grad = upstream + rms_back(normed_grad * gain_mlp, middle, scale_two)
    branch_grad = lax.all_gather(middle_grad.astype(jnp.bfloat16), "fsdp", axis=0, tiled=True)
    out_w_grad = left_trans(attended, branch_grad)
    attended_grad = (
        right_transposed(branch_grad, w_out)
        .astype(jnp.bfloat16)
        .reshape(shards, token_count, kv_heads, head_group, HEAD_WIDTH)
    )
    prob_grad = contract("bqkgd,bpkd->bkgqp", attended_grad, value)
    value_grad = contract("bkgqp,bqkgd->bpkd", probs_low, attended_grad)
    balance = jnp.sum(probs * prob_grad, axis=-1, keepdims=True)
    score_grad = (probs * (prob_grad - balance)).astype(jnp.bfloat16)
    query_norm_grad = contract("bkgqp,bpkd->bqkgd", score_grad, key) * HEAD_WIDTH ** (-0.5)
    query_norm_grad = query_norm_grad.reshape(shards, token_count, heads, HEAD_WIDTH)
    key_norm_grad = contract("bkgqp,bqkgd->bpkd", score_grad, query) * HEAD_WIDTH ** (-0.5)
    query_norm_grad = rotate_back(query_norm_grad, cosine, sine)
    key_norm_grad = rotate_back(key_norm_grad, cosine, sine)
    q_gain_grad = jnp.sum(query_norm_grad * query_hat, axis=(0, 1, 2))
    k_gain_grad = jnp.sum(key_norm_grad * key_hat, axis=(0, 1, 2))
    query_grad = rms_back(query_norm_grad * gain_query, query_raw, query_scale)
    key_grad = rms_back(key_norm_grad * gain_key, key_raw, key_scale)
    head_grads = jnp.concatenate(
        [
            query_grad.reshape(group, wide),
            key_grad.reshape(group, narrow),
            value_grad.reshape(group, narrow),
        ],
        axis=1,
    ).astype(jnp.bfloat16)
    head_grads = lax.all_gather(head_grads, "fsdp")
    hidden_grad = contract("ngc,nkc->gk", head_grads, joined).astype(jnp.bfloat16)
    first_grad = lax.all_to_all(
        hidden_grad, "fsdp", split_axis=0, concat_axis=1, tiled=True
    ).astype(jnp.float32)
    attn_gain_grad = jnp.sum(first_grad * inputs * scale_one, axis=0)
    input_grad = (middle_grad + rms_back(first_grad * gain_attn, inputs, scale_one)).astype(
        jnp.bfloat16
    )
    joined_grad = contract("gk,ngc->nkc", hidden, head_grads).astype(jnp.bfloat16)

    out_sum = lax.psum(out_w_grad.astype(jnp.bfloat16), "exp").astype(jnp.float32)
    if dense:
        joined_sum = reduce_over_members(joined_grad.reshape(2, 4, -1, wide + 2 * narrow), 3)
        joined_sum = joined_sum.reshape(joined_grad.shape).astype(jnp.float32)
    else:
        joined_sum = lax.psum(joined_grad, "exp").astype(jnp.float32)

    def all_summed(vectors, leaves):
        vectors, cuts, start = lax.psum(vectors, BOTH), [], 0
        for leaf in leaves:
            cut = lax.dynamic_slice_in_dim(vectors, start + place * leaf.size, leaf.size)
            cuts.append(cut.reshape(leaf.shape))
            start += leaf.size * shards
        return cuts

    router_sum, mlp_sum = all_summed(
        jnp.concatenate([router_grad.reshape(-1), mlp_gain_grad]), (w_router, mlp_gain)
    )
    attn_sum, q_sum, k_sum = all_summed(
        jnp.concatenate([attn_gain_grad, q_gain_grad, k_gain_grad]), (attn_gain, q_gain, k_gain)
    )

    def gather_heads(part):
        return part.transpose(1, 0, 2).reshape(depth, KEY_VALUE_HEADS, copies, HEAD_WIDTH).sum(
            axis=2
        ).reshape(depth, KEY_VALUE_HEADS * HEAD_WIDTH)

    return (
        layer_out,
        input_grad,
        attn_sum,
        joined_sum[:, :, :wide].transpose(1, 0, 2).reshape(depth, QUERY_HEADS * HEAD_WIDTH),
        gather_heads(joined_sum[:, :, wide : wide + narrow]),
        gather_heads(joined_sum[:, :, wide + narrow :]),
        q_sum,
        k_sum,
        out_sum,
        mlp_sum,
        router_sum,
        gate_w_grad[None],
        up_w_grad[None],
        down_grad[None],
    )


def solution(mesh):
    in_specs = (
        P(("exp", "fsdp"), None),
        P(("exp", "fsdp"), None),
        P(("exp", "fsdp"), None),
        P("fsdp"),
        P("fsdp", None),
        P("fsdp", None),
        P("fsdp", None),
        P("fsdp"),
        P("fsdp"),
        P("fsdp", None),
        P("fsdp"),
        P("fsdp", None),
        P(("exp", "fsdp"), None, None),
        P(("exp", "fsdp"), None, None),
        P(("exp", "fsdp"), None, None),
        P(("exp", "fsdp"), None),
    )
    out_specs = (
        P(("exp", "fsdp"), None),
        P(("exp", "fsdp"), None),
        P("fsdp"),
        P("fsdp", None),
        P("fsdp", None),
        P("fsdp", None),
        P("fsdp"),
        P("fsdp"),
        P("fsdp", None),
        P("fsdp"),
        P("fsdp", None),
        P(("exp", "fsdp"), None, None),
        P(("exp", "fsdp"), None, None),
        P(("exp", "fsdp"), None, None),
    )
    return jax.shard_map(local, mesh=mesh, in_specs=in_specs, out_specs=out_specs, check_vma=False)
```

```python
import math

import jax
import jax.numpy as jnp
from jax import lax
from jax.experimental import pallas as pl
from jax.experimental.pallas import tpu as pltpu
from jax.sharding import PartitionSpec as P

MODEL_WIDTH = 2048
QUERY_HEADS = 32
KEY_VALUE_HEADS = 4
HEAD_WIDTH = 128


EPSILON = 1e-06
THETA = 1000000.0
MASKED = -1e30
BOTH = ("exp", "fsdp")
MESH = pl.DeviceIdType.MESH


def matrix_product(left, right):
    return jnp.dot(left, right, preferred_element_type=jnp.float32)


def left_trans(left, right):
    return lax.dot_general(
        left, right, (((0,), (0,)), ((), ())), preferred_element_type=jnp.float32
    )


def right_transposed(left, right):
    return lax.dot_general(
        left, right, (((1,), (1,)), ((), ())), preferred_element_type=jnp.float32
    )


def contract(spec, left, right):
    return jnp.einsum(spec, left, right, preferred_element_type=jnp.float32)


def rms_scale(values):
    return lax.rsqrt(jnp.mean(values * values, axis=-1, keepdims=True) + EPSILON)


def rms_back(grad_hat, values, scale):
    normal = values * scale
    return scale * (grad_hat - normal * jnp.mean(grad_hat * normal, axis=-1, keepdims=True))


def seq_layout(length_row, token_count):
    ends = jnp.cumsum(length_row)
    starts = ends - length_row
    places = jnp.arange(token_count, dtype=jnp.int32)
    member = (places[:, None] >= starts[None, :]) & (places[:, None] < ends[None, :])
    numbers = jnp.arange(length_row.shape[0], dtype=jnp.int32)
    segment = jnp.sum(jnp.where(member, numbers[None, :], 0), axis=1)
    position = places - jnp.sum(jnp.where(member, starts[None, :], 0), axis=1)
    allowed = (segment[:, None] == segment[None, :]) & (places[None, :] <= places[:, None])
    return (position, allowed)


def rotary_tables(position, head_size):
    half = head_size // 2
    index = jnp.arange(head_size, dtype=jnp.int32) % half
    inverse = jnp.exp(index.astype(jnp.float32) * (-2.0 * math.log(THETA) / head_size))
    angles = position.astype(jnp.float32)[..., None] * inverse
    return (jnp.cos(angles)[..., None, :], jnp.sin(angles)[..., None, :])


def rotate(values, cosine, sine):
    half = values.shape[-1] // 2
    turned = jnp.concatenate([-values[..., half:], values[..., :half]], axis=-1)
    return values * cosine + turned * sine


def rotate_back(grads, cosine, sine):
    half = grads.shape[-1] // 2
    moved = grads * sine
    return grads * cosine + jnp.concatenate([moved[..., half:], -moved[..., :half]], axis=-1)


def slot_table(route_rows, experts, capacity):
    flat = route_rows.reshape(-1)
    onehot = (flat[:, None] == jnp.arange(experts, dtype=jnp.int32)[None, :]).astype(jnp.int32)
    ranks = jnp.cumsum(onehot, axis=0) - 1
    rank = jnp.sum(ranks * onehot, axis=1)
    return flat * capacity + rank


def exchange(buffer):
    return lax.all_to_all(buffer, BOTH, split_axis=0, concat_axis=0, tiled=True)


def two_halves(values):
    high = values.astype(jnp.bfloat16)
    low = (values - high.astype(jnp.float32)).astype(jnp.bfloat16)
    return high, low


def expert_forward(arrived, gate_w, up_w):
    gate_pre = matrix_product(arrived, gate_w)
    up_pre = matrix_product(arrived, up_w)
    sigma = jax.nn.sigmoid(gate_pre)
    active = (gate_pre * sigma * up_pre).astype(jnp.bfloat16)
    return gate_pre, up_pre, sigma, active


def expert_back(out_rows, hidden, gate_w, up_w, down_w):
    gate_pre, up_pre, sigma, _ = hidden
    active_grad = right_transposed(out_rows, down_w)
    gate_pre_grad = (active_grad * up_pre * (sigma * (1.0 + gate_pre * (1.0 - sigma)))).astype(
        jnp.bfloat16
    )
    up_pre_grad = (active_grad * (gate_pre * sigma)).astype(jnp.bfloat16)
    rows_back = right_transposed(gate_pre_grad, gate_w) + right_transposed(up_pre_grad, up_w)
    return rows_back.astype(jnp.bfloat16), gate_pre_grad, up_pre_grad


def gates_of(logits, routes, experts):
    picked = jnp.take_along_axis(logits, routes, axis=1)
    peak = jnp.max(picked, axis=1, keepdims=True)
    lifted = jnp.exp(picked - peak)
    return lifted / jnp.sum(lifted, axis=1, keepdims=True)


def spot():
    member, shard = lax.axis_index("exp"), lax.axis_index("fsdp")
    return member // 2, member % 2, shard // 2, shard % 2


def where_is(z, y, x, c):
    return (z * 2 + y, x * 2 + c)


def number(z, y, x, c):
    return z * 8 + y * 4 + x * 2 + c


def greet(peers):
    barrier = pltpu.get_barrier_semaphore()
    for peer in peers:
        pl.semaphore_signal(barrier, inc=1, device_id=peer, device_id_type=MESH)
    pl.semaphore_wait(barrier, len(peers))


def remote(source, target, sent, got, peer):
    return pltpu.make_async_remote_copy(
        src_ref=source,
        dst_ref=target,
        send_sem=sent,
        recv_sem=got,
        device_id=peer,
        device_id_type=MESH,
    )


def in_vmem(count):
    return [pl.BlockSpec(memory_space=pltpu.VMEM)] * count


def copies(*shape):
    return pltpu.SemaphoreType.DMA(shape)


def settings(collective_id):
    return pltpu.CompilerParams(
        collective_id=collective_id, has_side_effects=True, vmem_limit_bytes=60 << 20
    )


def gather_kernel(
    x_ref,
    select_ref,
    ahead_ref,
    named_ref,
    gate_ref,
    up_ref,
    router_ref,
    rows_out,
    active_out,
    gate_out,
    up_out,
    share_out,
    extra_out,
    held,
    picked,
    arrive,
    to_z,
    to_y,
    to_x,
    to_core,
):
    z, y, x, c = spot()
    half = x_ref.shape[0] // 2
    kept = select_ref.shape[1]
    y_peer, x_peer, core_peer = (
        where_is(z, 1 - y, x, c),
        where_is(z, y, 1 - x, c),
        where_is(z, y, x, 1 - c),
    )
    z_peers = [where_is((z + k) % 4, y, x, c) for k in range(1, 4)]
    greet([y_peer, x_peer, core_peer] + z_peers)
    mine = number(z, y, x, c)

    def copy(block, part, sem, peer):
        view = held.at[block, pl.ds(part * half, half)]
        return remote(view, view, sem, arrive.at[block, part], peer)

    def arrived(block, part):
        copy(block, part, to_core.at[0, 0, 0], core_peer).wait_recv()

    def block_of(group, k):
        other_y, other_x, other_core = group
        return number(
            (z + k) % 4,
            1 - y if other_y else y,
            1 - x if other_x else x,
            1 - c if other_core else c,
        )

    def work(group):
        blocks = [block_of(group, k) for k in range(4)]

        @pl.loop(0, 4)
        def _(k):
            block = block_of(group, k)
            rows = jnp.dot(
                select_ref[block], held[block], preferred_element_type=jnp.float32
            ).astype(picked.dtype)
            picked[pl.ds(k * kept, kept)] = rows
            rows_out[block] = rows

        rows = picked[...]
        gate_pre = jnp.dot(rows, gate_ref[...], preferred_element_type=jnp.float32)
        up_pre = jnp.dot(rows, up_ref[...], preferred_element_type=jnp.float32)
        logits = jnp.dot(rows, router_ref[...], preferred_element_type=jnp.float32)
        for k in range(4):
            part = slice(k * kept, (k + 1) * kept)
            block = blocks[k]
            masked = jnp.where(named_ref[block].astype(jnp.float32) > 0, logits[part], MASKED)
            lifted = jnp.exp(masked - jnp.max(masked, axis=1, keepdims=True))
            lanes = lax.broadcasted_iota(jnp.int32, lifted.shape, 1)
            share = jnp.sum(jnp.where(lanes == mine, lifted, 0.0), axis=1, keepdims=True)
            share = share / jnp.sum(lifted, axis=1, keepdims=True)
            gate, up, ahead = gate_pre[part], up_pre[part], ahead_ref[block]
            sigma = 1.0 / (1.0 + jnp.exp(-gate))
            silu = gate * sigma
            active = silu * up
            active_low = active.astype(active_out.dtype)
            grad = jnp.sum(active_low.astype(jnp.float32) * ahead, axis=1, keepdims=True)
            active_grad = share * ahead
            active_out[block] = active_low
            gate_out[block] = (active_grad * up * (sigma * (1.0 + gate * (1.0 - sigma)))).astype(
                gate_out.dtype
            )
            up_out[block] = (active_grad * silu).astype(up_out.dtype)
            share_out[block] = jnp.broadcast_to(share, share_out.shape[1:])
            high = grad.astype(extra_out.dtype).astype(jnp.float32)
            both = jnp.where(
                lanes == mine, high, jnp.where(lanes == 32 + mine, grad - high, 0.0)
            )
            extra_out[block] = both.astype(extra_out.dtype)

    held[mine] = x_ref[...]
    for k in range(1, 4):
        for part in range(2):
            copy(mine, part, to_z.at[k - 1, part], z_peers[k - 1]).start()

    def forward_first(k):
        block = block_of((0, 0, 0), k)
        copy(block, 0, to_y.at[0, k], y_peer).start()
        copy(block, 1, to_x.at[0, k], x_peer).start()
        copy(block, 0, to_x.at[1, k], x_peer).start()
        copy(block, 1, to_y.at[1, k], y_peer).start()
        copy(block, 0, to_core.at[0, 0, k], core_peer).start()
        copy(block, 1, to_core.at[0, 1, k], core_peer).start()

    forward_first(0)

    @pl.loop(1, 4)
    def _(k):
        block = block_of((0, 0, 0), k)
        arrived(block, 0)
        arrived(block, 1)
        forward_first(k)

    work((0, 0, 0))

    @pl.loop(0, 4)
    def _(k):
        block = block_of((1, 0, 0), k)
        arrived(block, 0)
        copy(block, 0, to_x.at[2, k], x_peer).start()
        copy(block, 0, to_core.at[1, 0, k], core_peer).start()
        block = block_of((0, 1, 0), k)
        arrived(block, 1)
        copy(block, 1, to_y.at[2, k], y_peer).start()
        copy(block, 1, to_core.at[2, 1, k], core_peer).start()
        block = block_of((0, 0, 1), k)
        arrived(block, 0)
        arrived(block, 1)

    work((0, 0, 1))

    @pl.loop(0, 4)
    def _(k):
        block = block_of((0, 1, 0), k)
        arrived(block, 0)
        copy(block, 0, to_core.at[2, 0, k], core_peer).start()
        block = block_of((1, 0, 0), k)
        arrived(block, 1)
        copy(block, 1, to_core.at[1, 1, k], core_peer).start()

    work((0, 1, 0))
    work((1, 0, 0))
    for group in ((0, 1, 1), (1, 0, 1)):

        @pl.loop(0, 4)
        def _(k):
            block = block_of(group, k)
            arrived(block, 0)
            arrived(block, 1)

        work(group)

    @pl.loop(0, 4)
    def _(k):
        block = block_of((1, 1, 0), k)
        arrived(block, 0)
        copy(block, 0, to_core.at[3, 0, k], core_peer).start()
        arrived(block, 1)
        copy(block, 1, to_core.at[3, 1, k], core_peer).start()

    work((1, 1, 0))

    @pl.loop(0, 4)
    def _(k):
        block = block_of((1, 1, 1), k)
        arrived(block, 0)
        arrived(block, 1)

    work((1, 1, 1))
    for k in range(1, 4):
        for part in range(2):
            copy(mine, part, to_z.at[k - 1, part], z_peers[k - 1]).wait_send()

    @pl.loop(0, 4)
    def _(k):
        for i in range(3):
            copy(mine, 0, to_y.at[i, k], y_peer).wait_send()
            copy(mine, 0, to_x.at[i, k], x_peer).wait_send()
        for i in range(4):
            for part in range(2):
                copy(mine, part, to_core.at[i, part, k], core_peer).wait_send()


def gather_experts(rows, select, ahead, named, gate_w, up_w, router):
    count, width = rows.shape
    blocks, kept = select.shape[:2]
    hidden = gate_w.shape[1]
    low = rows.dtype
    return pl.pallas_call(
        gather_kernel,
        out_shape=[
            jax.ShapeDtypeStruct((blocks, kept, width), low),
            jax.ShapeDtypeStruct((blocks, kept, hidden), low),
            jax.ShapeDtypeStruct((blocks, kept, hidden), low),
            jax.ShapeDtypeStruct((blocks, kept, hidden), low),
            jax.ShapeDtypeStruct((blocks, kept, 128), jnp.float32),
            jax.ShapeDtypeStruct((blocks, kept, 128), low),
        ],
        in_specs=in_vmem(7),
        out_specs=in_vmem(6),
        scratch_shapes=[
            pltpu.VMEM((blocks, count, width), low),
            pltpu.VMEM((4 * kept, width), low),
            copies(blocks, 2),
            copies(3, 2),
            copies(3, 4),
            copies(3, 4),
            copies(4, 2, 4),
        ],
        compiler_params=settings(1),
    )(rows, select, ahead, named, gate_w, up_w, router)


def scatter_kernel(
    spread_ref,
    gate_grad_ref,
    up_grad_ref,
    gate_ref,
    up_ref,
    extra_ref,
    out_ref,
    extra_out,
    outgoing,
    core_in,
    total,
    back,
    x_in,
    y_in,
    z_in,
    core_sent,
    core_got,
    x_sent,
    x_got,
    y_sent,
    y_got,
    z_sent,
    z_got,
):
    z, y, x, c = spot()
    width = out_ref.shape[1]
    half = out_ref.shape[0] // 2
    kept = spread_ref.shape[2]
    y_peer, x_peer, core_peer = (
        where_is(z, 1 - y, x, c),
        where_is(z, y, 1 - x, c),
        where_is(z, y, x, 1 - c),
    )
    greet([y_peer, x_peer, core_peer] + [where_is((z + k) % 4, y, x, c) for k in range(1, 4)])
    groups = ((1, 1), (0, 1), (1, 0), (0, 0))

    def block_of(group, k, core):
        other_y, other_x = groups[group]
        return number((z + k) % 4, 1 - y if other_y else y, 1 - x if other_x else x, core)

    def rows_back(group, core):
        gate_grads = jnp.concatenate(
            [gate_grad_ref[block_of(group, k, core)] for k in range(4)], axis=0
        )
        up_grads = jnp.concatenate(
            [up_grad_ref[block_of(group, k, core)] for k in range(4)], axis=0
        )
        sums = right_transposed(gate_grads, gate_ref[...])
        back[...] = (sums + right_transposed(up_grads, up_ref[...])).astype(back.dtype)

    def part(block, k, place):
        place[:, pl.ds(0, width)] = jnp.dot(
            spread_ref[block], back[pl.ds(k * kept, kept)], preferred_element_type=jnp.float32
        ).astype(place.dtype)
        place[:, pl.ds(width, 128)] = jnp.dot(
            spread_ref[block], extra_ref[block], preferred_element_type=jnp.float32
        ).astype(place.dtype)

    def across(group, k):
        return remote(
            outgoing.at[group, k],
            core_in.at[group, k],
            core_sent.at[group, k],
            core_got.at[group, k],
            core_peer,
        )

    def view(group, k, side):
        return total.at[group, k, pl.ds(side * half, half)]

    def x_copy(group, k, side, slot):
        return remote(
            view(group, k, side), x_in.at[slot, k], x_sent.at[slot, k], x_got.at[slot, k], x_peer
        )

    def y_copy(group, k, side, slot):
        return remote(
            view(group, k, side), y_in.at[slot, k], y_sent.at[slot, k], y_got.at[slot, k], y_peer
        )

    def z_copy(k, side):
        return remote(
            view(3, k, side),
            z_in.at[k, side],
            z_sent.at[k, side],
            z_got.at[k, side],
            where_is((z + k) % 4, y, x, c),
        )

    def add(group, k, side, source):
        rows = pl.ds(side * half, half)
        total[group, k, rows] = (
            total[group, k, rows].astype(jnp.float32) + source.astype(jnp.float32)
        ).astype(total.dtype)

    for group in range(4):
        rows_back(group, 1 - c)

        @pl.loop(0, 4)
        def _(i):
            k = (i + 1) % 4
            part(block_of(group, k, 1 - c), k, outgoing.at[group, k])
            across(group, k).start()

        rows_back(group, c)

        @pl.loop(0, 4)
        def _(i):
            k = (i + 1) % 4
            part(block_of(group, k, c), k, total.at[group, k])
            across(group, k).wait_recv()
            total[group, k] = (
                total[group, k].astype(jnp.float32) + core_in[group, k].astype(jnp.float32)
            ).astype(total.dtype)
            if group == 0:
                x_copy(0, k, 0, 0).start()
                y_copy(0, k, 1, 0).start()
            if group == 1:
                x_copy(1, k, 0, 1).start()
            if group == 2:
                y_copy(2, k, 1, 1).start()

    @pl.loop(0, 4)
    def _(i):
        k = (i + 1) % 4
        x_copy(0, k, 0, 0).wait_recv()
        add(2, k, 0, x_in[0, k])
        y_copy(2, k, 0, 2).start()
        y_copy(0, k, 1, 0).wait_recv()
        add(1, k, 1, y_in[0, k])
        x_copy(1, k, 1, 2).start()

    @pl.loop(0, 4)
    def _(i):
        k = (i + 1) % 4
        x_copy(1, k, 0, 1).wait_recv()
        add(3, k, 0, x_in[1, k])
        y_copy(2, k, 1, 1).wait_recv()
        add(3, k, 1, y_in[1, k])

    @pl.loop(0, 4)
    def _(i):
        k = (i + 1) % 4
        y_copy(2, k, 0, 2).wait_recv()
        add(3, k, 0, y_in[2, k])
        x_copy(1, k, 1, 2).wait_recv()
        add(3, k, 1, x_in[2, k])

        @pl.when(i < 3)
        def _():
            z_copy(k, 0).start()
            z_copy(k, 1).start()

    for k in range(1, 4):
        for side in range(2):
            z_copy(k, side).wait_recv()
    for side in range(2):
        rows = pl.ds(side * half, half)
        sums = total[3, 0, rows].astype(jnp.float32)
        for k in range(1, 4):
            sums = sums + z_in[k, side].astype(jnp.float32)
        out_ref[rows] = sums[:, :width]
        extra_out[rows] = sums[:, width:]

    for k in range(1, 4):
        for side in range(2):
            z_copy(k, side).wait_send()

    @pl.loop(0, 4)
    def _(k):
        for group in range(4):
            across(group, k).wait_send()
        x_copy(0, k, 0, 0).wait_send()
        x_copy(1, k, 0, 1).wait_send()
        x_copy(1, k, 1, 2).wait_send()
        y_copy(0, k, 1, 0).wait_send()
        y_copy(2, k, 1, 1).wait_send()
        y_copy(2, k, 0, 2).wait_send()


def scatter_experts(spread, gate_grad, up_grad, gate_w, up_w, extra):
    blocks, count, kept = spread.shape
    width = gate_w.shape[0]
    wide = width + 128
    low = gate_grad.dtype
    return pl.pallas_call(
        scatter_kernel,
        out_shape=(
            jax.ShapeDtypeStruct((count, width), jnp.float32),
            jax.ShapeDtypeStruct((count, 128), jnp.float32),
        ),
        in_specs=in_vmem(6),
        out_specs=tuple(in_vmem(2)),
        scratch_shapes=[
            pltpu.VMEM((4, 4, count, wide), low),
            pltpu.VMEM((4, 4, count, wide), low),
            pltpu.VMEM((4, 4, count, wide), low),
            pltpu.VMEM((4 * kept, width), low),
            pltpu.VMEM((3, 4, count // 2, wide), low),
            pltpu.VMEM((3, 4, count // 2, wide), low),
            pltpu.VMEM((4, 2, count // 2, wide), low),
            copies(4, 4),
            copies(4, 4),
            copies(3, 4),
            copies(3, 4),
            copies(3, 4),
            copies(3, 4),
            copies(4, 2),
            copies(4, 2),
        ],
        compiler_params=settings(2),
    )(spread, gate_grad, up_grad, gate_w, up_w, extra)


def reduce_kernel(
    first_ref,
    second_ref,
    vector_ref,
    first_out,
    second_out,
    vector_out,
    first_y,
    second_y,
    first_held,
    second_held,
    first_z,
    second_z,
    first_all,
    second_all,
    shard_in,
    member_own,
    member_in,
    y_sent,
    y_got,
    z_sent,
    z_got,
    back_sent,
    back_got,
    side_sent,
    side_got,
    shard_sent,
    shard_got,
    member_sent,
    member_got,
):
    z, y, x, c = spot()
    member, shard = lax.axis_index("exp"), lax.axis_index("fsdp")
    y_peer = where_is(z, 1 - y, x, c)
    members = [((member + j) % 8, shard) for j in range(8)]
    shards = [(member, (shard + j) % 4) for j in range(4)]
    greet(members[1:] + shards[1:])
    arrays = (
        (first_ref, first_out, first_y, first_held, first_z, first_all),
        (second_ref, second_out, second_y, second_held, second_z, second_all),
    )

    def shard_copy(j):
        return remote(
            vector_ref.at[(shard + j) % 4],
            shard_in.at[(4 - j) % 4],
            shard_sent.at[j],
            shard_got.at[(4 - j) % 4],
            shards[j],
        )

    def member_copy(j):
        return remote(
            member_own,
            member_in.at[(8 - j) % 8],
            member_sent.at[j],
            member_got.at[(8 - j) % 8],
            members[j],
        )

    def y_copy(which, k):
        source, _, target = arrays[which][:3]
        return remote(
            source.at[1 - y, (z + k) % 4],
            target.at[k],
            y_sent.at[which, k],
            y_got.at[which, k],
            y_peer,
        )

    def z_copy(which, k):
        return remote(
            arrays[which][3].at[k],
            arrays[which][4].at[k],
            z_sent.at[which, k],
            z_got.at[which, k],
            where_is((z + k) % 4, y, x, c),
        )

    def back_copy(which, k, slot):
        every = arrays[which][5]
        return remote(
            every.at[0, 0],
            every.at[0, slot],
            back_sent.at[which, k],
            back_got.at[which, slot],
            where_is((z + k) % 4, y, x, c),
        )

    def side_copy(which, k):
        every = arrays[which][5]
        return remote(
            every.at[0, k], every.at[1, k], side_sent.at[which, k], side_got.at[which, k], y_peer
        )

    for j in range(1, 4):
        shard_copy(j).start()

    @pl.loop(0, 4)
    def _(i):
        for which in range(2):
            y_copy(which, (i + 1) % 4).start()

    for j in range(1, 4):
        shard_copy(j).wait_recv()
    sums = vector_ref[shard]
    for j in range(1, 4):
        sums = sums + shard_in[j]
    member_own[...] = sums
    for j in range(1, 8):
        member_copy(j).start()

    @pl.loop(0, 4)
    def _(i):
        k = (i + 1) % 4
        for which in range(2):
            source, _, got, held = arrays[which][:4]
            y_copy(which, k).wait_recv()
            held[k] = (
                source[y, (z + k) % 4].astype(jnp.float32) + got[k].astype(jnp.float32)
            ).astype(held.dtype)

            @pl.when(i < 3)
            def _():
                z_copy(which, k).start()

    for which in range(2):
        _, out, _, held, got, every = arrays[which]
        for k in range(1, 4):
            z_copy(which, k).wait_recv()
        sums = held[0].astype(jnp.float32)
        for k in range(1, 4):
            sums = sums + got[k].astype(jnp.float32)
        every[0, 0] = sums.astype(every.dtype)
        for k in range(1, 4):
            back_copy(which, k, (4 - k) % 4).start()
        side_copy(which, 0).start()
        out[y, z] = every[0, 0]

    for j in range(1, 8):
        member_copy(j).wait_recv()
    sums = member_own[...]
    for j in range(1, 8):
        sums = sums + member_in[j]
    vector_out[...] = sums

    @pl.loop(1, 4)
    def _(k):
        for which in range(2):
            _, out, _, _, _, every = arrays[which]
            back_copy(which, k, k).wait_recv()
            side_copy(which, k).start()
            out[y, (z + k) % 4] = every[0, k]

    @pl.loop(0, 4)
    def _(k):
        for which in range(2):
            _, out, _, _, _, every = arrays[which]
            side_copy(which, k).wait_recv()
            out[1 - y, (z + k) % 4] = every[1, k]

    @pl.loop(0, 4)
    def _(k):
        for which in range(2):
            y_copy(which, k).wait_send()
            side_copy(which, k).wait_send()

    for k in range(1, 4):
        for which in range(2):
            z_copy(which, k).wait_send()
            back_copy(which, k, (4 - k) % 4).wait_send()
    for j in range(1, 4):
        shard_copy(j).wait_send()
    for j in range(1, 8):
        member_copy(j).wait_send()


def reduce_over_members(first, second, vectors):
    low = first.dtype

    def quarter(array, *lead):
        return pltpu.VMEM((*lead, *array.shape[2:]), low)

    return pl.pallas_call(
        reduce_kernel,
        out_shape=[
            jax.ShapeDtypeStruct(first.shape, low),
            jax.ShapeDtypeStruct(second.shape, low),
            jax.ShapeDtypeStruct(vectors.shape[1:], vectors.dtype),
        ],
        in_specs=in_vmem(3),
        out_specs=in_vmem(3),
        scratch_shapes=[
            quarter(first, 4),
            quarter(second, 4),
            quarter(first, 4),
            quarter(second, 4),
            quarter(first, 4),
            quarter(second, 4),
            quarter(first, 2, 4),
            quarter(second, 2, 4),
            pltpu.VMEM(vectors.shape, vectors.dtype),
            pltpu.VMEM(vectors.shape[1:], vectors.dtype),
            pltpu.VMEM((8, *vectors.shape[1:]), vectors.dtype),
        ]
        + [copies(2, 4)] * 8
        + [copies(4)] * 2
        + [copies(8)] * 2,
        compiler_params=settings(3),
    )(first, second, vectors)


def project_kernel(
    x_ref,
    routes_ref,
    gain_ref,
    query_ref,
    key_ref,
    value_ref,
    raw_out,
    hidden_out,
    routes_out,
    scale,
    x_in,
    scale_in,
    outgoing,
    core_in,
    across_x,
    x_sums,
    slice_sent,
    slice_got,
    scale_sent,
    scale_got,
    core_sent,
    core_got,
    x_sent,
    x_got,
    route_sent,
    route_got,
):
    z, y, x, c = spot()
    member, shard = lax.axis_index("exp"), lax.axis_index("fsdp")
    mine = number(z, y, x, c)
    count, depth = hidden_out.shape[1:]
    wide, narrow = query_ref.shape[1] // 4, key_ref.shape[1] // 4

    def everyone(j):
        other = (mine + j) % 32
        return (other // 4, other % 4)

    barrier = pltpu.get_barrier_semaphore()

    @pl.loop(1, 32)
    def _(j):
        pl.semaphore_signal(barrier, inc=1, device_id=everyone(j), device_id_type=MESH)

    pl.semaphore_wait(barrier, 31)

    def slice_copy(j):
        place = (shard + j) % 4
        return remote(
            x_ref.at[:, pl.ds(pl.multiple_of(place * depth, depth), depth)],
            x_in.at[(4 - j) % 4],
            slice_sent.at[j],
            slice_got.at[(4 - j) % 4],
            (member, place),
        )

    def scale_copy(j):
        return remote(
            scale,
            scale_in.at[(4 - j) % 4],
            scale_sent.at[j],
            scale_got.at[(4 - j) % 4],
            (member, (shard + j) % 4),
        )

    def route_copy(j):
        return remote(
            routes_ref, routes_out.at[mine], route_sent.at[j], route_got.at[(32 - j) % 32], everyone(j)
        )

    for j in range(1, 4):
        slice_copy(j).start()
    values = x_ref[...].astype(jnp.float32)
    scale[...] = jnp.broadcast_to(
        lax.rsqrt(jnp.mean(values * values, axis=1, keepdims=True) + EPSILON), scale.shape
    )
    for j in range(1, 4):
        scale_copy(j).start()
    routes_out[mine] = routes_ref[...]

    @pl.loop(1, 32)
    def _(j):
        route_copy(j).start()

    def hide(owner, piece, factor):
        gain = gain_ref[...].astype(jnp.float32)
        hidden = piece.astype(jnp.float32) * factor[:, :1] * gain
        hidden_out[owner] = hidden.astype(hidden_out.dtype)

    hide(shard, x_ref[:, pl.ds(pl.multiple_of(shard * depth, depth), depth)], scale[...])

    def take(owner):
        slot = (owner - shard + 4) % 4
        remote(x_in.at[slot], x_in.at[slot], slice_sent.at[slot], slice_got.at[slot], (member, owner)).wait_recv()
        remote(scale, scale_in.at[slot], scale_sent.at[slot], scale_got.at[slot], (member, owner)).wait_recv()
        hide(owner, x_in[slot], scale_in[slot])

    def partial(side, target):
        rows = jnp.concatenate([hidden_out[side * 2], hidden_out[side * 2 + 1]], axis=0)
        parts = []
        for weight, size in ((query_ref, wide), (key_ref, narrow), (value_ref, narrow)):
            columns = pl.ds(pl.multiple_of(target * size, size), size)
            parts.append(jnp.dot(rows, weight[:, columns], preferred_element_type=jnp.float32))
        return jnp.concatenate(parts, axis=1)

    core_peer, x_peer = where_is(z, y, x, 1 - c), where_is(z, y, 1 - x, c)

    def core_copy(turn, far):
        return remote(
            outgoing.at[turn, far],
            core_in.at[turn, far],
            core_sent.at[turn, far],
            core_got.at[turn, far],
            core_peer,
        )

    def x_copy(turn):
        return remote(across_x.at[turn], x_sums.at[turn], x_sent.at[turn], x_got.at[turn], x_peer)

    low = outgoing.dtype
    for turn in range(2):
        side = x if turn == 0 else 1 - x
        if turn == 0:
            take(side * 2 + 1 - c)
        else:
            take(side * 2 + c)
            take(side * 2 + 1 - c)
        outgoing[turn, 1] = partial(side, (1 - x) * 2 + 1 - c).astype(low)
        core_copy(turn, 1).start()
        sums = partial(side, (1 - x) * 2 + c)
        core_copy(turn, 1).wait_recv()
        across_x[turn] = (sums + core_in[turn, 1].astype(jnp.float32)).astype(low)
        x_copy(turn).start()
        outgoing[turn, 0] = partial(side, x * 2 + 1 - c).astype(low)
        core_copy(turn, 0).start()

    for turn in range(2):
        side = x if turn == 0 else 1 - x
        sums = partial(side, x * 2 + c)
        core_copy(turn, 0).wait_recv()
        sums = sums + core_in[turn, 0].astype(jnp.float32)
        raw_out[side * 2] = sums[:count]
        raw_out[side * 2 + 1] = sums[count:]

    for turn in range(2):
        side = 1 - x if turn == 0 else x
        x_copy(turn).wait_recv()
        raw_out[side * 2] += x_sums[turn, :count].astype(jnp.float32)
        raw_out[side * 2 + 1] += x_sums[turn, count:].astype(jnp.float32)

    @pl.loop(1, 32)
    def _(j):
        remote(
            routes_ref, routes_out.at[(mine + j) % 32], route_sent.at[j], route_got.at[j], everyone(j)
        ).wait_recv()

    @pl.loop(1, 32)
    def _(j):
        route_copy(j).wait_send()

    for j in range(1, 4):
        slice_copy(j).wait_send()
        scale_copy(j).wait_send()
    for turn in range(2):
        x_copy(turn).wait_send()
        for far in range(2):
            core_copy(turn, far).wait_send()


def project_tokens(tokens, routes, gain, w_query, key_weight, value_weight):
    count = tokens.shape[0]
    depth = w_query.shape[0]
    own = (w_query.shape[1] + key_weight.shape[1] + value_weight.shape[1]) // 4
    low = tokens.dtype
    return pl.pallas_call(
        project_kernel,
        out_shape=[
            jax.ShapeDtypeStruct((4, count, own), jnp.float32),
            jax.ShapeDtypeStruct((4, count, depth), low),
            jax.ShapeDtypeStruct((32, *routes.shape), routes.dtype),
        ],
        in_specs=in_vmem(6),
        out_specs=in_vmem(3),
        scratch_shapes=[
            pltpu.VMEM((count, 128), jnp.float32),
            pltpu.VMEM((4, count, depth), low),
            pltpu.VMEM((4, count, 128), jnp.float32),
            pltpu.VMEM((2, 2, 2 * count, own), low),
            pltpu.VMEM((2, 2, 2 * count, own), low),
            pltpu.VMEM((2, 2 * count, own), low),
            pltpu.VMEM((2, 2 * count, own), low),
            copies(4),
            copies(4),
            copies(4),
            copies(4),
            copies(2, 2),
            copies(2, 2),
            copies(2),
            copies(2),
            copies(32),
            copies(32),
        ],
        compiler_params=settings(4),
    )(tokens, routes, gain, w_query, key_weight, value_weight)


def finish_kernel(
    attended_ref,
    weight_ref,
    x_ref,
    gain_ref,
    middle_out,
    normed_out,
    outgoing,
    core_in,
    across_x,
    x_sums,
    core_sent,
    core_got,
    x_sent,
    x_got,
):
    z, y, x, c = spot()
    count = x_ref.shape[0]
    core_peer, x_peer = where_is(z, y, x, 1 - c), where_is(z, y, 1 - x, c)
    greet([core_peer, x_peer])

    def core_copy(far):
        return remote(
            outgoing.at[far], core_in.at[far], core_sent.at[far], core_got.at[far], core_peer
        )

    def x_copy():
        return remote(across_x, x_sums, x_sent, x_got, x_peer)

    def partial(side, core):
        return jnp.dot(
            attended_ref[side * 2 + core], weight_ref[...], preferred_element_type=jnp.float32
        )

    outgoing[1] = partial(1 - x, 1 - c).astype(outgoing.dtype)
    core_copy(1).start()
    sums = partial(1 - x, c)
    core_copy(1).wait_recv()
    across_x[...] = (sums + core_in[1].astype(jnp.float32)).astype(across_x.dtype)
    x_copy().start()
    outgoing[0] = partial(x, 1 - c).astype(outgoing.dtype)
    core_copy(0).start()
    sums = partial(x, c) + x_ref[...].astype(jnp.float32)
    core_copy(0).wait_recv()
    sums = sums + core_in[0].astype(jnp.float32)
    x_copy().wait_recv()
    middle = sums + x_sums[...].astype(jnp.float32)
    middle_out[...] = middle
    scale = lax.rsqrt(jnp.mean(middle * middle, axis=1, keepdims=True) + EPSILON)
    normed_out[...] = (middle * scale * gain_ref[...]).astype(normed_out.dtype)
    x_copy().wait_send()
    core_copy(0).wait_send()
    core_copy(1).wait_send()


def finish_attention(attended, w_out, tokens, gain):
    count, width = tokens.shape
    low = tokens.dtype
    return pl.pallas_call(
        finish_kernel,
        out_shape=[
            jax.ShapeDtypeStruct((count, width), jnp.float32),
            jax.ShapeDtypeStruct((count, width), low),
        ],
        in_specs=in_vmem(4),
        out_specs=in_vmem(2),
        scratch_shapes=[
            pltpu.VMEM((2, count, width), low),
            pltpu.VMEM((2, count, width), low),
            pltpu.VMEM((count, width), low),
            pltpu.VMEM((count, width), low),
            copies(2),
            copies(2),
            copies(),
            copies(),
        ],
        compiler_params=settings(5),
    )(attended, w_out, tokens, gain)


def branch_kernel(
    branch_ref, weight_ref, grad_out, every_out, x_sent, x_got, core_sent, core_got
):
    z, y, x, c = spot()
    mine = x * 2 + c
    core_peer, x_peer = where_is(z, y, x, 1 - c), where_is(z, y, 1 - x, c)
    greet([core_peer, x_peer])
    every_out[mine] = branch_ref[...]

    def x_copy():
        return remote(branch_ref, every_out.at[mine], x_sent, x_got, x_peer)

    def core_copy(far):
        place = (1 - x if far else x) * 2 + c
        return remote(
            every_out.at[place], every_out.at[place], core_sent.at[far], core_got.at[far], core_peer
        )

    def back(place):
        grad_out[place] = right_transposed(every_out[place], weight_ref[...]).astype(grad_out.dtype)

    x_copy().start()
    core_copy(0).start()
    back(mine)
    core_copy(0).wait_recv()
    back(x * 2 + 1 - c)
    x_copy().wait_recv()
    core_copy(1).start()
    back((1 - x) * 2 + c)
    core_copy(1).wait_recv()
    back((1 - x) * 2 + 1 - c)
    x_copy().wait_send()
    core_copy(0).wait_send()
    core_copy(1).wait_send()


def branch_back(branch, w_out):
    count, width = branch.shape
    low = branch.dtype
    return pl.pallas_call(
        branch_kernel,
        out_shape=[
            jax.ShapeDtypeStruct((4, count, w_out.shape[0]), low),
            jax.ShapeDtypeStruct((4, count, width), low),
        ],
        in_specs=in_vmem(2),
        out_specs=in_vmem(2),
        scratch_shapes=[copies(), copies(), copies(2), copies(2)],
        compiler_params=settings(6),
    )(branch, w_out)


def heads_kernel(
    grad_ref,
    hidden_ref,
    query_ref,
    key_ref,
    value_ref,
    weight_out,
    first_out,
    every,
    outgoing,
    x_sent,
    x_got,
    core_sent,
    core_got,
    back_sent,
    back_got,
):
    z, y, x, c = spot()
    member, shard = lax.axis_index("exp"), lax.axis_index("fsdp")
    core_peer, x_peer = where_is(z, y, x, 1 - c), where_is(z, y, 1 - x, c)
    peers = [(member, (shard + j) % 4) for j in range(1, 4)]
    greet(peers)
    rows = grad_ref.shape[0]
    half = rows // 2
    count = rows // 4
    depth = hidden_ref.shape[1]
    wide, narrow = query_ref.shape[1] // 4, key_ref.shape[1] // 4
    every[shard] = grad_ref[...]

    def x_copy(part):
        piece = pl.ds(part * half, half)
        return remote(
            grad_ref.at[piece], every.at[shard, piece], x_sent.at[part], x_got.at[part], x_peer
        )

    def core_copy(far, part):
        view = every.at[(1 - x if far else x) * 2 + c, pl.ds(part * half, half)]
        return remote(view, view, core_sent.at[far, part], core_got.at[far, part], core_peer)

    for part in range(2):
        x_copy(part).start()
    for part in range(2):
        core_copy(0, part).start()

    def weigh(place):
        weight_out[place] = left_trans(hidden_ref[...], every[place]).astype(weight_out.dtype)

    def back(place):
        grads = every[place]
        sums = None
        for weight, size, start in (
            (query_ref, wide, 0),
            (key_ref, narrow, wide),
            (value_ref, narrow, wide + narrow),
        ):
            columns = pl.ds(pl.multiple_of(place * size, size), size)
            term = right_transposed(grads[:, start : start + size], weight[:, columns])
            sums = term if sums is None else sums + term
        return sums

    total = back(shard)
    weigh(shard)
    near = x * 2 + 1 - c
    for part in range(2):
        core_copy(0, part).wait_recv()
    total = total + back(near)
    weigh(near)
    for part in range(2):
        x_copy(part).wait_recv()
        core_copy(1, part).start()
    far = (1 - x) * 2 + c
    total = total + back(far)
    for part in range(2):
        core_copy(1, part).wait_recv()
    total = total + back((1 - x) * 2 + 1 - c)
    for owner in range(4):
        outgoing[owner] = total[owner * count : (owner + 1) * count].astype(outgoing.dtype)

    def back_copy(j):
        place = (shard + j) % 4
        return remote(
            outgoing.at[place],
            first_out.at[shard],
            back_sent.at[j],
            back_got.at[(4 - j) % 4],
            (member, place),
        )

    for j in range(1, 4):
        back_copy(j).start()
    first_out[shard] = outgoing[shard]
    weigh(far)
    weigh((1 - x) * 2 + 1 - c)
    for j in range(1, 4):
        place = (shard + j) % 4
        remote(
            outgoing.at[place], first_out.at[place], back_sent.at[j], back_got.at[j], (member, place)
        ).wait_recv()
    for j in range(1, 4):
        back_copy(j).wait_send()
    for part in range(2):
        x_copy(part).wait_send()
        for far in range(2):
            core_copy(far, part).wait_send()


def heads_back(grads, hidden, w_query, key_weight, value_weight):
    rows, own = grads.shape
    depth = hidden.shape[1]
    low = grads.dtype
    return pl.pallas_call(
        heads_kernel,
        out_shape=[
            jax.ShapeDtypeStruct((4, depth, own), low),
            jax.ShapeDtypeStruct((4, rows // 4, depth), low),
        ],
        in_specs=in_vmem(5),
        out_specs=in_vmem(2),
        scratch_shapes=[
            pltpu.VMEM((4, rows, own), low),
            pltpu.VMEM((4, rows // 4, depth), low),
            copies(2),
            copies(2),
            copies(2, 2),
            copies(2, 2),
            copies(4),
            copies(4),
        ],
        compiler_params=settings(7),
    )(grads, hidden, w_query, key_weight, value_weight)


def moe_gathered(normed, router, routes, capacity, cotangent, weights, notes):
    gate_w, up_w, down_w = weights
    token_count, topk = routes.shape
    experts = router.shape[1]
    mine = lax.axis_index("exp") * lax.axis_size("fsdp") + lax.axis_index("fsdp")
    all_routes = notes[:, :topk]
    all_grads = lax.all_gather(cotangent, BOTH, axis=0, tiled=True)
    columns = jnp.arange(experts, dtype=jnp.int32)
    named = jnp.any(all_routes[:, :, None, :] == columns[None, None, :, None], axis=1)
    own = jnp.any(all_routes == mine, axis=1)
    before = jnp.tril(jnp.ones((token_count, token_count), jnp.bfloat16), -1)
    rank = right_transposed(own.astype(jnp.bfloat16), before).astype(jnp.int32)
    places = jnp.arange(capacity, dtype=jnp.int32)
    select = (own[:, None, :] & (rank[:, None, :] == places[None, :, None])).astype(jnp.bfloat16)
    spread = (own[:, :, None] & (rank[:, :, None] == places[None, None, :])).astype(jnp.bfloat16)
    grad_rows = contract(
        "bcj,bjd->bcd", select, all_grads.reshape(experts, token_count, MODEL_WIDTH)
    ).astype(jnp.bfloat16)
    named_rows = contract("bcj,bej->bce", select, named.astype(jnp.bfloat16))
    named_rows = jnp.pad(named_rows.astype(jnp.bfloat16), ((0, 0), (0, 0), (0, 128 - experts)))
    flat_grads = grad_rows.reshape(experts * capacity, MODEL_WIDTH)
    ahead = right_transposed(flat_grads, down_w).reshape(experts, capacity, -1)

    padded = jnp.pad(router, ((0, 0), (0, 128 - experts)))
    arrived, active, gate_pre_grad, up_pre_grad, share, extra = gather_experts(
        normed, select, ahead, named_rows, gate_w, up_w, padded
    )
    summed, back = scatter_experts(spread, gate_pre_grad, up_pre_grad, gate_w, up_w, extra)

    summed, back, arrived, gate_pre_grad, up_pre_grad, active, share = lax.optimization_barrier(
        (summed, back, arrived, gate_pre_grad, up_pre_grad, active, share)
    )

    def flat(rows):
        return rows.reshape(experts * capacity, rows.shape[2])

    share = flat(share)[:, :1]
    out_rows = (share * flat_grads.astype(jnp.float32)).astype(jnp.bfloat16)
    produced = matrix_product(flat(active), down_w).astype(jnp.bfloat16)
    weighted = (share * produced.astype(jnp.float32)).astype(jnp.bfloat16)
    full = contract("bjc,bcd->bjd", spread, weighted.reshape(experts, capacity, MODEL_WIDTH))
    full = full.astype(jnp.bfloat16).reshape(experts * token_count, MODEL_WIDTH)
    mixed = lax.psum_scatter(full, BOTH, scatter_dimension=0, tiled=True)
    weight_grads = (
        left_trans(flat(arrived), flat(gate_pre_grad)),
        left_trans(flat(arrived), flat(up_pre_grad)),
        left_trans(flat(active), out_rows),
    )
    gate_grad = back[:, :experts] + back[:, experts : 2 * experts]
    picks = jnp.any(routes[:, :, None] == columns[None, None, :], axis=1)
    gates = jax.nn.softmax(jnp.where(picks, matrix_product(normed, router), MASKED), axis=1)
    logit_grad = gates * (gate_grad - jnp.sum(gates * gate_grad, axis=1, keepdims=True))
    return mixed.astype(jnp.float32), summed, logit_grad.astype(jnp.bfloat16), *weight_grads


def moe_exchanged(normed, router, routes, capacity, cotangent, weights, notes):
    gate_w, up_w, down_w = weights
    token_count, topk = routes.shape
    experts = router.shape[1]
    gates = gates_of(matrix_product(normed, router), routes, experts)
    slots = slot_table(routes, experts, capacity)

    def send(rows):
        packed = jnp.zeros((experts * capacity, MODEL_WIDTH), jnp.bfloat16).at[slots].set(rows)
        return exchange(packed.reshape(experts, capacity, MODEL_WIDTH)).reshape(
            experts * capacity, MODEL_WIDTH
        )

    def bring(rows):
        rows = exchange(rows.reshape(experts, capacity, MODEL_WIDTH))
        return rows.reshape(experts * capacity, MODEL_WIDTH)[slots].reshape(
            token_count, topk, MODEL_WIDTH
        )

    arrived = send(jnp.repeat(normed, topk, axis=0))
    hidden = expert_forward(arrived, gate_w, up_w)
    scaled = (gates[:, :, None] * cotangent.astype(jnp.float32)[:, None, :]).astype(jnp.bfloat16)
    out_rows = send(scaled.reshape(token_count * topk, MODEL_WIDTH))
    rows_back, gate_pre_grad, up_pre_grad = expert_back(out_rows, hidden, gate_w, up_w, down_w)
    gate_w_grad = left_trans(arrived, gate_pre_grad)
    up_w_grad = left_trans(arrived, up_pre_grad)
    down_grad = left_trans(hidden[3], out_rows)
    returned = bring(matrix_product(hidden[3], down_w).astype(jnp.bfloat16))
    mixed = jnp.einsum("tk,tkd->td", gates, returned.astype(jnp.float32))
    gate_grad = jnp.einsum("td,tkd->tk", cotangent, returned, preferred_element_type=jnp.float32)
    summed = jnp.sum(bring(rows_back), axis=1, dtype=jnp.float32)
    picked_grad = gates * (gate_grad - jnp.sum(gates * gate_grad, axis=1, keepdims=True))
    onehot = routes[:, :, None] == jnp.arange(experts, dtype=jnp.int32)[None, None, :]
    logit_grad = jnp.sum(jnp.where(onehot, picked_grad[:, :, None], 0.0), axis=1)
    return mixed, summed, logit_grad.astype(jnp.bfloat16), gate_w_grad, up_w_grad, down_grad


def local(
    tokens,
    lengths,
    routes,
    attn_gain,
    w_query,
    key_weight,
    value_weight,
    q_gain,
    k_gain,
    w_out,
    mlp_gain,
    w_router,
    expert_gate,
    expert_up,
    expert_down,
    cotangent,
):
    shards, members = lax.axis_size("fsdp"), lax.axis_size("exp")
    experts = shards * members
    token_count, topk = routes.shape
    capacity = 2 * token_count * topk // experts
    group = shards * token_count
    depth = w_query.shape[0]
    heads = QUERY_HEADS // shards
    kv_heads = max(1, KEY_VALUE_HEADS // shards)
    copies_of = shards * kv_heads // KEY_VALUE_HEADS
    head_group = heads // kv_heads
    wide, narrow = heads * HEAD_WIDTH, kv_heads * HEAD_WIDTH
    place = lax.axis_index("fsdp")

    gathered = lax.all_gather(
        jnp.concatenate([w_router.reshape(-1), attn_gain, mlp_gain, q_gain, k_gain]), "fsdp"
    )
    cuts, start = [], 0
    for leaf in (w_router, attn_gain, mlp_gain, q_gain, k_gain):
        cuts.append(gathered[:, start : start + leaf.size])
        start += leaf.size
    router = cuts[0].reshape(MODEL_WIDTH, experts)
    gain_attn, gain_mlp, gain_query, gain_key = [
        cut.reshape(-1).astype(jnp.float32) for cut in cuts[1:]
    ]
    dense = (members, shards) == (8, 4) and 2 * capacity >= token_count
    inputs = tokens.astype(jnp.float32)
    scale_one = rms_scale(inputs)
    if dense:
        notes = jnp.pad(
            jnp.concatenate(
                [routes.T, jnp.pad(lengths, ((0, 0), (0, token_count - lengths.shape[1])))], axis=0
            ),
            ((0, 15 - topk), (0, 0)),
        )
        raw, hidden, notes = project_tokens(
            tokens, notes, attn_gain[None], w_query, key_weight, value_weight
        )
        hidden = hidden.reshape(group, depth)
        first = lax.axis_index("exp") * shards
        all_lengths = lax.dynamic_slice_in_dim(notes, first, shards)[:, topk, : lengths.shape[1]]
    else:
        notes = None
        all_lengths = lax.all_gather(lengths[0], "fsdp")

        def by_shard(weight):
            weight = weight.reshape(depth, KEY_VALUE_HEADS, HEAD_WIDTH)
            return jnp.repeat(weight, copies_of, axis=1).reshape(depth, shards, narrow)

        joined = jnp.concatenate(
            [w_query.reshape(depth, shards, wide), by_shard(key_weight), by_shard(value_weight)],
            axis=2,
        ).transpose(1, 0, 2)
        first_normed = (inputs * scale_one * gain_attn).astype(jnp.bfloat16)
        hidden = lax.all_to_all(first_normed, "fsdp", split_axis=1, concat_axis=0, tiled=True)
        partial = contract("gk,nkc->ngc", hidden, joined).astype(jnp.bfloat16)
        raw = lax.psum_scatter(partial, "fsdp", scatter_dimension=0, tiled=True)[0]
        raw = raw.astype(jnp.float32)
    raw = raw.reshape(shards, token_count, wide + 2 * narrow)
    query_raw = raw[:, :, :wide].reshape(shards, token_count, heads, HEAD_WIDTH)
    key_raw = raw[:, :, wide : wide + narrow].reshape(shards, token_count, kv_heads, HEAD_WIDTH)
    value = (
        raw[:, :, wide + narrow :]
        .astype(jnp.bfloat16)
        .reshape(shards, token_count, kv_heads, HEAD_WIDTH)
    )
    position, allowed = jax.vmap(lambda row: seq_layout(row, token_count))(all_lengths)
    cosine, sine = rotary_tables(position, HEAD_WIDTH)
    query_scale = rms_scale(query_raw)
    query_hat = query_raw * query_scale
    key_scale = rms_scale(key_raw)
    key_hat = key_raw * key_scale
    query = (
        rotate(query_hat * gain_query, cosine, sine)
        .astype(jnp.bfloat16)
        .reshape(shards, token_count, kv_heads, head_group, HEAD_WIDTH)
    )
    key = rotate(key_hat * gain_key, cosine, sine).astype(jnp.bfloat16)
    scores = contract("bqkgd,bpkd->bkgqp", query, key) * HEAD_WIDTH ** (-0.5)
    scores = jnp.where(allowed[:, None, None], scores, MASKED)
    top = jnp.max(scores, axis=-1, keepdims=True)
    raised = jnp.exp(scores - top)
    probs = raised / jnp.sum(raised, axis=-1, keepdims=True)
    probs_low = probs.astype(jnp.bfloat16)
    attended = contract("bkgqp,bpkd->bqkgd", probs_low, value).astype(jnp.bfloat16)
    attended = attended.reshape(group, wide)
    if dense:
        middle, normed = finish_attention(
            attended.reshape(shards, token_count, wide), w_out, tokens, gain_mlp[None]
        )
        scale_two = rms_scale(middle)
    else:
        mixed_heads = lax.psum_scatter(
            matrix_product(attended, w_out).astype(jnp.bfloat16),
            "fsdp",
            scatter_dimension=0,
            tiled=True,
        )
        middle = inputs + mixed_heads.astype(jnp.float32)
        scale_two = rms_scale(middle)
        normed = (middle * scale_two * gain_mlp).astype(jnp.bfloat16)

    moe = moe_gathered if dense else moe_exchanged
    mixed, summed, logit_grad, gate_w_grad, up_w_grad, down_grad = moe(
        normed,
        router,
        routes,
        capacity,
        cotangent,
        (expert_gate[0], expert_up[0], expert_down[0]),
        notes,
    )
    layer_out = (middle + mixed).astype(jnp.bfloat16)

    upstream = cotangent.astype(jnp.float32)
    normed_grad = summed + right_transposed(logit_grad, router)
    mlp_gain_grad = jnp.sum(normed_grad * middle * scale_two, axis=0)
    router_grad = left_trans(normed, logit_grad)
    middle_grad = upstream + rms_back(normed_grad * gain_mlp, middle, scale_two)
    branch_low = middle_grad.astype(jnp.bfloat16)
    if dense:
        attended_grad, branch_grad = branch_back(branch_low, w_out)
        branch_grad = branch_grad.reshape(group, MODEL_WIDTH)
    else:
        branch_grad = lax.all_gather(branch_low, "fsdp", axis=0, tiled=True)
        attended_grad = right_transposed(branch_grad, w_out).astype(jnp.bfloat16)
    out_w_grad = left_trans(attended, branch_grad)
    attended_grad = attended_grad.reshape(shards, token_count, kv_heads, head_group, HEAD_WIDTH)
    prob_grad = contract("bqkgd,bpkd->bkgqp", attended_grad, value)
    value_grad = contract("bkgqp,bqkgd->bpkd", probs_low, attended_grad)
    balance = jnp.sum(probs * prob_grad, axis=-1, keepdims=True)
    score_grad = (probs * (prob_grad - balance)).astype(jnp.bfloat16)
    query_norm_grad = contract("bkgqp,bpkd->bqkgd", score_grad, key) * HEAD_WIDTH ** (-0.5)
    query_norm_grad = query_norm_grad.reshape(shards, token_count, heads, HEAD_WIDTH)
    key_norm_grad = contract("bkgqp,bqkgd->bpkd", score_grad, query) * HEAD_WIDTH ** (-0.5)
    query_norm_grad = rotate_back(query_norm_grad, cosine, sine)
    key_norm_grad = rotate_back(key_norm_grad, cosine, sine)
    q_gain_grad = jnp.sum(query_norm_grad * query_hat, axis=(0, 1, 2))
    k_gain_grad = jnp.sum(key_norm_grad * key_hat, axis=(0, 1, 2))
    query_grad = rms_back(query_norm_grad * gain_query, query_raw, query_scale)
    key_grad = rms_back(key_norm_grad * gain_key, key_raw, key_scale)
    head_grads = jnp.concatenate(
        [
            query_grad.reshape(group, wide),
            key_grad.reshape(group, narrow),
            value_grad.reshape(group, narrow),
        ],
        axis=1,
    ).astype(jnp.bfloat16)
    if dense:
        joined_grad, first_grad = heads_back(head_grads, hidden, w_query, key_weight, value_weight)
        first_grad = first_grad.transpose(1, 0, 2).reshape(token_count, MODEL_WIDTH)
    else:
        head_grads = lax.all_gather(head_grads, "fsdp")
        hidden_grad = contract("ngc,nkc->gk", head_grads, joined).astype(jnp.bfloat16)
        first_grad = lax.all_to_all(
            hidden_grad, "fsdp", split_axis=0, concat_axis=1, tiled=True
        )
        joined_grad = contract("gk,ngc->nkc", hidden, head_grads).astype(jnp.bfloat16)
    first_grad = first_grad.astype(jnp.float32)
    attn_gain_grad = jnp.sum(first_grad * inputs * scale_one, axis=0)
    input_grad = (middle_grad + rms_back(first_grad * gain_attn, inputs, scale_one)).astype(
        jnp.bfloat16
    )

    out_w_grad = out_w_grad.astype(jnp.bfloat16)
    vectors = jnp.concatenate(
        [
            grad.reshape(shards, -1)
            for grad in (router_grad, attn_gain_grad, mlp_gain_grad, q_gain_grad, k_gain_grad)
        ],
        axis=1,
    )
    if dense:
        rows = -(-vectors.shape[1] // 1024) * 8
        padded = jnp.pad(vectors, ((0, 0), (0, rows * 128 - vectors.shape[1])))
        joined_sum, out_sum, vectors = reduce_over_members(
            joined_grad.reshape(2, 4, -1, wide + 2 * narrow),
            out_w_grad.reshape(2, 4, -1, MODEL_WIDTH),
            padded.reshape(shards, rows, 128),
        )
        joined_sum, out_sum = joined_sum.reshape(joined_grad.shape), out_sum.reshape(w_out.shape)
        vectors = vectors.reshape(-1)
    else:
        out_sum, joined_sum = lax.psum(out_w_grad, "exp"), lax.psum(joined_grad, "exp")
        vectors = lax.psum(vectors, BOTH)[place]
    out_sum, joined_sum = out_sum.astype(jnp.float32), joined_sum.astype(jnp.float32)
    sums, start = [], 0
    for leaf in (w_router, attn_gain, mlp_gain, q_gain, k_gain):
        sums.append(vectors[start : start + leaf.size].reshape(leaf.shape))
        start += leaf.size

    def gather_heads(part):
        return part.transpose(1, 0, 2).reshape(depth, KEY_VALUE_HEADS, copies_of, HEAD_WIDTH).sum(
            axis=2
        ).reshape(depth, KEY_VALUE_HEADS * HEAD_WIDTH)

    return (
        layer_out,
        input_grad,
        sums[1],
        joined_sum[:, :, :wide].transpose(1, 0, 2).reshape(depth, QUERY_HEADS * HEAD_WIDTH),
        gather_heads(joined_sum[:, :, wide : wide + narrow]),
        gather_heads(joined_sum[:, :, wide + narrow :]),
        sums[3],
        sums[4],
        out_sum,
        sums[2],
        sums[0],
        gate_w_grad[None],
        up_w_grad[None],
        down_grad[None],
    )


def solution(mesh):
    in_specs = (
        P(("exp", "fsdp"), None),
        P(("exp", "fsdp"), None),
        P(("exp", "fsdp"), None),
        P("fsdp"),
        P("fsdp", None),
        P("fsdp", None),
        P("fsdp", None),
        P("fsdp"),
        P("fsdp"),
        P("fsdp", None),
        P("fsdp"),
        P("fsdp", None),
        P(("exp", "fsdp"), None, None),
        P(("exp", "fsdp"), None, None),
        P(("exp", "fsdp"), None, None),
        P(("exp", "fsdp"), None),
    )
    out_specs = (
        P(("exp", "fsdp"), None),
        P(("exp", "fsdp"), None),
        P("fsdp"),
        P("fsdp", None),
        P("fsdp", None),
        P("fsdp", None),
        P("fsdp"),
        P("fsdp"),
        P("fsdp", None),
        P("fsdp"),
        P("fsdp", None),
        P(("exp", "fsdp"), None, None),
        P(("exp", "fsdp"), None, None),
        P(("exp", "fsdp"), None, None),
    )
    return jax.shard_map(local, mesh=mesh, in_specs=in_specs, out_specs=out_specs, check_vma=False)
```

```python
import functools
import math

import jax
import jax.numpy as jnp
from jax import lax
from jax.experimental import pallas as pl
from jax.experimental.pallas import tpu as pltpu
from jax.sharding import PartitionSpec as P

MODEL_WIDTH = 2048
QUERY_HEADS = 32
KEY_VALUE_HEADS = 4
HEAD_WIDTH = 128


EPSILON = 1e-06
THETA = 1000000.0
MASKED = -1e30
BOTH = ("exp", "fsdp")
MESH = pl.DeviceIdType.MESH


def matrix_product(left, right):
    return jnp.dot(left, right, preferred_element_type=jnp.float32)


def left_trans(left, right):
    return lax.dot_general(
        left, right, (((0,), (0,)), ((), ())), preferred_element_type=jnp.float32
    )


def right_transposed(left, right):
    return lax.dot_general(
        left, right, (((1,), (1,)), ((), ())), preferred_element_type=jnp.float32
    )


def contract(spec, left, right):
    return jnp.einsum(spec, left, right, preferred_element_type=jnp.float32)


def rms_scale(values):
    return lax.rsqrt(jnp.mean(values * values, axis=-1, keepdims=True) + EPSILON)


def rms_back(grad_hat, values, scale):
    normal = values * scale
    return scale * (grad_hat - normal * jnp.mean(grad_hat * normal, axis=-1, keepdims=True))


def seq_layout(length_row, token_count):
    ends = jnp.cumsum(length_row)
    starts = ends - length_row
    places = jnp.arange(token_count, dtype=jnp.int32)
    member = (places[:, None] >= starts[None, :]) & (places[:, None] < ends[None, :])
    numbers = jnp.arange(length_row.shape[0], dtype=jnp.int32)
    segment = jnp.sum(jnp.where(member, numbers[None, :], 0), axis=1)
    position = places - jnp.sum(jnp.where(member, starts[None, :], 0), axis=1)
    allowed = (segment[:, None] == segment[None, :]) & (places[None, :] <= places[:, None])
    return (position, allowed)


def rotary_tables(position, head_size):
    half = head_size // 2
    index = jnp.arange(head_size, dtype=jnp.int32) % half
    inverse = jnp.exp(index.astype(jnp.float32) * (-2.0 * math.log(THETA) / head_size))
    angles = position.astype(jnp.float32)[..., None] * inverse
    return (jnp.cos(angles)[..., None, :], jnp.sin(angles)[..., None, :])


def rotate(values, cosine, sine):
    half = values.shape[-1] // 2
    turned = jnp.concatenate([-values[..., half:], values[..., :half]], axis=-1)
    return values * cosine + turned * sine


def rotate_back(grads, cosine, sine):
    half = grads.shape[-1] // 2
    moved = grads * sine
    return grads * cosine + jnp.concatenate([moved[..., half:], -moved[..., :half]], axis=-1)


def slot_table(route_rows, experts, capacity):
    flat = route_rows.reshape(-1)
    onehot = (flat[:, None] == jnp.arange(experts, dtype=jnp.int32)[None, :]).astype(jnp.int32)
    ranks = jnp.cumsum(onehot, axis=0) - 1
    rank = jnp.sum(ranks * onehot, axis=1)
    return flat * capacity + rank


def exchange(buffer):
    return lax.all_to_all(buffer, BOTH, split_axis=0, concat_axis=0, tiled=True)


def two_halves(values):
    high = values.astype(jnp.bfloat16)
    low = (values - high.astype(jnp.float32)).astype(jnp.bfloat16)
    return high, low


def expert_forward(arrived, gate_w, up_w):
    gate_pre = matrix_product(arrived, gate_w)
    up_pre = matrix_product(arrived, up_w)
    sigma = jax.nn.sigmoid(gate_pre)
    active = (gate_pre * sigma * up_pre).astype(jnp.bfloat16)
    return gate_pre, up_pre, sigma, active


def expert_back(out_rows, hidden, gate_w, up_w, down_w):
    gate_pre, up_pre, sigma, _ = hidden
    active_grad = right_transposed(out_rows, down_w)
    gate_pre_grad = (active_grad * up_pre * (sigma * (1.0 + gate_pre * (1.0 - sigma)))).astype(
        jnp.bfloat16
    )
    up_pre_grad = (active_grad * (gate_pre * sigma)).astype(jnp.bfloat16)
    rows_back = right_transposed(gate_pre_grad, gate_w) + right_transposed(up_pre_grad, up_w)
    return rows_back.astype(jnp.bfloat16), gate_pre_grad, up_pre_grad


def gates_of(logits, routes, experts):
    picked = jnp.take_along_axis(logits, routes, axis=1)
    peak = jnp.max(picked, axis=1, keepdims=True)
    lifted = jnp.exp(picked - peak)
    return lifted / jnp.sum(lifted, axis=1, keepdims=True)


def spot():
    member, shard = lax.axis_index("exp"), lax.axis_index("fsdp")
    return member // 2, member % 2, shard // 2, shard % 2


def where_is(z, y, x, c):
    return (z * 2 + y, x * 2 + c)


def number(z, y, x, c):
    return z * 8 + y * 4 + x * 2 + c


def along_z(z, q):
    return (z // 2 + q // 2) % 2 * 2 + (z % 2 + q % 2) % 2


def greet(peers):
    barrier = pltpu.get_barrier_semaphore()
    for peer in peers:
        pl.semaphore_signal(barrier, inc=1, device_id=peer, device_id_type=MESH)
    pl.semaphore_wait(barrier, len(peers))


def remote(source, target, sent, got, peer):
    return pltpu.make_async_remote_copy(
        src_ref=source,
        dst_ref=target,
        send_sem=sent,
        recv_sem=got,
        device_id=peer,
        device_id_type=MESH,
    )


def in_vmem(count):
    return [pl.BlockSpec(memory_space=pltpu.VMEM)] * count


def copies(*shape):
    return pltpu.SemaphoreType.DMA(shape)


def settings(collective_id):
    return pltpu.CompilerParams(
        collective_id=collective_id, has_side_effects=True, vmem_limit_bytes=60 << 20
    )


def gather_kernel(
    x_ref,
    select_ref,
    ahead_hbm,
    named_ref,
    gate_hbm,
    up_hbm,
    router_ref,
    rows_out,
    active_out,
    gate_out,
    up_out,
    share_out,
    extra_out,
    held,
    ahead_ref,
    gate_ref,
    up_ref,
    picked,
    results,
    loaded,
    stored,
    arrive,
    to_z,
    to_y,
    to_x,
    to_core,
):
    z, y, x, c = spot()
    half = x_ref.shape[0] // 2
    kept = select_ref.shape[1]
    y_peer, x_peer, core_peer = (
        where_is(z, 1 - y, x, c),
        where_is(z, y, 1 - x, c),
        where_is(z, y, x, 1 - c),
    )
    near_z, far_z = where_is(along_z(z, 1), y, x, c), where_is(along_z(z, 2), y, x, c)
    loads = [
        pltpu.make_async_copy(source, target, loaded.at[i])
        for i, (source, target) in enumerate(
            ((gate_hbm, gate_ref), (up_hbm, up_ref), (ahead_hbm, ahead_ref))
        )
    ]
    for load in loads:
        load.start()
    greet([y_peer, x_peer, core_peer, near_z, far_z])
    mine = number(z, y, x, c)

    def copy(block, part, sem, peer):
        view = held.at[block, pl.ds(part * half, half)]
        return remote(view, view, sem, arrive.at[block, part], peer)

    def arrived(block, part):
        copy(block, part, to_core.at[0, 0, 0], core_peer).wait_recv()

    def block_of(q, other_y, other_x, core):
        return number(
            along_z(z, q), 1 - y if other_y else y, 1 - x if other_x else x, core
        )

    combos = ((0, 0), (0, 1), (1, 0), (1, 1))

    def stores(turn, blocks):
        slot = turn % 2
        made = []
        for k in range(4):
            part = pl.ds(k * kept, kept)
            made.append((picked.at[slot, part], rows_out.at[blocks[k]]))
            for i, out in enumerate((active_out, gate_out, up_out)):
                made.append((results.at[slot, i, part], out.at[blocks[k]]))
        return [
            pltpu.make_async_copy(source, target, stored.at[slot, i])
            for i, (source, target) in enumerate(made)
        ]

    def blocks_of(turn):
        q, other = turn // 2, turn % 2
        return [block_of(q, *combo, 1 - c if other else c) for combo in combos]

    def work(turn):
        blocks, slot = blocks_of(turn), turn % 2
        if turn >= 2:
            for store in stores(turn - 2, blocks_of(turn - 2)):
                store.wait()
        for k in range(4):
            rows = jnp.dot(
                select_ref[blocks[k]], held[blocks[k]], preferred_element_type=jnp.float32
            )
            picked[slot, k * kept : (k + 1) * kept] = rows.astype(picked.dtype)
        rows = picked[slot]
        gate_pre = jnp.dot(rows, gate_ref[...], preferred_element_type=jnp.float32)
        up_pre = jnp.dot(rows, up_ref[...], preferred_element_type=jnp.float32)
        logits = jnp.dot(rows, router_ref[...], preferred_element_type=jnp.float32)
        for k in range(4):
            part = slice(k * kept, (k + 1) * kept)
            block = blocks[k]
            masked = jnp.where(named_ref[block].astype(jnp.float32) > 0, logits[part], MASKED)
            lifted = jnp.exp(masked - jnp.max(masked, axis=1, keepdims=True))
            lanes = lax.broadcasted_iota(jnp.int32, lifted.shape, 1)
            share = jnp.sum(jnp.where(lanes == mine, lifted, 0.0), axis=1, keepdims=True)
            share = share / jnp.sum(lifted, axis=1, keepdims=True)
            gate, up, ahead = gate_pre[part], up_pre[part], ahead_ref[block]
            sigma = 1.0 / (1.0 + jnp.exp(-gate))
            silu = gate * sigma
            active_low = (silu * up).astype(results.dtype)
            grad = jnp.sum(active_low.astype(jnp.float32) * ahead, axis=1, keepdims=True)
            active_grad = share * ahead
            gate_grad = active_grad * up * (sigma * (1.0 + gate * (1.0 - sigma)))
            results[slot, 0, part] = active_low
            results[slot, 1, part] = gate_grad.astype(results.dtype)
            results[slot, 2, part] = (active_grad * silu).astype(results.dtype)
            share_out[block] = jnp.broadcast_to(share, share_out.shape[1:])
            high = grad.astype(extra_out.dtype).astype(jnp.float32)
            both = jnp.where(lanes == mine, high, jnp.where(lanes == 32 + mine, grad - high, 0.0))
            extra_out[block] = both.astype(extra_out.dtype)
        for store in stores(turn, blocks):
            store.start()

    def forward(q):
        block = block_of(q, 0, 0, c)
        if q:
            arrived(block, 0)
            arrived(block, 1)
        if q == 2:
            copy(block, 0, to_z.at[2, 0], near_z).start()
            copy(block, 1, to_z.at[2, 1], near_z).start()
        copy(block, 0, to_y.at[0, q], y_peer).start()
        copy(block, 1, to_x.at[0, q], x_peer).start()
        copy(block, 0, to_x.at[1, q], x_peer).start()
        copy(block, 1, to_y.at[1, q], y_peer).start()
        copy(block, 0, to_core.at[0, 0, q], core_peer).start()
        copy(block, 1, to_core.at[0, 1, q], core_peer).start()

    def second(q):
        block = block_of(q, 1, 0, c)
        arrived(block, 0)
        copy(block, 0, to_x.at[2, q], x_peer).start()
        copy(block, 0, to_core.at[1, 0, q], core_peer).start()
        block = block_of(q, 0, 1, c)
        arrived(block, 1)
        copy(block, 1, to_y.at[2, q], y_peer).start()
        copy(block, 1, to_core.at[2, 1, q], core_peer).start()

    def last(q):
        block = block_of(q, 0, 1, c)
        arrived(block, 0)
        copy(block, 0, to_core.at[2, 0, q], core_peer).start()
        block = block_of(q, 1, 0, c)
        arrived(block, 1)
        copy(block, 1, to_core.at[1, 1, q], core_peer).start()
        block = block_of(q, 1, 1, c)
        arrived(block, 0)
        copy(block, 0, to_core.at[3, 0, q], core_peer).start()
        arrived(block, 1)
        copy(block, 1, to_core.at[3, 1, q], core_peer).start()

    def others(q):
        for combo in combos:
            block = block_of(q, *combo, 1 - c)
            arrived(block, 0)
            arrived(block, 1)

    held[mine] = x_ref[...]
    for part in range(2):
        copy(mine, part, to_z.at[0, part], near_z).start()
    for part in range(2):
        copy(mine, part, to_z.at[1, part], far_z).start()
    forward(0)
    for load in loads:
        load.wait()
    forward(1)
    second(0)
    forward(2)
    second(1)
    last(0)
    work(0)
    others(0)
    work(1)
    forward(3)
    second(2)
    last(1)
    work(2)
    others(1)
    work(3)
    second(3)
    last(2)
    work(4)
    others(2)
    work(5)
    last(3)
    work(6)
    others(3)
    work(7)
    for turn in (6, 7):
        for store in stores(turn, blocks_of(turn)):
            store.wait()
    for part in range(2):
        copy(mine, part, to_z.at[0, part], near_z).wait_send()
        copy(mine, part, to_z.at[1, part], far_z).wait_send()
        copy(mine, part, to_z.at[2, part], near_z).wait_send()

    @pl.loop(0, 4)
    def _(q):
        for i in range(3):
            copy(mine, 0, to_y.at[i, q], y_peer).wait_send()
            copy(mine, 0, to_x.at[i, q], x_peer).wait_send()
        for i in range(4):
            for part in range(2):
                copy(mine, part, to_core.at[i, part, q], core_peer).wait_send()


def gather_experts(rows, select, ahead, named, gate_w, up_w, router):
    count, width = rows.shape
    blocks, kept = select.shape[:2]
    hidden = gate_w.shape[1]
    low = rows.dtype
    anywhere = pl.BlockSpec(memory_space=pl.ANY)
    vmem = pl.BlockSpec(memory_space=pltpu.VMEM)
    return pl.pallas_call(
        gather_kernel,
        out_shape=[
            jax.ShapeDtypeStruct((blocks, kept, width), low),
            jax.ShapeDtypeStruct((blocks, kept, hidden), low),
            jax.ShapeDtypeStruct((blocks, kept, hidden), low),
            jax.ShapeDtypeStruct((blocks, kept, hidden), low),
            jax.ShapeDtypeStruct((blocks, kept, 128), jnp.float32),
            jax.ShapeDtypeStruct((blocks, kept, 128), low),
        ],
        in_specs=[vmem, vmem, anywhere, vmem, anywhere, anywhere, vmem],
        out_specs=[anywhere] * 4 + [vmem] * 2,
        scratch_shapes=[
            pltpu.VMEM((blocks, count, width), low),
            pltpu.VMEM(ahead.shape, ahead.dtype),
            pltpu.VMEM(gate_w.shape, low),
            pltpu.VMEM(up_w.shape, low),
            pltpu.VMEM((2, 4 * kept, width), low),
            pltpu.VMEM((2, 3, 4 * kept, hidden), low),
            copies(3),
            copies(2, 16),
            copies(blocks, 2),
            copies(3, 2),
            copies(3, 4),
            copies(3, 4),
            copies(4, 2, 4),
        ],
        compiler_params=settings(1),
    )(rows, select, ahead, named, gate_w, up_w, router)


def scatter_kernel(
    extended,
    spread_ref,
    *refs,
):
    if extended:
        gate_grad_ref, up_grad_ref, gate_ref, up_ref, extra_ref, out_ref, extra_out = refs[:7]
        refs = refs[7:]
    else:
        active_ref, down_ref, share_ref, out_ref = refs[:4]
        refs = refs[4:]
    outgoing, core_in, total, back, x_in, y_in, z_in = refs[:7]
    core_sent, core_got, x_sent, x_got, y_sent, y_got, z_sent, z_got = refs[7:]
    z, y, x, c = spot()
    width = out_ref.shape[1]
    half = out_ref.shape[0] // 2
    kept = spread_ref.shape[2]
    y_peer, x_peer, core_peer = (
        where_is(z, 1 - y, x, c),
        where_is(z, y, 1 - x, c),
        where_is(z, y, x, 1 - c),
    )
    near_z, far_z = where_is(along_z(z, 1), y, x, c), where_is(along_z(z, 2), y, x, c)
    greet([y_peer, x_peer, core_peer, near_z, far_z])
    groups = ((1, 1), (0, 1), (1, 0), (0, 0))

    def block_of(group, q, core):
        other_y, other_x = groups[group]
        return number(along_z(z, q), 1 - y if other_y else y, 1 - x if other_x else x, core)

    def rows_of(ref, q, core):
        return jnp.concatenate([ref[block_of(group, q, core)] for group in range(4)], axis=0)

    def rows_back(q, core):
        if extended:
            sums = right_transposed(rows_of(gate_grad_ref, q, core), gate_ref[...])
            sums = sums + right_transposed(rows_of(up_grad_ref, q, core), up_ref[...])
        else:
            sums = jnp.dot(
                rows_of(active_ref, q, core), down_ref[...], preferred_element_type=jnp.float32
            )
            sums = sums.astype(back.dtype).astype(jnp.float32)
            sums = sums * rows_of(share_ref, q, core)[:, :1]
        back[...] = sums.astype(back.dtype)

    def part(block, group):
        rows = jnp.dot(
            spread_ref[block],
            back[group * kept : (group + 1) * kept],
            preferred_element_type=jnp.float32,
        )
        if not extended:
            return rows
        more = jnp.dot(spread_ref[block], extra_ref[block], preferred_element_type=jnp.float32)
        return jnp.concatenate([rows, more], axis=1)

    def across(group, q):
        return remote(
            outgoing.at[q, group],
            core_in.at[q, group],
            core_sent.at[q, group],
            core_got.at[q, group],
            core_peer,
        )

    def view(group, q, side):
        return total.at[q, group, pl.ds(side * half, half)]

    def x_copy(group, q, side, slot):
        return remote(
            view(group, q, side), x_in.at[slot, q], x_sent.at[slot, q], x_got.at[slot, q], x_peer
        )

    def y_copy(group, q, side, slot):
        return remote(
            view(group, q, side), y_in.at[slot, q], y_sent.at[slot, q], y_got.at[slot, q], y_peer
        )

    def z_copy(q):
        return remote(
            total.at[q, 3], z_in.at[q - 1], z_sent.at[q - 1], z_got.at[q - 1],
            far_z if q == 2 else near_z,
        )

    def add(group, q, side, source):
        rows = pl.ds(side * half, half)
        total[q, group, rows] = (
            total[q, group, rows].astype(jnp.float32) + source.astype(jnp.float32)
        ).astype(total.dtype)

    def begin(q):
        rows_back(q, 1 - c)
        for group in range(4):
            outgoing[q, group] = part(block_of(group, q, 1 - c), group).astype(total.dtype)
            across(group, q).start()
        rows_back(q, c)
        for group in range(4):
            sums = part(block_of(group, q, c), group)
            across(group, q).wait_recv()
            total[q, group] = (sums + core_in[q, group].astype(jnp.float32)).astype(total.dtype)
            if group == 0:
                x_copy(0, q, 0, 0).start()
                y_copy(0, q, 1, 0).start()
            if group == 1:
                x_copy(1, q, 0, 1).start()
            if group == 2:
                y_copy(2, q, 1, 1).start()

    def middle(q):
        x_copy(0, q, 0, 0).wait_recv()
        add(2, q, 0, x_in[0, q])
        y_copy(2, q, 0, 2).start()
        y_copy(0, q, 1, 0).wait_recv()
        add(1, q, 1, y_in[0, q])
        x_copy(1, q, 1, 2).start()

    def close(q):
        for side, arrivals in ((0, ((x_copy(1, q, 0, 1), x_in, 1), (y_copy(2, q, 0, 2), y_in, 2))),
                               (1, ((y_copy(2, q, 1, 1), y_in, 1), (x_copy(1, q, 1, 2), x_in, 2)))):
            for arrival, _, _ in arrivals:
                arrival.wait_recv()
            rows = pl.ds(side * half, half)
            sums = total[q, 3, rows].astype(jnp.float32)
            for _, source, slot in arrivals:
                sums = sums + source[slot, q].astype(jnp.float32)
            if q == 2:
                if side == 0:
                    z_copy(3).wait_recv()
                sums = sums + z_in[2, rows].astype(jnp.float32)
            if q:
                total[q, 3, rows] = sums.astype(total.dtype)
            else:
                if side == 0:
                    z_copy(1).wait_recv()
                    z_copy(2).wait_recv()
                for i in range(2):
                    sums = sums + z_in[i, rows].astype(jnp.float32)
                out_ref[rows] = sums[:, :width]
                if extended:
                    extra_out[rows] = sums[:, width:]
        if q:
            z_copy(q).start()

    begin(3)
    begin(2)
    middle(3)
    begin(1)
    middle(2)
    close(3)
    begin(0)
    middle(1)
    close(2)
    middle(0)
    close(1)
    close(0)
    for q in range(1, 4):
        z_copy(q).wait_send()

    @pl.loop(0, 4)
    def _(q):
        for group in range(4):
            across(group, q).wait_send()
        x_copy(0, q, 0, 0).wait_send()
        x_copy(1, q, 0, 1).wait_send()
        x_copy(1, q, 1, 2).wait_send()
        y_copy(0, q, 1, 0).wait_send()
        y_copy(2, q, 1, 1).wait_send()
        y_copy(2, q, 0, 2).wait_send()


def scatter_rows(spread, *operands):
    blocks, count, kept = spread.shape
    extended = len(operands) == 5
    width = operands[2].shape[0] if extended else operands[1].shape[1]
    wide = width + 128 if extended else width
    low = operands[0].dtype
    outs = [jax.ShapeDtypeStruct((count, width), jnp.float32)]
    if extended:
        outs.append(jax.ShapeDtypeStruct((count, 128), jnp.float32))
    return pl.pallas_call(
        functools.partial(scatter_kernel, extended),
        out_shape=outs,
        in_specs=in_vmem(1 + len(operands)),
        out_specs=in_vmem(len(outs)),
        scratch_shapes=[
            pltpu.VMEM((4, 4, count, wide), low),
            pltpu.VMEM((4, 4, count, wide), low),
            pltpu.VMEM((4, 4, count, wide), low),
            pltpu.VMEM((4 * kept, width), low),
            pltpu.VMEM((3, 4, count // 2, wide), low),
            pltpu.VMEM((3, 4, count // 2, wide), low),
            pltpu.VMEM((3, count, wide), low),
            copies(4, 4),
            copies(4, 4),
            copies(3, 4),
            copies(3, 4),
            copies(3, 4),
            copies(3, 4),
            copies(3),
            copies(3),
        ],
        compiler_params=settings(2 if extended else 8),
    )(spread, *operands)


def reduce_kernel(
    cuts,
    parts_ref,
    vector_ref,
    sums_out,
    vector_out,
    *refs,
):
    z, y, x, c = spot()
    member, shard = lax.axis_index("exp"), lax.axis_index("fsdp")
    y_peer = where_is(z, 1 - y, x, c)
    near_z, far_z = where_is(along_z(z, 1), y, x, c), where_is(along_z(z, 2), y, x, c)
    members = [((member + j) % 8, shard) for j in range(8)]
    shards = [(member, (shard + j) % 4) for j in range(4)]
    greet(members[1:] + shards[1:])
    pieces = len(cuts)
    first_got, first_held, first_z = refs[:3]
    y_got_in, y_held, y_z = refs[3:5], refs[5:7], refs[7:9]
    shard_in, member_own, member_in = refs[3 * pieces : 3 * pieces + 3]
    (
        y_sent,
        y_got,
        z_sent,
        z_got,
        back_sent,
        back_got,
        side_sent,
        side_got,
        shard_sent,
        shard_got,
        member_sent,
        member_got,
    ) = refs[3 * pieces + 3 :]

    def shard_copy(j):
        return remote(
            vector_ref.at[(shard + j) % 4],
            shard_in.at[(4 - j) % 4],
            shard_sent.at[j],
            shard_got.at[(4 - j) % 4],
            shards[j],
        )

    def member_copy(j):
        return remote(
            member_own,
            member_in.at[(8 - j) % 8],
            member_sent.at[j],
            member_got.at[(8 - j) % 8],
            members[j],
        )

    def rows(which):
        return pl.ds(*cuts[which])

    def z_peer(q):
        return far_z if q == 2 else near_z

    def y_copy(which, q):
        return remote(
            parts_ref.at[1 - y, along_z(z, q), rows(which)],
            y_got_in[which - 1].at[q],
            y_sent.at[which, q],
            y_got.at[which, q],
            y_peer,
        )

    def z_copy(which, q):
        if which:
            source, target = y_held[which - 1].at[q], y_z[which - 1].at[q]
        elif q == 2:
            source, target = first_held, first_z.at[2]
        else:
            source, target = parts_ref.at[:, along_z(z, q), rows(0)], first_z.at[q]
        return remote(source, target, z_sent.at[which, q], z_got.at[which, q], z_peer(q))

    def first_y():
        return remote(
            first_z.at[0, 1 - y], first_got, y_sent.at[0, 0], y_got.at[0, 0], y_peer
        )

    def place(side, q, which):
        return sums_out.at[side, along_z(z, q), rows(which)]

    def back_copy(which, q):
        held = along_z(z, 2) if q == 3 else z
        if which:
            view = sums_out.at[y, held, rows(which)]
        else:
            view = sums_out.at[:, held, rows(0)]
        return remote(view, view, back_sent.at[which, q], back_got.at[which, q], z_peer(q))

    def side_copy(which, q):
        view = place(y, q, which)
        return remote(view, view, side_sent.at[which, q], side_got.at[which, q], y_peer)

    later = range(1, pieces)
    for j in range(1, 4):
        shard_copy(j).start()
    z_copy(0, 3).start()
    for q in (3, 2, 1, 0):
        for which in later:
            y_copy(which, q).start()
    z_copy(0, 1).start()

    for j in range(1, 4):
        shard_copy(j).wait_recv()
    sums = vector_ref[shard]
    for j in range(1, 4):
        sums = sums + shard_in[j]
    member_own[...] = sums
    for j in range(1, 8):
        member_copy(j).start()

    def add_y(which, q):
        y_copy(which, q).wait_recv()
        sums = parts_ref[y, along_z(z, q), rows(which)].astype(jnp.float32)
        sums = sums + y_got_in[which - 1][q].astype(jnp.float32)
        held, z_in = y_held[which - 1], y_z[which - 1]
        if q == 2:
            z_copy(which, 3).wait_recv()
            sums = sums + z_in[3].astype(jnp.float32)
        if q:
            held[q] = sums.astype(held.dtype)
            z_copy(which, q).start()
            return
        for turn in (1, 2):
            z_copy(which, turn).wait_recv()
            sums = sums + z_in[turn].astype(jnp.float32)
        sums_out[y, z, rows(which)] = sums.astype(sums_out.dtype)
        side_copy(which, 0).start()
        back_copy(which, 2).start()
        back_copy(which, 1).start()

    for which in later:
        add_y(which, 3)
    z_copy(0, 3).wait_recv()
    first_held[...] = (
        parts_ref[:, along_z(z, 2), rows(0)].astype(jnp.float32) + first_z[3].astype(jnp.float32)
    ).astype(first_held.dtype)
    z_copy(0, 2).start()
    for which in later:
        add_y(which, 2)
    z_copy(0, 1).wait_recv()
    z_copy(0, 2).wait_recv()
    first_z[0] = (
        parts_ref[:, z, rows(0)].astype(jnp.float32)
        + first_z[1].astype(jnp.float32)
        + first_z[2].astype(jnp.float32)
    ).astype(first_z.dtype)
    first_y().start()
    for which in later:
        add_y(which, 1)
    first_y().wait_recv()
    sums = first_z[0, y].astype(jnp.float32) + first_got[...].astype(jnp.float32)
    sums_out[y, z, rows(0)] = sums.astype(sums_out.dtype)
    side_copy(0, 0).start()
    for which in later:
        add_y(which, 0)
    side_copy(0, 0).wait_recv()
    back_copy(0, 2).start()
    back_copy(0, 1).start()

    for j in range(1, 8):
        member_copy(j).wait_recv()
    sums = member_own[...]
    for j in range(1, 8):
        sums = sums + member_in[j]
    vector_out[...] = sums

    for q in (1, 2, 3):
        for which in later:
            back_copy(which, q).wait_recv()
            if q == 2:
                back_copy(which, 3).start()
            side_copy(which, q).start()
        back_copy(0, q).wait_recv()
        if q == 2:
            back_copy(0, 3).start()

    for which in later:
        for q in range(4):
            side_copy(which, q).wait_recv()
    for which in range(pieces):
        for q in range(4):
            if which:
                y_copy(which, q).wait_send()
                side_copy(which, q).wait_send()
            if q:
                z_copy(which, q).wait_send()
                back_copy(which, q).wait_send()
    side_copy(0, 0).wait_send()
    first_y().wait_send()
    for j in range(1, 4):
        shard_copy(j).wait_send()
    for j in range(1, 8):
        member_copy(j).wait_send()


def reduce_over_members(parts, vectors):
    low = parts.dtype
    depth, width = parts.shape[2:]
    early = depth * 3 // 16 // 16 * 16
    half = (depth - early) // 2 // 16 * 16
    cuts = ((0, early), (early, half), (early + half, depth - early - half))

    def quarters(*lead):
        return [pltpu.VMEM((*lead, size, width), low) for _, size in cuts[1:]]

    return pl.pallas_call(
        functools.partial(reduce_kernel, cuts),
        out_shape=[
            jax.ShapeDtypeStruct(parts.shape, low),
            jax.ShapeDtypeStruct(vectors.shape[1:], vectors.dtype),
        ],
        in_specs=in_vmem(2),
        out_specs=in_vmem(2),
        scratch_shapes=[
            pltpu.VMEM((early, width), low),
            pltpu.VMEM((2, early, width), low),
            pltpu.VMEM((4, 2, early, width), low),
            *quarters(4),
            *quarters(4),
            *quarters(4),
            pltpu.VMEM(vectors.shape, vectors.dtype),
            pltpu.VMEM(vectors.shape[1:], vectors.dtype),
            pltpu.VMEM((8, *vectors.shape[1:]), vectors.dtype),
        ]
        + [copies(3, 4)] * 8
        + [copies(4)] * 2
        + [copies(8)] * 2,
        compiler_params=settings(3),
    )(parts, vectors)


def project_kernel(
    x_ref,
    routes_ref,
    gain_ref,
    query_ref,
    key_ref,
    value_ref,
    raw_out,
    hidden_out,
    routes_out,
    scale,
    x_in,
    scale_in,
    outgoing,
    core_in,
    across_x,
    x_sums,
    slice_sent,
    slice_got,
    scale_sent,
    scale_got,
    core_sent,
    core_got,
    x_sent,
    x_got,
    route_sent,
    route_got,
):
    z, y, x, c = spot()
    member, shard = lax.axis_index("exp"), lax.axis_index("fsdp")
    mine = number(z, y, x, c)
    count, depth = hidden_out.shape[1:]
    wide, narrow = query_ref.shape[1] // 4, key_ref.shape[1] // 4

    def everyone(j):
        other = (mine + j) % 32
        return (other // 4, other % 4)

    barrier = pltpu.get_barrier_semaphore()

    @pl.loop(1, 32)
    def _(j):
        pl.semaphore_signal(barrier, inc=1, device_id=everyone(j), device_id_type=MESH)

    pl.semaphore_wait(barrier, 31)

    def slice_copy(j):
        place = (shard + j) % 4
        return remote(
            x_ref.at[:, pl.ds(pl.multiple_of(place * depth, depth), depth)],
            x_in.at[(4 - j) % 4],
            slice_sent.at[j],
            slice_got.at[(4 - j) % 4],
            (member, place),
        )

    def scale_copy(j):
        return remote(
            scale,
            scale_in.at[(4 - j) % 4],
            scale_sent.at[j],
            scale_got.at[(4 - j) % 4],
            (member, (shard + j) % 4),
        )

    def route_copy(j):
        return remote(
            routes_ref, routes_out.at[mine], route_sent.at[j], route_got.at[(32 - j) % 32], everyone(j)
        )

    for j in range(1, 4):
        slice_copy(j).start()
    values = x_ref[...].astype(jnp.float32)
    scale[...] = jnp.broadcast_to(
        lax.rsqrt(jnp.mean(values * values, axis=1, keepdims=True) + EPSILON), scale.shape
    )
    for j in range(1, 4):
        scale_copy(j).start()
    routes_out[mine] = routes_ref[...]

    @pl.loop(1, 32)
    def _(j):
        route_copy(j).start()

    def hide(owner, piece, factor):
        gain = gain_ref[...].astype(jnp.float32)
        hidden = piece.astype(jnp.float32) * factor[:, :1] * gain
        hidden_out[owner] = hidden.astype(hidden_out.dtype)

    hide(shard, x_ref[:, pl.ds(pl.multiple_of(shard * depth, depth), depth)], scale[...])

    def take(owner):
        slot = (owner - shard + 4) % 4
        remote(x_in.at[slot], x_in.at[slot], slice_sent.at[slot], slice_got.at[slot], (member, owner)).wait_recv()
        remote(scale, scale_in.at[slot], scale_sent.at[slot], scale_got.at[slot], (member, owner)).wait_recv()
        hide(owner, x_in[slot], scale_in[slot])

    def partial(side, target):
        rows = jnp.concatenate([hidden_out[side * 2], hidden_out[side * 2 + 1]], axis=0)
        parts = []
        for weight, size in ((query_ref, wide), (key_ref, narrow), (value_ref, narrow)):
            columns = pl.ds(pl.multiple_of(target * size, size), size)
            parts.append(jnp.dot(rows, weight[:, columns], preferred_element_type=jnp.float32))
        return jnp.concatenate(parts, axis=1)

    core_peer, x_peer = where_is(z, y, x, 1 - c), where_is(z, y, 1 - x, c)

    def core_copy(turn, far):
        return remote(
            outgoing.at[turn, far],
            core_in.at[turn, far],
            core_sent.at[turn, far],
            core_got.at[turn, far],
            core_peer,
        )

    def x_copy(turn):
        return remote(across_x.at[turn], x_sums.at[turn], x_sent.at[turn], x_got.at[turn], x_peer)

    low = outgoing.dtype
    for turn in range(2):
        side = x if turn == 0 else 1 - x
        if turn == 0:
            take(side * 2 + 1 - c)
        else:
            take(side * 2 + c)
            take(side * 2 + 1 - c)
        outgoing[turn, 1] = partial(side, (1 - x) * 2 + 1 - c).astype(low)
        core_copy(turn, 1).start()
        sums = partial(side, (1 - x) * 2 + c)
        core_copy(turn, 1).wait_recv()
        across_x[turn] = (sums + core_in[turn, 1].astype(jnp.float32)).astype(low)
        x_copy(turn).start()
        outgoing[turn, 0] = partial(side, x * 2 + 1 - c).astype(low)
        core_copy(turn, 0).start()

    for turn in range(2):
        side = x if turn == 0 else 1 - x
        sums = partial(side, x * 2 + c)
        core_copy(turn, 0).wait_recv()
        sums = sums + core_in[turn, 0].astype(jnp.float32)
        raw_out[side * 2] = sums[:count]
        raw_out[side * 2 + 1] = sums[count:]

    for turn in range(2):
        side = 1 - x if turn == 0 else x
        x_copy(turn).wait_recv()
        raw_out[side * 2] += x_sums[turn, :count].astype(jnp.float32)
        raw_out[side * 2 + 1] += x_sums[turn, count:].astype(jnp.float32)

    @pl.loop(1, 32)
    def _(j):
        remote(
            routes_ref, routes_out.at[(mine + j) % 32], route_sent.at[j], route_got.at[j], everyone(j)
        ).wait_recv()

    @pl.loop(1, 32)
    def _(j):
        route_copy(j).wait_send()

    for j in range(1, 4):
        slice_copy(j).wait_send()
        scale_copy(j).wait_send()
    for turn in range(2):
        x_copy(turn).wait_send()
        for far in range(2):
            core_copy(turn, far).wait_send()


def project_tokens(tokens, routes, gain, w_query, key_weight, value_weight):
    count = tokens.shape[0]
    depth = w_query.shape[0]
    own = (w_query.shape[1] + key_weight.shape[1] + value_weight.shape[1]) // 4
    low = tokens.dtype
    return pl.pallas_call(
        project_kernel,
        out_shape=[
            jax.ShapeDtypeStruct((4, count, own), jnp.float32),
            jax.ShapeDtypeStruct((4, count, depth), low),
            jax.ShapeDtypeStruct((32, *routes.shape), routes.dtype),
        ],
        in_specs=in_vmem(6),
        out_specs=in_vmem(3),
        scratch_shapes=[
            pltpu.VMEM((count, 128), jnp.float32),
            pltpu.VMEM((4, count, depth), low),
            pltpu.VMEM((4, count, 128), jnp.float32),
            pltpu.VMEM((2, 2, 2 * count, own), low),
            pltpu.VMEM((2, 2, 2 * count, own), low),
            pltpu.VMEM((2, 2 * count, own), low),
            pltpu.VMEM((2, 2 * count, own), low),
            copies(4),
            copies(4),
            copies(4),
            copies(4),
            copies(2, 2),
            copies(2, 2),
            copies(2),
            copies(2),
            copies(32),
            copies(32),
        ],
        compiler_params=settings(4),
    )(tokens, routes, gain, w_query, key_weight, value_weight)


def finish_kernel(
    attended_ref,
    weight_ref,
    x_ref,
    gain_ref,
    middle_out,
    normed_out,
    outgoing,
    core_in,
    across_x,
    x_sums,
    core_sent,
    core_got,
    x_sent,
    x_got,
):
    z, y, x, c = spot()
    count = x_ref.shape[0]
    core_peer, x_peer = where_is(z, y, x, 1 - c), where_is(z, y, 1 - x, c)
    greet([core_peer, x_peer])

    def core_copy(far):
        return remote(
            outgoing.at[far], core_in.at[far], core_sent.at[far], core_got.at[far], core_peer
        )

    def x_copy():
        return remote(across_x, x_sums, x_sent, x_got, x_peer)

    def partial(side, core):
        return jnp.dot(
            attended_ref[side * 2 + core], weight_ref[...], preferred_element_type=jnp.float32
        )

    outgoing[1] = partial(1 - x, 1 - c).astype(outgoing.dtype)
    core_copy(1).start()
    sums = partial(1 - x, c)
    core_copy(1).wait_recv()
    across_x[...] = (sums + core_in[1].astype(jnp.float32)).astype(across_x.dtype)
    x_copy().start()
    outgoing[0] = partial(x, 1 - c).astype(outgoing.dtype)
    core_copy(0).start()
    sums = partial(x, c) + x_ref[...].astype(jnp.float32)
    core_copy(0).wait_recv()
    sums = sums + core_in[0].astype(jnp.float32)
    x_copy().wait_recv()
    middle = sums + x_sums[...].astype(jnp.float32)
    middle_out[...] = middle
    scale = lax.rsqrt(jnp.mean(middle * middle, axis=1, keepdims=True) + EPSILON)
    normed_out[...] = (middle * scale * gain_ref[...]).astype(normed_out.dtype)
    x_copy().wait_send()
    core_copy(0).wait_send()
    core_copy(1).wait_send()


def finish_attention(attended, w_out, tokens, gain):
    count, width = tokens.shape
    low = tokens.dtype
    return pl.pallas_call(
        finish_kernel,
        out_shape=[
            jax.ShapeDtypeStruct((count, width), jnp.float32),
            jax.ShapeDtypeStruct((count, width), low),
        ],
        in_specs=in_vmem(4),
        out_specs=in_vmem(2),
        scratch_shapes=[
            pltpu.VMEM((2, count, width), low),
            pltpu.VMEM((2, count, width), low),
            pltpu.VMEM((count, width), low),
            pltpu.VMEM((count, width), low),
            copies(2),
            copies(2),
            copies(),
            copies(),
        ],
        compiler_params=settings(5),
    )(attended, w_out, tokens, gain)


def branch_kernel(
    branch_ref, weight_ref, grad_out, every_out, x_sent, x_got, core_sent, core_got
):
    z, y, x, c = spot()
    mine = x * 2 + c
    core_peer, x_peer = where_is(z, y, x, 1 - c), where_is(z, y, 1 - x, c)
    greet([core_peer, x_peer])
    every_out[mine] = branch_ref[...]

    def x_copy():
        return remote(branch_ref, every_out.at[mine], x_sent, x_got, x_peer)

    def core_copy(far):
        place = (1 - x if far else x) * 2 + c
        return remote(
            every_out.at[place], every_out.at[place], core_sent.at[far], core_got.at[far], core_peer
        )

    def back(place):
        grad_out[place] = right_transposed(every_out[place], weight_ref[...]).astype(grad_out.dtype)

    x_copy().start()
    core_copy(0).start()
    back(mine)
    core_copy(0).wait_recv()
    back(x * 2 + 1 - c)
    x_copy().wait_recv()
    core_copy(1).start()
    back((1 - x) * 2 + c)
    core_copy(1).wait_recv()
    back((1 - x) * 2 + 1 - c)
    x_copy().wait_send()
    core_copy(0).wait_send()
    core_copy(1).wait_send()


def branch_back(branch, w_out):
    count, width = branch.shape
    low = branch.dtype
    return pl.pallas_call(
        branch_kernel,
        out_shape=[
            jax.ShapeDtypeStruct((4, count, w_out.shape[0]), low),
            jax.ShapeDtypeStruct((4, count, width), low),
        ],
        in_specs=in_vmem(2),
        out_specs=in_vmem(2),
        scratch_shapes=[copies(), copies(), copies(2), copies(2)],
        compiler_params=settings(6),
    )(branch, w_out)


def heads_kernel(
    grad_ref,
    hidden_ref,
    query_ref,
    key_ref,
    value_ref,
    weight_out,
    first_out,
    every,
    outgoing,
    x_sent,
    x_got,
    core_sent,
    core_got,
    back_sent,
    back_got,
):
    z, y, x, c = spot()
    member, shard = lax.axis_index("exp"), lax.axis_index("fsdp")
    core_peer, x_peer = where_is(z, y, x, 1 - c), where_is(z, y, 1 - x, c)
    peers = [(member, (shard + j) % 4) for j in range(1, 4)]
    greet(peers)
    rows = grad_ref.shape[0]
    half = rows // 2
    count = rows // 4
    depth = hidden_ref.shape[1]
    wide, narrow = query_ref.shape[1] // 4, key_ref.shape[1] // 4
    every[shard] = grad_ref[...]

    def x_copy(part):
        piece = pl.ds(part * half, half)
        return remote(
            grad_ref.at[piece], every.at[shard, piece], x_sent.at[part], x_got.at[part], x_peer
        )

    def core_copy(far, part):
        view = every.at[(1 - x if far else x) * 2 + c, pl.ds(part * half, half)]
        return remote(view, view, core_sent.at[far, part], core_got.at[far, part], core_peer)

    for part in range(2):
        x_copy(part).start()
    for part in range(2):
        core_copy(0, part).start()

    def weigh(place):
        weight_out[place] = left_trans(hidden_ref[...], every[place]).astype(weight_out.dtype)

    def back(place):
        grads = every[place]
        sums = None
        for weight, size, start in (
            (query_ref, wide, 0),
            (key_ref, narrow, wide),
            (value_ref, narrow, wide + narrow),
        ):
            columns = pl.ds(pl.multiple_of(place * size, size), size)
            term = right_transposed(grads[:, start : start + size], weight[:, columns])
            sums = term if sums is None else sums + term
        return sums

    total = back(shard)
    weigh(shard)
    near = x * 2 + 1 - c
    for part in range(2):
        core_copy(0, part).wait_recv()
    total = total + back(near)
    weigh(near)
    for part in range(2):
        x_copy(part).wait_recv()
        core_copy(1, part).start()
    far = (1 - x) * 2 + c
    total = total + back(far)
    for part in range(2):
        core_copy(1, part).wait_recv()
    total = total + back((1 - x) * 2 + 1 - c)
    for owner in range(4):
        outgoing[owner] = total[owner * count : (owner + 1) * count].astype(outgoing.dtype)

    def back_copy(j):
        place = (shard + j) % 4
        return remote(
            outgoing.at[place],
            first_out.at[shard],
            back_sent.at[j],
            back_got.at[(4 - j) % 4],
            (member, place),
        )

    for j in range(1, 4):
        back_copy(j).start()
    first_out[shard] = outgoing[shard]
    weigh(far)
    weigh((1 - x) * 2 + 1 - c)
    for j in range(1, 4):
        place = (shard + j) % 4
        remote(
            outgoing.at[place], first_out.at[place], back_sent.at[j], back_got.at[j], (member, place)
        ).wait_recv()
    for j in range(1, 4):
        back_copy(j).wait_send()
    for part in range(2):
        x_copy(part).wait_send()
        for far in range(2):
            core_copy(far, part).wait_send()


def heads_back(grads, hidden, w_query, key_weight, value_weight):
    rows, own = grads.shape
    depth = hidden.shape[1]
    low = grads.dtype
    return pl.pallas_call(
        heads_kernel,
        out_shape=[
            jax.ShapeDtypeStruct((4, depth, own), low),
            jax.ShapeDtypeStruct((4, rows // 4, depth), low),
        ],
        in_specs=in_vmem(5),
        out_specs=in_vmem(2),
        scratch_shapes=[
            pltpu.VMEM((4, rows, own), low),
            pltpu.VMEM((4, rows // 4, depth), low),
            copies(2),
            copies(2),
            copies(2, 2),
            copies(2, 2),
            copies(4),
            copies(4),
        ],
        compiler_params=settings(7),
    )(grads, hidden, w_query, key_weight, value_weight)


def moe_gathered(normed, router, routes, capacity, cotangent, weights, notes):
    gate_w, up_w, down_w = weights
    token_count, topk = routes.shape
    experts = router.shape[1]
    mine = lax.axis_index("exp") * lax.axis_size("fsdp") + lax.axis_index("fsdp")
    all_routes = notes[:, :topk]
    all_grads = lax.all_gather(cotangent, BOTH, axis=0, tiled=True)
    columns = jnp.arange(experts, dtype=jnp.int32)
    named = jnp.any(all_routes[:, :, None, :] == columns[None, None, :, None], axis=1)
    own = jnp.any(all_routes == mine, axis=1)
    before = jnp.tril(jnp.ones((token_count, token_count), jnp.bfloat16), -1)
    rank = right_transposed(own.astype(jnp.bfloat16), before).astype(jnp.int32)
    places = jnp.arange(capacity, dtype=jnp.int32)
    select = (own[:, None, :] & (rank[:, None, :] == places[None, :, None])).astype(jnp.bfloat16)
    spread = (own[:, :, None] & (rank[:, :, None] == places[None, None, :])).astype(jnp.bfloat16)
    grad_rows = contract(
        "bcj,bjd->bcd", select, all_grads.reshape(experts, token_count, MODEL_WIDTH)
    ).astype(jnp.bfloat16)
    named_rows = contract("bcj,bej->bce", select, named.astype(jnp.bfloat16))
    named_rows = jnp.pad(named_rows.astype(jnp.bfloat16), ((0, 0), (0, 0), (0, 128 - experts)))
    flat_grads = grad_rows.reshape(experts * capacity, MODEL_WIDTH)
    ahead = right_transposed(flat_grads, down_w).reshape(experts, capacity, -1)

    padded = jnp.pad(router, ((0, 0), (0, 128 - experts)))
    arrived, active, gate_pre_grad, up_pre_grad, share, extra = gather_experts(
        normed, select, ahead, named_rows, gate_w, up_w, padded
    )
    summed, back = scatter_rows(spread, gate_pre_grad, up_pre_grad, gate_w, up_w, extra)
    (mixed,) = scatter_rows(spread, active, down_w, share)
    summed, back, mixed = lax.optimization_barrier((summed, back, mixed))

    def flat(rows):
        return rows.reshape(experts * capacity, rows.shape[2])

    share = flat(share)[:, :1]
    out_rows = (share * flat_grads.astype(jnp.float32)).astype(jnp.bfloat16)
    weight_grads = (
        left_trans(flat(arrived), flat(gate_pre_grad)),
        left_trans(flat(arrived), flat(up_pre_grad)),
        left_trans(flat(active), out_rows),
    )
    gate_grad = back[:, :experts] + back[:, experts : 2 * experts]
    picks = jnp.any(routes[:, :, None] == columns[None, None, :], axis=1)
    gates = jax.nn.softmax(jnp.where(picks, matrix_product(normed, router), MASKED), axis=1)
    logit_grad = gates * (gate_grad - jnp.sum(gates * gate_grad, axis=1, keepdims=True))
    return mixed, summed, logit_grad.astype(jnp.bfloat16), *weight_grads


def moe_exchanged(normed, router, routes, capacity, cotangent, weights, notes):
    gate_w, up_w, down_w = weights
    token_count, topk = routes.shape
    experts = router.shape[1]
    gates = gates_of(matrix_product(normed, router), routes, experts)
    slots = slot_table(routes, experts, capacity)

    def send(rows):
        packed = jnp.zeros((experts * capacity, MODEL_WIDTH), jnp.bfloat16).at[slots].set(rows)
        return exchange(packed.reshape(experts, capacity, MODEL_WIDTH)).reshape(
            experts * capacity, MODEL_WIDTH
        )

    def bring(rows):
        rows = exchange(rows.reshape(experts, capacity, MODEL_WIDTH))
        return rows.reshape(experts * capacity, MODEL_WIDTH)[slots].reshape(
            token_count, topk, MODEL_WIDTH
        )

    arrived = send(jnp.repeat(normed, topk, axis=0))
    hidden = expert_forward(arrived, gate_w, up_w)
    scaled = (gates[:, :, None] * cotangent.astype(jnp.float32)[:, None, :]).astype(jnp.bfloat16)
    out_rows = send(scaled.reshape(token_count * topk, MODEL_WIDTH))
    rows_back, gate_pre_grad, up_pre_grad = expert_back(out_rows, hidden, gate_w, up_w, down_w)
    gate_w_grad = left_trans(arrived, gate_pre_grad)
    up_w_grad = left_trans(arrived, up_pre_grad)
    down_grad = left_trans(hidden[3], out_rows)
    returned = bring(matrix_product(hidden[3], down_w).astype(jnp.bfloat16))
    mixed = jnp.einsum("tk,tkd->td", gates, returned.astype(jnp.float32))
    gate_grad = jnp.einsum("td,tkd->tk", cotangent, returned, preferred_element_type=jnp.float32)
    summed = jnp.sum(bring(rows_back), axis=1, dtype=jnp.float32)
    picked_grad = gates * (gate_grad - jnp.sum(gates * gate_grad, axis=1, keepdims=True))
    onehot = routes[:, :, None] == jnp.arange(experts, dtype=jnp.int32)[None, None, :]
    logit_grad = jnp.sum(jnp.where(onehot, picked_grad[:, :, None], 0.0), axis=1)
    return mixed, summed, logit_grad.astype(jnp.bfloat16), gate_w_grad, up_w_grad, down_grad


def local(
    tokens,
    lengths,
    routes,
    attn_gain,
    w_query,
    key_weight,
    value_weight,
    q_gain,
    k_gain,
    w_out,
    mlp_gain,
    w_router,
    expert_gate,
    expert_up,
    expert_down,
    cotangent,
):
    shards, members = lax.axis_size("fsdp"), lax.axis_size("exp")
    experts = shards * members
    token_count, topk = routes.shape
    capacity = 2 * token_count * topk // experts
    group = shards * token_count
    depth = w_query.shape[0]
    heads = QUERY_HEADS // shards
    kv_heads = max(1, KEY_VALUE_HEADS // shards)
    copies_of = shards * kv_heads // KEY_VALUE_HEADS
    head_group = heads // kv_heads
    wide, narrow = heads * HEAD_WIDTH, kv_heads * HEAD_WIDTH
    place = lax.axis_index("fsdp")

    gathered = lax.all_gather(
        jnp.concatenate([w_router.reshape(-1), attn_gain, mlp_gain, q_gain, k_gain]), "fsdp"
    )
    cuts, start = [], 0
    for leaf in (w_router, attn_gain, mlp_gain, q_gain, k_gain):
        cuts.append(gathered[:, start : start + leaf.size])
        start += leaf.size
    router = cuts[0].reshape(MODEL_WIDTH, experts)
    gain_attn, gain_mlp, gain_query, gain_key = [
        cut.reshape(-1).astype(jnp.float32) for cut in cuts[1:]
    ]
    dense = (members, shards) == (8, 4) and 2 * capacity >= token_count
    inputs = tokens.astype(jnp.float32)
    scale_one = rms_scale(inputs)
    if dense:
        notes = jnp.pad(
            jnp.concatenate(
                [routes.T, jnp.pad(lengths, ((0, 0), (0, token_count - lengths.shape[1])))], axis=0
            ),
            ((0, 15 - topk), (0, 0)),
        )
        raw, hidden, notes = project_tokens(
            tokens, notes, attn_gain[None], w_query, key_weight, value_weight
        )
        hidden = hidden.reshape(group, depth)
        first = lax.axis_index("exp") * shards
        all_lengths = lax.dynamic_slice_in_dim(notes, first, shards)[:, topk, : lengths.shape[1]]
    else:
        notes = None
        all_lengths = lax.all_gather(lengths[0], "fsdp")

        def by_shard(weight):
            weight = weight.reshape(depth, KEY_VALUE_HEADS, HEAD_WIDTH)
            return jnp.repeat(weight, copies_of, axis=1).reshape(depth, shards, narrow)

        joined = jnp.concatenate(
            [w_query.reshape(depth, shards, wide), by_shard(key_weight), by_shard(value_weight)],
            axis=2,
        ).transpose(1, 0, 2)
        first_normed = (inputs * scale_one * gain_attn).astype(jnp.bfloat16)
        hidden = lax.all_to_all(first_normed, "fsdp", split_axis=1, concat_axis=0, tiled=True)
        partial = contract("gk,nkc->ngc", hidden, joined).astype(jnp.bfloat16)
        raw = lax.psum_scatter(partial, "fsdp", scatter_dimension=0, tiled=True)[0]
        raw = raw.astype(jnp.float32)
    raw = raw.reshape(shards, token_count, wide + 2 * narrow)
    query_raw = raw[:, :, :wide].reshape(shards, token_count, heads, HEAD_WIDTH)
    key_raw = raw[:, :, wide : wide + narrow].reshape(shards, token_count, kv_heads, HEAD_WIDTH)
    value = (
        raw[:, :, wide + narrow :]
        .astype(jnp.bfloat16)
        .reshape(shards, token_count, kv_heads, HEAD_WIDTH)
    )
    position, allowed = jax.vmap(lambda row: seq_layout(row, token_count))(all_lengths)
    cosine, sine = rotary_tables(position, HEAD_WIDTH)
    query_scale = rms_scale(query_raw)
    query_hat = query_raw * query_scale
    key_scale = rms_scale(key_raw)
    key_hat = key_raw * key_scale
    query = (
        rotate(query_hat * gain_query, cosine, sine)
        .astype(jnp.bfloat16)
        .reshape(shards, token_count, kv_heads, head_group, HEAD_WIDTH)
    )
    key = rotate(key_hat * gain_key, cosine, sine).astype(jnp.bfloat16)
    scores = contract("bqkgd,bpkd->bkgqp", query, key) * HEAD_WIDTH ** (-0.5)
    scores = jnp.where(allowed[:, None, None], scores, MASKED)
    top = jnp.max(scores, axis=-1, keepdims=True)
    raised = jnp.exp(scores - top)
    probs = raised / jnp.sum(raised, axis=-1, keepdims=True)
    probs_low = probs.astype(jnp.bfloat16)
    attended = contract("bkgqp,bpkd->bqkgd", probs_low, value).astype(jnp.bfloat16)
    attended = attended.reshape(group, wide)
    if dense:
        middle, normed = finish_attention(
            attended.reshape(shards, token_count, wide), w_out, tokens, gain_mlp[None]
        )
        scale_two = rms_scale(middle)
    else:
        mixed_heads = lax.psum_scatter(
            matrix_product(attended, w_out).astype(jnp.bfloat16),
            "fsdp",
            scatter_dimension=0,
            tiled=True,
        )
        middle = inputs + mixed_heads.astype(jnp.float32)
        scale_two = rms_scale(middle)
        normed = (middle * scale_two * gain_mlp).astype(jnp.bfloat16)

    moe = moe_gathered if dense else moe_exchanged
    mixed, summed, logit_grad, gate_w_grad, up_w_grad, down_grad = moe(
        normed,
        router,
        routes,
        capacity,
        cotangent,
        (expert_gate[0], expert_up[0], expert_down[0]),
        notes,
    )
    layer_out = (middle + mixed).astype(jnp.bfloat16)

    upstream = cotangent.astype(jnp.float32)
    normed_grad = summed + right_transposed(logit_grad, router)
    mlp_gain_grad = jnp.sum(normed_grad * middle * scale_two, axis=0)
    router_grad = left_trans(normed, logit_grad)
    middle_grad = upstream + rms_back(normed_grad * gain_mlp, middle, scale_two)
    branch_low = middle_grad.astype(jnp.bfloat16)
    if dense:
        attended_grad, branch_grad = branch_back(branch_low, w_out)
        branch_grad = branch_grad.reshape(group, MODEL_WIDTH)
    else:
        branch_grad = lax.all_gather(branch_low, "fsdp", axis=0, tiled=True)
        attended_grad = right_transposed(branch_grad, w_out).astype(jnp.bfloat16)
    out_w_grad = left_trans(attended, branch_grad).astype(jnp.bfloat16)
    attended_grad, out_w_grad = lax.optimization_barrier((attended_grad, out_w_grad))
    attended_grad = attended_grad.reshape(shards, token_count, kv_heads, head_group, HEAD_WIDTH)
    prob_grad = contract("bqkgd,bpkd->bkgqp", attended_grad, value)
    value_grad = contract("bkgqp,bqkgd->bpkd", probs_low, attended_grad)
    balance = jnp.sum(probs * prob_grad, axis=-1, keepdims=True)
    score_grad = (probs * (prob_grad - balance)).astype(jnp.bfloat16)
    query_norm_grad = contract("bkgqp,bpkd->bqkgd", score_grad, key) * HEAD_WIDTH ** (-0.5)
    query_norm_grad = query_norm_grad.reshape(shards, token_count, heads, HEAD_WIDTH)
    key_norm_grad = contract("bkgqp,bqkgd->bpkd", score_grad, query) * HEAD_WIDTH ** (-0.5)
    query_norm_grad = rotate_back(query_norm_grad, cosine, sine)
    key_norm_grad = rotate_back(key_norm_grad, cosine, sine)
    q_gain_grad = jnp.sum(query_norm_grad * query_hat, axis=(0, 1, 2))
    k_gain_grad = jnp.sum(key_norm_grad * key_hat, axis=(0, 1, 2))
    query_grad = rms_back(query_norm_grad * gain_query, query_raw, query_scale)
    key_grad = rms_back(key_norm_grad * gain_key, key_raw, key_scale)
    head_grads = jnp.concatenate(
        [
            query_grad.reshape(group, wide),
            key_grad.reshape(group, narrow),
            value_grad.reshape(group, narrow),
        ],
        axis=1,
    ).astype(jnp.bfloat16)
    if dense:
        joined_grad, first_grad = heads_back(head_grads, hidden, w_query, key_weight, value_weight)
        first_grad = first_grad.transpose(1, 0, 2).reshape(token_count, MODEL_WIDTH)
    else:
        head_grads = lax.all_gather(head_grads, "fsdp")
        hidden_grad = contract("ngc,nkc->gk", head_grads, joined).astype(jnp.bfloat16)
        first_grad = lax.all_to_all(
            hidden_grad, "fsdp", split_axis=0, concat_axis=1, tiled=True
        )
        joined_grad = contract("gk,ngc->nkc", hidden, head_grads).astype(jnp.bfloat16)
    first_grad = first_grad.astype(jnp.float32)
    attn_gain_grad = jnp.sum(first_grad * inputs * scale_one, axis=0)
    input_grad = (middle_grad + rms_back(first_grad * gain_attn, inputs, scale_one)).astype(
        jnp.bfloat16
    )

    if dense:
        out_sum = lax.psum_scatter(out_w_grad, "exp", scatter_dimension=0, tiled=True)
        joined_grad, out_sum = lax.optimization_barrier((joined_grad, out_sum))
        out_sum = lax.all_gather(out_sum, "exp", axis=0, tiled=True)
    else:
        out_sum = lax.psum(out_w_grad, "exp")
    vectors = jnp.concatenate(
        [
            grad.reshape(shards, -1)
            for grad in (router_grad, attn_gain_grad, mlp_gain_grad, q_gain_grad, k_gain_grad)
        ],
        axis=1,
    )
    if dense:
        joined_grad, out_sum, gate_w_grad, up_w_grad, down_grad = lax.optimization_barrier(
            (joined_grad, out_sum, gate_w_grad, up_w_grad, down_grad)
        )
        rows = -(-vectors.shape[1] // 1024) * 8
        padded = jnp.pad(vectors, ((0, 0), (0, rows * 128 - vectors.shape[1])))
        joined_sum, vectors = reduce_over_members(
            joined_grad.reshape(2, 4, -1, wide + 2 * narrow), padded.reshape(shards, rows, 128)
        )
        joined_sum, vectors = joined_sum.reshape(joined_grad.shape), vectors.reshape(-1)
    else:
        joined_sum = lax.psum(joined_grad, "exp")
        vectors = lax.psum(vectors, BOTH)[place]
    out_sum, joined_sum = out_sum.astype(jnp.float32), joined_sum.astype(jnp.float32)
    sums, start = [], 0
    for leaf in (w_router, attn_gain, mlp_gain, q_gain, k_gain):
        sums.append(vectors[start : start + leaf.size].reshape(leaf.shape))
        start += leaf.size

    def gather_heads(part):
        return part.transpose(1, 0, 2).reshape(depth, KEY_VALUE_HEADS, copies_of, HEAD_WIDTH).sum(
            axis=2
        ).reshape(depth, KEY_VALUE_HEADS * HEAD_WIDTH)

    return (
        layer_out,
        input_grad,
        sums[1],
        joined_sum[:, :, :wide].transpose(1, 0, 2).reshape(depth, QUERY_HEADS * HEAD_WIDTH),
        gather_heads(joined_sum[:, :, wide : wide + narrow]),
        gather_heads(joined_sum[:, :, wide + narrow :]),
        sums[3],
        sums[4],
        out_sum,
        sums[2],
        sums[0],
        gate_w_grad[None],
        up_w_grad[None],
        down_grad[None],
    )


def solution(mesh):
    in_specs = (
        P(("exp", "fsdp"), None),
        P(("exp", "fsdp"), None),
        P(("exp", "fsdp"), None),
        P("fsdp"),
        P("fsdp", None),
        P("fsdp", None),
        P("fsdp", None),
        P("fsdp"),
        P("fsdp"),
        P("fsdp", None),
        P("fsdp"),
        P("fsdp", None),
        P(("exp", "fsdp"), None, None),
        P(("exp", "fsdp"), None, None),
        P(("exp", "fsdp"), None, None),
        P(("exp", "fsdp"), None),
    )
    out_specs = (
        P(("exp", "fsdp"), None),
        P(("exp", "fsdp"), None),
        P("fsdp"),
        P("fsdp", None),
        P("fsdp", None),
        P("fsdp", None),
        P("fsdp"),
        P("fsdp"),
        P("fsdp", None),
        P("fsdp"),
        P("fsdp", None),
        P(("exp", "fsdp"), None, None),
        P(("exp", "fsdp"), None, None),
        P(("exp", "fsdp"), None, None),
    )
    return jax.shard_map(local, mesh=mesh, in_specs=in_specs, out_specs=out_specs, check_vma=False)
```

```python
import functools
import math

import jax
import jax.numpy as jnp
from jax import lax
from jax.experimental import pallas as pl
from jax.experimental.pallas import tpu as pltpu
from jax.sharding import PartitionSpec as P

MODEL_WIDTH = 2048
QUERY_HEADS = 32
KEY_VALUE_HEADS = 4
HEAD_WIDTH = 128


EPSILON = 1e-06
THETA = 1000000.0
MASKED = -1e30
BOTH = ("exp", "fsdp")
MESH = pl.DeviceIdType.MESH


def matrix_product(left, right):
    return jnp.dot(left, right, preferred_element_type=jnp.float32)


def left_trans(left, right):
    return lax.dot_general(
        left, right, (((0,), (0,)), ((), ())), preferred_element_type=jnp.float32
    )


def right_transposed(left, right):
    return lax.dot_general(
        left, right, (((1,), (1,)), ((), ())), preferred_element_type=jnp.float32
    )


def contract(spec, left, right):
    return jnp.einsum(spec, left, right, preferred_element_type=jnp.float32)


def rms_scale(values):
    return lax.rsqrt(jnp.mean(values * values, axis=-1, keepdims=True) + EPSILON)


def rms_back(grad_hat, values, scale):
    normal = values * scale
    return scale * (grad_hat - normal * jnp.mean(grad_hat * normal, axis=-1, keepdims=True))


def seq_layout(length_row, token_count):
    ends = jnp.cumsum(length_row)
    starts = ends - length_row
    places = jnp.arange(token_count, dtype=jnp.int32)
    member = (places[:, None] >= starts[None, :]) & (places[:, None] < ends[None, :])
    numbers = jnp.arange(length_row.shape[0], dtype=jnp.int32)
    segment = jnp.sum(jnp.where(member, numbers[None, :], 0), axis=1)
    position = places - jnp.sum(jnp.where(member, starts[None, :], 0), axis=1)
    allowed = (segment[:, None] == segment[None, :]) & (places[None, :] <= places[:, None])
    return (position, allowed)


def rotary_tables(position, head_size):
    half = head_size // 2
    index = jnp.arange(head_size, dtype=jnp.int32) % half
    inverse = jnp.exp(index.astype(jnp.float32) * (-2.0 * math.log(THETA) / head_size))
    angles = position.astype(jnp.float32)[..., None] * inverse
    return (jnp.cos(angles)[..., None, :], jnp.sin(angles)[..., None, :])


def rotate(values, cosine, sine):
    half = values.shape[-1] // 2
    turned = jnp.concatenate([-values[..., half:], values[..., :half]], axis=-1)
    return values * cosine + turned * sine


def rotate_back(grads, cosine, sine):
    half = grads.shape[-1] // 2
    moved = grads * sine
    return grads * cosine + jnp.concatenate([moved[..., half:], -moved[..., :half]], axis=-1)


def slot_table(route_rows, experts, capacity):
    flat = route_rows.reshape(-1)
    onehot = (flat[:, None] == jnp.arange(experts, dtype=jnp.int32)[None, :]).astype(jnp.int32)
    ranks = jnp.cumsum(onehot, axis=0) - 1
    rank = jnp.sum(ranks * onehot, axis=1)
    return flat * capacity + rank


def exchange(buffer):
    return lax.all_to_all(buffer, BOTH, split_axis=0, concat_axis=0, tiled=True)


def two_halves(values):
    high = values.astype(jnp.bfloat16)
    low = (values - high.astype(jnp.float32)).astype(jnp.bfloat16)
    return high, low


def expert_forward(arrived, gate_w, up_w):
    gate_pre = matrix_product(arrived, gate_w)
    up_pre = matrix_product(arrived, up_w)
    sigma = jax.nn.sigmoid(gate_pre)
    active = (gate_pre * sigma * up_pre).astype(jnp.bfloat16)
    return gate_pre, up_pre, sigma, active


def expert_back(out_rows, hidden, gate_w, up_w, down_w):
    gate_pre, up_pre, sigma, _ = hidden
    active_grad = right_transposed(out_rows, down_w)
    gate_pre_grad = (active_grad * up_pre * (sigma * (1.0 + gate_pre * (1.0 - sigma)))).astype(
        jnp.bfloat16
    )
    up_pre_grad = (active_grad * (gate_pre * sigma)).astype(jnp.bfloat16)
    rows_back = right_transposed(gate_pre_grad, gate_w) + right_transposed(up_pre_grad, up_w)
    return rows_back.astype(jnp.bfloat16), gate_pre_grad, up_pre_grad


def gates_of(logits, routes, experts):
    picked = jnp.take_along_axis(logits, routes, axis=1)
    peak = jnp.max(picked, axis=1, keepdims=True)
    lifted = jnp.exp(picked - peak)
    return lifted / jnp.sum(lifted, axis=1, keepdims=True)


def spot():
    member, shard = lax.axis_index("exp"), lax.axis_index("fsdp")
    return member // 2, member % 2, shard // 2, shard % 2


def where_is(z, y, x, c):
    return (z * 2 + y, x * 2 + c)


def number(z, y, x, c):
    return z * 8 + y * 4 + x * 2 + c


def along_z(z, q):
    return (z // 2 + q // 2) % 2 * 2 + (z % 2 + q % 2) % 2


def greet(peers):
    barrier = pltpu.get_barrier_semaphore()
    for peer in peers:
        pl.semaphore_signal(barrier, inc=1, device_id=peer, device_id_type=MESH)
    pl.semaphore_wait(barrier, len(peers))


def remote(source, target, sent, got, peer):
    return pltpu.make_async_remote_copy(
        src_ref=source,
        dst_ref=target,
        send_sem=sent,
        recv_sem=got,
        device_id=peer,
        device_id_type=MESH,
    )


def in_vmem(count):
    return [pl.BlockSpec(memory_space=pltpu.VMEM)] * count


def copies(*shape):
    return pltpu.SemaphoreType.DMA(shape)


def settings(collective_id):
    return pltpu.CompilerParams(
        collective_id=collective_id, has_side_effects=True, vmem_limit_bytes=60 << 20
    )


def gather_kernel(
    x_ref,
    select_ref,
    named_ref,
    gate_hbm,
    up_hbm,
    router_ref,
    rows_out,
    active_out,
    gate_out,
    up_out,
    share_out,
    held,
    gate_ref,
    up_ref,
    picked,
    lively,
    results,
    loaded,
    stored,
    arrive,
    to_z,
    to_y,
    to_x,
    to_core,
):
    z, y, x, c = spot()
    half = x_ref.shape[0] // 2
    kept = select_ref.shape[1]
    y_peer, x_peer, core_peer = (
        where_is(z, 1 - y, x, c),
        where_is(z, y, 1 - x, c),
        where_is(z, y, x, 1 - c),
    )
    near_z, far_z = where_is(along_z(z, 1), y, x, c), where_is(along_z(z, 2), y, x, c)
    loads = [
        pltpu.make_async_copy(source, target, loaded.at[i])
        for i, (source, target) in enumerate(
            ((gate_hbm, gate_ref), (up_hbm, up_ref))
        )
    ]
    for load in loads:
        load.start()
    greet([y_peer, x_peer, core_peer, near_z, far_z])
    mine = number(z, y, x, c)

    def copy(block, part, sem, peer):
        view = held.at[block, pl.ds(part * half, half)]
        return remote(view, view, sem, arrive.at[block, part], peer)

    def arrived(block, part):
        copy(block, part, to_core.at[0, 0, 0], core_peer).wait_recv()

    def block_of(q, other_y, other_x, core):
        return number(
            along_z(z, q), 1 - y if other_y else y, 1 - x if other_x else x, core
        )

    combos = ((0, 0), (0, 1), (1, 0), (1, 1))

    def stores(slot, blocks):
        made = []
        for k in range(4):
            part = pl.ds(k * kept, kept)
            made.append((picked.at[slot, part], rows_out.at[blocks[k]]))
            made.append((lively.at[slot, part], active_out.at[blocks[k]]))
            for i, out in enumerate((gate_out, up_out)):
                made.append((results.at[slot, i, part], out.at[blocks[k]]))
        return [
            pltpu.make_async_copy(source, target, stored.at[slot, i])
            for i, (source, target) in enumerate(made)
        ]

    def work(q, slot):
        core = 1 - c if slot else c
        blocks = [block_of(q, *combo, core) for combo in combos]

        @pl.when(q > 0)
        def _():
            for store in stores(slot, [block_of(q - 1, *combo, core) for combo in combos]):
                store.wait()

        for k in range(4):
            rows = jnp.dot(
                select_ref[blocks[k]], held[blocks[k]], preferred_element_type=jnp.float32
            )
            picked[slot, k * kept : (k + 1) * kept] = rows.astype(picked.dtype)
        rows = picked[slot]
        gate_pre = jnp.dot(rows, gate_ref[...], preferred_element_type=jnp.float32)
        up_pre = jnp.dot(rows, up_ref[...], preferred_element_type=jnp.float32)
        logits = jnp.dot(rows, router_ref[...], preferred_element_type=jnp.float32)
        results[slot, 0] = gate_pre
        results[slot, 1] = up_pre
        active = gate_pre * (1.0 / (1.0 + jnp.exp(-gate_pre))) * up_pre
        lively[slot] = active.astype(lively.dtype)
        for k in range(4):
            part = slice(k * kept, (k + 1) * kept)
            block = blocks[k]
            masked = jnp.where(named_ref[block].astype(jnp.float32) > 0, logits[part], MASKED)
            lifted = jnp.exp(masked - jnp.max(masked, axis=1, keepdims=True))
            lanes = lax.broadcasted_iota(jnp.int32, lifted.shape, 1)
            share = jnp.sum(jnp.where(lanes == mine, lifted, 0.0), axis=1, keepdims=True)
            share = share / jnp.sum(lifted, axis=1, keepdims=True)
            share_out[block] = jnp.broadcast_to(share, share_out.shape[1:])
        for store in stores(slot, blocks):
            store.start()

    def forward(q):
        block = block_of(q, 0, 0, c)
        if q:
            arrived(block, 0)
            arrived(block, 1)
        if q == 2:
            copy(block, 0, to_z.at[2, 0], near_z).start()
            copy(block, 1, to_z.at[2, 1], near_z).start()
        copy(block, 0, to_y.at[0, q], y_peer).start()
        copy(block, 1, to_x.at[0, q], x_peer).start()
        copy(block, 0, to_x.at[1, q], x_peer).start()
        copy(block, 1, to_y.at[1, q], y_peer).start()
        copy(block, 0, to_core.at[0, 0, q], core_peer).start()
        copy(block, 1, to_core.at[0, 1, q], core_peer).start()

    def second(q):
        block = block_of(q, 1, 0, c)
        arrived(block, 0)
        copy(block, 0, to_x.at[2, q], x_peer).start()
        copy(block, 0, to_core.at[1, 0, q], core_peer).start()
        block = block_of(q, 0, 1, c)
        arrived(block, 1)
        copy(block, 1, to_y.at[2, q], y_peer).start()
        copy(block, 1, to_core.at[2, 1, q], core_peer).start()

    def last(q):
        block = block_of(q, 0, 1, c)
        arrived(block, 0)
        copy(block, 0, to_core.at[2, 0, q], core_peer).start()
        block = block_of(q, 1, 0, c)
        arrived(block, 1)
        copy(block, 1, to_core.at[1, 1, q], core_peer).start()
        block = block_of(q, 1, 1, c)
        arrived(block, 0)
        copy(block, 0, to_core.at[3, 0, q], core_peer).start()
        arrived(block, 1)
        copy(block, 1, to_core.at[3, 1, q], core_peer).start()

    def others(q):
        for combo in combos:
            block = block_of(q, *combo, 1 - c)
            arrived(block, 0)
            arrived(block, 1)

    held[mine] = x_ref[...]
    for part in range(2):
        copy(mine, part, to_z.at[0, part], near_z).start()
    for part in range(2):
        copy(mine, part, to_z.at[1, part], far_z).start()
    forward(0)
    for load in loads:
        load.wait()
    forward(1)
    second(0)
    forward(2)
    second(1)

    @pl.loop(0, 4)
    def _(q):
        last(q)
        work(q, 0)
        others(q)
        work(q, 1)

        @pl.when(q == 0)
        def _():
            forward(3)
            second(2)

        @pl.when(q == 1)
        def _():
            second(3)

    for slot in range(2):
        core = 1 - c if slot else c
        for store in stores(slot, [block_of(3, *combo, core) for combo in combos]):
            store.wait()
    for part in range(2):
        copy(mine, part, to_z.at[0, part], near_z).wait_send()
        copy(mine, part, to_z.at[1, part], far_z).wait_send()
        copy(mine, part, to_z.at[2, part], near_z).wait_send()

    @pl.loop(0, 4)
    def _(q):
        for i in range(3):
            copy(mine, 0, to_y.at[i, q], y_peer).wait_send()
            copy(mine, 0, to_x.at[i, q], x_peer).wait_send()
        for i in range(4):
            for part in range(2):
                copy(mine, part, to_core.at[i, part, q], core_peer).wait_send()


def gather_experts(rows, select, named, gate_w, up_w, router):
    count, width = rows.shape
    blocks, kept = select.shape[:2]
    hidden = gate_w.shape[1]
    low = rows.dtype
    anywhere = pl.BlockSpec(memory_space=pl.ANY)
    vmem = pl.BlockSpec(memory_space=pltpu.VMEM)
    return pl.pallas_call(
        gather_kernel,
        out_shape=[
            jax.ShapeDtypeStruct((blocks, kept, width), low),
            jax.ShapeDtypeStruct((blocks, kept, hidden), low),
            jax.ShapeDtypeStruct((blocks, kept, hidden), jnp.float32),
            jax.ShapeDtypeStruct((blocks, kept, hidden), jnp.float32),
            jax.ShapeDtypeStruct((blocks, kept, 128), jnp.float32),
        ],
        in_specs=[vmem, vmem, vmem, anywhere, anywhere, vmem],
        out_specs=[anywhere] * 4 + [vmem],
        scratch_shapes=[
            pltpu.VMEM((blocks, count, width), low),
            pltpu.VMEM(gate_w.shape, low),
            pltpu.VMEM(up_w.shape, low),
            pltpu.VMEM((2, 4 * kept, width), low),
            pltpu.VMEM((2, 4 * kept, hidden), low),
            pltpu.VMEM((2, 2, 4 * kept, hidden), jnp.float32),
            copies(2),
            copies(2, 16),
            copies(blocks, 2),
            copies(3, 2),
            copies(3, 4),
            copies(3, 4),
            copies(4, 2, 4),
        ],
        compiler_params=settings(1),
    )(rows, select, named, gate_w, up_w, router)


def scatter_kernel(
    extended,
    spread_ref,
    *refs,
):
    if extended:
        gate_grad_ref, up_grad_ref, gate_ref, up_ref, extra_ref, rows_hbm = refs[:6]
        out_ref, extra_out, gate_out, up_out = refs[6:10]
        tiles, staged, loaded, stored = refs[10:14]
        refs = refs[14:]
    else:
        active_ref, down_ref, share_ref, select_ref, grads_hbm, gate_hbm, up_hbm = refs[:7]
        out_ref, rows_out, gate_out, up_out, extra_ref = refs[7:12]
        grads_in, pre_in, rows_staged, staged, loaded, stored = refs[12:18]
        refs = refs[18:]
    outgoing, core_in, total, back, x_in, y_in, z_in = refs[:7]
    core_sent, core_got, x_sent, x_got, y_sent, y_got, z_sent, z_got = refs[7:]
    z, y, x, c = spot()
    width = out_ref.shape[1]
    half = out_ref.shape[0] // 2
    blocks, _, kept = spread_ref.shape
    y_peer, x_peer, core_peer = (
        where_is(z, 1 - y, x, c),
        where_is(z, y, 1 - x, c),
        where_is(z, y, x, 1 - c),
    )
    near_z, far_z = where_is(along_z(z, 1), y, x, c), where_is(along_z(z, 2), y, x, c)
    greet([y_peer, x_peer, core_peer, near_z, far_z])
    groups = ((1, 1), (0, 1), (1, 0), (0, 0))

    def block_of(group, q, core):
        other_y, other_x = groups[group]
        return number(along_z(z, q), 1 - y if other_y else y, 1 - x if other_x else x, core)

    def rows_of(ref, q, core):
        return jnp.concatenate([ref[block_of(group, q, core)] for group in range(4)], axis=0)

    def rows_back(q, core):
        if extended:
            sums = right_transposed(rows_of(gate_grad_ref, q, core), gate_ref[...])
            sums = sums + right_transposed(rows_of(up_grad_ref, q, core), up_ref[...])
        else:
            sums = jnp.dot(
                rows_of(active_ref, q, core), down_ref[...], preferred_element_type=jnp.float32
            )
            sums = sums.astype(back.dtype).astype(jnp.float32)
            sums = sums * rows_of(share_ref, q, core)[:, :1]
        back[...] = sums.astype(back.dtype)

    def turn_blocks(turn):
        core = (c + turn) % 2
        return [block_of(group, turn // 2, core) for group in range(4)]

    def loads(turn):
        slot, made = turn % 2, []
        if extended:
            columns = pl.ds(pl.multiple_of(turn * tiles.shape[3], tiles.shape[3]), tiles.shape[3])
            made.append((rows_hbm.at[:, :, columns], tiles.at[slot]))
        else:
            for group, block in enumerate(turn_blocks(turn)):
                rows = pl.ds(group * kept, kept)
                made.append((grads_hbm.at[block], grads_in.at[slot, group]))
                made.append((gate_hbm.at[block], pre_in.at[slot, 0, rows]))
                made.append((up_hbm.at[block], pre_in.at[slot, 1, rows]))
        return [
            pltpu.make_async_copy(source, target, loaded.at[slot, i])
            for i, (source, target) in enumerate(made)
        ]

    def stores(turn):
        slot, made = turn % 2, []
        if extended:
            columns = tiles.shape[3]
            rows = pl.ds(pl.multiple_of(turn * columns, columns), columns)
            made.append((staged.at[slot, 0], gate_out.at[rows]))
            made.append((staged.at[slot, 1], up_out.at[rows]))
        else:
            for group, block in enumerate(turn_blocks(turn)):
                rows = pl.ds(group * kept, kept)
                made.append((rows_staged.at[slot, rows], rows_out.at[block]))
                made.append((staged.at[slot, 0, rows], gate_out.at[block]))
                made.append((staged.at[slot, 1, rows], up_out.at[block]))
        return [
            pltpu.make_async_copy(source, target, stored.at[slot, i])
            for i, (source, target) in enumerate(made)
        ]

    def begin_loads(turn):
        for load in loads(turn):
            load.start()

    def fill(turn):
        for load in loads(turn):
            load.wait()

        @pl.when(turn >= 2)
        def _():
            for store in stores(turn - 2):
                store.wait()

        if extended:
            weigh(turn)
        else:
            prepare(turn)
        for store in stores(turn):
            store.start()

        @pl.when(turn < 6)
        def _():
            begin_loads(turn + 2)

    def weigh(turn):
        slot = turn % 2
        staged[slot] = jnp.zeros_like(staged[slot])

        @pl.loop(0, blocks // 4)
        def _(i):
            span = pl.ds(i * 4, 4)
            rows = tiles[slot, span].reshape(4 * kept, tiles.shape[3])
            for which, grads in enumerate((gate_grad_ref, up_grad_ref)):
                staged[slot, which] += left_trans(
                    rows, grads[span].reshape(4 * kept, grads.shape[2])
                )

    def prepare(turn):
        blocks, slot = turn_blocks(turn), turn % 2
        mine = number(z, y, x, c)
        parts = [
            jnp.dot(
                select_ref[blocks[group]],
                grads_in[slot, group],
                preferred_element_type=jnp.float32,
            )
            for group in range(4)
        ]
        share = jnp.concatenate([share_ref[block] for block in blocks], axis=0)[:, :1]
        picked = jnp.concatenate(parts, axis=0)
        rows_staged[slot] = (share * picked).astype(rows_staged.dtype)
        ahead = right_transposed(picked.astype(rows_staged.dtype), down_ref[...])
        gate, up = pre_in[slot, 0], pre_in[slot, 1]
        active = jnp.concatenate([active_ref[block] for block in blocks], axis=0)
        grad = jnp.sum(active.astype(jnp.float32) * ahead, axis=1, keepdims=True)
        active_grad = share * ahead
        sigma = 1.0 / (1.0 + jnp.exp(-gate))
        gate_grad = active_grad * up * (sigma * (1.0 + gate * (1.0 - sigma)))
        staged[slot, 0] = gate_grad.astype(staged.dtype)
        staged[slot, 1] = (active_grad * (gate * sigma)).astype(staged.dtype)
        lanes = lax.broadcasted_iota(jnp.int32, (4 * kept, 128), 1)
        high = grad.astype(extra_ref.dtype).astype(jnp.float32)
        both = jnp.where(lanes == mine, high, jnp.where(lanes == 32 + mine, grad - high, 0.0))
        both = both.astype(extra_ref.dtype)
        for group, block in enumerate(blocks):
            extra_ref[block] = both[group * kept : (group + 1) * kept]

    def part(block, group):
        rows = jnp.dot(
            spread_ref[block],
            back[group * kept : (group + 1) * kept],
            preferred_element_type=jnp.float32,
        )
        if not extended:
            return rows
        more = jnp.dot(spread_ref[block], extra_ref[block], preferred_element_type=jnp.float32)
        return jnp.concatenate([rows, more], axis=1)

    def across(group, q):
        return remote(
            outgoing.at[q, group],
            core_in.at[q, group],
            core_sent.at[q, group],
            core_got.at[q, group],
            core_peer,
        )

    def view(group, q, side):
        return total.at[q, group, pl.ds(side * half, half)]

    def x_copy(group, q, side, slot):
        return remote(
            view(group, q, side), x_in.at[slot, q], x_sent.at[slot, q], x_got.at[slot, q], x_peer
        )

    def y_copy(group, q, side, slot):
        return remote(
            view(group, q, side), y_in.at[slot, q], y_sent.at[slot, q], y_got.at[slot, q], y_peer
        )

    def z_copy(q):
        return remote(
            total.at[q, 3], z_in.at[q - 1], z_sent.at[q - 1], z_got.at[q - 1],
            where_is(along_z(z, 2 - q % 2), y, x, c),
        )

    def add(group, q, side, source):
        rows = pl.ds(side * half, half)
        total[q, group, rows] = (
            total[q, group, rows].astype(jnp.float32) + source.astype(jnp.float32)
        ).astype(total.dtype)

    def begin(q):
        rows_back(q, 1 - c)
        for group in range(4):
            outgoing[q, group] = part(block_of(group, q, 1 - c), group).astype(total.dtype)
            across(group, q).start()
        rows_back(q, c)
        for group in range(4):
            sums = part(block_of(group, q, c), group)
            across(group, q).wait_recv()
            total[q, group] = (sums + core_in[q, group].astype(jnp.float32)).astype(total.dtype)
            if group == 0:
                x_copy(0, q, 0, 0).start()
                y_copy(0, q, 1, 0).start()
            if group == 1:
                x_copy(1, q, 0, 1).start()
            if group == 2:
                y_copy(2, q, 1, 1).start()

    def middle(q):
        x_copy(0, q, 0, 0).wait_recv()
        add(2, q, 0, x_in[0, q])
        y_copy(2, q, 0, 2).start()
        y_copy(0, q, 1, 0).wait_recv()
        add(1, q, 1, y_in[0, q])
        x_copy(1, q, 1, 2).start()

    def close(q):
        arrivals = (
            ((x_copy(1, q, 0, 1), x_in, 1), (y_copy(2, q, 0, 2), y_in, 2)),
            ((y_copy(2, q, 1, 1), y_in, 1), (x_copy(1, q, 1, 2), x_in, 2)),
        )
        for side in range(2):
            for arrival, _, _ in arrivals[side]:
                arrival.wait_recv()
            rows = pl.ds(side * half, half)
            sums = total[q, 3, rows].astype(jnp.float32)
            for _, source, slot in arrivals[side]:
                sums = sums + source[slot, q].astype(jnp.float32)
            total[q, 3, rows] = sums.astype(total.dtype)

        @pl.when(q == 2)
        def _():
            z_copy(3).wait_recv()
            total[2, 3] = (
                total[2, 3].astype(jnp.float32) + z_in[2].astype(jnp.float32)
            ).astype(total.dtype)

        @pl.when(q > 0)
        def _():
            z_copy(q).start()

    def done(i):
        return jnp.maximum(i, 0) + jnp.maximum(i - 2, 0)

    begin_loads(0)
    begin_loads(1)

    @pl.loop(0, 6)
    def _(i):
        @pl.when(i < 4)
        def _():
            begin(3 - i)

        @pl.loop(done(i - 1), done(i))
        def _(turn):
            fill(turn)

        @pl.when((i > 0) & (i < 5))
        def _():
            middle(4 - i)

        @pl.when(i > 1)
        def _():
            close(5 - i)

    for turn in (6, 7):
        for store in stores(turn):
            store.wait()
    for q in (1, 2):
        z_copy(q).wait_recv()
    sums = total[0, 3].astype(jnp.float32)
    sums = sums + z_in[0].astype(jnp.float32) + z_in[1].astype(jnp.float32)
    out_ref[...] = sums[:, :width]
    if extended:
        extra_out[...] = sums[:, width:]
    for q in range(1, 4):
        z_copy(q).wait_send()

    @pl.loop(0, 4)
    def _(q):
        for group in range(4):
            across(group, q).wait_send()
        x_copy(0, q, 0, 0).wait_send()
        x_copy(1, q, 0, 1).wait_send()
        x_copy(1, q, 1, 2).wait_send()
        y_copy(0, q, 1, 0).wait_send()
        y_copy(2, q, 1, 1).wait_send()
        y_copy(2, q, 0, 2).wait_send()


def scatter_rows(spread, *operands):
    blocks, count, kept = spread.shape
    extended = len(operands) == 6
    width = operands[2].shape[0] if extended else operands[1].shape[1]
    wide = width + 128 if extended else width
    low = operands[0].dtype
    anywhere = pl.BlockSpec(memory_space=pl.ANY)
    outs = [jax.ShapeDtypeStruct((count, width), jnp.float32)]
    if extended:
        outs.append(jax.ShapeDtypeStruct((count, 128), jnp.float32))
        hidden = operands[0].shape[2]
        outs += [jax.ShapeDtypeStruct((width, hidden), jnp.float32)] * 2
        in_specs = in_vmem(6) + [anywhere]
        out_specs = in_vmem(2) + [anywhere] * 2
        filler = [
            pltpu.VMEM((2, blocks, kept, width // 8), low),
            pltpu.VMEM((2, 2, width // 8, hidden), jnp.float32),
            copies(2, 1),
            copies(2, 2),
        ]
    else:
        hidden = operands[0].shape[2]
        outs += [
            jax.ShapeDtypeStruct((blocks, kept, width), low),
            jax.ShapeDtypeStruct((blocks, kept, hidden), low),
            jax.ShapeDtypeStruct((blocks, kept, hidden), low),
            jax.ShapeDtypeStruct((blocks, kept, 128), low),
        ]
        in_specs = in_vmem(5) + [anywhere] * 3
        out_specs = in_vmem(1) + [anywhere] * 3 + in_vmem(1)
        filler = [
            pltpu.VMEM((2, 4, count, width), low),
            pltpu.VMEM((2, 2, 4 * kept, hidden), jnp.float32),
            pltpu.VMEM((2, 4 * kept, width), low),
            pltpu.VMEM((2, 2, 4 * kept, hidden), low),
            copies(2, 12),
            copies(2, 12),
        ]
    return pl.pallas_call(
        functools.partial(scatter_kernel, extended),
        out_shape=outs,
        in_specs=in_specs,
        out_specs=out_specs,
        scratch_shapes=filler
        + [
            pltpu.VMEM((4, 4, count, wide), low),
            pltpu.VMEM((4, 4, count, wide), low),
            pltpu.VMEM((4, 4, count, wide), low),
            pltpu.VMEM((4 * kept, width), low),
            pltpu.VMEM((3, 4, count // 2, wide), low),
            pltpu.VMEM((3, 4, count // 2, wide), low),
            pltpu.VMEM((3, count, wide), low),
            copies(4, 4),
            copies(4, 4),
            copies(3, 4),
            copies(3, 4),
            copies(3, 4),
            copies(3, 4),
            copies(3),
            copies(3),
        ],
        compiler_params=settings(2 if extended else 8),
    )(spread, *operands)


def reduce_kernel(
    cuts,
    parts_ref,
    vector_ref,
    sums_out,
    vector_out,
    *refs,
):
    z, y, x, c = spot()
    member, shard = lax.axis_index("exp"), lax.axis_index("fsdp")
    y_peer = where_is(z, 1 - y, x, c)
    near_z, far_z = where_is(along_z(z, 1), y, x, c), where_is(along_z(z, 2), y, x, c)
    members = [((member + j) % 8, shard) for j in range(8)]
    shards = [(member, (shard + j) % 4) for j in range(4)]
    greet(members[1:] + shards[1:])
    pieces = len(cuts)
    first_got, first_held, first_z = refs[:3]
    y_got_in, y_held, y_z = refs[3:5], refs[5:7], refs[7:9]
    shard_in, member_own, member_in = refs[3 * pieces : 3 * pieces + 3]
    (
        y_sent,
        y_got,
        z_sent,
        z_got,
        back_sent,
        back_got,
        side_sent,
        side_got,
        shard_sent,
        shard_got,
        member_sent,
        member_got,
    ) = refs[3 * pieces + 3 :]

    def shard_copy(j):
        return remote(
            vector_ref.at[(shard + j) % 4],
            shard_in.at[(4 - j) % 4],
            shard_sent.at[j],
            shard_got.at[(4 - j) % 4],
            shards[j],
        )

    def member_copy(j):
        return remote(
            member_own,
            member_in.at[(8 - j) % 8],
            member_sent.at[j],
            member_got.at[(8 - j) % 8],
            members[j],
        )

    def rows(which):
        return pl.ds(*cuts[which])

    def z_peer(q):
        return far_z if q == 2 else near_z

    def y_copy(which, q):
        return remote(
            parts_ref.at[1 - y, along_z(z, q), rows(which)],
            y_got_in[which - 1].at[q],
            y_sent.at[which, q],
            y_got.at[which, q],
            y_peer,
        )

    def z_copy(which, q):
        if which:
            source, target = y_held[which - 1].at[q], y_z[which - 1].at[q]
        elif q == 2:
            source, target = first_held, first_z.at[2]
        else:
            source, target = parts_ref.at[:, along_z(z, q), rows(0)], first_z.at[q]
        return remote(source, target, z_sent.at[which, q], z_got.at[which, q], z_peer(q))

    def first_y():
        return remote(
            first_z.at[0, 1 - y], first_got, y_sent.at[0, 0], y_got.at[0, 0], y_peer
        )

    def place(side, q, which):
        return sums_out.at[side, along_z(z, q), rows(which)]

    def back_copy(which, q):
        held = along_z(z, 2) if q == 3 else z
        if which:
            view = sums_out.at[y, held, rows(which)]
        else:
            view = sums_out.at[:, held, rows(0)]
        return remote(view, view, back_sent.at[which, q], back_got.at[which, q], z_peer(q))

    def side_copy(which, q):
        view = place(y, q, which)
        return remote(view, view, side_sent.at[which, q], side_got.at[which, q], y_peer)

    later = range(1, pieces)
    for j in range(1, 4):
        shard_copy(j).start()
    z_copy(0, 3).start()
    for q in (3, 2, 1, 0):
        for which in later:
            y_copy(which, q).start()
    z_copy(0, 1).start()

    for j in range(1, 4):
        shard_copy(j).wait_recv()
    sums = vector_ref[shard]
    for j in range(1, 4):
        sums = sums + shard_in[j]
    member_own[...] = sums
    for j in range(1, 8):
        member_copy(j).start()

    def add_y(which, q):
        y_copy(which, q).wait_recv()
        sums = parts_ref[y, along_z(z, q), rows(which)].astype(jnp.float32)
        sums = sums + y_got_in[which - 1][q].astype(jnp.float32)
        held, z_in = y_held[which - 1], y_z[which - 1]
        if q == 2:
            z_copy(which, 3).wait_recv()
            sums = sums + z_in[3].astype(jnp.float32)
        if q:
            held[q] = sums.astype(held.dtype)
            z_copy(which, q).start()
            return
        for turn in (1, 2):
            z_copy(which, turn).wait_recv()
            sums = sums + z_in[turn].astype(jnp.float32)
        sums_out[y, z, rows(which)] = sums.astype(sums_out.dtype)
        side_copy(which, 0).start()
        back_copy(which, 2).start()
        back_copy(which, 1).start()

    for which in later:
        add_y(which, 3)
    z_copy(0, 3).wait_recv()
    first_held[...] = (
        parts_ref[:, along_z(z, 2), rows(0)].astype(jnp.float32) + first_z[3].astype(jnp.float32)
    ).astype(first_held.dtype)
    z_copy(0, 2).start()
    for which in later:
        add_y(which, 2)
    z_copy(0, 1).wait_recv()
    z_copy(0, 2).wait_recv()
    first_z[0] = (
        parts_ref[:, z, rows(0)].astype(jnp.float32)
        + first_z[1].astype(jnp.float32)
        + first_z[2].astype(jnp.float32)
    ).astype(first_z.dtype)
    first_y().start()
    for which in later:
        add_y(which, 1)
    first_y().wait_recv()
    sums = first_z[0, y].astype(jnp.float32) + first_got[...].astype(jnp.float32)
    sums_out[y, z, rows(0)] = sums.astype(sums_out.dtype)
    side_copy(0, 0).start()
    for which in later:
        add_y(which, 0)
    side_copy(0, 0).wait_recv()
    back_copy(0, 2).start()
    back_copy(0, 1).start()

    for j in range(1, 8):
        member_copy(j).wait_recv()
    sums = member_own[...]
    for j in range(1, 8):
        sums = sums + member_in[j]
    vector_out[...] = sums

    for q in (1, 2, 3):
        for which in later:
            back_copy(which, q).wait_recv()
            if q == 2:
                back_copy(which, 3).start()
            side_copy(which, q).start()
        back_copy(0, q).wait_recv()
        if q == 2:
            back_copy(0, 3).start()

    for which in later:
        for q in range(4):
            side_copy(which, q).wait_recv()
    for which in range(pieces):
        for q in range(4):
            if which:
                y_copy(which, q).wait_send()
                side_copy(which, q).wait_send()
            if q:
                z_copy(which, q).wait_send()
                back_copy(which, q).wait_send()
    side_copy(0, 0).wait_send()
    first_y().wait_send()
    for j in range(1, 4):
        shard_copy(j).wait_send()
    for j in range(1, 8):
        member_copy(j).wait_send()


def reduce_over_members(parts, vectors):
    low = parts.dtype
    depth, width = parts.shape[2:]
    early = depth * 3 // 16 // 16 * 16
    half = (depth - early) // 2 // 16 * 16
    cuts = ((0, early), (early, half), (early + half, depth - early - half))

    def quarters(*lead):
        return [pltpu.VMEM((*lead, size, width), low) for _, size in cuts[1:]]

    return pl.pallas_call(
        functools.partial(reduce_kernel, cuts),
        out_shape=[
            jax.ShapeDtypeStruct(parts.shape, low),
            jax.ShapeDtypeStruct(vectors.shape[1:], vectors.dtype),
        ],
        in_specs=in_vmem(2),
        out_specs=in_vmem(2),
        scratch_shapes=[
            pltpu.VMEM((early, width), low),
            pltpu.VMEM((2, early, width), low),
            pltpu.VMEM((4, 2, early, width), low),
            *quarters(4),
            *quarters(4),
            *quarters(4),
            pltpu.VMEM(vectors.shape, vectors.dtype),
            pltpu.VMEM(vectors.shape[1:], vectors.dtype),
            pltpu.VMEM((8, *vectors.shape[1:]), vectors.dtype),
        ]
        + [copies(3, 4)] * 8
        + [copies(4)] * 2
        + [copies(8)] * 2,
        compiler_params=settings(3),
    )(parts, vectors)


def project_kernel(
    x_ref,
    routes_ref,
    gain_ref,
    query_ref,
    key_ref,
    value_ref,
    raw_out,
    hidden_out,
    routes_out,
    scale,
    x_in,
    scale_in,
    outgoing,
    core_in,
    across_x,
    x_sums,
    slice_sent,
    slice_got,
    scale_sent,
    scale_got,
    core_sent,
    core_got,
    x_sent,
    x_got,
    route_sent,
    route_got,
):
    z, y, x, c = spot()
    member, shard = lax.axis_index("exp"), lax.axis_index("fsdp")
    mine = number(z, y, x, c)
    count, depth = hidden_out.shape[1:]
    wide, narrow = query_ref.shape[1] // 4, key_ref.shape[1] // 4

    def everyone(j):
        other = (mine + j) % 32
        return (other // 4, other % 4)

    barrier = pltpu.get_barrier_semaphore()

    @pl.loop(1, 32)
    def _(j):
        pl.semaphore_signal(barrier, inc=1, device_id=everyone(j), device_id_type=MESH)

    pl.semaphore_wait(barrier, 31)

    def slice_copy(j):
        place = (shard + j) % 4
        return remote(
            x_ref.at[:, pl.ds(pl.multiple_of(place * depth, depth), depth)],
            x_in.at[(4 - j) % 4],
            slice_sent.at[j],
            slice_got.at[(4 - j) % 4],
            (member, place),
        )

    def scale_copy(j):
        return remote(
            scale,
            scale_in.at[(4 - j) % 4],
            scale_sent.at[j],
            scale_got.at[(4 - j) % 4],
            (member, (shard + j) % 4),
        )

    def route_copy(j):
        return remote(
            routes_ref, routes_out.at[mine], route_sent.at[j], route_got.at[(32 - j) % 32], everyone(j)
        )

    for j in range(1, 4):
        slice_copy(j).start()
    values = x_ref[...].astype(jnp.float32)
    scale[...] = jnp.broadcast_to(
        lax.rsqrt(jnp.mean(values * values, axis=1, keepdims=True) + EPSILON), scale.shape
    )
    for j in range(1, 4):
        scale_copy(j).start()
    routes_out[mine] = routes_ref[...]

    @pl.loop(1, 32)
    def _(j):
        route_copy(j).start()

    def hide(owner, piece, factor):
        gain = gain_ref[...].astype(jnp.float32)
        hidden = piece.astype(jnp.float32) * factor[:, :1] * gain
        hidden_out[owner] = hidden.astype(hidden_out.dtype)

    hide(shard, x_ref[:, pl.ds(pl.multiple_of(shard * depth, depth), depth)], scale[...])

    def take(owner):
        slot = (owner - shard + 4) % 4
        remote(x_in.at[slot], x_in.at[slot], slice_sent.at[slot], slice_got.at[slot], (member, owner)).wait_recv()
        remote(scale, scale_in.at[slot], scale_sent.at[slot], scale_got.at[slot], (member, owner)).wait_recv()
        hide(owner, x_in[slot], scale_in[slot])

    def partial(side, target):
        rows = jnp.concatenate([hidden_out[side * 2], hidden_out[side * 2 + 1]], axis=0)
        parts = []
        for weight, size in ((query_ref, wide), (key_ref, narrow), (value_ref, narrow)):
            columns = pl.ds(pl.multiple_of(target * size, size), size)
            parts.append(jnp.dot(rows, weight[:, columns], preferred_element_type=jnp.float32))
        return jnp.concatenate(parts, axis=1)

    core_peer, x_peer = where_is(z, y, x, 1 - c), where_is(z, y, 1 - x, c)

    def core_copy(turn, far):
        return remote(
            outgoing.at[turn, far],
            core_in.at[turn, far],
            core_sent.at[turn, far],
            core_got.at[turn, far],
            core_peer,
        )

    def x_copy(turn):
        return remote(across_x.at[turn], x_sums.at[turn], x_sent.at[turn], x_got.at[turn], x_peer)

    low = outgoing.dtype
    for turn in range(2):
        side = x if turn == 0 else 1 - x
        if turn == 0:
            take(side * 2 + 1 - c)
        else:
            take(side * 2 + c)
            take(side * 2 + 1 - c)
        outgoing[turn, 1] = partial(side, (1 - x) * 2 + 1 - c).astype(low)
        core_copy(turn, 1).start()
        sums = partial(side, (1 - x) * 2 + c)
        core_copy(turn, 1).wait_recv()
        across_x[turn] = (sums + core_in[turn, 1].astype(jnp.float32)).astype(low)
        x_copy(turn).start()
        outgoing[turn, 0] = partial(side, x * 2 + 1 - c).astype(low)
        core_copy(turn, 0).start()

    for turn in range(2):
        side = x if turn == 0 else 1 - x
        sums = partial(side, x * 2 + c)
        core_copy(turn, 0).wait_recv()
        sums = sums + core_in[turn, 0].astype(jnp.float32)
        raw_out[side * 2] = sums[:count]
        raw_out[side * 2 + 1] = sums[count:]

    for turn in range(2):
        side = 1 - x if turn == 0 else x
        x_copy(turn).wait_recv()
        raw_out[side * 2] += x_sums[turn, :count].astype(jnp.float32)
        raw_out[side * 2 + 1] += x_sums[turn, count:].astype(jnp.float32)

    @pl.loop(1, 32)
    def _(j):
        remote(
            routes_ref, routes_out.at[(mine + j) % 32], route_sent.at[j], route_got.at[j], everyone(j)
        ).wait_recv()

    @pl.loop(1, 32)
    def _(j):
        route_copy(j).wait_send()

    for j in range(1, 4):
        slice_copy(j).wait_send()
        scale_copy(j).wait_send()
    for turn in range(2):
        x_copy(turn).wait_send()
        for far in range(2):
            core_copy(turn, far).wait_send()


def project_tokens(tokens, routes, gain, w_query, key_weight, value_weight):
    count = tokens.shape[0]
    depth = w_query.shape[0]
    own = (w_query.shape[1] + key_weight.shape[1] + value_weight.shape[1]) // 4
    low = tokens.dtype
    return pl.pallas_call(
        project_kernel,
        out_shape=[
            jax.ShapeDtypeStruct((4, count, own), jnp.float32),
            jax.ShapeDtypeStruct((4, count, depth), low),
            jax.ShapeDtypeStruct((32, *routes.shape), routes.dtype),
        ],
        in_specs=in_vmem(6),
        out_specs=in_vmem(3),
        scratch_shapes=[
            pltpu.VMEM((count, 128), jnp.float32),
            pltpu.VMEM((4, count, depth), low),
            pltpu.VMEM((4, count, 128), jnp.float32),
            pltpu.VMEM((2, 2, 2 * count, own), low),
            pltpu.VMEM((2, 2, 2 * count, own), low),
            pltpu.VMEM((2, 2 * count, own), low),
            pltpu.VMEM((2, 2 * count, own), low),
            copies(4),
            copies(4),
            copies(4),
            copies(4),
            copies(2, 2),
            copies(2, 2),
            copies(2),
            copies(2),
            copies(32),
            copies(32),
        ],
        compiler_params=settings(4),
    )(tokens, routes, gain, w_query, key_weight, value_weight)


def turned(values):
    return pltpu.roll(values, HEAD_WIDTH // 2, 1)


def signed(sine):
    lanes = lax.broadcasted_iota(jnp.int32, sine.shape, 1)
    return jnp.where(lanes < HEAD_WIDTH // 2, -sine, sine)


def nt_product(left, right):
    return lax.dot_general(
        left, right, (((1,), (1,)), ((), ())), preferred_element_type=jnp.float32
    )


def finish_kernel(
    row,
    sequences,
    raw_ref,
    notes_ref,
    query_gain_ref,
    key_gain_ref,
    weight_ref,
    x_ref,
    gain_ref,
    middle_out,
    normed_out,
    attended_out,
    probs_out,
    query_out,
    key_out,
    cosine_out,
    sine_out,
    outgoing,
    core_in,
    across_x,
    x_sums,
    core_sent,
    core_got,
    x_sent,
    x_got,
):
    z, y, x, c = spot()
    count = x_ref.shape[0]
    core_peer, x_peer = where_is(z, y, x, 1 - c), where_is(z, y, 1 - x, c)
    greet([core_peer, x_peer])
    heads = query_out.shape[2] // HEAD_WIDTH
    wide = heads * HEAD_WIDTH

    def place(block):
        down = lax.broadcasted_iota(jnp.int32, (count, count), 0)
        along = lax.broadcasted_iota(jnp.int32, (count, count), 1)
        end = jnp.zeros((1, 1), jnp.int32)
        start = jnp.zeros((count, count), jnp.int32)
        own, other = start, start
        for i in range(sequences - 1):
            length = notes_ref[block, row : row + 1, i : i + 1]
            end = end + length
            own = own + jnp.where(down >= end, 1, 0)
            other = other + jnp.where(along >= end, 1, 0)
            start = start + jnp.where(down >= end, length, 0)
        return down - start, (own == other) & (along <= down)

    def attend(block):
        position, allowed = place(block)
        lanes = lax.broadcasted_iota(jnp.int32, position.shape, 1)
        spin = lanes % (HEAD_WIDTH // 2)
        inverse = jnp.exp(spin.astype(jnp.float32) * (-2.0 * math.log(THETA) / HEAD_WIDTH))
        angles = position.astype(jnp.float32) * inverse
        cosine, sine = jnp.cos(angles), jnp.sin(angles)
        cosine_out[block] = cosine
        sine_out[block] = sine
        flipped = signed(sine)

        def normal(values, gain):
            scale = lax.rsqrt(jnp.mean(values * values, axis=1, keepdims=True) + EPSILON)
            values = values * scale * gain
            return (values * cosine + turned(values) * flipped).astype(query_out.dtype)

        key = normal(raw_ref[block, :, wide : wide + HEAD_WIDTH], key_gain_ref[...])
        key_out[block] = key
        value = raw_ref[block, :, wide + HEAD_WIDTH :].astype(query_out.dtype)
        for head in range(heads):
            columns = slice(head * HEAD_WIDTH, (head + 1) * HEAD_WIDTH)
            query = normal(raw_ref[block, :, columns], query_gain_ref[...])
            query_out[block, :, columns] = query
            scores = nt_product(query, key) * HEAD_WIDTH ** (-0.5)
            scores = jnp.where(allowed, scores, MASKED)
            raised = jnp.exp(scores - jnp.max(scores, axis=1, keepdims=True))
            probs = raised / jnp.sum(raised, axis=1, keepdims=True)
            probs_out[block, head] = probs
            attended_out[block, :, columns] = jnp.dot(
                probs.astype(value.dtype), value, preferred_element_type=jnp.float32
            ).astype(attended_out.dtype)

    def core_copy(far):
        return remote(
            outgoing.at[far], core_in.at[far], core_sent.at[far], core_got.at[far], core_peer
        )

    def x_copy():
        return remote(across_x, x_sums, x_sent, x_got, x_peer)

    def partial(side, core):
        block = side * 2 + core
        attend(block)
        return jnp.dot(attended_out[block], weight_ref[...], preferred_element_type=jnp.float32)

    outgoing[1] = partial(1 - x, 1 - c).astype(outgoing.dtype)
    core_copy(1).start()
    sums = partial(1 - x, c)
    core_copy(1).wait_recv()
    across_x[...] = (sums + core_in[1].astype(jnp.float32)).astype(across_x.dtype)
    x_copy().start()
    outgoing[0] = partial(x, 1 - c).astype(outgoing.dtype)
    core_copy(0).start()
    sums = partial(x, c) + x_ref[...].astype(jnp.float32)
    core_copy(0).wait_recv()
    sums = sums + core_in[0].astype(jnp.float32)
    x_copy().wait_recv()
    middle = sums + x_sums[...].astype(jnp.float32)
    middle_out[...] = middle
    scale = lax.rsqrt(jnp.mean(middle * middle, axis=1, keepdims=True) + EPSILON)
    normed_out[...] = (middle * scale * gain_ref[...]).astype(normed_out.dtype)
    x_copy().wait_send()
    core_copy(0).wait_send()
    core_copy(1).wait_send()


def finish_attention(raw, notes, row, sequences, q_gain, k_gain, w_out, tokens, gain):
    count, width = tokens.shape
    low = tokens.dtype
    wide = w_out.shape[0]
    heads = wide // HEAD_WIDTH
    return pl.pallas_call(
        functools.partial(finish_kernel, row, sequences),
        out_shape=[
            jax.ShapeDtypeStruct((count, width), jnp.float32),
            jax.ShapeDtypeStruct((count, width), low),
            jax.ShapeDtypeStruct((4, count, wide), low),
            jax.ShapeDtypeStruct((4, heads, count, count), jnp.float32),
            jax.ShapeDtypeStruct((4, count, wide), low),
            jax.ShapeDtypeStruct((4, count, HEAD_WIDTH), low),
            jax.ShapeDtypeStruct((4, count, HEAD_WIDTH), jnp.float32),
            jax.ShapeDtypeStruct((4, count, HEAD_WIDTH), jnp.float32),
        ],
        in_specs=in_vmem(7),
        out_specs=in_vmem(8),
        scratch_shapes=[
            pltpu.VMEM((2, count, width), low),
            pltpu.VMEM((2, count, width), low),
            pltpu.VMEM((count, width), low),
            pltpu.VMEM((count, width), low),
            copies(2),
            copies(2),
            copies(),
            copies(),
        ],
        compiler_params=settings(5),
    )(raw, notes, q_gain, k_gain, w_out, tokens, gain)


def branch_kernel(
    branch_ref, weight_ref, grad_out, every_out, x_sent, x_got, core_sent, core_got
):
    z, y, x, c = spot()
    mine = x * 2 + c
    core_peer, x_peer = where_is(z, y, x, 1 - c), where_is(z, y, 1 - x, c)
    greet([core_peer, x_peer])
    every_out[mine] = branch_ref[...]

    def x_copy():
        return remote(branch_ref, every_out.at[mine], x_sent, x_got, x_peer)

    def core_copy(far):
        place = (1 - x if far else x) * 2 + c
        return remote(
            every_out.at[place], every_out.at[place], core_sent.at[far], core_got.at[far], core_peer
        )

    def back(place):
        grad_out[place] = right_transposed(every_out[place], weight_ref[...]).astype(grad_out.dtype)

    x_copy().start()
    core_copy(0).start()
    back(mine)
    core_copy(0).wait_recv()
    back(x * 2 + 1 - c)
    x_copy().wait_recv()
    core_copy(1).start()
    back((1 - x) * 2 + c)
    core_copy(1).wait_recv()
    back((1 - x) * 2 + 1 - c)
    x_copy().wait_send()
    core_copy(0).wait_send()
    core_copy(1).wait_send()


def branch_back(branch, w_out):
    count, width = branch.shape
    low = branch.dtype
    return pl.pallas_call(
        branch_kernel,
        out_shape=[
            jax.ShapeDtypeStruct((4, count, w_out.shape[0]), low),
            jax.ShapeDtypeStruct((4, count, width), low),
        ],
        in_specs=in_vmem(2),
        out_specs=in_vmem(2),
        scratch_shapes=[copies(), copies(), copies(2), copies(2)],
        compiler_params=settings(6),
    )(branch, w_out)


def heads_kernel(
    branch_ref,
    raw_ref,
    probs_ref,
    rotated_ref,
    rotated_key_ref,
    cosine_ref,
    sine_ref,
    query_gain_ref,
    key_gain_ref,
    hidden_ref,
    query_ref,
    key_ref,
    value_ref,
    weight_out,
    first_out,
    gains_out,
    every,
    outgoing,
    x_sent,
    x_got,
    core_sent,
    core_got,
    back_sent,
    back_got,
):
    z, y, x, c = spot()
    member, shard = lax.axis_index("exp"), lax.axis_index("fsdp")
    core_peer, x_peer = where_is(z, y, x, 1 - c), where_is(z, y, 1 - x, c)
    peers = [(member, (shard + j) % 4) for j in range(1, 4)]
    greet(peers)
    rows = every.shape[1]
    half = rows // 2
    count = rows // 4
    depth = hidden_ref.shape[1]
    wide, narrow = query_ref.shape[1] // 4, key_ref.shape[1] // 4
    low = every.dtype

    def attention_back(block):
        cosine = cosine_ref[block]
        flipped = signed(sine_ref[block])

        def unturn(grads):
            return grads * cosine + turned(grads * flipped)

        def normal_back(grads, values, gain, into):
            scale = lax.rsqrt(jnp.mean(values * values, axis=1, keepdims=True) + EPSILON)
            hat = values * scale
            gains_out[into : into + 1] += jnp.sum(grads * hat, axis=0, keepdims=True)
            grads = grads * gain
            return scale * (grads - hat * jnp.mean(grads * hat, axis=1, keepdims=True))

        rotated_key = rotated_key_ref[block]
        value = raw_ref[block, :, wide + narrow :].astype(low)
        place = pl.ds(block * count, count)
        value_grad = key_grad = None
        for head in range(wide // HEAD_WIDTH):
            columns = slice(head * HEAD_WIDTH, (head + 1) * HEAD_WIDTH)
            grads = branch_ref[block, :, columns]
            probs = probs_ref[block, head]
            prob_grad = nt_product(grads, value)
            term = left_trans(probs.astype(low), grads)
            value_grad = term if value_grad is None else value_grad + term
            balance = jnp.sum(probs * prob_grad, axis=1, keepdims=True)
            score_grad = (probs * (prob_grad - balance)).astype(low)
            query_grad = jnp.dot(score_grad, rotated_key, preferred_element_type=jnp.float32)
            term = left_trans(score_grad, rotated_ref[block, :, columns])
            key_grad = term if key_grad is None else key_grad + term
            query_grad = unturn(query_grad * HEAD_WIDTH ** (-0.5))
            query_grad = normal_back(
                query_grad, raw_ref[block, :, columns], query_gain_ref[...], 0
            )
            every[shard, place, columns] = query_grad.astype(low)
        key_grad = unturn(key_grad * HEAD_WIDTH ** (-0.5))
        key_grad = normal_back(
            key_grad, raw_ref[block, :, wide : wide + narrow], key_gain_ref[...], 1
        )
        every[shard, place, wide : wide + narrow] = key_grad.astype(low)
        every[shard, place, wide + narrow :] = value_grad.astype(low)

    def x_copy(part):
        view = every.at[shard, pl.ds(part * half, half)]
        return remote(view, view, x_sent.at[part], x_got.at[part], x_peer)

    def core_copy(far, part):
        view = every.at[(1 - x if far else x) * 2 + c, pl.ds(part * half, half)]
        return remote(view, view, core_sent.at[far, part], core_got.at[far, part], core_peer)

    gains_out[...] = jnp.zeros_like(gains_out)
    for part in range(2):

        @pl.loop(part * 2, part * 2 + 2)
        def _(block):
            attention_back(block)

        x_copy(part).start()
        core_copy(0, part).start()

    def weigh(place):
        weight_out[place] = left_trans(hidden_ref[...], every[place]).astype(weight_out.dtype)

    def back(place):
        grads = every[place]
        sums = None
        for weight, size, start in (
            (query_ref, wide, 0),
            (key_ref, narrow, wide),
            (value_ref, narrow, wide + narrow),
        ):
            columns = pl.ds(pl.multiple_of(place * size, size), size)
            term = right_transposed(grads[:, start : start + size], weight[:, columns])
            sums = term if sums is None else sums + term
        return sums

    total = back(shard)
    weigh(shard)
    near = x * 2 + 1 - c
    for part in range(2):
        core_copy(0, part).wait_recv()
    total = total + back(near)
    weigh(near)
    for part in range(2):
        x_copy(part).wait_recv()
        core_copy(1, part).start()
    far = (1 - x) * 2 + c
    total = total + back(far)
    for part in range(2):
        core_copy(1, part).wait_recv()
    total = total + back((1 - x) * 2 + 1 - c)
    for owner in range(4):
        outgoing[owner] = total[owner * count : (owner + 1) * count].astype(outgoing.dtype)

    def back_copy(j):
        place = (shard + j) % 4
        return remote(
            outgoing.at[place],
            first_out.at[shard],
            back_sent.at[j],
            back_got.at[(4 - j) % 4],
            (member, place),
        )

    for j in range(1, 4):
        back_copy(j).start()
    first_out[shard] = outgoing[shard]
    weigh(far)
    weigh((1 - x) * 2 + 1 - c)
    for j in range(1, 4):
        place = (shard + j) % 4
        remote(
            outgoing.at[place], first_out.at[place], back_sent.at[j], back_got.at[j], (member, place)
        ).wait_recv()
    for j in range(1, 4):
        back_copy(j).wait_send()
    for part in range(2):
        x_copy(part).wait_send()
        for far in range(2):
            core_copy(far, part).wait_send()


def heads_back(branch, raw, probs, rotated, tables, gains, hidden, weights):
    rows = 4 * raw.shape[1]
    own = raw.shape[2]
    depth = hidden.shape[1]
    low = hidden.dtype
    operands = (branch, raw, probs, *rotated, *tables, *gains, hidden, *weights)
    return pl.pallas_call(
        heads_kernel,
        out_shape=[
            jax.ShapeDtypeStruct((4, depth, own), low),
            jax.ShapeDtypeStruct((4, rows // 4, depth), low),
            jax.ShapeDtypeStruct((8, HEAD_WIDTH), jnp.float32),
        ],
        in_specs=in_vmem(len(operands)),
        out_specs=in_vmem(3),
        scratch_shapes=[
            pltpu.VMEM((4, rows, own), low),
            pltpu.VMEM((4, rows // 4, depth), low),
            copies(2),
            copies(2),
            copies(2, 2),
            copies(2, 2),
            copies(4),
            copies(4),
        ],
        compiler_params=settings(7),
    )(*operands)


def moe_gathered(normed, router, routes, capacity, cotangent, weights, notes):
    gate_w, up_w, down_w = weights
    token_count, topk = routes.shape
    experts = router.shape[1]
    mine = lax.axis_index("exp") * lax.axis_size("fsdp") + lax.axis_index("fsdp")
    all_routes = notes[:, :topk]
    all_grads = lax.all_gather(cotangent, BOTH, axis=0, tiled=True)
    columns = jnp.arange(experts, dtype=jnp.int32)
    named = jnp.any(all_routes[:, :, None, :] == columns[None, None, :, None], axis=1)
    own = jnp.any(all_routes == mine, axis=1)
    before = jnp.tril(jnp.ones((token_count, token_count), jnp.bfloat16), -1)
    rank = right_transposed(own.astype(jnp.bfloat16), before).astype(jnp.int32)
    places = jnp.arange(capacity, dtype=jnp.int32)
    select = (own[:, None, :] & (rank[:, None, :] == places[None, :, None])).astype(jnp.bfloat16)
    spread = (own[:, :, None] & (rank[:, :, None] == places[None, None, :])).astype(jnp.bfloat16)
    named_rows = contract("bcj,bej->bce", select, named.astype(jnp.bfloat16))
    named_rows = jnp.pad(named_rows.astype(jnp.bfloat16), ((0, 0), (0, 0), (0, 128 - experts)))
    padded = jnp.pad(router, ((0, 0), (0, 128 - experts)))
    arrived, active, gate_pre, up_pre, share = gather_experts(
        normed, select, named_rows, gate_w, up_w, padded
    )
    mixed, out_rows, gate_pre_grad, up_pre_grad, extra = scatter_rows(
        spread,
        active,
        down_w,
        share,
        select,
        all_grads.reshape(experts, token_count, MODEL_WIDTH),
        gate_pre,
        up_pre,
    )
    summed, back, gate_w_grad, up_w_grad = scatter_rows(
        spread, gate_pre_grad, up_pre_grad, gate_w, up_w, extra, arrived
    )

    def flat(rows):
        return rows.reshape(experts * capacity, rows.shape[2])

    weight_grads = (gate_w_grad, up_w_grad, left_trans(flat(active), flat(out_rows)))
    gate_grad = back[:, :experts] + back[:, experts : 2 * experts]
    picks = jnp.any(routes[:, :, None] == columns[None, None, :], axis=1)
    gates = jax.nn.softmax(jnp.where(picks, matrix_product(normed, router), MASKED), axis=1)
    logit_grad = gates * (gate_grad - jnp.sum(gates * gate_grad, axis=1, keepdims=True))
    return mixed, summed, logit_grad.astype(jnp.bfloat16), *weight_grads


def moe_exchanged(normed, router, routes, capacity, cotangent, weights, notes):
    gate_w, up_w, down_w = weights
    token_count, topk = routes.shape
    experts = router.shape[1]
    gates = gates_of(matrix_product(normed, router), routes, experts)
    slots = slot_table(routes, experts, capacity)

    def send(rows):
        packed = jnp.zeros((experts * capacity, MODEL_WIDTH), jnp.bfloat16).at[slots].set(rows)
        return exchange(packed.reshape(experts, capacity, MODEL_WIDTH)).reshape(
            experts * capacity, MODEL_WIDTH
        )

    def bring(rows):
        rows = exchange(rows.reshape(experts, capacity, MODEL_WIDTH))
        return rows.reshape(experts * capacity, MODEL_WIDTH)[slots].reshape(
            token_count, topk, MODEL_WIDTH
        )

    arrived = send(jnp.repeat(normed, topk, axis=0))
    hidden = expert_forward(arrived, gate_w, up_w)
    scaled = (gates[:, :, None] * cotangent.astype(jnp.float32)[:, None, :]).astype(jnp.bfloat16)
    out_rows = send(scaled.reshape(token_count * topk, MODEL_WIDTH))
    rows_back, gate_pre_grad, up_pre_grad = expert_back(out_rows, hidden, gate_w, up_w, down_w)
    gate_w_grad = left_trans(arrived, gate_pre_grad)
    up_w_grad = left_trans(arrived, up_pre_grad)
    down_grad = left_trans(hidden[3], out_rows)
    returned = bring(matrix_product(hidden[3], down_w).astype(jnp.bfloat16))
    mixed = jnp.einsum("tk,tkd->td", gates, returned.astype(jnp.float32))
    gate_grad = jnp.einsum("td,tkd->tk", cotangent, returned, preferred_element_type=jnp.float32)
    summed = jnp.sum(bring(rows_back), axis=1, dtype=jnp.float32)
    picked_grad = gates * (gate_grad - jnp.sum(gates * gate_grad, axis=1, keepdims=True))
    onehot = routes[:, :, None] == jnp.arange(experts, dtype=jnp.int32)[None, None, :]
    logit_grad = jnp.sum(jnp.where(onehot, picked_grad[:, :, None], 0.0), axis=1)
    return mixed, summed, logit_grad.astype(jnp.bfloat16), gate_w_grad, up_w_grad, down_grad


def local(
    tokens,
    lengths,
    routes,
    attn_gain,
    w_query,
    key_weight,
    value_weight,
    q_gain,
    k_gain,
    w_out,
    mlp_gain,
    w_router,
    expert_gate,
    expert_up,
    expert_down,
    cotangent,
):
    shards, members = lax.axis_size("fsdp"), lax.axis_size("exp")
    experts = shards * members
    token_count, topk = routes.shape
    capacity = 2 * token_count * topk // experts
    group = shards * token_count
    depth = w_query.shape[0]
    heads = QUERY_HEADS // shards
    kv_heads = max(1, KEY_VALUE_HEADS // shards)
    copies_of = shards * kv_heads // KEY_VALUE_HEADS
    head_group = heads // kv_heads
    wide, narrow = heads * HEAD_WIDTH, kv_heads * HEAD_WIDTH
    place = lax.axis_index("fsdp")

    gathered = lax.all_gather(
        jnp.concatenate([w_router.reshape(-1), attn_gain, mlp_gain, q_gain, k_gain]), "fsdp"
    )
    cuts, start = [], 0
    for leaf in (w_router, attn_gain, mlp_gain, q_gain, k_gain):
        cuts.append(gathered[:, start : start + leaf.size])
        start += leaf.size
    router = cuts[0].reshape(MODEL_WIDTH, experts)
    gain_attn, gain_mlp, gain_query, gain_key = [
        cut.reshape(-1).astype(jnp.float32) for cut in cuts[1:]
    ]
    dense = (members, shards) == (8, 4) and 2 * capacity >= token_count
    inputs = tokens.astype(jnp.float32)
    scale_one = rms_scale(inputs)
    if dense:
        notes = jnp.pad(
            jnp.concatenate(
                [routes.T, jnp.pad(lengths, ((0, 0), (0, token_count - lengths.shape[1])))], axis=0
            ),
            ((0, 15 - topk), (0, 0)),
        )
        raw, hidden, notes = project_tokens(
            tokens, notes, attn_gain[None], w_query, key_weight, value_weight
        )
        hidden = hidden.reshape(group, depth)
        first = lax.axis_index("exp") * shards
        notes_own = lax.dynamic_slice_in_dim(notes, first, shards)
    else:
        notes = None
        all_lengths = lax.all_gather(lengths[0], "fsdp")

        def by_shard(weight):
            weight = weight.reshape(depth, KEY_VALUE_HEADS, HEAD_WIDTH)
            return jnp.repeat(weight, copies_of, axis=1).reshape(depth, shards, narrow)

        joined = jnp.concatenate(
            [w_query.reshape(depth, shards, wide), by_shard(key_weight), by_shard(value_weight)],
            axis=2,
        ).transpose(1, 0, 2)
        first_normed = (inputs * scale_one * gain_attn).astype(jnp.bfloat16)
        hidden = lax.all_to_all(first_normed, "fsdp", split_axis=1, concat_axis=0, tiled=True)
        partial = contract("gk,nkc->ngc", hidden, joined).astype(jnp.bfloat16)
        raw = lax.psum_scatter(partial, "fsdp", scatter_dimension=0, tiled=True)[0]
        raw = raw.astype(jnp.float32)
    if dense:
        gains = (gain_query[None], gain_key[None])
        middle, normed, attended, probs, *rotated, cosine, sine = finish_attention(
            raw, notes_own, topk, lengths.shape[1], *gains, w_out, tokens, gain_mlp[None]
        )
        attended = attended.reshape(group, wide)
        scale_two = rms_scale(middle)
    else:
        raw = raw.reshape(shards, token_count, wide + 2 * narrow)
        query_raw = raw[:, :, :wide].reshape(shards, token_count, heads, HEAD_WIDTH)
        key_raw = raw[:, :, wide : wide + narrow].reshape(shards, token_count, kv_heads, HEAD_WIDTH)
        value = (
            raw[:, :, wide + narrow :]
            .astype(jnp.bfloat16)
            .reshape(shards, token_count, kv_heads, HEAD_WIDTH)
        )
        position, allowed = jax.vmap(lambda row: seq_layout(row, token_count))(all_lengths)
        cosine, sine = rotary_tables(position, HEAD_WIDTH)
        query_scale = rms_scale(query_raw)
        query_hat = query_raw * query_scale
        key_scale = rms_scale(key_raw)
        key_hat = key_raw * key_scale
        query = (
            rotate(query_hat * gain_query, cosine, sine)
            .astype(jnp.bfloat16)
            .reshape(shards, token_count, kv_heads, head_group, HEAD_WIDTH)
        )
        key = rotate(key_hat * gain_key, cosine, sine).astype(jnp.bfloat16)
        scores = contract("bqkgd,bpkd->bkgqp", query, key) * HEAD_WIDTH ** (-0.5)
        scores = jnp.where(allowed[:, None, None], scores, MASKED)
        top = jnp.max(scores, axis=-1, keepdims=True)
        raised = jnp.exp(scores - top)
        probs = raised / jnp.sum(raised, axis=-1, keepdims=True)
        probs_low = probs.astype(jnp.bfloat16)
        attended = contract("bkgqp,bpkd->bqkgd", probs_low, value).astype(jnp.bfloat16)
        attended = attended.reshape(group, wide)
        mixed_heads = lax.psum_scatter(
            matrix_product(attended, w_out).astype(jnp.bfloat16),
            "fsdp",
            scatter_dimension=0,
            tiled=True,
        )
        middle = inputs + mixed_heads.astype(jnp.float32)
        scale_two = rms_scale(middle)
        normed = (middle * scale_two * gain_mlp).astype(jnp.bfloat16)

    moe = moe_gathered if dense else moe_exchanged
    mixed, summed, logit_grad, gate_w_grad, up_w_grad, down_grad = moe(
        normed,
        router,
        routes,
        capacity,
        cotangent,
        (expert_gate[0], expert_up[0], expert_down[0]),
        notes,
    )
    layer_out = (middle + mixed).astype(jnp.bfloat16)

    upstream = cotangent.astype(jnp.float32)
    normed_grad = summed + right_transposed(logit_grad, router)
    mlp_gain_grad = jnp.sum(normed_grad * middle * scale_two, axis=0)
    router_grad = left_trans(normed, logit_grad)
    middle_grad = upstream + rms_back(normed_grad * gain_mlp, middle, scale_two)
    branch_low = middle_grad.astype(jnp.bfloat16)
    if dense:
        attended_grad, branch_grad = branch_back(branch_low, w_out)
        branch_grad = branch_grad.reshape(group, MODEL_WIDTH)
    else:
        branch_grad = lax.all_gather(branch_low, "fsdp", axis=0, tiled=True)
        attended_grad = right_transposed(branch_grad, w_out).astype(jnp.bfloat16)
    out_w_grad = left_trans(attended, branch_grad).astype(jnp.bfloat16)
    attended_grad, out_w_grad = lax.optimization_barrier((attended_grad, out_w_grad))
    if dense:
        joined_grad, first_grad, gain_grads = heads_back(
            attended_grad,
            raw,
            probs,
            rotated,
            (cosine, sine),
            gains,
            hidden,
            (w_query, key_weight, value_weight),
        )
        first_grad = first_grad.transpose(1, 0, 2).reshape(token_count, MODEL_WIDTH)
        q_gain_grad, k_gain_grad = gain_grads[0], gain_grads[1]
    else:
        attended_grad = attended_grad.reshape(shards, token_count, kv_heads, head_group, HEAD_WIDTH)
        prob_grad = contract("bqkgd,bpkd->bkgqp", attended_grad, value)
        value_grad = contract("bkgqp,bqkgd->bpkd", probs_low, attended_grad)
        balance = jnp.sum(probs * prob_grad, axis=-1, keepdims=True)
        score_grad = (probs * (prob_grad - balance)).astype(jnp.bfloat16)
        query_norm_grad = contract("bkgqp,bpkd->bqkgd", score_grad, key) * HEAD_WIDTH ** (-0.5)
        query_norm_grad = query_norm_grad.reshape(shards, token_count, heads, HEAD_WIDTH)
        key_norm_grad = contract("bkgqp,bqkgd->bpkd", score_grad, query) * HEAD_WIDTH ** (-0.5)
        query_norm_grad = rotate_back(query_norm_grad, cosine, sine)
        key_norm_grad = rotate_back(key_norm_grad, cosine, sine)
        q_gain_grad = jnp.sum(query_norm_grad * query_hat, axis=(0, 1, 2))
        k_gain_grad = jnp.sum(key_norm_grad * key_hat, axis=(0, 1, 2))
        query_grad = rms_back(query_norm_grad * gain_query, query_raw, query_scale)
        key_grad = rms_back(key_norm_grad * gain_key, key_raw, key_scale)
        head_grads = jnp.concatenate(
            [
                query_grad.reshape(group, wide),
                key_grad.reshape(group, narrow),
                value_grad.reshape(group, narrow),
            ],
            axis=1,
        ).astype(jnp.bfloat16)
        head_grads = lax.all_gather(head_grads, "fsdp")
        hidden_grad = contract("ngc,nkc->gk", head_grads, joined).astype(jnp.bfloat16)
        first_grad = lax.all_to_all(
            hidden_grad, "fsdp", split_axis=0, concat_axis=1, tiled=True
        )
        joined_grad = contract("gk,ngc->nkc", hidden, head_grads).astype(jnp.bfloat16)
    first_grad = first_grad.astype(jnp.float32)
    attn_gain_grad = jnp.sum(first_grad * inputs * scale_one, axis=0)
    input_grad = (middle_grad + rms_back(first_grad * gain_attn, inputs, scale_one)).astype(
        jnp.bfloat16
    )

    vectors = jnp.concatenate(
        [
            grad.reshape(shards, -1)
            for grad in (router_grad, attn_gain_grad, mlp_gain_grad, q_gain_grad, k_gain_grad)
        ],
        axis=1,
    )
    if dense:
        rows = -(-vectors.shape[1] // 1024) * 8
        vectors = jnp.pad(vectors, ((0, 0), (0, rows * 128 - vectors.shape[1])))
        started = lengths[0, 0] > 0
        gate_w_grad, up_w_grad = (
            jnp.where(started, grad, 0.0) for grad in (gate_w_grad, up_w_grad)
        )
        out_sum = lax.psum_scatter(out_w_grad, "exp", scatter_dimension=0, tiled=True)
        joined_grad, vectors, out_sum, gate_w_grad, up_w_grad, down_grad = (
            lax.optimization_barrier(
                (joined_grad, vectors, out_sum, gate_w_grad, up_w_grad, down_grad)
            )
        )
        out_sum = lax.all_gather(out_sum, "exp", axis=0, tiled=True)
        joined_sum, vectors = reduce_over_members(
            joined_grad.reshape(2, 4, -1, wide + 2 * narrow), vectors.reshape(shards, rows, 128)
        )
        joined_sum, vectors = joined_sum.reshape(joined_grad.shape), vectors.reshape(-1)
    else:
        out_sum = lax.psum(out_w_grad, "exp")
        joined_sum = lax.psum(joined_grad, "exp")
        vectors = lax.psum(vectors, BOTH)[place]
    out_sum, joined_sum = out_sum.astype(jnp.float32), joined_sum.astype(jnp.float32)
    sums, start = [], 0
    for leaf in (w_router, attn_gain, mlp_gain, q_gain, k_gain):
        sums.append(vectors[start : start + leaf.size].reshape(leaf.shape))
        start += leaf.size

    def gather_heads(part):
        return part.transpose(1, 0, 2).reshape(depth, KEY_VALUE_HEADS, copies_of, HEAD_WIDTH).sum(
            axis=2
        ).reshape(depth, KEY_VALUE_HEADS * HEAD_WIDTH)

    return (
        layer_out,
        input_grad,
        sums[1],
        joined_sum[:, :, :wide].transpose(1, 0, 2).reshape(depth, QUERY_HEADS * HEAD_WIDTH),
        gather_heads(joined_sum[:, :, wide : wide + narrow]),
        gather_heads(joined_sum[:, :, wide + narrow :]),
        sums[3],
        sums[4],
        out_sum,
        sums[2],
        sums[0],
        gate_w_grad[None],
        up_w_grad[None],
        down_grad[None],
    )


def solution(mesh):
    in_specs = (
        P(("exp", "fsdp"), None),
        P(("exp", "fsdp"), None),
        P(("exp", "fsdp"), None),
        P("fsdp"),
        P("fsdp", None),
        P("fsdp", None),
        P("fsdp", None),
        P("fsdp"),
        P("fsdp"),
        P("fsdp", None),
        P("fsdp"),
        P("fsdp", None),
        P(("exp", "fsdp"), None, None),
        P(("exp", "fsdp"), None, None),
        P(("exp", "fsdp"), None, None),
        P(("exp", "fsdp"), None),
    )
    out_specs = (
        P(("exp", "fsdp"), None),
        P(("exp", "fsdp"), None),
        P("fsdp"),
        P("fsdp", None),
        P("fsdp", None),
        P("fsdp", None),
        P("fsdp"),
        P("fsdp"),
        P("fsdp", None),
        P("fsdp"),
        P("fsdp", None),
        P(("exp", "fsdp"), None, None),
        P(("exp", "fsdp"), None, None),
        P(("exp", "fsdp"), None, None),
    )
    return jax.shard_map(local, mesh=mesh, in_specs=in_specs, out_specs=out_specs, check_vma=False)
```

```python
import functools
import math

import jax
import jax.numpy as jnp
from jax import lax
from jax.experimental import pallas as pl
from jax.experimental.pallas import tpu as pltpu
from jax.sharding import PartitionSpec as P

MODEL_WIDTH = 2048
QUERY_HEADS = 32
KEY_VALUE_HEADS = 4
HEAD_WIDTH = 128


EPSILON = 1e-06
THETA = 1000000.0
MASKED = -1e30
BOTH = ("exp", "fsdp")
MESH = pl.DeviceIdType.MESH


def matrix_product(left, right):
    return jnp.dot(left, right, preferred_element_type=jnp.float32)


def left_trans(left, right):
    return lax.dot_general(
        left, right, (((0,), (0,)), ((), ())), preferred_element_type=jnp.float32
    )


def right_transposed(left, right):
    return lax.dot_general(
        left, right, (((1,), (1,)), ((), ())), preferred_element_type=jnp.float32
    )


def contract(spec, left, right):
    return jnp.einsum(spec, left, right, preferred_element_type=jnp.float32)


def rms_scale(values):
    return lax.rsqrt(jnp.mean(values * values, axis=-1, keepdims=True) + EPSILON)


def rms_back(grad_hat, values, scale):
    normal = values * scale
    return scale * (grad_hat - normal * jnp.mean(grad_hat * normal, axis=-1, keepdims=True))


def seq_layout(length_row, token_count):
    ends = jnp.cumsum(length_row)
    starts = ends - length_row
    places = jnp.arange(token_count, dtype=jnp.int32)
    member = (places[:, None] >= starts[None, :]) & (places[:, None] < ends[None, :])
    numbers = jnp.arange(length_row.shape[0], dtype=jnp.int32)
    segment = jnp.sum(jnp.where(member, numbers[None, :], 0), axis=1)
    position = places - jnp.sum(jnp.where(member, starts[None, :], 0), axis=1)
    allowed = (segment[:, None] == segment[None, :]) & (places[None, :] <= places[:, None])
    return (position, allowed)


def rotary_tables(position, head_size):
    half = head_size // 2
    index = jnp.arange(head_size, dtype=jnp.int32) % half
    inverse = jnp.exp(index.astype(jnp.float32) * (-2.0 * math.log(THETA) / head_size))
    angles = position.astype(jnp.float32)[..., None] * inverse
    return (jnp.cos(angles)[..., None, :], jnp.sin(angles)[..., None, :])


def rotate(values, cosine, sine):
    half = values.shape[-1] // 2
    turned = jnp.concatenate([-values[..., half:], values[..., :half]], axis=-1)
    return values * cosine + turned * sine


def rotate_back(grads, cosine, sine):
    half = grads.shape[-1] // 2
    moved = grads * sine
    return grads * cosine + jnp.concatenate([moved[..., half:], -moved[..., :half]], axis=-1)


def slot_table(route_rows, experts, capacity):
    flat = route_rows.reshape(-1)
    onehot = (flat[:, None] == jnp.arange(experts, dtype=jnp.int32)[None, :]).astype(jnp.int32)
    ranks = jnp.cumsum(onehot, axis=0) - 1
    rank = jnp.sum(ranks * onehot, axis=1)
    return flat * capacity + rank


def exchange(buffer):
    return lax.all_to_all(buffer, BOTH, split_axis=0, concat_axis=0, tiled=True)


def two_halves(values):
    high = values.astype(jnp.bfloat16)
    low = (values - high.astype(jnp.float32)).astype(jnp.bfloat16)
    return high, low


def expert_forward(arrived, gate_w, up_w):
    gate_pre = matrix_product(arrived, gate_w)
    up_pre = matrix_product(arrived, up_w)
    sigma = jax.nn.sigmoid(gate_pre)
    active = (gate_pre * sigma * up_pre).astype(jnp.bfloat16)
    return gate_pre, up_pre, sigma, active


def expert_back(out_rows, hidden, gate_w, up_w, down_w):
    gate_pre, up_pre, sigma, _ = hidden
    active_grad = right_transposed(out_rows, down_w)
    gate_pre_grad = (active_grad * up_pre * (sigma * (1.0 + gate_pre * (1.0 - sigma)))).astype(
        jnp.bfloat16
    )
    up_pre_grad = (active_grad * (gate_pre * sigma)).astype(jnp.bfloat16)
    rows_back = right_transposed(gate_pre_grad, gate_w) + right_transposed(up_pre_grad, up_w)
    return rows_back.astype(jnp.bfloat16), gate_pre_grad, up_pre_grad


def gates_of(logits, routes, experts):
    picked = jnp.take_along_axis(logits, routes, axis=1)
    peak = jnp.max(picked, axis=1, keepdims=True)
    lifted = jnp.exp(picked - peak)
    return lifted / jnp.sum(lifted, axis=1, keepdims=True)


def spot():
    member, shard = lax.axis_index("exp"), lax.axis_index("fsdp")
    return member // 2, member % 2, shard // 2, shard % 2


def where_is(z, y, x, c):
    return (z * 2 + y, x * 2 + c)


def number(z, y, x, c):
    return z * 8 + y * 4 + x * 2 + c


def along_z(z, q):
    return (z // 2 + q // 2) % 2 * 2 + (z % 2 + q % 2) % 2


def greet(peers):
    barrier = pltpu.get_barrier_semaphore()
    for peer in peers:
        pl.semaphore_signal(barrier, inc=1, device_id=peer, device_id_type=MESH)
    pl.semaphore_wait(barrier, len(peers))


def remote(source, target, sent, got, peer):
    return pltpu.make_async_remote_copy(
        src_ref=source,
        dst_ref=target,
        send_sem=sent,
        recv_sem=got,
        device_id=peer,
        device_id_type=MESH,
    )


def in_vmem(count):
    return [pl.BlockSpec(memory_space=pltpu.VMEM)] * count


def copies(*shape):
    return pltpu.SemaphoreType.DMA(shape)


def settings(collective_id):
    return pltpu.CompilerParams(
        collective_id=collective_id, has_side_effects=True, vmem_limit_bytes=60 << 20
    )


def gather_kernel(
    x_ref,
    select_ref,
    named_ref,
    gate_hbm,
    up_hbm,
    router_ref,
    rows_out,
    active_out,
    gate_out,
    up_out,
    share_out,
    held,
    gate_ref,
    up_ref,
    picked,
    lively,
    results,
    loaded,
    stored,
    arrive,
    to_z,
    to_y,
    to_x,
    to_core,
):
    z, y, x, c = spot()
    half = x_ref.shape[0] // 2
    kept = select_ref.shape[1]
    y_peer, x_peer, core_peer = (
        where_is(z, 1 - y, x, c),
        where_is(z, y, 1 - x, c),
        where_is(z, y, x, 1 - c),
    )
    near_z, far_z = where_is(along_z(z, 1), y, x, c), where_is(along_z(z, 2), y, x, c)
    loads = [
        pltpu.make_async_copy(source, target, loaded.at[i])
        for i, (source, target) in enumerate(
            ((gate_hbm, gate_ref), (up_hbm, up_ref))
        )
    ]
    for load in loads:
        load.start()
    greet([y_peer, x_peer, core_peer, near_z, far_z])
    mine = number(z, y, x, c)

    def copy(block, part, sem, peer):
        view = held.at[block, pl.ds(part * half, half)]
        return remote(view, view, sem, arrive.at[block, part], peer)

    def arrived(block, part):
        copy(block, part, to_core.at[0, 0, 0], core_peer).wait_recv()

    def block_of(q, other_y, other_x, core):
        return number(
            along_z(z, q), 1 - y if other_y else y, 1 - x if other_x else x, core
        )

    combos = ((0, 0), (0, 1), (1, 0), (1, 1))

    def stores(slot, blocks):
        made = []
        for k in range(4):
            part = pl.ds(k * kept, kept)
            made.append((picked.at[slot, part], rows_out.at[blocks[k]]))
            made.append((lively.at[slot, part], active_out.at[blocks[k]]))
            for i, out in enumerate((gate_out, up_out)):
                made.append((results.at[slot, i, part], out.at[blocks[k]]))
        return [
            pltpu.make_async_copy(source, target, stored.at[slot, i])
            for i, (source, target) in enumerate(made)
        ]

    def work(q, slot):
        core = 1 - c if slot else c
        blocks = [block_of(q, *combo, core) for combo in combos]

        @pl.when(q > 0)
        def _():
            for store in stores(slot, [block_of(q - 1, *combo, core) for combo in combos]):
                store.wait()

        for k in range(4):
            rows = jnp.dot(
                select_ref[blocks[k]], held[blocks[k]], preferred_element_type=jnp.float32
            )
            picked[slot, k * kept : (k + 1) * kept] = rows.astype(picked.dtype)
        rows = picked[slot]
        gate_pre = jnp.dot(rows, gate_ref[...], preferred_element_type=jnp.float32)
        up_pre = jnp.dot(rows, up_ref[...], preferred_element_type=jnp.float32)
        logits = jnp.dot(rows, router_ref[...], preferred_element_type=jnp.float32)
        results[slot, 0] = gate_pre
        results[slot, 1] = up_pre
        active = gate_pre * (1.0 / (1.0 + jnp.exp(-gate_pre))) * up_pre
        lively[slot] = active.astype(lively.dtype)
        for k in range(4):
            part = slice(k * kept, (k + 1) * kept)
            block = blocks[k]
            masked = jnp.where(named_ref[block].astype(jnp.float32) > 0, logits[part], MASKED)
            lifted = jnp.exp(masked - jnp.max(masked, axis=1, keepdims=True))
            lanes = lax.broadcasted_iota(jnp.int32, lifted.shape, 1)
            share = jnp.sum(jnp.where(lanes == mine, lifted, 0.0), axis=1, keepdims=True)
            share = share / jnp.sum(lifted, axis=1, keepdims=True)
            share_out[block] = jnp.broadcast_to(share, share_out.shape[1:])
        for store in stores(slot, blocks):
            store.start()

    def forward(q):
        block = block_of(q, 0, 0, c)
        if q:
            arrived(block, 0)
            arrived(block, 1)
        if q == 2:
            copy(block, 0, to_z.at[2, 0], near_z).start()
            copy(block, 1, to_z.at[2, 1], near_z).start()
        copy(block, 0, to_y.at[0, q], y_peer).start()
        copy(block, 1, to_x.at[0, q], x_peer).start()
        copy(block, 0, to_x.at[1, q], x_peer).start()
        copy(block, 1, to_y.at[1, q], y_peer).start()
        copy(block, 0, to_core.at[0, 0, q], core_peer).start()
        copy(block, 1, to_core.at[0, 1, q], core_peer).start()

    def second(q):
        block = block_of(q, 1, 0, c)
        arrived(block, 0)
        copy(block, 0, to_x.at[2, q], x_peer).start()
        copy(block, 0, to_core.at[1, 0, q], core_peer).start()
        block = block_of(q, 0, 1, c)
        arrived(block, 1)
        copy(block, 1, to_y.at[2, q], y_peer).start()
        copy(block, 1, to_core.at[2, 1, q], core_peer).start()

    def last(q):
        block = block_of(q, 0, 1, c)
        arrived(block, 0)
        copy(block, 0, to_core.at[2, 0, q], core_peer).start()
        block = block_of(q, 1, 0, c)
        arrived(block, 1)
        copy(block, 1, to_core.at[1, 1, q], core_peer).start()
        block = block_of(q, 1, 1, c)
        arrived(block, 0)
        copy(block, 0, to_core.at[3, 0, q], core_peer).start()
        arrived(block, 1)
        copy(block, 1, to_core.at[3, 1, q], core_peer).start()

    def others(q):
        for combo in combos:
            block = block_of(q, *combo, 1 - c)
            arrived(block, 0)
            arrived(block, 1)

    held[mine] = x_ref[...]
    for part in range(2):
        copy(mine, part, to_z.at[0, part], near_z).start()
    for part in range(2):
        copy(mine, part, to_z.at[1, part], far_z).start()
    forward(0)
    for load in loads:
        load.wait()
    forward(1)
    second(0)
    forward(2)
    second(1)

    @pl.loop(0, 4)
    def _(q):
        last(q)
        work(q, 0)
        others(q)
        work(q, 1)

        @pl.when(q == 0)
        def _():
            forward(3)
            second(2)

        @pl.when(q == 1)
        def _():
            second(3)

    for slot in range(2):
        core = 1 - c if slot else c
        for store in stores(slot, [block_of(3, *combo, core) for combo in combos]):
            store.wait()
    for part in range(2):
        copy(mine, part, to_z.at[0, part], near_z).wait_send()
        copy(mine, part, to_z.at[1, part], far_z).wait_send()
        copy(mine, part, to_z.at[2, part], near_z).wait_send()

    @pl.loop(0, 4)
    def _(q):
        for i in range(3):
            copy(mine, 0, to_y.at[i, q], y_peer).wait_send()
            copy(mine, 0, to_x.at[i, q], x_peer).wait_send()
        for i in range(4):
            for part in range(2):
                copy(mine, part, to_core.at[i, part, q], core_peer).wait_send()


def gather_experts(rows, select, named, gate_w, up_w, router):
    count, width = rows.shape
    blocks, kept = select.shape[:2]
    hidden = gate_w.shape[1]
    low = rows.dtype
    anywhere = pl.BlockSpec(memory_space=pl.ANY)
    vmem = pl.BlockSpec(memory_space=pltpu.VMEM)
    return pl.pallas_call(
        gather_kernel,
        out_shape=[
            jax.ShapeDtypeStruct((blocks, kept, width), low),
            jax.ShapeDtypeStruct((blocks, kept, hidden), low),
            jax.ShapeDtypeStruct((blocks, kept, hidden), jnp.float32),
            jax.ShapeDtypeStruct((blocks, kept, hidden), jnp.float32),
            jax.ShapeDtypeStruct((blocks, kept, 128), jnp.float32),
        ],
        in_specs=[vmem, vmem, vmem, anywhere, anywhere, vmem],
        out_specs=[anywhere] * 4 + [vmem],
        scratch_shapes=[
            pltpu.VMEM((blocks, count, width), low),
            pltpu.VMEM(gate_w.shape, low),
            pltpu.VMEM(up_w.shape, low),
            pltpu.VMEM((2, 4 * kept, width), low),
            pltpu.VMEM((2, 4 * kept, hidden), low),
            pltpu.VMEM((2, 2, 4 * kept, hidden), jnp.float32),
            copies(2),
            copies(2, 16),
            copies(blocks, 2),
            copies(3, 2),
            copies(3, 4),
            copies(3, 4),
            copies(4, 2, 4),
        ],
        compiler_params=settings(1),
    )(rows, select, named, gate_w, up_w, router)


def scatter_kernel(
    extended,
    spread_ref,
    *refs,
):
    if extended:
        gate_grad_ref, up_grad_ref, gate_ref, up_ref, extra_ref, rows_hbm = refs[:6]
        out_ref, extra_out, gate_out, up_out = refs[6:10]
        tiles, staged, loaded, stored = refs[10:14]
        refs = refs[14:]
    else:
        active_ref, down_ref, share_ref, select_ref, grads_hbm, gate_hbm, up_hbm = refs[:7]
        out_ref, rows_out, gate_out, up_out, extra_ref = refs[7:12]
        grads_in, pre_in, rows_staged, staged, loaded, stored = refs[12:18]
        refs = refs[18:]
    outgoing, core_in, total, back, x_in, y_in, z_in, deep_in, deep_x, deep_y = refs[:10]
    core_sent, core_got, x_sent, x_got, y_sent, y_got, z_sent, z_got = refs[10:18]
    deep_sent, deep_got, corner_sent, corner_got = refs[18:]
    z, y, x, c = spot()
    width = out_ref.shape[1]
    count = out_ref.shape[0]
    half, thin = count * 3 // 8, count // 8
    wide = 2 * half
    blocks, _, kept = spread_ref.shape
    y_peer, x_peer, core_peer = (
        where_is(z, 1 - y, x, c),
        where_is(z, y, 1 - x, c),
        where_is(z, y, x, 1 - c),
    )
    near_z, far_z = where_is(along_z(z, 1), y, x, c), where_is(along_z(z, 2), y, x, c)
    greet([y_peer, x_peer, core_peer, near_z, far_z])
    groups = ((1, 1), (0, 1), (1, 0), (0, 0))

    def block_of(group, q, core):
        other_y, other_x = groups[group]
        return number(along_z(z, q), 1 - y if other_y else y, 1 - x if other_x else x, core)

    def rows_of(ref, q, core):
        return jnp.concatenate([ref[block_of(group, q, core)] for group in range(4)], axis=0)

    def rows_back(q, core):
        if extended:
            sums = right_transposed(rows_of(gate_grad_ref, q, core), gate_ref[...])
            sums = sums + right_transposed(rows_of(up_grad_ref, q, core), up_ref[...])
        else:
            sums = jnp.dot(
                rows_of(active_ref, q, core), down_ref[...], preferred_element_type=jnp.float32
            )
            sums = sums.astype(back.dtype).astype(jnp.float32)
            sums = sums * rows_of(share_ref, q, core)[:, :1]
        back[...] = sums.astype(back.dtype)

    def turn_blocks(turn):
        core = (c + turn) % 2
        return [block_of(group, turn // 2, core) for group in range(4)]

    def loads(turn):
        slot, made = turn % 2, []
        if extended:
            columns = pl.ds(pl.multiple_of(turn * tiles.shape[3], tiles.shape[3]), tiles.shape[3])
            made.append((rows_hbm.at[:, :, columns], tiles.at[slot]))
        else:
            for group, block in enumerate(turn_blocks(turn)):
                rows = pl.ds(group * kept, kept)
                made.append((grads_hbm.at[block], grads_in.at[slot, group]))
                made.append((gate_hbm.at[block], pre_in.at[slot, 0, rows]))
                made.append((up_hbm.at[block], pre_in.at[slot, 1, rows]))
        return [
            pltpu.make_async_copy(source, target, loaded.at[slot, i])
            for i, (source, target) in enumerate(made)
        ]

    def stores(turn):
        slot, made = turn % 2, []
        if extended:
            columns = tiles.shape[3]
            rows = pl.ds(pl.multiple_of(turn * columns, columns), columns)
            made.append((staged.at[slot, 0], gate_out.at[rows]))
            made.append((staged.at[slot, 1], up_out.at[rows]))
        else:
            for group, block in enumerate(turn_blocks(turn)):
                rows = pl.ds(group * kept, kept)
                made.append((rows_staged.at[slot, rows], rows_out.at[block]))
                made.append((staged.at[slot, 0, rows], gate_out.at[block]))
                made.append((staged.at[slot, 1, rows], up_out.at[block]))
        return [
            pltpu.make_async_copy(source, target, stored.at[slot, i])
            for i, (source, target) in enumerate(made)
        ]

    def begin_loads(turn):
        for load in loads(turn):
            load.start()

    def fill(turn):
        for load in loads(turn):
            load.wait()

        @pl.when(turn >= 2)
        def _():
            for store in stores(turn - 2):
                store.wait()

        if extended:
            weigh(turn)
        else:
            prepare(turn)
        for store in stores(turn):
            store.start()

        @pl.when(turn < 6)
        def _():
            begin_loads(turn + 2)

    def weigh(turn):
        slot = turn % 2
        staged[slot] = jnp.zeros_like(staged[slot])

        @pl.loop(0, blocks // 4)
        def _(i):
            span = pl.ds(i * 4, 4)
            rows = tiles[slot, span].reshape(4 * kept, tiles.shape[3])
            for which, grads in enumerate((gate_grad_ref, up_grad_ref)):
                staged[slot, which] += left_trans(
                    rows, grads[span].reshape(4 * kept, grads.shape[2])
                )

    def prepare(turn):
        blocks, slot = turn_blocks(turn), turn % 2
        mine = number(z, y, x, c)
        parts = [
            jnp.dot(
                select_ref[blocks[group]],
                grads_in[slot, group],
                preferred_element_type=jnp.float32,
            )
            for group in range(4)
        ]
        share = jnp.concatenate([share_ref[block] for block in blocks], axis=0)[:, :1]
        picked = jnp.concatenate(parts, axis=0)
        rows_staged[slot] = (share * picked).astype(rows_staged.dtype)
        ahead = right_transposed(picked.astype(rows_staged.dtype), down_ref[...])
        gate, up = pre_in[slot, 0], pre_in[slot, 1]
        active = jnp.concatenate([active_ref[block] for block in blocks], axis=0)
        grad = jnp.sum(active.astype(jnp.float32) * ahead, axis=1, keepdims=True)
        active_grad = share * ahead
        sigma = 1.0 / (1.0 + jnp.exp(-gate))
        gate_grad = active_grad * up * (sigma * (1.0 + gate * (1.0 - sigma)))
        staged[slot, 0] = gate_grad.astype(staged.dtype)
        staged[slot, 1] = (active_grad * (gate * sigma)).astype(staged.dtype)
        lanes = lax.broadcasted_iota(jnp.int32, (4 * kept, 128), 1)
        high = grad.astype(extra_ref.dtype).astype(jnp.float32)
        both = jnp.where(lanes == mine, high, jnp.where(lanes == 32 + mine, grad - high, 0.0))
        both = both.astype(extra_ref.dtype)
        for group, block in enumerate(blocks):
            extra_ref[block] = both[group * kept : (group + 1) * kept]

    def part(block, group):
        rows = jnp.dot(
            spread_ref[block],
            back[group * kept : (group + 1) * kept],
            preferred_element_type=jnp.float32,
        )
        if not extended:
            return rows
        more = jnp.dot(spread_ref[block], extra_ref[block], preferred_element_type=jnp.float32)
        return jnp.concatenate([rows, more], axis=1)

    def across(group, q):
        return remote(
            outgoing.at[q, group],
            core_in.at[q, group],
            core_sent.at[q, group],
            core_got.at[q, group],
            core_peer,
        )

    def view(group, q, side):
        return total.at[q, group, pl.ds(side * half, half)]

    def x_copy(group, q, side, slot):
        return remote(
            view(group, q, side), x_in.at[slot, q], x_sent.at[slot, q], x_got.at[slot, q], x_peer
        )

    def y_copy(group, q, side, slot):
        return remote(
            view(group, q, side), y_in.at[slot, q], y_sent.at[slot, q], y_got.at[slot, q], y_peer
        )

    def z_copy(q):
        return remote(
            total.at[q, 3, pl.ds(0, wide)],
            z_in.at[q - 1],
            z_sent.at[q - 1],
            z_got.at[q - 1],
            where_is(along_z(z, 2 - q % 2), y, x, c),
        )

    def deep_copy(q):
        return remote(
            total.at[q, :, pl.ds(wide, 2 * thin)],
            deep_in.at[q - 1],
            deep_sent.at[q - 1],
            deep_got.at[q - 1],
            far_z if q == 2 else near_z,
        )

    def corner_copy(over_x, group, side, slot):
        place, peer = (deep_x, x_peer) if over_x else (deep_y, y_peer)
        return remote(
            total.at[0, group, pl.ds(wide + side * thin, thin)],
            place.at[slot],
            corner_sent.at[over_x, slot],
            corner_got.at[over_x, slot],
            peer,
        )

    y_corners = [corner_copy(0, 0, 0, 0), corner_copy(0, 2, 0, 1), corner_copy(0, 2, 1, 2)]
    x_corners = [corner_copy(1, 0, 1, 0), corner_copy(1, 1, 1, 1), corner_copy(1, 1, 0, 2)]

    def add_deep(q, *arrivals):
        rows = pl.ds(wide, 2 * thin)
        sums = total[q, :, rows].astype(jnp.float32)
        for arrival in arrivals:
            deep_copy(arrival).wait_recv()
            sums = sums + deep_in[arrival - 1].astype(jnp.float32)
        total[q, :, rows] = sums.astype(total.dtype)

    def add_corner(group, side, source):
        rows = pl.ds(wide + side * thin, thin)
        total[0, group, rows] = (
            total[0, group, rows].astype(jnp.float32) + source.astype(jnp.float32)
        ).astype(total.dtype)

    def deep_step(i):
        @pl.when(i == 0)
        def _():
            deep_copy(3).start()

        @pl.when(i == 1)
        def _():
            add_deep(2, 3)
            deep_copy(2).start()

        @pl.when(i == 2)
        def _():
            deep_copy(1).start()

        @pl.when(i == 3)
        def _():
            add_deep(0, 1, 2)
            for corner in (*y_corners[:2], *x_corners[:2]):
                corner.start()

        @pl.when(i == 4)
        def _():
            y_corners[0].wait_recv()
            add_corner(1, 0, deep_y[0])
            x_corners[2].start()
            x_corners[0].wait_recv()
            add_corner(2, 1, deep_x[0])
            y_corners[2].start()

    def add(group, q, side, source):
        rows = pl.ds(side * half, half)
        total[q, group, rows] = (
            total[q, group, rows].astype(jnp.float32) + source.astype(jnp.float32)
        ).astype(total.dtype)

    def begin(q):
        rows_back(q, 1 - c)
        for group in range(4):
            outgoing[q, group] = part(block_of(group, q, 1 - c), group).astype(total.dtype)
            across(group, q).start()
        rows_back(q, c)
        for group in range(4):
            sums = part(block_of(group, q, c), group)
            across(group, q).wait_recv()
            total[q, group] = (sums + core_in[q, group].astype(jnp.float32)).astype(total.dtype)
            if group == 0:
                x_copy(0, q, 0, 0).start()
                y_copy(0, q, 1, 0).start()
            if group == 1:
                x_copy(1, q, 0, 1).start()
            if group == 2:
                y_copy(2, q, 1, 1).start()

    def middle(q):
        x_copy(0, q, 0, 0).wait_recv()
        add(2, q, 0, x_in[0, q])
        y_copy(2, q, 0, 2).start()
        y_copy(0, q, 1, 0).wait_recv()
        add(1, q, 1, y_in[0, q])
        x_copy(1, q, 1, 2).start()

    def close(q):
        arrivals = (
            ((x_copy(1, q, 0, 1), x_in, 1), (y_copy(2, q, 0, 2), y_in, 2)),
            ((y_copy(2, q, 1, 1), y_in, 1), (x_copy(1, q, 1, 2), x_in, 2)),
        )
        for side in range(2):
            for arrival, _, _ in arrivals[side]:
                arrival.wait_recv()
            rows = pl.ds(side * half, half)
            sums = total[q, 3, rows].astype(jnp.float32)
            for _, source, slot in arrivals[side]:
                sums = sums + source[slot, q].astype(jnp.float32)
            total[q, 3, rows] = sums.astype(total.dtype)

        @pl.when(q == 2)
        def _():
            z_copy(3).wait_recv()
            rows = pl.ds(0, wide)
            total[2, 3, rows] = (
                total[2, 3, rows].astype(jnp.float32) + z_in[2].astype(jnp.float32)
            ).astype(total.dtype)

        @pl.when(q > 0)
        def _():
            z_copy(q).start()

    def done(i):
        return jnp.maximum(i, 0) + jnp.maximum(i - 2, 0)

    begin_loads(0)
    begin_loads(1)

    @pl.loop(0, 6)
    def _(i):
        @pl.when(i < 4)
        def _():
            begin(3 - i)

        @pl.loop(done(i - 1), done(i))
        def _(turn):
            fill(turn)

        deep_step(i)

        @pl.when((i > 0) & (i < 5))
        def _():
            middle(4 - i)

        @pl.when(i > 1)
        def _():
            close(5 - i)

    for turn in (6, 7):
        for store in stores(turn):
            store.wait()
    for q in (1, 2):
        z_copy(q).wait_recv()

    def finish(start, size, *more):
        rows = pl.ds(start, size)
        sums = total[0, 3, rows].astype(jnp.float32)
        for source in more:
            sums = sums + source.astype(jnp.float32)
        out_ref[rows] = sums[:, :width]
        if extended:
            extra_out[rows] = sums[:, width:]

    finish(0, wide, z_in[0], z_in[1])
    for slot in (1, 2):
        y_corners[slot].wait_recv()
        x_corners[slot].wait_recv()
    finish(wide, thin, deep_y[1], deep_x[2])
    finish(wide + thin, thin, deep_x[1], deep_y[2])
    for corner in (*y_corners, *x_corners):
        corner.wait_send()
    for q in range(1, 4):
        z_copy(q).wait_send()
        deep_copy(q).wait_send()

    @pl.loop(0, 4)
    def _(q):
        for group in range(4):
            across(group, q).wait_send()
        x_copy(0, q, 0, 0).wait_send()
        x_copy(1, q, 0, 1).wait_send()
        x_copy(1, q, 1, 2).wait_send()
        y_copy(0, q, 1, 0).wait_send()
        y_copy(2, q, 1, 1).wait_send()
        y_copy(2, q, 0, 2).wait_send()


def scatter_rows(spread, *operands):
    blocks, count, kept = spread.shape
    extended = len(operands) == 6
    width = operands[2].shape[0] if extended else operands[1].shape[1]
    wide = width + 128 if extended else width
    low = operands[0].dtype
    anywhere = pl.BlockSpec(memory_space=pl.ANY)
    outs = [jax.ShapeDtypeStruct((count, width), jnp.float32)]
    if extended:
        outs.append(jax.ShapeDtypeStruct((count, 128), jnp.float32))
        hidden = operands[0].shape[2]
        outs += [jax.ShapeDtypeStruct((width, hidden), jnp.float32)] * 2
        in_specs = in_vmem(6) + [anywhere]
        out_specs = in_vmem(2) + [anywhere] * 2
        filler = [
            pltpu.VMEM((2, blocks, kept, width // 8), low),
            pltpu.VMEM((2, 2, width // 8, hidden), jnp.float32),
            copies(2, 1),
            copies(2, 2),
        ]
    else:
        hidden = operands[0].shape[2]
        outs += [
            jax.ShapeDtypeStruct((blocks, kept, width), low),
            jax.ShapeDtypeStruct((blocks, kept, hidden), low),
            jax.ShapeDtypeStruct((blocks, kept, hidden), low),
            jax.ShapeDtypeStruct((blocks, kept, 128), low),
        ]
        in_specs = in_vmem(5) + [anywhere] * 3
        out_specs = in_vmem(1) + [anywhere] * 3 + in_vmem(1)
        filler = [
            pltpu.VMEM((2, 4, count, width), low),
            pltpu.VMEM((2, 2, 4 * kept, hidden), jnp.float32),
            pltpu.VMEM((2, 4 * kept, width), low),
            pltpu.VMEM((2, 2, 4 * kept, hidden), low),
            copies(2, 12),
            copies(2, 12),
        ]
    return pl.pallas_call(
        functools.partial(scatter_kernel, extended),
        out_shape=outs,
        in_specs=in_specs,
        out_specs=out_specs,
        scratch_shapes=filler
        + [
            pltpu.VMEM((4, 4, count, wide), low),
            pltpu.VMEM((4, 4, count, wide), low),
            pltpu.VMEM((4, 4, count, wide), low),
            pltpu.VMEM((4 * kept, width), low),
            pltpu.VMEM((3, 4, count * 3 // 8, wide), low),
            pltpu.VMEM((3, 4, count * 3 // 8, wide), low),
            pltpu.VMEM((3, count * 3 // 4, wide), low),
            pltpu.VMEM((3, 4, count // 4, wide), low),
            pltpu.VMEM((3, count // 8, wide), low),
            pltpu.VMEM((3, count // 8, wide), low),
            copies(4, 4),
            copies(4, 4),
            copies(3, 4),
            copies(3, 4),
            copies(3, 4),
            copies(3, 4),
            copies(3),
            copies(3),
            copies(3),
            copies(3),
            copies(2, 3),
            copies(2, 3),
        ],
        compiler_params=settings(2 if extended else 8),
    )(spread, *operands)


def reduce_kernel(
    cuts,
    parts_ref,
    own_ref,
    vector_ref,
    query_out,
    key_out,
    value_out,
    every_out,
    vector_out,
    sums_out,
    own_sent,
    own_got,
    own_side_sent,
    own_side_got,
    stored,
    *refs,
):
    z, y, x, c = spot()
    member, shard = lax.axis_index("exp"), lax.axis_index("fsdp")
    y_peer = where_is(z, 1 - y, x, c)
    near_z, far_z = where_is(along_z(z, 1), y, x, c), where_is(along_z(z, 2), y, x, c)
    members = [((member + j) % 8, shard) for j in range(8)]
    shards = [(member, (shard + j) % 4) for j in range(4)]
    greet(members[1:] + shards[1:])
    pieces = len(cuts)
    first_got, first_held, first_z = refs[:3]
    y_got_in, y_held, y_z = refs[3:5], refs[5:7], refs[7:9]
    shard_in, member_own, member_in = refs[3 * pieces : 3 * pieces + 3]
    (
        y_sent,
        y_got,
        z_sent,
        z_got,
        back_sent,
        back_got,
        side_sent,
        side_got,
        shard_sent,
        shard_got,
        member_sent,
        member_got,
    ) = refs[3 * pieces + 3 :]

    def shard_copy(j):
        return remote(
            vector_ref.at[(shard + j) % 4],
            shard_in.at[(4 - j) % 4],
            shard_sent.at[j],
            shard_got.at[(4 - j) % 4],
            shards[j],
        )

    def member_copy(j):
        return remote(
            member_own,
            member_in.at[(8 - j) % 8],
            member_sent.at[j],
            member_got.at[(8 - j) % 8],
            members[j],
        )

    def rows(which):
        return pl.ds(*cuts[which])

    def z_peer(q):
        return far_z if q == 2 else near_z

    def y_copy(which, q):
        return remote(
            parts_ref.at[1 - y, along_z(z, q), rows(which)],
            y_got_in[which - 1].at[q],
            y_sent.at[which, q],
            y_got.at[which, q],
            y_peer,
        )

    def z_copy(which, q):
        if which:
            source, target = y_held[which - 1].at[q], y_z[which - 1].at[q]
        elif q == 2:
            source, target = first_held, first_z.at[2]
        else:
            source, target = parts_ref.at[:, along_z(z, q), rows(0)], first_z.at[q]
        return remote(source, target, z_sent.at[which, q], z_got.at[which, q], z_peer(q))

    def first_y():
        return remote(
            first_z.at[0, 1 - y], first_got, y_sent.at[0, 0], y_got.at[0, 0], y_peer
        )

    def place(side, q, which):
        return sums_out.at[side, along_z(z, q), rows(which)]

    def back_copy(which, q):
        held = along_z(z, 2) if q == 3 else z
        if which:
            view = sums_out.at[y, held, rows(which)]
        else:
            view = sums_out.at[:, held, rows(0)]
        return remote(view, view, back_sent.at[which, q], back_got.at[which, q], z_peer(q))

    def side_copy(which, q):
        view = place(y, q, which)
        return remote(view, view, side_sent.at[which, q], side_got.at[which, q], y_peer)

    def own_copy(q):
        view = every_out.at[along_z(z, 2) if q == 3 else z, y]
        return remote(view, view, own_sent.at[q], own_got.at[q], z_peer(q))

    def own_side(q):
        view = every_out.at[along_z(z, q), y]
        return remote(view, view, own_side_sent.at[q], own_side_got.at[q], y_peer)

    def pass_on(q):
        own_copy(q).wait_recv()
        if q == 2:
            own_copy(3).start()
        own_side(q).start()

    def exports(side, q):
        zone = along_z(z, q)
        head, rows = side * 2 + zone // 2, zone % 2
        made, start = [], 0
        for i, out in enumerate((query_out, key_out, value_out)):
            size, depth = out.shape[1] // 4, parts_ref.shape[2]
            source = sums_out.at[side, zone, :, pl.ds(start, size)]
            target = out.at[
                pl.ds(pl.multiple_of(rows * depth, depth), depth),
                pl.ds(pl.multiple_of(head * size, size), size),
            ]
            made.append(pltpu.make_async_copy(source, target, stored.at[side, q, i]))
            start += size
        return made

    later = range(1, pieces)
    every_out[z, y] = own_ref[...]
    for j in range(1, 4):
        shard_copy(j).start()
    z_copy(0, 3).start()
    own_copy(1).start()
    own_copy(2).start()
    for q in (3, 2, 1, 0):
        for which in later:
            y_copy(which, q).start()
    z_copy(0, 1).start()
    own_side(0).start()

    for j in range(1, 4):
        shard_copy(j).wait_recv()
    sums = vector_ref[shard]
    for j in range(1, 4):
        sums = sums + shard_in[j]
    member_own[...] = sums
    for j in range(1, 8):
        member_copy(j).start()

    def add_y(which, q):
        y_copy(which, q).wait_recv()
        sums = parts_ref[y, along_z(z, q), rows(which)].astype(jnp.float32)
        sums = sums + y_got_in[which - 1][q].astype(jnp.float32)
        held, z_in = y_held[which - 1], y_z[which - 1]
        if q == 2:
            z_copy(which, 3).wait_recv()
            sums = sums + z_in[3].astype(jnp.float32)
        if q:
            held[q] = sums.astype(held.dtype)
            z_copy(which, q).start()
            return
        for turn in (1, 2):
            z_copy(which, turn).wait_recv()
            sums = sums + z_in[turn].astype(jnp.float32)
        sums_out[y, z, rows(which)] = sums.astype(sums_out.dtype)
        side_copy(which, 0).start()
        back_copy(which, 2).start()
        back_copy(which, 1).start()

    for which in later:
        add_y(which, 3)
    z_copy(0, 3).wait_recv()
    first_held[...] = (
        parts_ref[:, along_z(z, 2), rows(0)].astype(jnp.float32) + first_z[3].astype(jnp.float32)
    ).astype(first_held.dtype)
    z_copy(0, 2).start()
    pass_on(1)
    for which in later:
        add_y(which, 2)
    pass_on(2)
    z_copy(0, 1).wait_recv()
    z_copy(0, 2).wait_recv()
    first_z[0] = (
        parts_ref[:, z, rows(0)].astype(jnp.float32)
        + first_z[1].astype(jnp.float32)
        + first_z[2].astype(jnp.float32)
    ).astype(first_z.dtype)
    first_y().start()
    for which in later:
        add_y(which, 1)
    pass_on(3)
    first_y().wait_recv()
    sums = first_z[0, y].astype(jnp.float32) + first_got[...].astype(jnp.float32)
    sums_out[y, z, rows(0)] = sums.astype(sums_out.dtype)
    side_copy(0, 0).start()
    for which in later:
        add_y(which, 0)
    side_copy(0, 0).wait_recv()
    back_copy(0, 2).start()
    back_copy(0, 1).start()

    for j in range(1, 8):
        member_copy(j).wait_recv()
    sums = member_own[...]
    for j in range(1, 8):
        sums = sums + member_in[j]
    vector_out[...] = sums

    for q in (1, 2, 3):
        for which in later:
            back_copy(which, q).wait_recv()
            if q == 2:
                back_copy(which, 3).start()
            side_copy(which, q).start()
        back_copy(0, q).wait_recv()
        if q == 2:
            back_copy(0, 3).start()

    for q in range(4):
        for export in exports(y, q):
            export.start()
    for q in range(4):
        for which in later:
            side_copy(which, q).wait_recv()
        for export in exports(1 - y, q):
            export.start()
    for q in range(4):
        own_side(q).wait_recv()
    for q in range(4):
        for side in (y, 1 - y):
            for export in exports(side, q):
                export.wait()
    for q in range(4):
        own_side(q).wait_send()
        if q:
            own_copy(q).wait_send()
    for which in range(pieces):
        for q in range(4):
            if which:
                y_copy(which, q).wait_send()
                side_copy(which, q).wait_send()
            if q:
                z_copy(which, q).wait_send()
                back_copy(which, q).wait_send()
    side_copy(0, 0).wait_send()
    first_y().wait_send()
    for j in range(1, 4):
        shard_copy(j).wait_send()
    for j in range(1, 8):
        member_copy(j).wait_send()


def reduce_over_members(parts, own, vectors, widths):
    low = parts.dtype
    depth, width = parts.shape[2:]
    early = depth // 4 // 16 * 16
    half = (depth - early) // 2 // 16 * 16
    cuts = ((0, early), (early, half), (early + half, depth - early - half))
    anywhere = pl.BlockSpec(memory_space=pl.ANY)

    def quarters(*lead):
        return [pltpu.VMEM((*lead, size, width), low) for _, size in cuts[1:]]

    return pl.pallas_call(
        functools.partial(reduce_kernel, cuts),
        out_shape=[jax.ShapeDtypeStruct((2 * depth, size), low) for size in widths]
        + [
            jax.ShapeDtypeStruct((4, 2, *own.shape), low),
            jax.ShapeDtypeStruct(vectors.shape[1:], vectors.dtype),
        ],
        in_specs=in_vmem(3),
        out_specs=[anywhere] * 3 + in_vmem(2),
        scratch_shapes=[
            pltpu.VMEM(parts.shape, low),
            copies(4),
            copies(4),
            copies(4),
            copies(4),
            copies(2, 4, 3),
            pltpu.VMEM((early, width), low),
            pltpu.VMEM((2, early, width), low),
            pltpu.VMEM((4, 2, early, width), low),
            *quarters(4),
            *quarters(4),
            *quarters(4),
            pltpu.VMEM(vectors.shape, vectors.dtype),
            pltpu.VMEM(vectors.shape[1:], vectors.dtype),
            pltpu.VMEM((8, *vectors.shape[1:]), vectors.dtype),
        ]
        + [copies(3, 4)] * 8
        + [copies(4)] * 2
        + [copies(8)] * 2,
        compiler_params=settings(3),
    )(parts, own, vectors)


def project_kernel(
    x_ref,
    routes_ref,
    gain_ref,
    query_ref,
    key_ref,
    value_ref,
    raw_out,
    hidden_out,
    routes_out,
    scale,
    x_in,
    scale_in,
    outgoing,
    core_in,
    across_x,
    x_sums,
    slice_sent,
    slice_got,
    scale_sent,
    scale_got,
    core_sent,
    core_got,
    x_sent,
    x_got,
    route_sent,
    route_got,
):
    z, y, x, c = spot()
    member, shard = lax.axis_index("exp"), lax.axis_index("fsdp")
    mine = number(z, y, x, c)
    count, depth = hidden_out.shape[1:]
    wide, narrow = query_ref.shape[1] // 4, key_ref.shape[1] // 4

    def everyone(j):
        other = (mine + j) % 32
        return (other // 4, other % 4)

    barrier = pltpu.get_barrier_semaphore()

    @pl.loop(1, 32)
    def _(j):
        pl.semaphore_signal(barrier, inc=1, device_id=everyone(j), device_id_type=MESH)

    pl.semaphore_wait(barrier, 31)

    def slice_copy(j):
        place = (shard + j) % 4
        return remote(
            x_ref.at[:, pl.ds(pl.multiple_of(place * depth, depth), depth)],
            x_in.at[(4 - j) % 4],
            slice_sent.at[j],
            slice_got.at[(4 - j) % 4],
            (member, place),
        )

    def scale_copy(j):
        return remote(
            scale,
            scale_in.at[(4 - j) % 4],
            scale_sent.at[j],
            scale_got.at[(4 - j) % 4],
            (member, (shard + j) % 4),
        )

    def route_copy(j):
        return remote(
            routes_ref, routes_out.at[mine], route_sent.at[j], route_got.at[(32 - j) % 32], everyone(j)
        )

    for j in range(1, 4):
        slice_copy(j).start()
    values = x_ref[...].astype(jnp.float32)
    scale[...] = jnp.broadcast_to(
        lax.rsqrt(jnp.mean(values * values, axis=1, keepdims=True) + EPSILON), scale.shape
    )
    for j in range(1, 4):
        scale_copy(j).start()
    routes_out[mine] = routes_ref[...]

    @pl.loop(1, 32)
    def _(j):
        route_copy(j).start()

    def hide(owner, piece, factor):
        gain = gain_ref[...].astype(jnp.float32)
        hidden = piece.astype(jnp.float32) * factor[:, :1] * gain
        hidden_out[owner] = hidden.astype(hidden_out.dtype)

    hide(shard, x_ref[:, pl.ds(pl.multiple_of(shard * depth, depth), depth)], scale[...])

    def take(owner):
        slot = (owner - shard + 4) % 4
        remote(x_in.at[slot], x_in.at[slot], slice_sent.at[slot], slice_got.at[slot], (member, owner)).wait_recv()
        remote(scale, scale_in.at[slot], scale_sent.at[slot], scale_got.at[slot], (member, owner)).wait_recv()
        hide(owner, x_in[slot], scale_in[slot])

    def partial(side, target):
        rows = jnp.concatenate([hidden_out[side * 2], hidden_out[side * 2 + 1]], axis=0)
        parts = []
        for weight, size in ((query_ref, wide), (key_ref, narrow), (value_ref, narrow)):
            columns = pl.ds(pl.multiple_of(target * size, size), size)
            parts.append(jnp.dot(rows, weight[:, columns], preferred_element_type=jnp.float32))
        return jnp.concatenate(parts, axis=1)

    core_peer, x_peer = where_is(z, y, x, 1 - c), where_is(z, y, 1 - x, c)

    def core_copy(turn, far):
        return remote(
            outgoing.at[turn, far],
            core_in.at[turn, far],
            core_sent.at[turn, far],
            core_got.at[turn, far],
            core_peer,
        )

    def x_copy(turn):
        return remote(across_x.at[turn], x_sums.at[turn], x_sent.at[turn], x_got.at[turn], x_peer)

    low = outgoing.dtype
    for turn in range(2):
        side = x if turn == 0 else 1 - x
        if turn == 0:
            take(side * 2 + 1 - c)
        else:
            take(side * 2 + c)
            take(side * 2 + 1 - c)
        outgoing[turn, 1] = partial(side, (1 - x) * 2 + 1 - c).astype(low)
        core_copy(turn, 1).start()
        sums = partial(side, (1 - x) * 2 + c)
        core_copy(turn, 1).wait_recv()
        across_x[turn] = (sums + core_in[turn, 1].astype(jnp.float32)).astype(low)
        x_copy(turn).start()
        outgoing[turn, 0] = partial(side, x * 2 + 1 - c).astype(low)
        core_copy(turn, 0).start()

    for turn in range(2):
        side = x if turn == 0 else 1 - x
        sums = partial(side, x * 2 + c)
        core_copy(turn, 0).wait_recv()
        sums = sums + core_in[turn, 0].astype(jnp.float32)
        raw_out[side * 2] = sums[:count]
        raw_out[side * 2 + 1] = sums[count:]

    for turn in range(2):
        side = 1 - x if turn == 0 else x
        x_copy(turn).wait_recv()
        raw_out[side * 2] += x_sums[turn, :count].astype(jnp.float32)
        raw_out[side * 2 + 1] += x_sums[turn, count:].astype(jnp.float32)

    @pl.loop(1, 32)
    def _(j):
        remote(
            routes_ref, routes_out.at[(mine + j) % 32], route_sent.at[j], route_got.at[j], everyone(j)
        ).wait_recv()

    @pl.loop(1, 32)
    def _(j):
        route_copy(j).wait_send()

    for j in range(1, 4):
        slice_copy(j).wait_send()
        scale_copy(j).wait_send()
    for turn in range(2):
        x_copy(turn).wait_send()
        for far in range(2):
            core_copy(turn, far).wait_send()


def project_tokens(tokens, routes, gain, w_query, key_weight, value_weight):
    count = tokens.shape[0]
    depth = w_query.shape[0]
    own = (w_query.shape[1] + key_weight.shape[1] + value_weight.shape[1]) // 4
    low = tokens.dtype
    return pl.pallas_call(
        project_kernel,
        out_shape=[
            jax.ShapeDtypeStruct((4, count, own), jnp.float32),
            jax.ShapeDtypeStruct((4, count, depth), low),
            jax.ShapeDtypeStruct((32, *routes.shape), routes.dtype),
        ],
        in_specs=in_vmem(6),
        out_specs=in_vmem(3),
        scratch_shapes=[
            pltpu.VMEM((count, 128), jnp.float32),
            pltpu.VMEM((4, count, depth), low),
            pltpu.VMEM((4, count, 128), jnp.float32),
            pltpu.VMEM((2, 2, 2 * count, own), low),
            pltpu.VMEM((2, 2, 2 * count, own), low),
            pltpu.VMEM((2, 2 * count, own), low),
            pltpu.VMEM((2, 2 * count, own), low),
            copies(4),
            copies(4),
            copies(4),
            copies(4),
            copies(2, 2),
            copies(2, 2),
            copies(2),
            copies(2),
            copies(32),
            copies(32),
        ],
        compiler_params=settings(4),
    )(tokens, routes, gain, w_query, key_weight, value_weight)


def turned(values):
    return pltpu.roll(values, HEAD_WIDTH // 2, 1)


def signed(sine):
    lanes = lax.broadcasted_iota(jnp.int32, sine.shape, 1)
    return jnp.where(lanes < HEAD_WIDTH // 2, -sine, sine)


def nt_product(left, right):
    return lax.dot_general(
        left, right, (((1,), (1,)), ((), ())), preferred_element_type=jnp.float32
    )


def finish_kernel(
    row,
    sequences,
    raw_ref,
    notes_ref,
    query_gain_ref,
    key_gain_ref,
    weight_ref,
    x_ref,
    gain_ref,
    middle_out,
    normed_out,
    attended_out,
    probs_out,
    query_out,
    key_out,
    cosine_out,
    sine_out,
    outgoing,
    core_in,
    across_x,
    x_sums,
    core_sent,
    core_got,
    x_sent,
    x_got,
):
    z, y, x, c = spot()
    count = x_ref.shape[0]
    core_peer, x_peer = where_is(z, y, x, 1 - c), where_is(z, y, 1 - x, c)
    greet([core_peer, x_peer])
    heads = query_out.shape[2] // HEAD_WIDTH
    wide = heads * HEAD_WIDTH

    def place(block):
        down = lax.broadcasted_iota(jnp.int32, (count, count), 0)
        along = lax.broadcasted_iota(jnp.int32, (count, count), 1)
        end = jnp.zeros((1, 1), jnp.int32)
        start = jnp.zeros((count, count), jnp.int32)
        own, other = start, start
        for i in range(sequences - 1):
            length = notes_ref[block, row : row + 1, i : i + 1]
            end = end + length
            own = own + jnp.where(down >= end, 1, 0)
            other = other + jnp.where(along >= end, 1, 0)
            start = start + jnp.where(down >= end, length, 0)
        return down - start, (own == other) & (along <= down)

    def attend(block):
        position, allowed = place(block)
        lanes = lax.broadcasted_iota(jnp.int32, position.shape, 1)
        spin = lanes % (HEAD_WIDTH // 2)
        inverse = jnp.exp(spin.astype(jnp.float32) * (-2.0 * math.log(THETA) / HEAD_WIDTH))
        angles = position.astype(jnp.float32) * inverse
        cosine, sine = jnp.cos(angles), jnp.sin(angles)
        cosine_out[block] = cosine
        sine_out[block] = sine
        flipped = signed(sine)

        def normal(values, gain):
            scale = lax.rsqrt(jnp.mean(values * values, axis=1, keepdims=True) + EPSILON)
            values = values * scale * gain
            return (values * cosine + turned(values) * flipped).astype(query_out.dtype)

        key = normal(raw_ref[block, :, wide : wide + HEAD_WIDTH], key_gain_ref[...])
        key_out[block] = key
        value = raw_ref[block, :, wide + HEAD_WIDTH :].astype(query_out.dtype)
        for head in range(heads):
            columns = slice(head * HEAD_WIDTH, (head + 1) * HEAD_WIDTH)
            query = normal(raw_ref[block, :, columns], query_gain_ref[...])
            query_out[block, :, columns] = query
            scores = nt_product(query, key) * HEAD_WIDTH ** (-0.5)
            scores = jnp.where(allowed, scores, MASKED)
            raised = jnp.exp(scores - jnp.max(scores, axis=1, keepdims=True))
            probs = raised / jnp.sum(raised, axis=1, keepdims=True)
            probs_out[block, head] = probs
            attended_out[block, :, columns] = jnp.dot(
                probs.astype(value.dtype), value, preferred_element_type=jnp.float32
            ).astype(attended_out.dtype)

    def core_copy(far):
        return remote(
            outgoing.at[far], core_in.at[far], core_sent.at[far], core_got.at[far], core_peer
        )

    def x_copy():
        return remote(across_x, x_sums, x_sent, x_got, x_peer)

    def partial(side, core):
        block = side * 2 + core
        attend(block)
        return jnp.dot(attended_out[block], weight_ref[...], preferred_element_type=jnp.float32)

    outgoing[1] = partial(1 - x, 1 - c).astype(outgoing.dtype)
    core_copy(1).start()
    sums = partial(1 - x, c)
    core_copy(1).wait_recv()
    across_x[...] = (sums + core_in[1].astype(jnp.float32)).astype(across_x.dtype)
    x_copy().start()
    outgoing[0] = partial(x, 1 - c).astype(outgoing.dtype)
    core_copy(0).start()
    sums = partial(x, c) + x_ref[...].astype(jnp.float32)
    core_copy(0).wait_recv()
    sums = sums + core_in[0].astype(jnp.float32)
    x_copy().wait_recv()
    middle = sums + x_sums[...].astype(jnp.float32)
    middle_out[...] = middle
    scale = lax.rsqrt(jnp.mean(middle * middle, axis=1, keepdims=True) + EPSILON)
    normed_out[...] = (middle * scale * gain_ref[...]).astype(normed_out.dtype)
    x_copy().wait_send()
    core_copy(0).wait_send()
    core_copy(1).wait_send()


def finish_attention(raw, notes, row, sequences, q_gain, k_gain, w_out, tokens, gain):
    count, width = tokens.shape
    low = tokens.dtype
    wide = w_out.shape[0]
    heads = wide // HEAD_WIDTH
    return pl.pallas_call(
        functools.partial(finish_kernel, row, sequences),
        out_shape=[
            jax.ShapeDtypeStruct((count, width), jnp.float32),
            jax.ShapeDtypeStruct((count, width), low),
            jax.ShapeDtypeStruct((4, count, wide), low),
            jax.ShapeDtypeStruct((4, heads, count, count), jnp.float32),
            jax.ShapeDtypeStruct((4, count, wide), low),
            jax.ShapeDtypeStruct((4, count, HEAD_WIDTH), low),
            jax.ShapeDtypeStruct((4, count, HEAD_WIDTH), jnp.float32),
            jax.ShapeDtypeStruct((4, count, HEAD_WIDTH), jnp.float32),
        ],
        in_specs=in_vmem(7),
        out_specs=in_vmem(8),
        scratch_shapes=[
            pltpu.VMEM((2, count, width), low),
            pltpu.VMEM((2, count, width), low),
            pltpu.VMEM((count, width), low),
            pltpu.VMEM((count, width), low),
            copies(2),
            copies(2),
            copies(),
            copies(),
        ],
        compiler_params=settings(5),
    )(raw, notes, q_gain, k_gain, w_out, tokens, gain)


def branch_kernel(
    branch_ref, weight_ref, grad_out, every_out, x_sent, x_got, core_sent, core_got
):
    z, y, x, c = spot()
    mine = x * 2 + c
    core_peer, x_peer = where_is(z, y, x, 1 - c), where_is(z, y, 1 - x, c)
    greet([core_peer, x_peer])
    every_out[mine] = branch_ref[...]

    def x_copy():
        return remote(branch_ref, every_out.at[mine], x_sent, x_got, x_peer)

    def core_copy(far):
        place = (1 - x if far else x) * 2 + c
        return remote(
            every_out.at[place], every_out.at[place], core_sent.at[far], core_got.at[far], core_peer
        )

    def back(place):
        grad_out[place] = right_transposed(every_out[place], weight_ref[...]).astype(grad_out.dtype)

    x_copy().start()
    core_copy(0).start()
    back(mine)
    core_copy(0).wait_recv()
    back(x * 2 + 1 - c)
    x_copy().wait_recv()
    core_copy(1).start()
    back((1 - x) * 2 + c)
    core_copy(1).wait_recv()
    back((1 - x) * 2 + 1 - c)
    x_copy().wait_send()
    core_copy(0).wait_send()
    core_copy(1).wait_send()


def branch_back(branch, w_out):
    count, width = branch.shape
    low = branch.dtype
    return pl.pallas_call(
        branch_kernel,
        out_shape=[
            jax.ShapeDtypeStruct((4, count, w_out.shape[0]), low),
            jax.ShapeDtypeStruct((4, count, width), low),
        ],
        in_specs=in_vmem(2),
        out_specs=in_vmem(2),
        scratch_shapes=[copies(), copies(), copies(2), copies(2)],
        compiler_params=settings(6),
    )(branch, w_out)


def heads_kernel(
    branch_ref,
    raw_ref,
    probs_ref,
    rotated_ref,
    rotated_key_ref,
    cosine_ref,
    sine_ref,
    query_gain_ref,
    key_gain_ref,
    hidden_ref,
    query_ref,
    key_ref,
    value_ref,
    weight_out,
    first_out,
    gains_out,
    every,
    outgoing,
    x_sent,
    x_got,
    core_sent,
    core_got,
    back_sent,
    back_got,
):
    z, y, x, c = spot()
    member, shard = lax.axis_index("exp"), lax.axis_index("fsdp")
    core_peer, x_peer = where_is(z, y, x, 1 - c), where_is(z, y, 1 - x, c)
    peers = [(member, (shard + j) % 4) for j in range(1, 4)]
    greet(peers)
    rows = every.shape[1]
    half = rows // 2
    count = rows // 4
    depth = hidden_ref.shape[1]
    wide, narrow = query_ref.shape[1] // 4, key_ref.shape[1] // 4
    low = every.dtype

    def attention_back(block):
        cosine = cosine_ref[block]
        flipped = signed(sine_ref[block])

        def unturn(grads):
            return grads * cosine + turned(grads * flipped)

        def normal_back(grads, values, gain, into):
            scale = lax.rsqrt(jnp.mean(values * values, axis=1, keepdims=True) + EPSILON)
            hat = values * scale
            gains_out[into : into + 1] += jnp.sum(grads * hat, axis=0, keepdims=True)
            grads = grads * gain
            return scale * (grads - hat * jnp.mean(grads * hat, axis=1, keepdims=True))

        rotated_key = rotated_key_ref[block]
        value = raw_ref[block, :, wide + narrow :].astype(low)
        place = pl.ds(block * count, count)
        value_grad = key_grad = None
        for head in range(wide // HEAD_WIDTH):
            columns = slice(head * HEAD_WIDTH, (head + 1) * HEAD_WIDTH)
            grads = branch_ref[block, :, columns]
            probs = probs_ref[block, head]
            prob_grad = nt_product(grads, value)
            term = left_trans(probs.astype(low), grads)
            value_grad = term if value_grad is None else value_grad + term
            balance = jnp.sum(probs * prob_grad, axis=1, keepdims=True)
            score_grad = (probs * (prob_grad - balance)).astype(low)
            query_grad = jnp.dot(score_grad, rotated_key, preferred_element_type=jnp.float32)
            term = left_trans(score_grad, rotated_ref[block, :, columns])
            key_grad = term if key_grad is None else key_grad + term
            query_grad = unturn(query_grad * HEAD_WIDTH ** (-0.5))
            query_grad = normal_back(
                query_grad, raw_ref[block, :, columns], query_gain_ref[...], 0
            )
            every[shard, place, columns] = query_grad.astype(low)
        key_grad = unturn(key_grad * HEAD_WIDTH ** (-0.5))
        key_grad = normal_back(
            key_grad, raw_ref[block, :, wide : wide + narrow], key_gain_ref[...], 1
        )
        every[shard, place, wide : wide + narrow] = key_grad.astype(low)
        every[shard, place, wide + narrow :] = value_grad.astype(low)

    def x_copy(part):
        view = every.at[shard, pl.ds(part * half, half)]
        return remote(view, view, x_sent.at[part], x_got.at[part], x_peer)

    def core_copy(far, part):
        view = every.at[(1 - x if far else x) * 2 + c, pl.ds(part * half, half)]
        return remote(view, view, core_sent.at[far, part], core_got.at[far, part], core_peer)

    gains_out[...] = jnp.zeros_like(gains_out)
    for part in range(2):

        @pl.loop(part * 2, part * 2 + 2)
        def _(block):
            attention_back(block)

        x_copy(part).start()
        core_copy(0, part).start()

    def weigh(place):
        weight_out[place] = left_trans(hidden_ref[...], every[place]).astype(weight_out.dtype)

    def back(place):
        grads = every[place]
        sums = None
        for weight, size, start in (
            (query_ref, wide, 0),
            (key_ref, narrow, wide),
            (value_ref, narrow, wide + narrow),
        ):
            columns = pl.ds(pl.multiple_of(place * size, size), size)
            term = right_transposed(grads[:, start : start + size], weight[:, columns])
            sums = term if sums is None else sums + term
        return sums

    total = back(shard)
    weigh(shard)
    near = x * 2 + 1 - c
    for part in range(2):
        core_copy(0, part).wait_recv()
    total = total + back(near)
    weigh(near)
    for part in range(2):
        x_copy(part).wait_recv()
        core_copy(1, part).start()
    far = (1 - x) * 2 + c
    total = total + back(far)
    for part in range(2):
        core_copy(1, part).wait_recv()
    total = total + back((1 - x) * 2 + 1 - c)
    for owner in range(4):
        outgoing[owner] = total[owner * count : (owner + 1) * count].astype(outgoing.dtype)

    def back_copy(j):
        place = (shard + j) % 4
        return remote(
            outgoing.at[place],
            first_out.at[shard],
            back_sent.at[j],
            back_got.at[(4 - j) % 4],
            (member, place),
        )

    for j in range(1, 4):
        back_copy(j).start()
    first_out[shard] = outgoing[shard]
    weigh(far)
    weigh((1 - x) * 2 + 1 - c)
    for j in range(1, 4):
        place = (shard + j) % 4
        remote(
            outgoing.at[place], first_out.at[place], back_sent.at[j], back_got.at[j], (member, place)
        ).wait_recv()
    for j in range(1, 4):
        back_copy(j).wait_send()
    for part in range(2):
        x_copy(part).wait_send()
        for far in range(2):
            core_copy(far, part).wait_send()


def heads_back(branch, raw, probs, rotated, tables, gains, hidden, weights):
    rows = 4 * raw.shape[1]
    own = raw.shape[2]
    depth = hidden.shape[1]
    low = hidden.dtype
    operands = (branch, raw, probs, *rotated, *tables, *gains, hidden, *weights)
    return pl.pallas_call(
        heads_kernel,
        out_shape=[
            jax.ShapeDtypeStruct((4, depth, own), low),
            jax.ShapeDtypeStruct((4, rows // 4, depth), low),
            jax.ShapeDtypeStruct((8, HEAD_WIDTH), jnp.float32),
        ],
        in_specs=in_vmem(len(operands)),
        out_specs=in_vmem(3),
        scratch_shapes=[
            pltpu.VMEM((4, rows, own), low),
            pltpu.VMEM((4, rows // 4, depth), low),
            copies(2),
            copies(2),
            copies(2, 2),
            copies(2, 2),
            copies(4),
            copies(4),
        ],
        compiler_params=settings(7),
    )(*operands)


def moe_gathered(normed, router, routes, capacity, cotangent, weights, notes):
    gate_w, up_w, down_w = weights
    token_count, topk = routes.shape
    experts = router.shape[1]
    mine = lax.axis_index("exp") * lax.axis_size("fsdp") + lax.axis_index("fsdp")
    all_routes = notes[:, :topk]
    all_grads = lax.all_gather(cotangent, BOTH, axis=0, tiled=True)
    columns = jnp.arange(experts, dtype=jnp.int32)
    named = jnp.any(all_routes[:, :, None, :] == columns[None, None, :, None], axis=1)
    own = jnp.any(all_routes == mine, axis=1)
    before = jnp.tril(jnp.ones((token_count, token_count), jnp.bfloat16), -1)
    rank = right_transposed(own.astype(jnp.bfloat16), before).astype(jnp.int32)
    places = jnp.arange(capacity, dtype=jnp.int32)
    select = (own[:, None, :] & (rank[:, None, :] == places[None, :, None])).astype(jnp.bfloat16)
    spread = (own[:, :, None] & (rank[:, :, None] == places[None, None, :])).astype(jnp.bfloat16)
    named_rows = contract("bcj,bej->bce", select, named.astype(jnp.bfloat16))
    named_rows = jnp.pad(named_rows.astype(jnp.bfloat16), ((0, 0), (0, 0), (0, 128 - experts)))
    padded = jnp.pad(router, ((0, 0), (0, 128 - experts)))
    arrived, active, gate_pre, up_pre, share = gather_experts(
        normed, select, named_rows, gate_w, up_w, padded
    )
    mixed, out_rows, gate_pre_grad, up_pre_grad, extra = scatter_rows(
        spread,
        active,
        down_w,
        share,
        select,
        all_grads.reshape(experts, token_count, MODEL_WIDTH),
        gate_pre,
        up_pre,
    )
    summed, back, gate_w_grad, up_w_grad = scatter_rows(
        spread, gate_pre_grad, up_pre_grad, gate_w, up_w, extra, arrived
    )

    def flat(rows):
        return rows.reshape(experts * capacity, rows.shape[2])

    weight_grads = (gate_w_grad, up_w_grad, left_trans(flat(active), flat(out_rows)))
    gate_grad = back[:, :experts] + back[:, experts : 2 * experts]
    picks = jnp.any(routes[:, :, None] == columns[None, None, :], axis=1)
    gates = jax.nn.softmax(jnp.where(picks, matrix_product(normed, router), MASKED), axis=1)
    logit_grad = gates * (gate_grad - jnp.sum(gates * gate_grad, axis=1, keepdims=True))
    return mixed, summed, logit_grad.astype(jnp.bfloat16), *weight_grads


def moe_exchanged(normed, router, routes, capacity, cotangent, weights, notes):
    gate_w, up_w, down_w = weights
    token_count, topk = routes.shape
    experts = router.shape[1]
    gates = gates_of(matrix_product(normed, router), routes, experts)
    slots = slot_table(routes, experts, capacity)

    def send(rows):
        packed = jnp.zeros((experts * capacity, MODEL_WIDTH), jnp.bfloat16).at[slots].set(rows)
        return exchange(packed.reshape(experts, capacity, MODEL_WIDTH)).reshape(
            experts * capacity, MODEL_WIDTH
        )

    def bring(rows):
        rows = exchange(rows.reshape(experts, capacity, MODEL_WIDTH))
        return rows.reshape(experts * capacity, MODEL_WIDTH)[slots].reshape(
            token_count, topk, MODEL_WIDTH
        )

    arrived = send(jnp.repeat(normed, topk, axis=0))
    hidden = expert_forward(arrived, gate_w, up_w)
    scaled = (gates[:, :, None] * cotangent.astype(jnp.float32)[:, None, :]).astype(jnp.bfloat16)
    out_rows = send(scaled.reshape(token_count * topk, MODEL_WIDTH))
    rows_back, gate_pre_grad, up_pre_grad = expert_back(out_rows, hidden, gate_w, up_w, down_w)
    gate_w_grad = left_trans(arrived, gate_pre_grad)
    up_w_grad = left_trans(arrived, up_pre_grad)
    down_grad = left_trans(hidden[3], out_rows)
    returned = bring(matrix_product(hidden[3], down_w).astype(jnp.bfloat16))
    mixed = jnp.einsum("tk,tkd->td", gates, returned.astype(jnp.float32))
    gate_grad = jnp.einsum("td,tkd->tk", cotangent, returned, preferred_element_type=jnp.float32)
    summed = jnp.sum(bring(rows_back), axis=1, dtype=jnp.float32)
    picked_grad = gates * (gate_grad - jnp.sum(gates * gate_grad, axis=1, keepdims=True))
    onehot = routes[:, :, None] == jnp.arange(experts, dtype=jnp.int32)[None, None, :]
    logit_grad = jnp.sum(jnp.where(onehot, picked_grad[:, :, None], 0.0), axis=1)
    return mixed, summed, logit_grad.astype(jnp.bfloat16), gate_w_grad, up_w_grad, down_grad


def local(
    tokens,
    lengths,
    routes,
    attn_gain,
    w_query,
    key_weight,
    value_weight,
    q_gain,
    k_gain,
    w_out,
    mlp_gain,
    w_router,
    expert_gate,
    expert_up,
    expert_down,
    cotangent,
):
    shards, members = lax.axis_size("fsdp"), lax.axis_size("exp")
    experts = shards * members
    token_count, topk = routes.shape
    capacity = 2 * token_count * topk // experts
    group = shards * token_count
    depth = w_query.shape[0]
    heads = QUERY_HEADS // shards
    kv_heads = max(1, KEY_VALUE_HEADS // shards)
    copies_of = shards * kv_heads // KEY_VALUE_HEADS
    head_group = heads // kv_heads
    wide, narrow = heads * HEAD_WIDTH, kv_heads * HEAD_WIDTH
    place = lax.axis_index("fsdp")

    gathered = lax.all_gather(
        jnp.concatenate([w_router.reshape(-1), attn_gain, mlp_gain, q_gain, k_gain]), "fsdp"
    )
    cuts, start = [], 0
    for leaf in (w_router, attn_gain, mlp_gain, q_gain, k_gain):
        cuts.append(gathered[:, start : start + leaf.size])
        start += leaf.size
    router = cuts[0].reshape(MODEL_WIDTH, experts)
    gain_attn, gain_mlp, gain_query, gain_key = [
        cut.reshape(-1).astype(jnp.float32) for cut in cuts[1:]
    ]
    dense = (members, shards) == (8, 4) and 2 * capacity >= token_count
    inputs = tokens.astype(jnp.float32)
    scale_one = rms_scale(inputs)
    if dense:
        notes = jnp.pad(
            jnp.concatenate(
                [routes.T, jnp.pad(lengths, ((0, 0), (0, token_count - lengths.shape[1])))], axis=0
            ),
            ((0, 15 - topk), (0, 0)),
        )
        raw, hidden, notes = project_tokens(
            tokens, notes, attn_gain[None], w_query, key_weight, value_weight
        )
        hidden = hidden.reshape(group, depth)
        first = lax.axis_index("exp") * shards
        notes_own = lax.dynamic_slice_in_dim(notes, first, shards)
    else:
        notes = None
        all_lengths = lax.all_gather(lengths[0], "fsdp")

        def by_shard(weight):
            weight = weight.reshape(depth, KEY_VALUE_HEADS, HEAD_WIDTH)
            return jnp.repeat(weight, copies_of, axis=1).reshape(depth, shards, narrow)

        joined = jnp.concatenate(
            [w_query.reshape(depth, shards, wide), by_shard(key_weight), by_shard(value_weight)],
            axis=2,
        ).transpose(1, 0, 2)
        first_normed = (inputs * scale_one * gain_attn).astype(jnp.bfloat16)
        hidden = lax.all_to_all(first_normed, "fsdp", split_axis=1, concat_axis=0, tiled=True)
        partial = contract("gk,nkc->ngc", hidden, joined).astype(jnp.bfloat16)
        raw = lax.psum_scatter(partial, "fsdp", scatter_dimension=0, tiled=True)[0]
        raw = raw.astype(jnp.float32)
    if dense:
        gains = (gain_query[None], gain_key[None])
        middle, normed, attended, probs, *rotated, cosine, sine = finish_attention(
            raw, notes_own, topk, lengths.shape[1], *gains, w_out, tokens, gain_mlp[None]
        )
        attended = attended.reshape(group, wide)
        scale_two = rms_scale(middle)
    else:
        raw = raw.reshape(shards, token_count, wide + 2 * narrow)
        query_raw = raw[:, :, :wide].reshape(shards, token_count, heads, HEAD_WIDTH)
        key_raw = raw[:, :, wide : wide + narrow].reshape(shards, token_count, kv_heads, HEAD_WIDTH)
        value = (
            raw[:, :, wide + narrow :]
            .astype(jnp.bfloat16)
            .reshape(shards, token_count, kv_heads, HEAD_WIDTH)
        )
        position, allowed = jax.vmap(lambda row: seq_layout(row, token_count))(all_lengths)
        cosine, sine = rotary_tables(position, HEAD_WIDTH)
        query_scale = rms_scale(query_raw)
        query_hat = query_raw * query_scale
        key_scale = rms_scale(key_raw)
        key_hat = key_raw * key_scale
        query = (
            rotate(query_hat * gain_query, cosine, sine)
            .astype(jnp.bfloat16)
            .reshape(shards, token_count, kv_heads, head_group, HEAD_WIDTH)
        )
        key = rotate(key_hat * gain_key, cosine, sine).astype(jnp.bfloat16)
        scores = contract("bqkgd,bpkd->bkgqp", query, key) * HEAD_WIDTH ** (-0.5)
        scores = jnp.where(allowed[:, None, None], scores, MASKED)
        top = jnp.max(scores, axis=-1, keepdims=True)
        raised = jnp.exp(scores - top)
        probs = raised / jnp.sum(raised, axis=-1, keepdims=True)
        probs_low = probs.astype(jnp.bfloat16)
        attended = contract("bkgqp,bpkd->bqkgd", probs_low, value).astype(jnp.bfloat16)
        attended = attended.reshape(group, wide)
        mixed_heads = lax.psum_scatter(
            matrix_product(attended, w_out).astype(jnp.bfloat16),
            "fsdp",
            scatter_dimension=0,
            tiled=True,
        )
        middle = inputs + mixed_heads.astype(jnp.float32)
        scale_two = rms_scale(middle)
        normed = (middle * scale_two * gain_mlp).astype(jnp.bfloat16)

    moe = moe_gathered if dense else moe_exchanged
    mixed, summed, logit_grad, gate_w_grad, up_w_grad, down_grad = moe(
        normed,
        router,
        routes,
        capacity,
        cotangent,
        (expert_gate[0], expert_up[0], expert_down[0]),
        notes,
    )
    layer_out = (middle + mixed).astype(jnp.bfloat16)

    upstream = cotangent.astype(jnp.float32)
    normed_grad = summed + right_transposed(logit_grad, router)
    mlp_gain_grad = jnp.sum(normed_grad * middle * scale_two, axis=0)
    router_grad = left_trans(normed, logit_grad)
    middle_grad = upstream + rms_back(normed_grad * gain_mlp, middle, scale_two)
    branch_low = middle_grad.astype(jnp.bfloat16)
    if dense:
        attended_grad, branch_grad = branch_back(branch_low, w_out)
        branch_grad = branch_grad.reshape(group, MODEL_WIDTH)
    else:
        branch_grad = lax.all_gather(branch_low, "fsdp", axis=0, tiled=True)
        attended_grad = right_transposed(branch_grad, w_out).astype(jnp.bfloat16)
    out_w_grad = left_trans(attended, branch_grad).astype(jnp.bfloat16)
    attended_grad, out_w_grad = lax.optimization_barrier((attended_grad, out_w_grad))
    if dense:
        joined_grad, first_grad, gain_grads = heads_back(
            attended_grad,
            raw,
            probs,
            rotated,
            (cosine, sine),
            gains,
            hidden,
            (w_query, key_weight, value_weight),
        )
        first_grad = first_grad.transpose(1, 0, 2).reshape(token_count, MODEL_WIDTH)
        q_gain_grad, k_gain_grad = gain_grads[0], gain_grads[1]
    else:
        attended_grad = attended_grad.reshape(shards, token_count, kv_heads, head_group, HEAD_WIDTH)
        prob_grad = contract("bqkgd,bpkd->bkgqp", attended_grad, value)
        value_grad = contract("bkgqp,bqkgd->bpkd", probs_low, attended_grad)
        balance = jnp.sum(probs * prob_grad, axis=-1, keepdims=True)
        score_grad = (probs * (prob_grad - balance)).astype(jnp.bfloat16)
        query_norm_grad = contract("bkgqp,bpkd->bqkgd", score_grad, key) * HEAD_WIDTH ** (-0.5)
        query_norm_grad = query_norm_grad.reshape(shards, token_count, heads, HEAD_WIDTH)
        key_norm_grad = contract("bkgqp,bqkgd->bpkd", score_grad, query) * HEAD_WIDTH ** (-0.5)
        query_norm_grad = rotate_back(query_norm_grad, cosine, sine)
        key_norm_grad = rotate_back(key_norm_grad, cosine, sine)
        q_gain_grad = jnp.sum(query_norm_grad * query_hat, axis=(0, 1, 2))
        k_gain_grad = jnp.sum(key_norm_grad * key_hat, axis=(0, 1, 2))
        query_grad = rms_back(query_norm_grad * gain_query, query_raw, query_scale)
        key_grad = rms_back(key_norm_grad * gain_key, key_raw, key_scale)
        head_grads = jnp.concatenate(
            [
                query_grad.reshape(group, wide),
                key_grad.reshape(group, narrow),
                value_grad.reshape(group, narrow),
            ],
            axis=1,
        ).astype(jnp.bfloat16)
        head_grads = lax.all_gather(head_grads, "fsdp")
        hidden_grad = contract("ngc,nkc->gk", head_grads, joined).astype(jnp.bfloat16)
        first_grad = lax.all_to_all(
            hidden_grad, "fsdp", split_axis=0, concat_axis=1, tiled=True
        )
        joined_grad = contract("gk,ngc->nkc", hidden, head_grads).astype(jnp.bfloat16)
    first_grad = first_grad.astype(jnp.float32)
    attn_gain_grad = jnp.sum(first_grad * inputs * scale_one, axis=0)
    input_grad = (middle_grad + rms_back(first_grad * gain_attn, inputs, scale_one)).astype(
        jnp.bfloat16
    )

    vectors = jnp.concatenate(
        [
            grad.reshape(shards, -1)
            for grad in (router_grad, attn_gain_grad, mlp_gain_grad, q_gain_grad, k_gain_grad)
        ],
        axis=1,
    )
    if dense:
        rows = -(-vectors.shape[1] // 1024) * 8
        vectors = jnp.pad(vectors, ((0, 0), (0, rows * 128 - vectors.shape[1])))
        started = lengths[0, 0] > 0
        gate_w_grad, up_w_grad = (
            jnp.where(started, grad, 0.0) for grad in (gate_w_grad, up_w_grad)
        )
        out_sum = lax.psum_scatter(out_w_grad, "exp", scatter_dimension=0, tiled=True)
        joined_grad, vectors, out_sum, gate_w_grad, up_w_grad, down_grad = (
            lax.optimization_barrier(
                (joined_grad, vectors, out_sum, gate_w_grad, up_w_grad, down_grad)
            )
        )
        *joined_sum, out_sum, vectors = reduce_over_members(
            joined_grad.reshape(2, 4, -1, wide + 2 * narrow),
            out_sum,
            vectors.reshape(shards, rows, 128),
            (shards * wide, shards * narrow, shards * narrow),
        )
        out_sum, vectors = out_sum.reshape(w_out.shape), vectors.reshape(-1)
    else:
        out_sum = lax.psum(out_w_grad, "exp")
        joined_sum = lax.psum(joined_grad, "exp").astype(jnp.float32)
        vectors = lax.psum(vectors, BOTH)[place]
    if not dense:

        def gather_heads(part):
            part = part.transpose(1, 0, 2).reshape(depth, KEY_VALUE_HEADS, copies_of, HEAD_WIDTH)
            return part.sum(axis=2).reshape(depth, KEY_VALUE_HEADS * HEAD_WIDTH)

        joined_sum = (
            joined_sum[:, :, :wide].transpose(1, 0, 2).reshape(depth, QUERY_HEADS * HEAD_WIDTH),
            gather_heads(joined_sum[:, :, wide : wide + narrow]),
            gather_heads(joined_sum[:, :, wide + narrow :]),
        )
    query_sum, key_sum, value_sum = (part.astype(jnp.float32) for part in joined_sum)
    sums, start = [], 0
    for leaf in (w_router, attn_gain, mlp_gain, q_gain, k_gain):
        sums.append(vectors[start : start + leaf.size].reshape(leaf.shape))
        start += leaf.size

    return (
        layer_out,
        input_grad,
        sums[1],
        query_sum,
        key_sum,
        value_sum,
        sums[3],
        sums[4],
        out_sum.astype(jnp.float32),
        sums[2],
        sums[0],
        gate_w_grad[None],
        up_w_grad[None],
        down_grad[None],
    )


def solution(mesh):
    in_specs = (
        P(("exp", "fsdp"), None),
        P(("exp", "fsdp"), None),
        P(("exp", "fsdp"), None),
        P("fsdp"),
        P("fsdp", None),
        P("fsdp", None),
        P("fsdp", None),
        P("fsdp"),
        P("fsdp"),
        P("fsdp", None),
        P("fsdp"),
        P("fsdp", None),
        P(("exp", "fsdp"), None, None),
        P(("exp", "fsdp"), None, None),
        P(("exp", "fsdp"), None, None),
        P(("exp", "fsdp"), None),
    )
    out_specs = (
        P(("exp", "fsdp"), None),
        P(("exp", "fsdp"), None),
        P("fsdp"),
        P("fsdp", None),
        P("fsdp", None),
        P("fsdp", None),
        P("fsdp"),
        P("fsdp"),
        P("fsdp", None),
        P("fsdp"),
        P("fsdp", None),
        P(("exp", "fsdp"), None, None),
        P(("exp", "fsdp"), None, None),
        P(("exp", "fsdp"), None, None),
    )
    return jax.shard_map(local, mesh=mesh, in_specs=in_specs, out_specs=out_specs, check_vma=False)
```

```python
import functools
import math

import jax
import jax.numpy as jnp
from jax import lax
from jax.experimental import pallas as pl
from jax.experimental.pallas import tpu as pltpu
from jax.sharding import PartitionSpec as P

MODEL_WIDTH = 2048
QUERY_HEADS = 32
KEY_VALUE_HEADS = 4
HEAD_WIDTH = 128


EPSILON = 1e-06
THETA = 1000000.0
MASKED = -1e30
BOTH = ("exp", "fsdp")
MESH = pl.DeviceIdType.MESH


def matrix_product(left, right):
    return jnp.dot(left, right, preferred_element_type=jnp.float32)


def left_trans(left, right):
    return lax.dot_general(
        left, right, (((0,), (0,)), ((), ())), preferred_element_type=jnp.float32
    )


def right_transposed(left, right):
    return lax.dot_general(
        left, right, (((1,), (1,)), ((), ())), preferred_element_type=jnp.float32
    )


def contract(spec, left, right):
    return jnp.einsum(spec, left, right, preferred_element_type=jnp.float32)


def rms_scale(values):
    return lax.rsqrt(jnp.mean(values * values, axis=-1, keepdims=True) + EPSILON)


def rms_back(grad_hat, values, scale):
    normal = values * scale
    return scale * (grad_hat - normal * jnp.mean(grad_hat * normal, axis=-1, keepdims=True))


def seq_layout(length_row, token_count):
    ends = jnp.cumsum(length_row)
    starts = ends - length_row
    places = jnp.arange(token_count, dtype=jnp.int32)
    member = (places[:, None] >= starts[None, :]) & (places[:, None] < ends[None, :])
    numbers = jnp.arange(length_row.shape[0], dtype=jnp.int32)
    segment = jnp.sum(jnp.where(member, numbers[None, :], 0), axis=1)
    position = places - jnp.sum(jnp.where(member, starts[None, :], 0), axis=1)
    allowed = (segment[:, None] == segment[None, :]) & (places[None, :] <= places[:, None])
    return (position, allowed)


def rotary_tables(position, head_size):
    half = head_size // 2
    index = jnp.arange(head_size, dtype=jnp.int32) % half
    inverse = jnp.exp(index.astype(jnp.float32) * (-2.0 * math.log(THETA) / head_size))
    angles = position.astype(jnp.float32)[..., None] * inverse
    return (jnp.cos(angles)[..., None, :], jnp.sin(angles)[..., None, :])


def rotate(values, cosine, sine):
    half = values.shape[-1] // 2
    turned = jnp.concatenate([-values[..., half:], values[..., :half]], axis=-1)
    return values * cosine + turned * sine


def rotate_back(grads, cosine, sine):
    half = grads.shape[-1] // 2
    moved = grads * sine
    return grads * cosine + jnp.concatenate([moved[..., half:], -moved[..., :half]], axis=-1)


def slot_table(route_rows, experts, capacity):
    flat = route_rows.reshape(-1)
    onehot = (flat[:, None] == jnp.arange(experts, dtype=jnp.int32)[None, :]).astype(jnp.int32)
    ranks = jnp.cumsum(onehot, axis=0) - 1
    rank = jnp.sum(ranks * onehot, axis=1)
    return flat * capacity + rank


def exchange(buffer):
    return lax.all_to_all(buffer, BOTH, split_axis=0, concat_axis=0, tiled=True)


def two_halves(values):
    high = values.astype(jnp.bfloat16)
    low = (values - high.astype(jnp.float32)).astype(jnp.bfloat16)
    return high, low


def expert_forward(arrived, gate_w, up_w):
    gate_pre = matrix_product(arrived, gate_w)
    up_pre = matrix_product(arrived, up_w)
    sigma = jax.nn.sigmoid(gate_pre)
    active = (gate_pre * sigma * up_pre).astype(jnp.bfloat16)
    return gate_pre, up_pre, sigma, active


def expert_back(out_rows, hidden, gate_w, up_w, down_w):
    gate_pre, up_pre, sigma, _ = hidden
    active_grad = right_transposed(out_rows, down_w)
    gate_pre_grad = (active_grad * up_pre * (sigma * (1.0 + gate_pre * (1.0 - sigma)))).astype(
        jnp.bfloat16
    )
    up_pre_grad = (active_grad * (gate_pre * sigma)).astype(jnp.bfloat16)
    rows_back = right_transposed(gate_pre_grad, gate_w) + right_transposed(up_pre_grad, up_w)
    return rows_back.astype(jnp.bfloat16), gate_pre_grad, up_pre_grad


def gates_of(logits, routes, experts):
    picked = jnp.take_along_axis(logits, routes, axis=1)
    peak = jnp.max(picked, axis=1, keepdims=True)
    lifted = jnp.exp(picked - peak)
    return lifted / jnp.sum(lifted, axis=1, keepdims=True)


def spot():
    member, shard = lax.axis_index("exp"), lax.axis_index("fsdp")
    return member // 2, member % 2, shard // 2, shard % 2


def where_is(z, y, x, c):
    return (z * 2 + y, x * 2 + c)


def number(z, y, x, c):
    return z * 8 + y * 4 + x * 2 + c


def along_z(z, q):
    return (z // 2 + q // 2) % 2 * 2 + (z % 2 + q % 2) % 2


def greet(peers):
    barrier = pltpu.get_barrier_semaphore()
    for peer in peers:
        pl.semaphore_signal(barrier, inc=1, device_id=peer, device_id_type=MESH)
    pl.semaphore_wait(barrier, len(peers))


def remote(source, target, sent, got, peer):
    return pltpu.make_async_remote_copy(
        src_ref=source,
        dst_ref=target,
        send_sem=sent,
        recv_sem=got,
        device_id=peer,
        device_id_type=MESH,
    )


def in_vmem(count):
    return [pl.BlockSpec(memory_space=pltpu.VMEM)] * count


def copies(*shape):
    return pltpu.SemaphoreType.DMA(shape)


def settings(collective_id):
    return pltpu.CompilerParams(
        collective_id=collective_id, has_side_effects=True, vmem_limit_bytes=60 << 20
    )


def gather_kernel(
    topk,
    x_ref,
    notes_ref,
    gate_hbm,
    up_hbm,
    router_ref,
    rows_out,
    active_out,
    gate_out,
    up_out,
    share_out,
    select_out,
    spread_out,
    held,
    gate_ref,
    up_ref,
    picked,
    lively,
    results,
    loaded,
    stored,
    arrive,
    to_z,
    to_y,
    to_x,
    to_core,
    corners,
    deep_z,
    deep_core,
):
    z, y, x, c = spot()
    count = x_ref.shape[0]
    half, thin = count * 3 // 8, count // 8
    cuts = ((0, half), (half, half), (2 * half, thin), (2 * half + thin, thin), (2 * half, 2 * thin))
    kept = select_out.shape[1]
    y_peer, x_peer, core_peer = (
        where_is(z, 1 - y, x, c),
        where_is(z, y, 1 - x, c),
        where_is(z, y, x, 1 - c),
    )
    near_z, far_z = where_is(along_z(z, 1), y, x, c), where_is(along_z(z, 2), y, x, c)
    loads = [
        pltpu.make_async_copy(source, target, loaded.at[i])
        for i, (source, target) in enumerate(
            ((gate_hbm, gate_ref), (up_hbm, up_ref))
        )
    ]
    for load in loads:
        load.start()
    greet([y_peer, x_peer, core_peer, near_z, far_z])
    mine = number(z, y, x, c)

    def copy(block, part, sem, peer):
        view = held.at[block, pl.ds(*cuts[part])]
        return remote(view, view, sem, arrive.at[block, 2 if part == 4 else part], peer)

    def arrived(block, part):
        copy(block, part, to_core.at[0, 0, 0], core_peer).wait_recv()

    def block_of(q, other_y, other_x, core):
        return number(
            along_z(z, q), 1 - y if other_y else y, 1 - x if other_x else x, core
        )

    combos = ((0, 0), (0, 1), (1, 0), (1, 1))

    def stores(slot, blocks):
        made = []
        for k in range(4):
            part = pl.ds(k * kept, kept)
            made.append((picked.at[slot, part], rows_out.at[blocks[k]]))
            made.append((lively.at[slot, part], active_out.at[blocks[k]]))
            for i, out in enumerate((gate_out, up_out)):
                made.append((results.at[slot, i, part], out.at[blocks[k]]))
        return [
            pltpu.make_async_copy(source, target, stored.at[slot, i])
            for i, (source, target) in enumerate(made)
        ]

    def choose(block):
        notes = notes_ref[block]
        own = jnp.zeros((1, count), jnp.float32)
        lines = lax.broadcasted_iota(jnp.int32, (128, count), 0)
        names = jnp.zeros((128, count), jnp.float32)
        for k in range(topk):
            line = notes[k : k + 1]
            own = own + jnp.where(line == mine, 1.0, 0.0)
            names = names + jnp.where(lines == line, 1.0, 0.0)
        before = lax.broadcasted_iota(jnp.int32, (count, count), 0)
        before = before < lax.broadcasted_iota(jnp.int32, (count, count), 1)
        rank = jnp.dot(
            jnp.broadcast_to(own, (8, count)).astype(x_ref.dtype),
            jnp.where(before, 1.0, 0.0).astype(x_ref.dtype),
            preferred_element_type=jnp.float32,
        )[:1]
        places = lax.broadcasted_iota(jnp.int32, (kept, count), 0).astype(jnp.float32)
        chosen = jnp.where((rank == places) & (own > 0), 1.0, 0.0)
        spread_out[block] = jnp.transpose(chosen).astype(spread_out.dtype)
        chosen = chosen.astype(select_out.dtype)
        select_out[block] = chosen
        return chosen, right_transposed(chosen, names.astype(chosen.dtype))

    def work(q, slot):
        core = 1 - c if slot else c
        blocks = [block_of(q, *combo, core) for combo in combos]

        @pl.when(q > 0)
        def _():
            for store in stores(slot, [block_of(q - 1, *combo, core) for combo in combos]):
                store.wait()

        named = []
        for k in range(4):
            chosen, names = choose(blocks[k])
            named.append(names)
            rows = jnp.dot(chosen, held[blocks[k]], preferred_element_type=jnp.float32)
            picked[slot, k * kept : (k + 1) * kept] = rows.astype(picked.dtype)
        rows = picked[slot]
        gate_pre = jnp.dot(rows, gate_ref[...], preferred_element_type=jnp.float32)
        up_pre = jnp.dot(rows, up_ref[...], preferred_element_type=jnp.float32)
        logits = jnp.dot(rows, router_ref[...], preferred_element_type=jnp.float32)
        results[slot, 0] = gate_pre
        results[slot, 1] = up_pre
        active = gate_pre * (1.0 / (1.0 + jnp.exp(-gate_pre))) * up_pre
        lively[slot] = active.astype(lively.dtype)
        for k in range(4):
            part = slice(k * kept, (k + 1) * kept)
            block = blocks[k]
            masked = jnp.where(named[k] > 0, logits[part], MASKED)
            lifted = jnp.exp(masked - jnp.max(masked, axis=1, keepdims=True))
            lanes = lax.broadcasted_iota(jnp.int32, lifted.shape, 1)
            share = jnp.sum(jnp.where(lanes == mine, lifted, 0.0), axis=1, keepdims=True)
            share = share / jnp.sum(lifted, axis=1, keepdims=True)
            share_out[block] = jnp.broadcast_to(share, share_out.shape[1:])
        for store in stores(slot, blocks):
            store.start()

    def forward(q):
        block = block_of(q, 0, 0, c)
        if q:
            arrived(block, 0)
            arrived(block, 1)
        if q == 2:
            copy(block, 0, to_z.at[2, 0], near_z).start()
            copy(block, 1, to_z.at[2, 1], near_z).start()
        copy(block, 0, to_y.at[0, q], y_peer).start()
        copy(block, 1, to_x.at[0, q], x_peer).start()
        copy(block, 0, to_x.at[1, q], x_peer).start()
        copy(block, 1, to_y.at[1, q], y_peer).start()
        copy(block, 0, to_core.at[0, 0, q], core_peer).start()
        copy(block, 1, to_core.at[0, 1, q], core_peer).start()

    def second(q):
        block = block_of(q, 1, 0, c)
        arrived(block, 0)
        copy(block, 0, to_x.at[2, q], x_peer).start()
        copy(block, 0, to_core.at[1, 0, q], core_peer).start()
        block = block_of(q, 0, 1, c)
        arrived(block, 1)
        copy(block, 1, to_y.at[2, q], y_peer).start()
        copy(block, 1, to_core.at[2, 1, q], core_peer).start()

    def last(q):
        block = block_of(q, 0, 1, c)
        arrived(block, 0)
        copy(block, 0, to_core.at[2, 0, q], core_peer).start()
        block = block_of(q, 1, 0, c)
        arrived(block, 1)
        copy(block, 1, to_core.at[1, 1, q], core_peer).start()
        block = block_of(q, 1, 1, c)
        arrived(block, 0)
        copy(block, 0, to_core.at[3, 0, q], core_peer).start()
        arrived(block, 1)
        copy(block, 1, to_core.at[3, 1, q], core_peer).start()

    def others(q):
        for combo in combos:
            block = block_of(q, *combo, 1 - c)
            for part in (0, 1, 4):
                arrived(block, part)

    beside_x, beside_y, across = (block_of(0, *combo, c) for combo in combos[1:])

    def corner(i):
        block = (mine, mine, mine, mine, beside_x, beside_y)[i]
        part, peer = ((2, x_peer), (3, y_peer), (2, y_peer), (3, x_peer), (2, y_peer), (3, x_peer))[i]
        return copy(block, part, corners.at[i], peer)

    def deep_copy(kind, i, block):
        return copy(block, 4, deep_z.at[kind, i], far_z if kind == 1 else near_z)

    def deep_core_copy(q, i, block):
        return copy(block, 4, deep_core.at[q, i], core_peer)

    def deep_first():
        arrived(beside_x, 3)
        arrived(beside_y, 2)
        arrived(across, 2)
        arrived(across, 3)
        for i, combo in enumerate(combos):
            block = block_of(0, *combo, c)
            deep_copy(0, i, block).start()
            deep_copy(1, i, block).start()
            deep_core_copy(0, i, block).start()

    def deep_next(q):
        for i, combo in enumerate(combos):
            block = block_of(q, *combo, c)
            arrived(block, 4)
            if q == 2:
                deep_copy(2, i, block).start()
            deep_core_copy(q, i, block).start()

    held[mine] = x_ref[...]
    for part in range(2):
        copy(mine, part, to_z.at[0, part], near_z).start()
    for part in range(2):
        copy(mine, part, to_z.at[1, part], far_z).start()
    for i in range(4):
        corner(i).start()
    forward(0)
    for load in loads:
        load.wait()
    arrived(beside_x, 2)
    corner(4).start()
    arrived(beside_y, 3)
    corner(5).start()
    forward(1)
    second(0)
    deep_first()
    forward(2)
    second(1)

    @pl.loop(0, 4)
    def _(q):
        last(q)
        work(q, 0)
        others(q)
        work(q, 1)

        @pl.when(q == 0)
        def _():
            forward(3)
            deep_next(1)
            second(2)
            deep_next(2)

        @pl.when(q == 1)
        def _():
            second(3)
            deep_next(3)

    for slot in range(2):
        core = 1 - c if slot else c
        for store in stores(slot, [block_of(3, *combo, core) for combo in combos]):
            store.wait()
    for part in range(2):
        copy(mine, part, to_z.at[0, part], near_z).wait_send()
        copy(mine, part, to_z.at[1, part], far_z).wait_send()
        copy(mine, part, to_z.at[2, part], near_z).wait_send()

    for i in range(6):
        corner(i).wait_send()
    for i in range(4):
        for kind in range(3):
            deep_copy(kind, i, mine).wait_send()

    @pl.loop(0, 4)
    def _(q):
        for i in range(4):
            deep_core_copy(q, i, mine).wait_send()
        for i in range(3):
            copy(mine, 0, to_y.at[i, q], y_peer).wait_send()
            copy(mine, 0, to_x.at[i, q], x_peer).wait_send()
        for i in range(4):
            for part in range(2):
                copy(mine, part, to_core.at[i, part, q], core_peer).wait_send()


def gather_experts(rows, notes, topk, kept, gate_w, up_w, router):
    count, width = rows.shape
    blocks = notes.shape[0]
    hidden = gate_w.shape[1]
    low = rows.dtype
    anywhere = pl.BlockSpec(memory_space=pl.ANY)
    vmem = pl.BlockSpec(memory_space=pltpu.VMEM)
    return pl.pallas_call(
        functools.partial(gather_kernel, topk),
        out_shape=[
            jax.ShapeDtypeStruct((blocks, kept, width), low),
            jax.ShapeDtypeStruct((blocks, kept, hidden), low),
            jax.ShapeDtypeStruct((blocks, kept, hidden), jnp.float32),
            jax.ShapeDtypeStruct((blocks, kept, hidden), jnp.float32),
            jax.ShapeDtypeStruct((blocks, kept, 128), jnp.float32),
            jax.ShapeDtypeStruct((blocks, kept, count), low),
            jax.ShapeDtypeStruct((blocks, count, kept), low),
        ],
        in_specs=[vmem, vmem, anywhere, anywhere, vmem],
        out_specs=[anywhere] * 4 + [vmem] * 3,
        scratch_shapes=[
            pltpu.VMEM((blocks, count, width), low),
            pltpu.VMEM(gate_w.shape, low),
            pltpu.VMEM(up_w.shape, low),
            pltpu.VMEM((2, 4 * kept, width), low),
            pltpu.VMEM((2, 4 * kept, hidden), low),
            pltpu.VMEM((2, 2, 4 * kept, hidden), jnp.float32),
            copies(2),
            copies(2, 16),
            copies(blocks, 4),
            copies(3, 2),
            copies(3, 4),
            copies(3, 4),
            copies(4, 2, 4),
            copies(6),
            copies(3, 4),
            copies(4, 4),
        ],
        compiler_params=settings(1),
    )(rows, notes, gate_w, up_w, router)


def scatter_kernel(
    extended,
    spread_ref,
    *refs,
):
    if extended:
        gate_grad_ref, up_grad_ref, gate_ref, up_ref, extra_ref, rows_hbm = refs[:6]
        out_ref, extra_out, gate_out, up_out = refs[6:10]
        tiles, staged, loaded, stored = refs[10:14]
        refs = refs[14:]
    else:
        active_ref, down_ref, share_ref, select_ref, grads_hbm, gate_hbm, up_hbm = refs[:7]
        out_ref, rows_out, gate_out, up_out, extra_ref = refs[7:12]
        grads_in, pre_in, rows_staged, staged, loaded, stored = refs[12:18]
        refs = refs[18:]
    outgoing, core_in, total, back, x_in, y_in, z_in, deep_in, deep_x, deep_y = refs[:10]
    core_sent, core_got, x_sent, x_got, y_sent, y_got, z_sent, z_got = refs[10:18]
    deep_sent, deep_got, corner_sent, corner_got = refs[18:]
    z, y, x, c = spot()
    width = out_ref.shape[1]
    count = out_ref.shape[0]
    half, thin = count * 3 // 8, count // 8
    wide = 2 * half
    blocks, _, kept = spread_ref.shape
    y_peer, x_peer, core_peer = (
        where_is(z, 1 - y, x, c),
        where_is(z, y, 1 - x, c),
        where_is(z, y, x, 1 - c),
    )
    near_z, far_z = where_is(along_z(z, 1), y, x, c), where_is(along_z(z, 2), y, x, c)
    greet([y_peer, x_peer, core_peer, near_z, far_z])
    groups = ((1, 1), (0, 1), (1, 0), (0, 0))

    def block_of(group, q, core):
        other_y, other_x = groups[group]
        return number(along_z(z, q), 1 - y if other_y else y, 1 - x if other_x else x, core)

    def rows_of(ref, q, core):
        return jnp.concatenate([ref[block_of(group, q, core)] for group in range(4)], axis=0)

    def rows_back(q, core):
        if extended:
            sums = right_transposed(rows_of(gate_grad_ref, q, core), gate_ref[...])
            sums = sums + right_transposed(rows_of(up_grad_ref, q, core), up_ref[...])
        else:
            sums = jnp.dot(
                rows_of(active_ref, q, core), down_ref[...], preferred_element_type=jnp.float32
            )
            sums = sums.astype(back.dtype).astype(jnp.float32)
            sums = sums * rows_of(share_ref, q, core)[:, :1]
        back[...] = sums.astype(back.dtype)

    def turn_blocks(turn):
        core = (c + turn) % 2
        return [block_of(group, turn // 2, core) for group in range(4)]

    def loads(turn):
        slot, made = turn % 2, []
        if extended:
            columns = pl.ds(pl.multiple_of(turn * tiles.shape[3], tiles.shape[3]), tiles.shape[3])
            made.append((rows_hbm.at[:, :, columns], tiles.at[slot]))
        else:
            for group, block in enumerate(turn_blocks(turn)):
                rows = pl.ds(group * kept, kept)
                made.append((grads_hbm.at[block], grads_in.at[slot, group]))
                made.append((gate_hbm.at[block], pre_in.at[slot, 0, rows]))
                made.append((up_hbm.at[block], pre_in.at[slot, 1, rows]))
        return [
            pltpu.make_async_copy(source, target, loaded.at[slot, i])
            for i, (source, target) in enumerate(made)
        ]

    def stores(turn):
        slot, made = turn % 2, []
        if extended:
            columns = tiles.shape[3]
            rows = pl.ds(pl.multiple_of(turn * columns, columns), columns)
            made.append((staged.at[slot, 0], gate_out.at[rows]))
            made.append((staged.at[slot, 1], up_out.at[rows]))
        else:
            for group, block in enumerate(turn_blocks(turn)):
                rows = pl.ds(group * kept, kept)
                made.append((rows_staged.at[slot, rows], rows_out.at[block]))
                made.append((staged.at[slot, 0, rows], gate_out.at[block]))
                made.append((staged.at[slot, 1, rows], up_out.at[block]))
        return [
            pltpu.make_async_copy(source, target, stored.at[slot, i])
            for i, (source, target) in enumerate(made)
        ]

    def begin_loads(turn):
        for load in loads(turn):
            load.start()

    def fill(turn):
        for load in loads(turn):
            load.wait()

        @pl.when(turn >= 2)
        def _():
            for store in stores(turn - 2):
                store.wait()

        if extended:
            weigh(turn)
        else:
            prepare(turn)
        for store in stores(turn):
            store.start()

        @pl.when(turn < 6)
        def _():
            begin_loads(turn + 2)

    def weigh(turn):
        slot = turn % 2
        staged[slot] = jnp.zeros_like(staged[slot])

        @pl.loop(0, blocks // 4)
        def _(i):
            span = pl.ds(i * 4, 4)
            rows = tiles[slot, span].reshape(4 * kept, tiles.shape[3])
            for which, grads in enumerate((gate_grad_ref, up_grad_ref)):
                staged[slot, which] += left_trans(
                    rows, grads[span].reshape(4 * kept, grads.shape[2])
                )

    def prepare(turn):
        blocks, slot = turn_blocks(turn), turn % 2
        mine = number(z, y, x, c)
        parts = [
            jnp.dot(
                select_ref[blocks[group]],
                grads_in[slot, group],
                preferred_element_type=jnp.float32,
            )
            for group in range(4)
        ]
        share = jnp.concatenate([share_ref[block] for block in blocks], axis=0)[:, :1]
        picked = jnp.concatenate(parts, axis=0)
        rows_staged[slot] = (share * picked).astype(rows_staged.dtype)
        ahead = right_transposed(picked.astype(rows_staged.dtype), down_ref[...])
        gate, up = pre_in[slot, 0], pre_in[slot, 1]
        active = jnp.concatenate([active_ref[block] for block in blocks], axis=0)
        grad = jnp.sum(active.astype(jnp.float32) * ahead, axis=1, keepdims=True)
        active_grad = share * ahead
        sigma = 1.0 / (1.0 + jnp.exp(-gate))
        gate_grad = active_grad * up * (sigma * (1.0 + gate * (1.0 - sigma)))
        staged[slot, 0] = gate_grad.astype(staged.dtype)
        staged[slot, 1] = (active_grad * (gate * sigma)).astype(staged.dtype)
        lanes = lax.broadcasted_iota(jnp.int32, (4 * kept, 128), 1)
        high = grad.astype(extra_ref.dtype).astype(jnp.float32)
        both = jnp.where(lanes == mine, high, jnp.where(lanes == 32 + mine, grad - high, 0.0))
        both = both.astype(extra_ref.dtype)
        for group, block in enumerate(blocks):
            extra_ref[block] = both[group * kept : (group + 1) * kept]

    def part(block, group):
        rows = jnp.dot(
            spread_ref[block],
            back[group * kept : (group + 1) * kept],
            preferred_element_type=jnp.float32,
        )
        if not extended:
            return rows
        more = jnp.dot(spread_ref[block], extra_ref[block], preferred_element_type=jnp.float32)
        return jnp.concatenate([rows, more], axis=1)

    def across(group, q):
        return remote(
            outgoing.at[q, group],
            core_in.at[q, group],
            core_sent.at[q, group],
            core_got.at[q, group],
            core_peer,
        )

    def view(group, q, side):
        return total.at[q, group, pl.ds(side * half, half)]

    def x_copy(group, q, side, slot):
        return remote(
            view(group, q, side), x_in.at[slot, q], x_sent.at[slot, q], x_got.at[slot, q], x_peer
        )

    def y_copy(group, q, side, slot):
        return remote(
            view(group, q, side), y_in.at[slot, q], y_sent.at[slot, q], y_got.at[slot, q], y_peer
        )

    def z_copy(q):
        return remote(
            total.at[q, 3, pl.ds(0, wide)],
            z_in.at[q - 1],
            z_sent.at[q - 1],
            z_got.at[q - 1],
            where_is(along_z(z, 2 - q % 2), y, x, c),
        )

    def deep_copy(q):
        return remote(
            total.at[q, :, pl.ds(wide, 2 * thin)],
            deep_in.at[q - 1],
            deep_sent.at[q - 1],
            deep_got.at[q - 1],
            far_z if q == 2 else near_z,
        )

    def corner_copy(over_x, group, side, slot):
        place, peer = (deep_x, x_peer) if over_x else (deep_y, y_peer)
        return remote(
            total.at[0, group, pl.ds(wide + side * thin, thin)],
            place.at[slot],
            corner_sent.at[over_x, slot],
            corner_got.at[over_x, slot],
            peer,
        )

    y_corners = [corner_copy(0, 0, 0, 0), corner_copy(0, 2, 0, 1), corner_copy(0, 2, 1, 2)]
    x_corners = [corner_copy(1, 0, 1, 0), corner_copy(1, 1, 1, 1), corner_copy(1, 1, 0, 2)]

    def add_deep(q, *arrivals):
        rows = pl.ds(wide, 2 * thin)
        sums = total[q, :, rows].astype(jnp.float32)
        for arrival in arrivals:
            deep_copy(arrival).wait_recv()
            sums = sums + deep_in[arrival - 1].astype(jnp.float32)
        total[q, :, rows] = sums.astype(total.dtype)

    def add_corner(group, side, source):
        rows = pl.ds(wide + side * thin, thin)
        total[0, group, rows] = (
            total[0, group, rows].astype(jnp.float32) + source.astype(jnp.float32)
        ).astype(total.dtype)

    def deep_step(i):
        @pl.when(i == 0)
        def _():
            deep_copy(3).start()

        @pl.when(i == 1)
        def _():
            add_deep(2, 3)
            deep_copy(2).start()

        @pl.when(i == 2)
        def _():
            deep_copy(1).start()

        @pl.when(i == 3)
        def _():
            add_deep(0, 1, 2)
            for corner in (*y_corners[:2], *x_corners[:2]):
                corner.start()

        @pl.when(i == 4)
        def _():
            y_corners[0].wait_recv()
            add_corner(1, 0, deep_y[0])
            x_corners[2].start()
            x_corners[0].wait_recv()
            add_corner(2, 1, deep_x[0])
            y_corners[2].start()

    def add(group, q, side, source):
        rows = pl.ds(side * half, half)
        total[q, group, rows] = (
            total[q, group, rows].astype(jnp.float32) + source.astype(jnp.float32)
        ).astype(total.dtype)

    def begin(q):
        rows_back(q, 1 - c)
        for group in range(4):
            outgoing[q, group] = part(block_of(group, q, 1 - c), group).astype(total.dtype)
            across(group, q).start()
        rows_back(q, c)
        for group in range(4):
            sums = part(block_of(group, q, c), group)
            across(group, q).wait_recv()
            total[q, group] = (sums + core_in[q, group].astype(jnp.float32)).astype(total.dtype)
            if group == 0:
                x_copy(0, q, 0, 0).start()
                y_copy(0, q, 1, 0).start()
            if group == 1:
                x_copy(1, q, 0, 1).start()
            if group == 2:
                y_copy(2, q, 1, 1).start()

    def middle(q):
        x_copy(0, q, 0, 0).wait_recv()
        add(2, q, 0, x_in[0, q])
        y_copy(2, q, 0, 2).start()
        y_copy(0, q, 1, 0).wait_recv()
        add(1, q, 1, y_in[0, q])
        x_copy(1, q, 1, 2).start()

    def close(q):
        arrivals = (
            ((x_copy(1, q, 0, 1), x_in, 1), (y_copy(2, q, 0, 2), y_in, 2)),
            ((y_copy(2, q, 1, 1), y_in, 1), (x_copy(1, q, 1, 2), x_in, 2)),
        )
        for side in range(2):
            for arrival, _, _ in arrivals[side]:
                arrival.wait_recv()
            rows = pl.ds(side * half, half)
            sums = total[q, 3, rows].astype(jnp.float32)
            for _, source, slot in arrivals[side]:
                sums = sums + source[slot, q].astype(jnp.float32)
            total[q, 3, rows] = sums.astype(total.dtype)

        @pl.when(q == 2)
        def _():
            z_copy(3).wait_recv()
            rows = pl.ds(0, wide)
            total[2, 3, rows] = (
                total[2, 3, rows].astype(jnp.float32) + z_in[2].astype(jnp.float32)
            ).astype(total.dtype)

        @pl.when(q > 0)
        def _():
            z_copy(q).start()

    def done(i):
        return jnp.maximum(i, 0) + jnp.maximum(i - 2, 0)

    begin_loads(0)
    begin_loads(1)

    @pl.loop(0, 6)
    def _(i):
        @pl.when(i < 4)
        def _():
            begin(3 - i)

        @pl.loop(done(i - 1), done(i))
        def _(turn):
            fill(turn)

        deep_step(i)

        @pl.when((i > 0) & (i < 5))
        def _():
            middle(4 - i)

        @pl.when(i > 1)
        def _():
            close(5 - i)

    for turn in (6, 7):
        for store in stores(turn):
            store.wait()
    for q in (1, 2):
        z_copy(q).wait_recv()

    def finish(start, size, *more):
        rows = pl.ds(start, size)
        sums = total[0, 3, rows].astype(jnp.float32)
        for source in more:
            sums = sums + source.astype(jnp.float32)
        out_ref[rows] = sums[:, :width]
        if extended:
            extra_out[rows] = sums[:, width:]

    finish(0, wide, z_in[0], z_in[1])
    for slot in (1, 2):
        y_corners[slot].wait_recv()
        x_corners[slot].wait_recv()
    finish(wide, thin, deep_y[1], deep_x[2])
    finish(wide + thin, thin, deep_x[1], deep_y[2])
    for corner in (*y_corners, *x_corners):
        corner.wait_send()
    for q in range(1, 4):
        z_copy(q).wait_send()
        deep_copy(q).wait_send()

    @pl.loop(0, 4)
    def _(q):
        for group in range(4):
            across(group, q).wait_send()
        x_copy(0, q, 0, 0).wait_send()
        x_copy(1, q, 0, 1).wait_send()
        x_copy(1, q, 1, 2).wait_send()
        y_copy(0, q, 1, 0).wait_send()
        y_copy(2, q, 1, 1).wait_send()
        y_copy(2, q, 0, 2).wait_send()


def scatter_rows(spread, *operands):
    blocks, count, kept = spread.shape
    extended = len(operands) == 6
    width = operands[2].shape[0] if extended else operands[1].shape[1]
    wide = width + 128 if extended else width
    low = operands[0].dtype
    anywhere = pl.BlockSpec(memory_space=pl.ANY)
    outs = [jax.ShapeDtypeStruct((count, width), jnp.float32)]
    if extended:
        outs.append(jax.ShapeDtypeStruct((count, 128), jnp.float32))
        hidden = operands[0].shape[2]
        outs += [jax.ShapeDtypeStruct((width, hidden), jnp.float32)] * 2
        in_specs = in_vmem(6) + [anywhere]
        out_specs = in_vmem(2) + [anywhere] * 2
        filler = [
            pltpu.VMEM((2, blocks, kept, width // 8), low),
            pltpu.VMEM((2, 2, width // 8, hidden), jnp.float32),
            copies(2, 1),
            copies(2, 2),
        ]
    else:
        hidden = operands[0].shape[2]
        outs += [
            jax.ShapeDtypeStruct((blocks, kept, width), low),
            jax.ShapeDtypeStruct((blocks, kept, hidden), low),
            jax.ShapeDtypeStruct((blocks, kept, hidden), low),
            jax.ShapeDtypeStruct((blocks, kept, 128), low),
        ]
        in_specs = in_vmem(5) + [anywhere] * 3
        out_specs = in_vmem(1) + [anywhere] * 3 + in_vmem(1)
        filler = [
            pltpu.VMEM((2, 4, count, width), low),
            pltpu.VMEM((2, 2, 4 * kept, hidden), jnp.float32),
            pltpu.VMEM((2, 4 * kept, width), low),
            pltpu.VMEM((2, 2, 4 * kept, hidden), low),
            copies(2, 12),
            copies(2, 12),
        ]
    return pl.pallas_call(
        functools.partial(scatter_kernel, extended),
        out_shape=outs,
        in_specs=in_specs,
        out_specs=out_specs,
        scratch_shapes=filler
        + [
            pltpu.VMEM((4, 4, count, wide), low),
            pltpu.VMEM((4, 4, count, wide), low),
            pltpu.VMEM((4, 4, count, wide), low),
            pltpu.VMEM((4 * kept, width), low),
            pltpu.VMEM((3, 4, count * 3 // 8, wide), low),
            pltpu.VMEM((3, 4, count * 3 // 8, wide), low),
            pltpu.VMEM((3, count * 3 // 4, wide), low),
            pltpu.VMEM((3, 4, count // 4, wide), low),
            pltpu.VMEM((3, count // 8, wide), low),
            pltpu.VMEM((3, count // 8, wide), low),
            copies(4, 4),
            copies(4, 4),
            copies(3, 4),
            copies(3, 4),
            copies(3, 4),
            copies(3, 4),
            copies(3),
            copies(3),
            copies(3),
            copies(3),
            copies(2, 3),
            copies(2, 3),
        ],
        compiler_params=settings(2 if extended else 8),
    )(spread, *operands)


def reduce_kernel(
    cuts,
    parts_ref,
    own_ref,
    vector_ref,
    query_out,
    key_out,
    value_out,
    every_out,
    vector_out,
    sums_out,
    own_sent,
    own_got,
    own_side_sent,
    own_side_got,
    stored,
    *refs,
):
    z, y, x, c = spot()
    member, shard = lax.axis_index("exp"), lax.axis_index("fsdp")
    y_peer = where_is(z, 1 - y, x, c)
    near_z, far_z = where_is(along_z(z, 1), y, x, c), where_is(along_z(z, 2), y, x, c)
    members = [((member + j) % 8, shard) for j in range(8)]
    shards = [(member, (shard + j) % 4) for j in range(4)]
    greet(members[1:] + shards[1:])
    pieces = len(cuts)
    first_got, first_held, first_z = refs[:3]
    y_got_in, y_held, y_z = refs[3:5], refs[5:7], refs[7:9]
    shard_in, member_own, member_in = refs[3 * pieces : 3 * pieces + 3]
    (
        y_sent,
        y_got,
        z_sent,
        z_got,
        back_sent,
        back_got,
        side_sent,
        side_got,
        shard_sent,
        shard_got,
        member_sent,
        member_got,
    ) = refs[3 * pieces + 3 :]

    def shard_copy(j):
        return remote(
            vector_ref.at[(shard + j) % 4],
            shard_in.at[(4 - j) % 4],
            shard_sent.at[j],
            shard_got.at[(4 - j) % 4],
            shards[j],
        )

    def member_copy(j):
        return remote(
            member_own,
            member_in.at[(8 - j) % 8],
            member_sent.at[j],
            member_got.at[(8 - j) % 8],
            members[j],
        )

    def rows(which):
        return pl.ds(*cuts[which])

    def z_peer(q):
        return far_z if q == 2 else near_z

    def y_copy(which, q):
        return remote(
            parts_ref.at[1 - y, along_z(z, q), rows(which)],
            y_got_in[which - 1].at[q],
            y_sent.at[which, q],
            y_got.at[which, q],
            y_peer,
        )

    def z_copy(which, q):
        if which:
            source, target = y_held[which - 1].at[q], y_z[which - 1].at[q]
        elif q == 2:
            source, target = first_held, first_z.at[2]
        else:
            source, target = parts_ref.at[:, along_z(z, q), rows(0)], first_z.at[q]
        return remote(source, target, z_sent.at[which, q], z_got.at[which, q], z_peer(q))

    def first_y():
        return remote(
            first_z.at[0, 1 - y], first_got, y_sent.at[0, 0], y_got.at[0, 0], y_peer
        )

    def place(side, q, which):
        return sums_out.at[side, along_z(z, q), rows(which)]

    def back_copy(which, q):
        held = along_z(z, 2) if q == 3 else z
        if which:
            view = sums_out.at[y, held, rows(which)]
        else:
            view = sums_out.at[:, held, rows(0)]
        return remote(view, view, back_sent.at[which, q], back_got.at[which, q], z_peer(q))

    def side_copy(which, q):
        view = place(y, q, which)
        return remote(view, view, side_sent.at[which, q], side_got.at[which, q], y_peer)

    def own_copy(q):
        view = every_out.at[along_z(z, 2) if q == 3 else z, y]
        return remote(view, view, own_sent.at[q], own_got.at[q], z_peer(q))

    def own_side(q):
        view = every_out.at[along_z(z, q), y]
        return remote(view, view, own_side_sent.at[q], own_side_got.at[q], y_peer)

    def pass_on(q):
        own_copy(q).wait_recv()
        if q == 2:
            own_copy(3).start()
        own_side(q).start()

    def exports(side, q):
        zone = along_z(z, q)
        head, rows = side * 2 + zone // 2, zone % 2
        made, start = [], 0
        for i, out in enumerate((query_out, key_out, value_out)):
            size, depth = out.shape[1] // 4, parts_ref.shape[2]
            source = sums_out.at[side, zone, :, pl.ds(start, size)]
            target = out.at[
                pl.ds(pl.multiple_of(rows * depth, depth), depth),
                pl.ds(pl.multiple_of(head * size, size), size),
            ]
            made.append(pltpu.make_async_copy(source, target, stored.at[side, q, i]))
            start += size
        return made

    later = range(1, pieces)
    every_out[z, y] = own_ref[...]
    for j in range(1, 4):
        shard_copy(j).start()
    z_copy(0, 3).start()
    own_copy(1).start()
    own_copy(2).start()
    for q in (3, 2, 1, 0):
        for which in later:
            y_copy(which, q).start()
    z_copy(0, 1).start()
    own_side(0).start()

    for j in range(1, 4):
        shard_copy(j).wait_recv()
    sums = vector_ref[shard]
    for j in range(1, 4):
        sums = sums + shard_in[j]
    member_own[...] = sums
    for j in range(1, 8):
        member_copy(j).start()

    def add_y(which, q):
        y_copy(which, q).wait_recv()
        sums = parts_ref[y, along_z(z, q), rows(which)].astype(jnp.float32)
        sums = sums + y_got_in[which - 1][q].astype(jnp.float32)
        held, z_in = y_held[which - 1], y_z[which - 1]
        if q == 2:
            z_copy(which, 3).wait_recv()
            sums = sums + z_in[3].astype(jnp.float32)
        if q:
            held[q] = sums.astype(held.dtype)
            z_copy(which, q).start()
            return
        for turn in (1, 2):
            z_copy(which, turn).wait_recv()
            sums = sums + z_in[turn].astype(jnp.float32)
        sums_out[y, z, rows(which)] = sums.astype(sums_out.dtype)
        side_copy(which, 0).start()
        back_copy(which, 2).start()
        back_copy(which, 1).start()

    for which in later:
        add_y(which, 3)
    z_copy(0, 3).wait_recv()
    first_held[...] = (
        parts_ref[:, along_z(z, 2), rows(0)].astype(jnp.float32) + first_z[3].astype(jnp.float32)
    ).astype(first_held.dtype)
    z_copy(0, 2).start()
    pass_on(1)
    for which in later:
        add_y(which, 2)
    pass_on(2)
    z_copy(0, 1).wait_recv()
    z_copy(0, 2).wait_recv()
    first_z[0] = (
        parts_ref[:, z, rows(0)].astype(jnp.float32)
        + first_z[1].astype(jnp.float32)
        + first_z[2].astype(jnp.float32)
    ).astype(first_z.dtype)
    first_y().start()
    for which in later:
        add_y(which, 1)
    pass_on(3)
    first_y().wait_recv()
    sums = first_z[0, y].astype(jnp.float32) + first_got[...].astype(jnp.float32)
    sums_out[y, z, rows(0)] = sums.astype(sums_out.dtype)
    side_copy(0, 0).start()
    for which in later:
        add_y(which, 0)
    side_copy(0, 0).wait_recv()
    back_copy(0, 2).start()
    back_copy(0, 1).start()

    for j in range(1, 8):
        member_copy(j).wait_recv()
    sums = member_own[...]
    for j in range(1, 8):
        sums = sums + member_in[j]
    vector_out[...] = sums

    for q in (1, 2, 3):
        for which in later:
            back_copy(which, q).wait_recv()
            if q == 2:
                back_copy(which, 3).start()
            side_copy(which, q).start()
        back_copy(0, q).wait_recv()
        if q == 2:
            back_copy(0, 3).start()

    for q in range(4):
        for export in exports(y, q):
            export.start()
    for q in range(4):
        for which in later:
            side_copy(which, q).wait_recv()
        for export in exports(1 - y, q):
            export.start()
    for q in range(4):
        own_side(q).wait_recv()
    for q in range(4):
        for side in (y, 1 - y):
            for export in exports(side, q):
                export.wait()
    for q in range(4):
        own_side(q).wait_send()
        if q:
            own_copy(q).wait_send()
    for which in range(pieces):
        for q in range(4):
            if which:
                y_copy(which, q).wait_send()
                side_copy(which, q).wait_send()
            if q:
                z_copy(which, q).wait_send()
                back_copy(which, q).wait_send()
    side_copy(0, 0).wait_send()
    first_y().wait_send()
    for j in range(1, 4):
        shard_copy(j).wait_send()
    for j in range(1, 8):
        member_copy(j).wait_send()


def reduce_over_members(parts, own, vectors, widths):
    low = parts.dtype
    depth, width = parts.shape[2:]
    early = depth // 4 // 16 * 16
    half = (depth - early) // 2 // 16 * 16
    cuts = ((0, early), (early, half), (early + half, depth - early - half))
    anywhere = pl.BlockSpec(memory_space=pl.ANY)

    def quarters(*lead):
        return [pltpu.VMEM((*lead, size, width), low) for _, size in cuts[1:]]

    return pl.pallas_call(
        functools.partial(reduce_kernel, cuts),
        out_shape=[jax.ShapeDtypeStruct((2 * depth, size), low) for size in widths]
        + [
            jax.ShapeDtypeStruct((4, 2, *own.shape), low),
            jax.ShapeDtypeStruct(vectors.shape[1:], vectors.dtype),
        ],
        in_specs=in_vmem(3),
        out_specs=[anywhere] * 3 + in_vmem(2),
        scratch_shapes=[
            pltpu.VMEM(parts.shape, low),
            copies(4),
            copies(4),
            copies(4),
            copies(4),
            copies(2, 4, 3),
            pltpu.VMEM((early, width), low),
            pltpu.VMEM((2, early, width), low),
            pltpu.VMEM((4, 2, early, width), low),
            *quarters(4),
            *quarters(4),
            *quarters(4),
            pltpu.VMEM(vectors.shape, vectors.dtype),
            pltpu.VMEM(vectors.shape[1:], vectors.dtype),
            pltpu.VMEM((8, *vectors.shape[1:]), vectors.dtype),
        ]
        + [copies(3, 4)] * 8
        + [copies(4)] * 2
        + [copies(8)] * 2,
        compiler_params=settings(3),
    )(parts, own, vectors)


def project_kernel(
    x_ref,
    routes_ref,
    gain_ref,
    query_ref,
    key_ref,
    value_ref,
    raw_out,
    hidden_out,
    routes_out,
    scale,
    x_in,
    scale_in,
    outgoing,
    core_in,
    across_x,
    x_sums,
    slice_sent,
    slice_got,
    scale_sent,
    scale_got,
    core_sent,
    core_got,
    x_sent,
    x_got,
    route_sent,
    route_got,
):
    z, y, x, c = spot()
    member, shard = lax.axis_index("exp"), lax.axis_index("fsdp")
    mine = number(z, y, x, c)
    count, depth = hidden_out.shape[1:]
    wide, narrow = query_ref.shape[1] // 4, key_ref.shape[1] // 4

    def everyone(j):
        other = (mine + j) % 32
        return (other // 4, other % 4)

    barrier = pltpu.get_barrier_semaphore()

    @pl.loop(1, 32)
    def _(j):
        pl.semaphore_signal(barrier, inc=1, device_id=everyone(j), device_id_type=MESH)

    pl.semaphore_wait(barrier, 31)

    def slice_copy(j):
        place = (shard + j) % 4
        return remote(
            x_ref.at[:, pl.ds(pl.multiple_of(place * depth, depth), depth)],
            x_in.at[(4 - j) % 4],
            slice_sent.at[j],
            slice_got.at[(4 - j) % 4],
            (member, place),
        )

    def scale_copy(j):
        return remote(
            scale,
            scale_in.at[(4 - j) % 4],
            scale_sent.at[j],
            scale_got.at[(4 - j) % 4],
            (member, (shard + j) % 4),
        )

    def route_copy(j):
        return remote(
            routes_ref, routes_out.at[mine], route_sent.at[j], route_got.at[(32 - j) % 32], everyone(j)
        )

    for j in range(1, 4):
        slice_copy(j).start()
    values = x_ref[...].astype(jnp.float32)
    scale[...] = jnp.broadcast_to(
        lax.rsqrt(jnp.mean(values * values, axis=1, keepdims=True) + EPSILON), scale.shape
    )
    for j in range(1, 4):
        scale_copy(j).start()
    routes_out[mine] = routes_ref[...]

    @pl.loop(1, 32)
    def _(j):
        route_copy(j).start()

    def hide(owner, piece, factor):
        gain = gain_ref[...].astype(jnp.float32)
        hidden = piece.astype(jnp.float32) * factor[:, :1] * gain
        hidden_out[owner] = hidden.astype(hidden_out.dtype)

    hide(shard, x_ref[:, pl.ds(pl.multiple_of(shard * depth, depth), depth)], scale[...])

    def take(owner):
        slot = (owner - shard + 4) % 4
        remote(x_in.at[slot], x_in.at[slot], slice_sent.at[slot], slice_got.at[slot], (member, owner)).wait_recv()
        remote(scale, scale_in.at[slot], scale_sent.at[slot], scale_got.at[slot], (member, owner)).wait_recv()
        hide(owner, x_in[slot], scale_in[slot])

    def partial(side, target):
        rows = jnp.concatenate([hidden_out[side * 2], hidden_out[side * 2 + 1]], axis=0)
        parts = []
        for weight, size in ((query_ref, wide), (key_ref, narrow), (value_ref, narrow)):
            columns = pl.ds(pl.multiple_of(target * size, size), size)
            parts.append(jnp.dot(rows, weight[:, columns], preferred_element_type=jnp.float32))
        return jnp.concatenate(parts, axis=1)

    core_peer, x_peer = where_is(z, y, x, 1 - c), where_is(z, y, 1 - x, c)

    def core_copy(turn, far):
        return remote(
            outgoing.at[turn, far],
            core_in.at[turn, far],
            core_sent.at[turn, far],
            core_got.at[turn, far],
            core_peer,
        )

    def x_copy(turn):
        return remote(across_x.at[turn], x_sums.at[turn], x_sent.at[turn], x_got.at[turn], x_peer)

    low = outgoing.dtype
    for turn in range(2):
        side = x if turn == 0 else 1 - x
        if turn == 0:
            take(side * 2 + 1 - c)
        else:
            take(side * 2 + c)
            take(side * 2 + 1 - c)
        outgoing[turn, 1] = partial(side, (1 - x) * 2 + 1 - c).astype(low)
        core_copy(turn, 1).start()
        sums = partial(side, (1 - x) * 2 + c)
        core_copy(turn, 1).wait_recv()
        across_x[turn] = (sums + core_in[turn, 1].astype(jnp.float32)).astype(low)
        x_copy(turn).start()
        outgoing[turn, 0] = partial(side, x * 2 + 1 - c).astype(low)
        core_copy(turn, 0).start()

    for turn in range(2):
        side = x if turn == 0 else 1 - x
        sums = partial(side, x * 2 + c)
        core_copy(turn, 0).wait_recv()
        sums = sums + core_in[turn, 0].astype(jnp.float32)
        raw_out[side * 2] = sums[:count]
        raw_out[side * 2 + 1] = sums[count:]

    for turn in range(2):
        side = 1 - x if turn == 0 else x
        x_copy(turn).wait_recv()
        raw_out[side * 2] += x_sums[turn, :count].astype(jnp.float32)
        raw_out[side * 2 + 1] += x_sums[turn, count:].astype(jnp.float32)

    @pl.loop(1, 32)
    def _(j):
        remote(
            routes_ref, routes_out.at[(mine + j) % 32], route_sent.at[j], route_got.at[j], everyone(j)
        ).wait_recv()

    @pl.loop(1, 32)
    def _(j):
        route_copy(j).wait_send()

    for j in range(1, 4):
        slice_copy(j).wait_send()
        scale_copy(j).wait_send()
    for turn in range(2):
        x_copy(turn).wait_send()
        for far in range(2):
            core_copy(turn, far).wait_send()


def project_tokens(tokens, routes, gain, w_query, key_weight, value_weight):
    count = tokens.shape[0]
    depth = w_query.shape[0]
    own = (w_query.shape[1] + key_weight.shape[1] + value_weight.shape[1]) // 4
    low = tokens.dtype
    return pl.pallas_call(
        project_kernel,
        out_shape=[
            jax.ShapeDtypeStruct((4, count, own), jnp.float32),
            jax.ShapeDtypeStruct((4, count, depth), low),
            jax.ShapeDtypeStruct((32, *routes.shape), routes.dtype),
        ],
        in_specs=in_vmem(6),
        out_specs=in_vmem(3),
        scratch_shapes=[
            pltpu.VMEM((count, 128), jnp.float32),
            pltpu.VMEM((4, count, depth), low),
            pltpu.VMEM((4, count, 128), jnp.float32),
            pltpu.VMEM((2, 2, 2 * count, own), low),
            pltpu.VMEM((2, 2, 2 * count, own), low),
            pltpu.VMEM((2, 2 * count, own), low),
            pltpu.VMEM((2, 2 * count, own), low),
            copies(4),
            copies(4),
            copies(4),
            copies(4),
            copies(2, 2),
            copies(2, 2),
            copies(2),
            copies(2),
            copies(32),
            copies(32),
        ],
        compiler_params=settings(4),
    )(tokens, routes, gain, w_query, key_weight, value_weight)


def turned(values):
    return pltpu.roll(values, HEAD_WIDTH // 2, 1)


def signed(sine):
    lanes = lax.broadcasted_iota(jnp.int32, sine.shape, 1)
    return jnp.where(lanes < HEAD_WIDTH // 2, -sine, sine)


def finish_kernel(
    row,
    sequences,
    raw_ref,
    notes_ref,
    query_gain_ref,
    key_gain_ref,
    weight_ref,
    x_ref,
    gain_ref,
    middle_out,
    normed_out,
    attended_out,
    probs_out,
    query_out,
    key_out,
    cosine_out,
    sine_out,
    outgoing,
    core_in,
    across_x,
    x_sums,
    core_sent,
    core_got,
    x_sent,
    x_got,
):
    z, y, x, c = spot()
    count = x_ref.shape[0]
    core_peer, x_peer = where_is(z, y, x, 1 - c), where_is(z, y, 1 - x, c)
    greet([core_peer, x_peer])
    heads = query_out.shape[2] // HEAD_WIDTH
    wide = heads * HEAD_WIDTH

    def place(block):
        down = lax.broadcasted_iota(jnp.int32, (count, count), 0)
        along = lax.broadcasted_iota(jnp.int32, (count, count), 1)
        end = jnp.zeros((1, 1), jnp.int32)
        start = jnp.zeros((count, count), jnp.int32)
        own, other = start, start
        for i in range(sequences - 1):
            length = notes_ref[block, row : row + 1, i : i + 1]
            end = end + length
            own = own + jnp.where(down >= end, 1, 0)
            other = other + jnp.where(along >= end, 1, 0)
            start = start + jnp.where(down >= end, length, 0)
        return down - start, (own == other) & (along <= down)

    def attend(block):
        position, allowed = place(block)
        lanes = lax.broadcasted_iota(jnp.int32, position.shape, 1)
        spin = lanes % (HEAD_WIDTH // 2)
        inverse = jnp.exp(spin.astype(jnp.float32) * (-2.0 * math.log(THETA) / HEAD_WIDTH))
        angles = position.astype(jnp.float32) * inverse
        cosine, sine = jnp.cos(angles), jnp.sin(angles)
        cosine_out[block] = cosine
        sine_out[block] = sine
        flipped = signed(sine)

        def normal(values, gain):
            scale = lax.rsqrt(jnp.mean(values * values, axis=1, keepdims=True) + EPSILON)
            values = values * scale * gain
            return (values * cosine + turned(values) * flipped).astype(query_out.dtype)

        key = normal(raw_ref[block, :, wide : wide + HEAD_WIDTH], key_gain_ref[...])
        key_out[block] = key
        value = raw_ref[block, :, wide + HEAD_WIDTH :].astype(query_out.dtype)
        for head in range(heads):
            columns = slice(head * HEAD_WIDTH, (head + 1) * HEAD_WIDTH)
            query = normal(raw_ref[block, :, columns], query_gain_ref[...])
            query_out[block, :, columns] = query
            scores = right_transposed(query, key) * HEAD_WIDTH ** (-0.5)
            scores = jnp.where(allowed, scores, MASKED)
            raised = jnp.exp(scores - jnp.max(scores, axis=1, keepdims=True))
            probs = raised / jnp.sum(raised, axis=1, keepdims=True)
            probs_out[block, head] = probs
            attended_out[block, :, columns] = jnp.dot(
                probs.astype(value.dtype), value, preferred_element_type=jnp.float32
            ).astype(attended_out.dtype)

    def core_copy(far):
        return remote(
            outgoing.at[far], core_in.at[far], core_sent.at[far], core_got.at[far], core_peer
        )

    def x_copy():
        return remote(across_x, x_sums, x_sent, x_got, x_peer)

    @pl.loop(0, 4)
    def _(i):
        block = (1 - x + i // 2) % 2 * 2 + (1 - c + i) % 2
        far = 1 - i // 2
        attend(block)
        product = jnp.dot(attended_out[block], weight_ref[...], preferred_element_type=jnp.float32)

        @pl.when(i % 2 == 0)
        def _():
            outgoing[far] = product.astype(outgoing.dtype)
            core_copy(far).start()

        @pl.when(i == 1)
        def _():
            core_copy(1).wait_recv()
            across_x[...] = (product + core_in[1].astype(jnp.float32)).astype(across_x.dtype)
            x_copy().start()

        @pl.when(i == 3)
        def _():
            core_copy(0).wait_recv()
            sums = product + x_ref[...].astype(jnp.float32)
            middle_out[...] = sums + core_in[0].astype(jnp.float32)

    x_copy().wait_recv()
    middle = middle_out[...] + x_sums[...].astype(jnp.float32)
    middle_out[...] = middle
    scale = lax.rsqrt(jnp.mean(middle * middle, axis=1, keepdims=True) + EPSILON)
    normed_out[...] = (middle * scale * gain_ref[...]).astype(normed_out.dtype)
    x_copy().wait_send()
    core_copy(0).wait_send()
    core_copy(1).wait_send()


def finish_attention(raw, notes, row, sequences, q_gain, k_gain, w_out, tokens, gain):
    count, width = tokens.shape
    low = tokens.dtype
    wide = w_out.shape[0]
    heads = wide // HEAD_WIDTH
    return pl.pallas_call(
        functools.partial(finish_kernel, row, sequences),
        out_shape=[
            jax.ShapeDtypeStruct((count, width), jnp.float32),
            jax.ShapeDtypeStruct((count, width), low),
            jax.ShapeDtypeStruct((4, count, wide), low),
            jax.ShapeDtypeStruct((4, heads, count, count), jnp.float32),
            jax.ShapeDtypeStruct((4, count, wide), low),
            jax.ShapeDtypeStruct((4, count, HEAD_WIDTH), low),
            jax.ShapeDtypeStruct((4, count, HEAD_WIDTH), jnp.float32),
            jax.ShapeDtypeStruct((4, count, HEAD_WIDTH), jnp.float32),
        ],
        in_specs=in_vmem(7),
        out_specs=in_vmem(8),
        scratch_shapes=[
            pltpu.VMEM((2, count, width), low),
            pltpu.VMEM((2, count, width), low),
            pltpu.VMEM((count, width), low),
            pltpu.VMEM((count, width), low),
            copies(2),
            copies(2),
            copies(),
            copies(),
        ],
        compiler_params=settings(5),
    )(raw, notes, q_gain, k_gain, w_out, tokens, gain)


def branch_kernel(
    branch_ref, weight_ref, grad_out, every_out, x_sent, x_got, core_sent, core_got
):
    z, y, x, c = spot()
    mine = x * 2 + c
    core_peer, x_peer = where_is(z, y, x, 1 - c), where_is(z, y, 1 - x, c)
    half = branch_ref.shape[0] // 2
    greet([core_peer, x_peer])
    every_out[mine] = branch_ref[...]

    def x_copy(part):
        rows = pl.ds(part * half, half)
        return remote(
            branch_ref.at[rows], every_out.at[mine, rows], x_sent.at[part], x_got.at[part], x_peer
        )

    def core_copy(far, part):
        view = every_out.at[(1 - x if far else x) * 2 + c, pl.ds(part * half, half)]
        return remote(view, view, core_sent.at[far, part], core_got.at[far, part], core_peer)

    def back(place):
        grad_out[place] = right_transposed(every_out[place], weight_ref[...]).astype(grad_out.dtype)

    for part in range(2):
        x_copy(part).start()
        core_copy(0, part).start()
    back(mine)
    for part in range(2):
        core_copy(0, part).wait_recv()
    back(x * 2 + 1 - c)
    for part in range(2):
        x_copy(part).wait_recv()
        core_copy(1, part).start()
    back((1 - x) * 2 + c)
    for part in range(2):
        core_copy(1, part).wait_recv()
    back((1 - x) * 2 + 1 - c)
    for part in range(2):
        x_copy(part).wait_send()
        core_copy(0, part).wait_send()
        core_copy(1, part).wait_send()


def branch_back(branch, w_out):
    count, width = branch.shape
    low = branch.dtype
    return pl.pallas_call(
        branch_kernel,
        out_shape=[
            jax.ShapeDtypeStruct((4, count, w_out.shape[0]), low),
            jax.ShapeDtypeStruct((4, count, width), low),
        ],
        in_specs=in_vmem(2),
        out_specs=in_vmem(2),
        scratch_shapes=[copies(2), copies(2), copies(2, 2), copies(2, 2)],
        compiler_params=settings(6),
    )(branch, w_out)


def heads_kernel(
    branch_ref,
    raw_ref,
    probs_ref,
    rotated_ref,
    rotated_key_ref,
    cosine_ref,
    sine_ref,
    query_gain_ref,
    key_gain_ref,
    hidden_ref,
    query_ref,
    key_ref,
    value_ref,
    weight_out,
    first_out,
    gains_out,
    every,
    outgoing,
    total,
    x_sent,
    x_got,
    core_sent,
    core_got,
    back_sent,
    back_got,
):
    z, y, x, c = spot()
    member, shard = lax.axis_index("exp"), lax.axis_index("fsdp")
    core_peer, x_peer = where_is(z, y, x, 1 - c), where_is(z, y, 1 - x, c)
    peers = [(member, (shard + j) % 4) for j in range(1, 4)]
    greet(peers)
    rows = every.shape[1]
    count = rows // 4
    depth = hidden_ref.shape[1]
    wide, narrow = query_ref.shape[1] // 4, key_ref.shape[1] // 4
    low = every.dtype

    def attention_back(block):
        cosine = cosine_ref[block]
        flipped = signed(sine_ref[block])

        def unturn(grads):
            return grads * cosine + turned(grads * flipped)

        def normal_back(grads, values, gain, into):
            scale = lax.rsqrt(jnp.mean(values * values, axis=1, keepdims=True) + EPSILON)
            hat = values * scale
            gains_out[into : into + 1] += jnp.sum(grads * hat, axis=0, keepdims=True)
            grads = grads * gain
            return scale * (grads - hat * jnp.mean(grads * hat, axis=1, keepdims=True))

        rotated_key = rotated_key_ref[block]
        value = raw_ref[block, :, wide + narrow :].astype(low)
        place = pl.ds(block * count, count)
        value_grad = key_grad = None
        for head in range(wide // HEAD_WIDTH):
            columns = slice(head * HEAD_WIDTH, (head + 1) * HEAD_WIDTH)
            grads = branch_ref[block, :, columns]
            probs = probs_ref[block, head]
            prob_grad = right_transposed(grads, value)
            term = left_trans(probs.astype(low), grads)
            value_grad = term if value_grad is None else value_grad + term
            balance = jnp.sum(probs * prob_grad, axis=1, keepdims=True)
            score_grad = (probs * (prob_grad - balance)).astype(low)
            query_grad = jnp.dot(score_grad, rotated_key, preferred_element_type=jnp.float32)
            term = left_trans(score_grad, rotated_ref[block, :, columns])
            key_grad = term if key_grad is None else key_grad + term
            query_grad = unturn(query_grad * HEAD_WIDTH ** (-0.5))
            query_grad = normal_back(
                query_grad, raw_ref[block, :, columns], query_gain_ref[...], 0
            )
            every[shard, place, columns] = query_grad.astype(low)
        key_grad = unturn(key_grad * HEAD_WIDTH ** (-0.5))
        key_grad = normal_back(
            key_grad, raw_ref[block, :, wide : wide + narrow], key_gain_ref[...], 1
        )
        every[shard, place, wide : wide + narrow] = key_grad.astype(low)
        every[shard, place, wide + narrow :] = value_grad.astype(low)

    def x_copy(part):
        view = every.at[shard, pl.ds(part * count, count)]
        return remote(view, view, x_sent.at[part], x_got.at[part], x_peer)

    def core_copy(far, part):
        view = every.at[(1 - x if far else x) * 2 + c, pl.ds(part * count, count)]
        return remote(view, view, core_sent.at[far, part], core_got.at[far, part], core_peer)

    gains_out[...] = jnp.zeros_like(gains_out)

    @pl.loop(0, 4)
    def _(block):
        attention_back(block)
        x_copy(block).start()
        core_copy(0, block).start()

    def weigh(place):
        weight_out[place] = left_trans(hidden_ref[...], every[place]).astype(weight_out.dtype)

    def back(place):
        grads = every[place]
        sums = None
        for weight, size, start in (
            (query_ref, wide, 0),
            (key_ref, narrow, wide),
            (value_ref, narrow, wide + narrow),
        ):
            columns = pl.ds(pl.multiple_of(place * size, size), size)
            term = right_transposed(grads[:, start : start + size], weight[:, columns])
            sums = term if sums is None else sums + term
        return sums

    def place_of(i):
        return (x + i // 2) % 2 * 2 + (c + i) % 2

    @pl.loop(0, 4)
    def _(i):
        @pl.when(i == 1)
        def _():
            for part in range(4):
                core_copy(0, part).wait_recv()

        @pl.when(i == 2)
        def _():
            for part in range(4):
                x_copy(part).wait_recv()
                core_copy(1, part).start()

        @pl.when(i == 3)
        def _():
            for part in range(4):
                core_copy(1, part).wait_recv()

        sums = back(place_of(i))

        @pl.when(i == 0)
        def _():
            total[...] = sums

        @pl.when(i > 0)
        def _():
            total[...] += sums

        @pl.when(i < 2)
        def _():
            weigh(place_of(i))

    for owner in range(4):
        outgoing[owner] = total[owner * count : (owner + 1) * count].astype(outgoing.dtype)

    def back_copy(j):
        place = (shard + j) % 4
        return remote(
            outgoing.at[place],
            first_out.at[shard],
            back_sent.at[j],
            back_got.at[(4 - j) % 4],
            (member, place),
        )

    for j in range(1, 4):
        back_copy(j).start()
    first_out[shard] = outgoing[shard]

    @pl.loop(2, 4)
    def _(i):
        weigh(place_of(i))

    for j in range(1, 4):
        place = (shard + j) % 4
        remote(
            outgoing.at[place], first_out.at[place], back_sent.at[j], back_got.at[j], (member, place)
        ).wait_recv()
    for j in range(1, 4):
        back_copy(j).wait_send()
    for part in range(4):
        x_copy(part).wait_send()
        for far in range(2):
            core_copy(far, part).wait_send()


def heads_back(branch, raw, probs, rotated, tables, gains, hidden, weights):
    rows = 4 * raw.shape[1]
    own = raw.shape[2]
    depth = hidden.shape[1]
    low = hidden.dtype
    operands = (branch, raw, probs, *rotated, *tables, *gains, hidden, *weights)
    return pl.pallas_call(
        heads_kernel,
        out_shape=[
            jax.ShapeDtypeStruct((4, depth, own), low),
            jax.ShapeDtypeStruct((4, rows // 4, depth), low),
            jax.ShapeDtypeStruct((8, HEAD_WIDTH), jnp.float32),
        ],
        in_specs=in_vmem(len(operands)),
        out_specs=in_vmem(3),
        scratch_shapes=[
            pltpu.VMEM((4, rows, own), low),
            pltpu.VMEM((4, rows // 4, depth), low),
            pltpu.VMEM((rows, depth), jnp.float32),
            copies(4),
            copies(4),
            copies(2, 4),
            copies(2, 4),
            copies(4),
            copies(4),
        ],
        compiler_params=settings(7),
    )(*operands)


def moe_gathered(normed, router, routes, capacity, cotangent, weights, notes):
    gate_w, up_w, down_w = weights
    token_count, topk = routes.shape
    experts = router.shape[1]
    all_grads = lax.all_gather(cotangent, BOTH, axis=0, tiled=True)
    padded = jnp.pad(router, ((0, 0), (0, 128 - experts)))
    arrived, active, gate_pre, up_pre, share, select, spread = gather_experts(
        normed, notes, topk, capacity, gate_w, up_w, padded
    )
    mixed, out_rows, gate_pre_grad, up_pre_grad, extra = scatter_rows(
        spread,
        active,
        down_w,
        share,
        select,
        all_grads.reshape(experts, token_count, MODEL_WIDTH),
        gate_pre,
        up_pre,
    )
    summed, back, gate_w_grad, up_w_grad = scatter_rows(
        spread, gate_pre_grad, up_pre_grad, gate_w, up_w, extra, arrived
    )

    def flat(rows):
        return rows.reshape(experts * capacity, rows.shape[2])

    weight_grads = (gate_w_grad, up_w_grad, left_trans(flat(active), flat(out_rows)))
    columns = jnp.arange(experts, dtype=jnp.int32)
    gate_grad = back[:, :experts] + back[:, experts : 2 * experts]
    picks = jnp.any(routes[:, :, None] == columns[None, None, :], axis=1)
    gates = jax.nn.softmax(jnp.where(picks, matrix_product(normed, router), MASKED), axis=1)
    logit_grad = gates * (gate_grad - jnp.sum(gates * gate_grad, axis=1, keepdims=True))
    return mixed, summed, logit_grad.astype(jnp.bfloat16), *weight_grads


def moe_exchanged(normed, router, routes, capacity, cotangent, weights, notes):
    gate_w, up_w, down_w = weights
    token_count, topk = routes.shape
    experts = router.shape[1]
    gates = gates_of(matrix_product(normed, router), routes, experts)
    slots = slot_table(routes, experts, capacity)

    def send(rows):
        packed = jnp.zeros((experts * capacity, MODEL_WIDTH), jnp.bfloat16).at[slots].set(rows)
        return exchange(packed.reshape(experts, capacity, MODEL_WIDTH)).reshape(
            experts * capacity, MODEL_WIDTH
        )

    def bring(rows):
        rows = exchange(rows.reshape(experts, capacity, MODEL_WIDTH))
        return rows.reshape(experts * capacity, MODEL_WIDTH)[slots].reshape(
            token_count, topk, MODEL_WIDTH
        )

    arrived = send(jnp.repeat(normed, topk, axis=0))
    hidden = expert_forward(arrived, gate_w, up_w)
    scaled = (gates[:, :, None] * cotangent.astype(jnp.float32)[:, None, :]).astype(jnp.bfloat16)
    out_rows = send(scaled.reshape(token_count * topk, MODEL_WIDTH))
    rows_back, gate_pre_grad, up_pre_grad = expert_back(out_rows, hidden, gate_w, up_w, down_w)
    gate_w_grad = left_trans(arrived, gate_pre_grad)
    up_w_grad = left_trans(arrived, up_pre_grad)
    down_grad = left_trans(hidden[3], out_rows)
    returned = bring(matrix_product(hidden[3], down_w).astype(jnp.bfloat16))
    mixed = jnp.einsum("tk,tkd->td", gates, returned.astype(jnp.float32))
    gate_grad = jnp.einsum("td,tkd->tk", cotangent, returned, preferred_element_type=jnp.float32)
    summed = jnp.sum(bring(rows_back), axis=1, dtype=jnp.float32)
    picked_grad = gates * (gate_grad - jnp.sum(gates * gate_grad, axis=1, keepdims=True))
    onehot = routes[:, :, None] == jnp.arange(experts, dtype=jnp.int32)[None, None, :]
    logit_grad = jnp.sum(jnp.where(onehot, picked_grad[:, :, None], 0.0), axis=1)
    return mixed, summed, logit_grad.astype(jnp.bfloat16), gate_w_grad, up_w_grad, down_grad


def local(
    tokens,
    lengths,
    routes,
    attn_gain,
    w_query,
    key_weight,
    value_weight,
    q_gain,
    k_gain,
    w_out,
    mlp_gain,
    w_router,
    expert_gate,
    expert_up,
    expert_down,
    cotangent,
):
    shards, members = lax.axis_size("fsdp"), lax.axis_size("exp")
    experts = shards * members
    token_count, topk = routes.shape
    capacity = 2 * token_count * topk // experts
    group = shards * token_count
    depth = w_query.shape[0]
    heads = QUERY_HEADS // shards
    kv_heads = max(1, KEY_VALUE_HEADS // shards)
    copies_of = shards * kv_heads // KEY_VALUE_HEADS
    head_group = heads // kv_heads
    wide, narrow = heads * HEAD_WIDTH, kv_heads * HEAD_WIDTH
    place = lax.axis_index("fsdp")

    gathered = lax.all_gather(
        jnp.concatenate([w_router.reshape(-1), attn_gain, mlp_gain, q_gain, k_gain]), "fsdp"
    )
    cuts, start = [], 0
    for leaf in (w_router, attn_gain, mlp_gain, q_gain, k_gain):
        cuts.append(gathered[:, start : start + leaf.size])
        start += leaf.size
    router = cuts[0].reshape(MODEL_WIDTH, experts)
    gain_attn, gain_mlp, gain_query, gain_key = [
        cut.reshape(-1).astype(jnp.float32) for cut in cuts[1:]
    ]
    dense = (members, shards) == (8, 4) and 2 * capacity >= token_count
    inputs = tokens.astype(jnp.float32)
    scale_one = rms_scale(inputs)
    if dense:
        notes = jnp.pad(
            jnp.concatenate(
                [routes.T, jnp.pad(lengths, ((0, 0), (0, token_count - lengths.shape[1])))], axis=0
            ),
            ((0, 15 - topk), (0, 0)),
        )
        raw, hidden, notes = project_tokens(
            tokens, notes, attn_gain[None], w_query, key_weight, value_weight
        )
        hidden = hidden.reshape(group, depth)
        first = lax.axis_index("exp") * shards
        notes_own = lax.dynamic_slice_in_dim(notes, first, shards)
    else:
        notes = None
        all_lengths = lax.all_gather(lengths[0], "fsdp")

        def by_shard(weight):
            weight = weight.reshape(depth, KEY_VALUE_HEADS, HEAD_WIDTH)
            return jnp.repeat(weight, copies_of, axis=1).reshape(depth, shards, narrow)

        joined = jnp.concatenate(
            [w_query.reshape(depth, shards, wide), by_shard(key_weight), by_shard(value_weight)],
            axis=2,
        ).transpose(1, 0, 2)
        first_normed = (inputs * scale_one * gain_attn).astype(jnp.bfloat16)
        hidden = lax.all_to_all(first_normed, "fsdp", split_axis=1, concat_axis=0, tiled=True)
        partial = contract("gk,nkc->ngc", hidden, joined).astype(jnp.bfloat16)
        raw = lax.psum_scatter(partial, "fsdp", scatter_dimension=0, tiled=True)[0]
        raw = raw.astype(jnp.float32)
    if dense:
        gains = (gain_query[None], gain_key[None])
        middle, normed, attended, probs, *rotated, cosine, sine = finish_attention(
            raw, notes_own, topk, lengths.shape[1], *gains, w_out, tokens, gain_mlp[None]
        )
        attended = attended.reshape(group, wide)
        scale_two = rms_scale(middle)
    else:
        raw = raw.reshape(shards, token_count, wide + 2 * narrow)
        query_raw = raw[:, :, :wide].reshape(shards, token_count, heads, HEAD_WIDTH)
        key_raw = raw[:, :, wide : wide + narrow].reshape(shards, token_count, kv_heads, HEAD_WIDTH)
        value = (
            raw[:, :, wide + narrow :]
            .astype(jnp.bfloat16)
            .reshape(shards, token_count, kv_heads, HEAD_WIDTH)
        )
        position, allowed = jax.vmap(lambda row: seq_layout(row, token_count))(all_lengths)
        cosine, sine = rotary_tables(position, HEAD_WIDTH)
        query_scale = rms_scale(query_raw)
        query_hat = query_raw * query_scale
        key_scale = rms_scale(key_raw)
        key_hat = key_raw * key_scale
        query = (
            rotate(query_hat * gain_query, cosine, sine)
            .astype(jnp.bfloat16)
            .reshape(shards, token_count, kv_heads, head_group, HEAD_WIDTH)
        )
        key = rotate(key_hat * gain_key, cosine, sine).astype(jnp.bfloat16)
        scores = contract("bqkgd,bpkd->bkgqp", query, key) * HEAD_WIDTH ** (-0.5)
        scores = jnp.where(allowed[:, None, None], scores, MASKED)
        top = jnp.max(scores, axis=-1, keepdims=True)
        raised = jnp.exp(scores - top)
        probs = raised / jnp.sum(raised, axis=-1, keepdims=True)
        probs_low = probs.astype(jnp.bfloat16)
        attended = contract("bkgqp,bpkd->bqkgd", probs_low, value).astype(jnp.bfloat16)
        attended = attended.reshape(group, wide)
        mixed_heads = lax.psum_scatter(
            matrix_product(attended, w_out).astype(jnp.bfloat16),
            "fsdp",
            scatter_dimension=0,
            tiled=True,
        )
        middle = inputs + mixed_heads.astype(jnp.float32)
        scale_two = rms_scale(middle)
        normed = (middle * scale_two * gain_mlp).astype(jnp.bfloat16)

    moe = moe_gathered if dense else moe_exchanged
    mixed, summed, logit_grad, gate_w_grad, up_w_grad, down_grad = moe(
        normed,
        router,
        routes,
        capacity,
        cotangent,
        (expert_gate[0], expert_up[0], expert_down[0]),
        notes,
    )
    layer_out = (middle + mixed).astype(jnp.bfloat16)

    upstream = cotangent.astype(jnp.float32)
    normed_grad = summed + right_transposed(logit_grad, router)
    mlp_gain_grad = jnp.sum(normed_grad * middle * scale_two, axis=0)
    router_grad = left_trans(normed, logit_grad)
    middle_grad = upstream + rms_back(normed_grad * gain_mlp, middle, scale_two)
    branch_low = middle_grad.astype(jnp.bfloat16)
    if dense:
        attended_grad, branch_grad = branch_back(branch_low, w_out)
        branch_grad = branch_grad.reshape(group, MODEL_WIDTH)
    else:
        branch_grad = lax.all_gather(branch_low, "fsdp", axis=0, tiled=True)
        attended_grad = right_transposed(branch_grad, w_out).astype(jnp.bfloat16)
    out_w_grad = left_trans(attended, branch_grad).astype(jnp.bfloat16)
    attended_grad, out_w_grad = lax.optimization_barrier((attended_grad, out_w_grad))
    if dense:
        joined_grad, first_grad, gain_grads = heads_back(
            attended_grad,
            raw,
            probs,
            rotated,
            (cosine, sine),
            gains,
            hidden,
            (w_query, key_weight, value_weight),
        )
        first_grad = first_grad.transpose(1, 0, 2).reshape(token_count, MODEL_WIDTH)
        q_gain_grad, k_gain_grad = gain_grads[0], gain_grads[1]
    else:
        attended_grad = attended_grad.reshape(shards, token_count, kv_heads, head_group, HEAD_WIDTH)
        prob_grad = contract("bqkgd,bpkd->bkgqp", attended_grad, value)
        value_grad = contract("bkgqp,bqkgd->bpkd", probs_low, attended_grad)
        balance = jnp.sum(probs * prob_grad, axis=-1, keepdims=True)
        score_grad = (probs * (prob_grad - balance)).astype(jnp.bfloat16)
        query_norm_grad = contract("bkgqp,bpkd->bqkgd", score_grad, key) * HEAD_WIDTH ** (-0.5)
        query_norm_grad = query_norm_grad.reshape(shards, token_count, heads, HEAD_WIDTH)
        key_norm_grad = contract("bkgqp,bqkgd->bpkd", score_grad, query) * HEAD_WIDTH ** (-0.5)
        query_norm_grad = rotate_back(query_norm_grad, cosine, sine)
        key_norm_grad = rotate_back(key_norm_grad, cosine, sine)
        q_gain_grad = jnp.sum(query_norm_grad * query_hat, axis=(0, 1, 2))
        k_gain_grad = jnp.sum(key_norm_grad * key_hat, axis=(0, 1, 2))
        query_grad = rms_back(query_norm_grad * gain_query, query_raw, query_scale)
        key_grad = rms_back(key_norm_grad * gain_key, key_raw, key_scale)
        head_grads = jnp.concatenate(
            [
                query_grad.reshape(group, wide),
                key_grad.reshape(group, narrow),
                value_grad.reshape(group, narrow),
            ],
            axis=1,
        ).astype(jnp.bfloat16)
        head_grads = lax.all_gather(head_grads, "fsdp")
        hidden_grad = contract("ngc,nkc->gk", head_grads, joined).astype(jnp.bfloat16)
        first_grad = lax.all_to_all(
            hidden_grad, "fsdp", split_axis=0, concat_axis=1, tiled=True
        )
        joined_grad = contract("gk,ngc->nkc", hidden, head_grads).astype(jnp.bfloat16)
    first_grad = first_grad.astype(jnp.float32)
    attn_gain_grad = jnp.sum(first_grad * inputs * scale_one, axis=0)
    input_grad = (middle_grad + rms_back(first_grad * gain_attn, inputs, scale_one)).astype(
        jnp.bfloat16
    )

    vectors = jnp.concatenate(
        [
            grad.reshape(shards, -1)
            for grad in (router_grad, attn_gain_grad, mlp_gain_grad, q_gain_grad, k_gain_grad)
        ],
        axis=1,
    )
    if dense:
        rows = -(-vectors.shape[1] // 1024) * 8
        vectors = jnp.pad(vectors, ((0, 0), (0, rows * 128 - vectors.shape[1])))
        started = lengths[0, 0] > 0
        gate_w_grad, up_w_grad = (
            jnp.where(started, grad, 0.0) for grad in (gate_w_grad, up_w_grad)
        )
        out_sum = lax.psum_scatter(out_w_grad, "exp", scatter_dimension=0, tiled=True)
        joined_grad, vectors, out_sum, gate_w_grad, up_w_grad, down_grad = (
            lax.optimization_barrier(
                (joined_grad, vectors, out_sum, gate_w_grad, up_w_grad, down_grad)
            )
        )
        *joined_sum, out_sum, vectors = reduce_over_members(
            joined_grad.reshape(2, 4, -1, wide + 2 * narrow),
            out_sum,
            vectors.reshape(shards, rows, 128),
            (shards * wide, shards * narrow, shards * narrow),
        )
        out_sum, vectors = out_sum.reshape(w_out.shape), vectors.reshape(-1)
    else:
        out_sum = lax.psum(out_w_grad, "exp")
        joined_sum = lax.psum(joined_grad, "exp").astype(jnp.float32)
        vectors = lax.psum(vectors, BOTH)[place]
    if not dense:

        def gather_heads(part):
            part = part.transpose(1, 0, 2).reshape(depth, KEY_VALUE_HEADS, copies_of, HEAD_WIDTH)
            return part.sum(axis=2).reshape(depth, KEY_VALUE_HEADS * HEAD_WIDTH)

        joined_sum = (
            joined_sum[:, :, :wide].transpose(1, 0, 2).reshape(depth, QUERY_HEADS * HEAD_WIDTH),
            gather_heads(joined_sum[:, :, wide : wide + narrow]),
            gather_heads(joined_sum[:, :, wide + narrow :]),
        )
    query_sum, key_sum, value_sum = (part.astype(jnp.float32) for part in joined_sum)
    sums, start = [], 0
    for leaf in (w_router, attn_gain, mlp_gain, q_gain, k_gain):
        sums.append(vectors[start : start + leaf.size].reshape(leaf.shape))
        start += leaf.size

    return (
        layer_out,
        input_grad,
        sums[1],
        query_sum,
        key_sum,
        value_sum,
        sums[3],
        sums[4],
        out_sum.astype(jnp.float32),
        sums[2],
        sums[0],
        gate_w_grad[None],
        up_w_grad[None],
        down_grad[None],
    )


def solution(mesh):
    in_specs = (
        P(("exp", "fsdp"), None),
        P(("exp", "fsdp"), None),
        P(("exp", "fsdp"), None),
        P("fsdp"),
        P("fsdp", None),
        P("fsdp", None),
        P("fsdp", None),
        P("fsdp"),
        P("fsdp"),
        P("fsdp", None),
        P("fsdp"),
        P("fsdp", None),
        P(("exp", "fsdp"), None, None),
        P(("exp", "fsdp"), None, None),
        P(("exp", "fsdp"), None, None),
        P(("exp", "fsdp"), None),
    )
    out_specs = (
        P(("exp", "fsdp"), None),
        P(("exp", "fsdp"), None),
        P("fsdp"),
        P("fsdp", None),
        P("fsdp", None),
        P("fsdp", None),
        P("fsdp"),
        P("fsdp"),
        P("fsdp", None),
        P("fsdp"),
        P("fsdp", None),
        P(("exp", "fsdp"), None, None),
        P(("exp", "fsdp"), None, None),
        P(("exp", "fsdp"), None, None),
    )
    return jax.shard_map(local, mesh=mesh, in_specs=in_specs, out_specs=out_specs, check_vma=False)
```

```python
import functools
import math

import jax
import jax.numpy as jnp
from jax import lax
from jax.experimental import pallas as pl
from jax.experimental.pallas import tpu as pltpu
from jax.sharding import PartitionSpec as P

MODEL_WIDTH = 2048
QUERY_HEADS = 32
KEY_VALUE_HEADS = 4
HEAD_WIDTH = 128


EPSILON = 1e-06
THETA = 1000000.0
MASKED = -1e30
BOTH = ("exp", "fsdp")
MESH = pl.DeviceIdType.MESH


def matrix_product(left, right):
    return jnp.dot(left, right, preferred_element_type=jnp.float32)


def left_trans(left, right):
    return lax.dot_general(
        left, right, (((0,), (0,)), ((), ())), preferred_element_type=jnp.float32
    )


def right_transposed(left, right):
    return lax.dot_general(
        left, right, (((1,), (1,)), ((), ())), preferred_element_type=jnp.float32
    )


def contract(spec, left, right):
    return jnp.einsum(spec, left, right, preferred_element_type=jnp.float32)


def rms_scale(values):
    return lax.rsqrt(jnp.mean(values * values, axis=-1, keepdims=True) + EPSILON)


def rms_back(grad_hat, values, scale):
    normal = values * scale
    return scale * (grad_hat - normal * jnp.mean(grad_hat * normal, axis=-1, keepdims=True))


def seq_layout(length_row, token_count):
    ends = jnp.cumsum(length_row)
    starts = ends - length_row
    places = jnp.arange(token_count, dtype=jnp.int32)
    member = (places[:, None] >= starts[None, :]) & (places[:, None] < ends[None, :])
    numbers = jnp.arange(length_row.shape[0], dtype=jnp.int32)
    segment = jnp.sum(jnp.where(member, numbers[None, :], 0), axis=1)
    position = places - jnp.sum(jnp.where(member, starts[None, :], 0), axis=1)
    allowed = (segment[:, None] == segment[None, :]) & (places[None, :] <= places[:, None])
    return (position, allowed)


def rotary_tables(position, head_size):
    half = head_size // 2
    index = jnp.arange(head_size, dtype=jnp.int32) % half
    inverse = jnp.exp(index.astype(jnp.float32) * (-2.0 * math.log(THETA) / head_size))
    angles = position.astype(jnp.float32)[..., None] * inverse
    return (jnp.cos(angles)[..., None, :], jnp.sin(angles)[..., None, :])


def rotate(values, cosine, sine):
    half = values.shape[-1] // 2
    turned = jnp.concatenate([-values[..., half:], values[..., :half]], axis=-1)
    return values * cosine + turned * sine


def rotate_back(grads, cosine, sine):
    half = grads.shape[-1] // 2
    moved = grads * sine
    return grads * cosine + jnp.concatenate([moved[..., half:], -moved[..., :half]], axis=-1)


def slot_table(route_rows, experts, capacity):
    flat = route_rows.reshape(-1)
    onehot = (flat[:, None] == jnp.arange(experts, dtype=jnp.int32)[None, :]).astype(jnp.int32)
    ranks = jnp.cumsum(onehot, axis=0) - 1
    rank = jnp.sum(ranks * onehot, axis=1)
    return flat * capacity + rank


def exchange(buffer):
    return lax.all_to_all(buffer, BOTH, split_axis=0, concat_axis=0, tiled=True)


def two_halves(values):
    high = values.astype(jnp.bfloat16)
    low = (values - high.astype(jnp.float32)).astype(jnp.bfloat16)
    return high, low


def expert_forward(arrived, gate_w, up_w):
    gate_pre = matrix_product(arrived, gate_w)
    up_pre = matrix_product(arrived, up_w)
    sigma = jax.nn.sigmoid(gate_pre)
    active = (gate_pre * sigma * up_pre).astype(jnp.bfloat16)
    return gate_pre, up_pre, sigma, active


def expert_back(out_rows, hidden, gate_w, up_w, down_w):
    gate_pre, up_pre, sigma, _ = hidden
    active_grad = right_transposed(out_rows, down_w)
    gate_pre_grad = (active_grad * up_pre * (sigma * (1.0 + gate_pre * (1.0 - sigma)))).astype(
        jnp.bfloat16
    )
    up_pre_grad = (active_grad * (gate_pre * sigma)).astype(jnp.bfloat16)
    rows_back = right_transposed(gate_pre_grad, gate_w) + right_transposed(up_pre_grad, up_w)
    return rows_back.astype(jnp.bfloat16), gate_pre_grad, up_pre_grad


def gates_of(logits, routes, experts):
    picked = jnp.take_along_axis(logits, routes, axis=1)
    peak = jnp.max(picked, axis=1, keepdims=True)
    lifted = jnp.exp(picked - peak)
    return lifted / jnp.sum(lifted, axis=1, keepdims=True)


def spot():
    member, shard = lax.axis_index("exp"), lax.axis_index("fsdp")
    return member // 2, member % 2, shard // 2, shard % 2


def where_is(z, y, x, c):
    return (z * 2 + y, x * 2 + c)


def number(z, y, x, c):
    return z * 8 + y * 4 + x * 2 + c


def along_z(z, q):
    return (z // 2 + q // 2) % 2 * 2 + (z % 2 + q % 2) % 2


def greet(peers):
    barrier = pltpu.get_barrier_semaphore()
    for peer in peers:
        pl.semaphore_signal(barrier, inc=1, device_id=peer, device_id_type=MESH)
    pl.semaphore_wait(barrier, len(peers))


def remote(source, target, sent, got, peer):
    return pltpu.make_async_remote_copy(
        src_ref=source,
        dst_ref=target,
        send_sem=sent,
        recv_sem=got,
        device_id=peer,
        device_id_type=MESH,
    )


def in_vmem(count):
    return [pl.BlockSpec(memory_space=pltpu.VMEM)] * count


def copies(*shape):
    return pltpu.SemaphoreType.DMA(shape)


def settings(collective_id):
    return pltpu.CompilerParams(
        collective_id=collective_id, has_side_effects=True, vmem_limit_bytes=60 << 20
    )


def gather_kernel(
    topk,
    x_ref,
    notes_ref,
    gate_hbm,
    up_hbm,
    router_ref,
    rows_out,
    active_out,
    gate_out,
    up_out,
    share_out,
    select_out,
    spread_out,
    held,
    gate_ref,
    up_ref,
    picked,
    lively,
    results,
    loaded,
    stored,
    arrive,
    to_z,
    to_y,
    to_x,
    to_core,
    corners,
    deep_z,
    deep_core,
):
    z, y, x, c = spot()
    count = x_ref.shape[0]
    half, thin = count * 3 // 8, count // 8
    cuts = ((0, half), (half, half), (2 * half, thin), (2 * half + thin, thin), (2 * half, 2 * thin))
    kept = select_out.shape[1]
    y_peer, x_peer, core_peer = (
        where_is(z, 1 - y, x, c),
        where_is(z, y, 1 - x, c),
        where_is(z, y, x, 1 - c),
    )
    near_z, far_z = where_is(along_z(z, 1), y, x, c), where_is(along_z(z, 2), y, x, c)
    loads = [
        pltpu.make_async_copy(source, target, loaded.at[i])
        for i, (source, target) in enumerate(
            ((gate_hbm, gate_ref), (up_hbm, up_ref))
        )
    ]
    for load in loads:
        load.start()
    greet([y_peer, x_peer, core_peer, near_z, far_z])
    mine = number(z, y, x, c)

    def copy(block, part, sem, peer):
        view = held.at[block, pl.ds(*cuts[part])]
        return remote(view, view, sem, arrive.at[block, 2 if part == 4 else part], peer)

    def arrived(block, part):
        copy(block, part, to_core.at[0, 0, 0], core_peer).wait_recv()

    def block_of(q, other_y, other_x, core):
        return number(
            along_z(z, q), 1 - y if other_y else y, 1 - x if other_x else x, core
        )

    combos = ((0, 0), (0, 1), (1, 0), (1, 1))

    def stores(slot, blocks):
        made = []
        for k in range(4):
            part = pl.ds(k * kept, kept)
            made.append((picked.at[slot, part], rows_out.at[blocks[k]]))
            made.append((lively.at[slot, part], active_out.at[blocks[k]]))
            for i, out in enumerate((gate_out, up_out)):
                made.append((results.at[slot, i, part], out.at[blocks[k]]))
        return [
            pltpu.make_async_copy(source, target, stored.at[slot, i])
            for i, (source, target) in enumerate(made)
        ]

    def choose(block):
        notes = notes_ref[block]
        own = jnp.zeros((1, count), jnp.float32)
        lines = lax.broadcasted_iota(jnp.int32, (128, count), 0)
        names = jnp.zeros((128, count), jnp.float32)
        for k in range(topk):
            line = notes[k : k + 1]
            own = own + jnp.where(line == mine, 1.0, 0.0)
            names = names + jnp.where(lines == line, 1.0, 0.0)
        before = lax.broadcasted_iota(jnp.int32, (count, count), 0)
        before = before < lax.broadcasted_iota(jnp.int32, (count, count), 1)
        rank = jnp.dot(
            jnp.broadcast_to(own, (8, count)).astype(x_ref.dtype),
            jnp.where(before, 1.0, 0.0).astype(x_ref.dtype),
            preferred_element_type=jnp.float32,
        )[:1]
        places = lax.broadcasted_iota(jnp.int32, (kept, count), 0).astype(jnp.float32)
        chosen = jnp.where((rank == places) & (own > 0), 1.0, 0.0)
        spread_out[block] = jnp.transpose(chosen).astype(spread_out.dtype)
        chosen = chosen.astype(select_out.dtype)
        select_out[block] = chosen
        return chosen, right_transposed(chosen, names.astype(chosen.dtype))

    def work(q, slot):
        core = 1 - c if slot else c
        blocks = [block_of(q, *combo, core) for combo in combos]

        @pl.when(q > 0)
        def _():
            for store in stores(slot, [block_of(q - 1, *combo, core) for combo in combos]):
                store.wait()

        named = []
        for k in range(4):
            chosen, names = choose(blocks[k])
            named.append(names)
            rows = jnp.dot(chosen, held[blocks[k]], preferred_element_type=jnp.float32)
            picked[slot, k * kept : (k + 1) * kept] = rows.astype(picked.dtype)
        rows = picked[slot]
        gate_pre = jnp.dot(rows, gate_ref[...], preferred_element_type=jnp.float32)
        up_pre = jnp.dot(rows, up_ref[...], preferred_element_type=jnp.float32)
        logits = jnp.dot(rows, router_ref[...], preferred_element_type=jnp.float32)
        results[slot, 0] = gate_pre
        results[slot, 1] = up_pre
        active = gate_pre * (1.0 / (1.0 + jnp.exp(-gate_pre))) * up_pre
        lively[slot] = active.astype(lively.dtype)
        for k in range(4):
            part = slice(k * kept, (k + 1) * kept)
            block = blocks[k]
            masked = jnp.where(named[k] > 0, logits[part], MASKED)
            lifted = jnp.exp(masked - jnp.max(masked, axis=1, keepdims=True))
            lanes = lax.broadcasted_iota(jnp.int32, lifted.shape, 1)
            share = jnp.sum(jnp.where(lanes == mine, lifted, 0.0), axis=1, keepdims=True)
            share = share / jnp.sum(lifted, axis=1, keepdims=True)
            share_out[block] = jnp.broadcast_to(share, share_out.shape[1:])
        for store in stores(slot, blocks):
            store.start()

    def forward(q):
        block = block_of(q, 0, 0, c)
        if q:
            arrived(block, 0)
            arrived(block, 1)
        if q == 2:
            copy(block, 0, to_z.at[2, 0], near_z).start()
            copy(block, 1, to_z.at[2, 1], near_z).start()
        copy(block, 0, to_y.at[0, q], y_peer).start()
        copy(block, 1, to_x.at[0, q], x_peer).start()
        copy(block, 0, to_x.at[1, q], x_peer).start()
        copy(block, 1, to_y.at[1, q], y_peer).start()
        copy(block, 0, to_core.at[0, 0, q], core_peer).start()
        copy(block, 1, to_core.at[0, 1, q], core_peer).start()

    def second(q):
        block = block_of(q, 1, 0, c)
        arrived(block, 0)
        copy(block, 0, to_x.at[2, q], x_peer).start()
        copy(block, 0, to_core.at[1, 0, q], core_peer).start()
        block = block_of(q, 0, 1, c)
        arrived(block, 1)
        copy(block, 1, to_y.at[2, q], y_peer).start()
        copy(block, 1, to_core.at[2, 1, q], core_peer).start()

    def last(q):
        block = block_of(q, 0, 1, c)
        arrived(block, 0)
        copy(block, 0, to_core.at[2, 0, q], core_peer).start()
        block = block_of(q, 1, 0, c)
        arrived(block, 1)
        copy(block, 1, to_core.at[1, 1, q], core_peer).start()
        block = block_of(q, 1, 1, c)
        arrived(block, 0)
        copy(block, 0, to_core.at[3, 0, q], core_peer).start()
        arrived(block, 1)
        copy(block, 1, to_core.at[3, 1, q], core_peer).start()

    def others(q):
        for combo in combos:
            block = block_of(q, *combo, 1 - c)
            for part in (0, 1, 4):
                arrived(block, part)

    beside_x, beside_y, across = (block_of(0, *combo, c) for combo in combos[1:])

    def corner(i):
        block = (mine, mine, mine, mine, beside_x, beside_y)[i]
        part, peer = ((2, x_peer), (3, y_peer), (2, y_peer), (3, x_peer), (2, y_peer), (3, x_peer))[i]
        return copy(block, part, corners.at[i], peer)

    def deep_copy(kind, i, block):
        return copy(block, 4, deep_z.at[kind, i], far_z if kind == 1 else near_z)

    def deep_core_copy(q, i, block):
        return copy(block, 4, deep_core.at[q, i], core_peer)

    def deep_first():
        arrived(beside_x, 3)
        arrived(beside_y, 2)
        arrived(across, 2)
        arrived(across, 3)
        for i, combo in enumerate(combos):
            block = block_of(0, *combo, c)
            deep_copy(0, i, block).start()
            deep_copy(1, i, block).start()
            deep_core_copy(0, i, block).start()

    def deep_next(q):
        for i, combo in enumerate(combos):
            block = block_of(q, *combo, c)
            arrived(block, 4)
            if q == 2:
                deep_copy(2, i, block).start()
            deep_core_copy(q, i, block).start()

    held[mine] = x_ref[...]
    for part in range(2):
        copy(mine, part, to_z.at[0, part], near_z).start()
    for part in range(2):
        copy(mine, part, to_z.at[1, part], far_z).start()
    for i in range(4):
        corner(i).start()
    forward(0)
    for load in loads:
        load.wait()
    arrived(beside_x, 2)
    corner(4).start()
    arrived(beside_y, 3)
    corner(5).start()
    forward(1)
    second(0)
    deep_first()
    forward(2)
    second(1)

    @pl.loop(0, 4)
    def _(q):
        last(q)
        work(q, 0)
        others(q)
        work(q, 1)

        @pl.when(q == 0)
        def _():
            forward(3)
            deep_next(1)
            second(2)
            deep_next(2)

        @pl.when(q == 1)
        def _():
            second(3)
            deep_next(3)

    for slot in range(2):
        core = 1 - c if slot else c
        for store in stores(slot, [block_of(3, *combo, core) for combo in combos]):
            store.wait()
    for part in range(2):
        copy(mine, part, to_z.at[0, part], near_z).wait_send()
        copy(mine, part, to_z.at[1, part], far_z).wait_send()
        copy(mine, part, to_z.at[2, part], near_z).wait_send()

    for i in range(6):
        corner(i).wait_send()
    for i in range(4):
        for kind in range(3):
            deep_copy(kind, i, mine).wait_send()

    @pl.loop(0, 4)
    def _(q):
        for i in range(4):
            deep_core_copy(q, i, mine).wait_send()
        for i in range(3):
            copy(mine, 0, to_y.at[i, q], y_peer).wait_send()
            copy(mine, 0, to_x.at[i, q], x_peer).wait_send()
        for i in range(4):
            for part in range(2):
                copy(mine, part, to_core.at[i, part, q], core_peer).wait_send()


def gather_experts(rows, notes, topk, kept, gate_w, up_w, router):
    count, width = rows.shape
    blocks = notes.shape[0]
    hidden = gate_w.shape[1]
    low = rows.dtype
    anywhere = pl.BlockSpec(memory_space=pl.ANY)
    vmem = pl.BlockSpec(memory_space=pltpu.VMEM)
    return pl.pallas_call(
        functools.partial(gather_kernel, topk),
        out_shape=[
            jax.ShapeDtypeStruct((blocks, kept, width), low),
            jax.ShapeDtypeStruct((blocks, kept, hidden), low),
            jax.ShapeDtypeStruct((blocks, kept, hidden), jnp.float32),
            jax.ShapeDtypeStruct((blocks, kept, hidden), jnp.float32),
            jax.ShapeDtypeStruct((blocks, kept, 128), jnp.float32),
            jax.ShapeDtypeStruct((blocks, kept, count), low),
            jax.ShapeDtypeStruct((blocks, count, kept), low),
        ],
        in_specs=[vmem, vmem, anywhere, anywhere, vmem],
        out_specs=[anywhere] * 4 + [vmem] * 3,
        scratch_shapes=[
            pltpu.VMEM((blocks, count, width), low),
            pltpu.VMEM(gate_w.shape, low),
            pltpu.VMEM(up_w.shape, low),
            pltpu.VMEM((2, 4 * kept, width), low),
            pltpu.VMEM((2, 4 * kept, hidden), low),
            pltpu.VMEM((2, 2, 4 * kept, hidden), jnp.float32),
            copies(2),
            copies(2, 16),
            copies(blocks, 4),
            copies(3, 2),
            copies(3, 4),
            copies(3, 4),
            copies(4, 2, 4),
            copies(6),
            copies(3, 4),
            copies(4, 4),
        ],
        compiler_params=settings(1),
    )(rows, notes, gate_w, up_w, router)


def scatter_kernel(
    extended,
    *refs,
):
    resident = 6 if extended else 5
    streamed = 1 if extended else 3
    given, refs = refs[:resident], refs[resident:]
    sources, refs = refs[:streamed], refs[streamed:]
    if extended:
        (rows_hbm,) = sources
        out_ref, extra_out, gate_out, up_out = refs[:4]
        tiles, staged, loaded, stored = refs[4:8]
        refs = refs[8:]
    else:
        grads_hbm, gate_hbm, up_hbm = sources
        out_ref, rows_out, gate_out, up_out, extra_ref = refs[:5]
        grads_in, pre_in, rows_staged, staged, loaded, stored = refs[5:11]
        refs = refs[11:]
    held, (fetched, *refs) = refs[:resident], refs[resident:]
    if extended:
        spread_ref, gate_grad_ref, up_grad_ref, gate_ref, up_ref, extra_ref = held
    else:
        spread_ref, active_ref, down_ref, share_ref, select_ref = held
    outgoing, core_in, total, back, x_in, y_in, z_in, deep_in, deep_x, deep_y = refs[:10]
    core_sent, core_got, x_sent, x_got, y_sent, y_got, z_sent, z_got = refs[10:18]
    deep_sent, deep_got, corner_sent, corner_got = refs[18:]
    fetches = [
        pltpu.make_async_copy(source, target, fetched.at[i])
        for i, (source, target) in enumerate(zip(given, held))
    ]
    for fetch in fetches:
        fetch.start()
    z, y, x, c = spot()
    width = out_ref.shape[1]
    count = out_ref.shape[0]
    half, thin = count * 3 // 8, count // 8
    wide = 2 * half
    blocks, _, kept = spread_ref.shape
    y_peer, x_peer, core_peer = (
        where_is(z, 1 - y, x, c),
        where_is(z, y, 1 - x, c),
        where_is(z, y, x, 1 - c),
    )
    near_z, far_z = where_is(along_z(z, 1), y, x, c), where_is(along_z(z, 2), y, x, c)
    greet([y_peer, x_peer, core_peer, near_z, far_z])
    for fetch in fetches:
        fetch.wait()
    groups = ((1, 1), (0, 1), (1, 0), (0, 0))

    def block_of(group, q, core):
        other_y, other_x = groups[group]
        return number(along_z(z, q), 1 - y if other_y else y, 1 - x if other_x else x, core)

    def rows_of(ref, q, core):
        return jnp.concatenate([ref[block_of(group, q, core)] for group in range(4)], axis=0)

    def rows_back(q, core):
        if extended:
            sums = right_transposed(rows_of(gate_grad_ref, q, core), gate_ref[...])
            sums = sums + right_transposed(rows_of(up_grad_ref, q, core), up_ref[...])
        else:
            sums = jnp.dot(
                rows_of(active_ref, q, core), down_ref[...], preferred_element_type=jnp.float32
            )
            sums = sums.astype(back.dtype).astype(jnp.float32)
            sums = sums * rows_of(share_ref, q, core)[:, :1]
        back[...] = sums.astype(back.dtype)

    def turn_blocks(turn):
        core = (c + turn) % 2
        return [block_of(group, turn // 2, core) for group in range(4)]

    def loads(turn):
        slot, made = turn % 2, []
        if extended:
            columns = pl.ds(pl.multiple_of(turn * tiles.shape[3], tiles.shape[3]), tiles.shape[3])
            made.append((rows_hbm.at[:, :, columns], tiles.at[slot]))
        else:
            for group, block in enumerate(turn_blocks(turn)):
                rows = pl.ds(group * kept, kept)
                made.append((grads_hbm.at[block], grads_in.at[slot, group]))
                made.append((gate_hbm.at[block], pre_in.at[slot, 0, rows]))
                made.append((up_hbm.at[block], pre_in.at[slot, 1, rows]))
        return [
            pltpu.make_async_copy(source, target, loaded.at[slot, i])
            for i, (source, target) in enumerate(made)
        ]

    def stores(turn):
        slot, made = turn % 2, []
        if extended:
            columns = tiles.shape[3]
            rows = pl.ds(pl.multiple_of(turn * columns, columns), columns)
            made.append((staged.at[slot, 0], gate_out.at[rows]))
            made.append((staged.at[slot, 1], up_out.at[rows]))
        else:
            for group, block in enumerate(turn_blocks(turn)):
                rows = pl.ds(group * kept, kept)
                made.append((rows_staged.at[slot, rows], rows_out.at[block]))
                made.append((staged.at[slot, 0, rows], gate_out.at[block]))
                made.append((staged.at[slot, 1, rows], up_out.at[block]))
        return [
            pltpu.make_async_copy(source, target, stored.at[slot, i])
            for i, (source, target) in enumerate(made)
        ]

    def begin_loads(turn):
        for load in loads(turn):
            load.start()

    def fill(turn):
        for load in loads(turn):
            load.wait()

        @pl.when(turn >= 2)
        def _():
            for store in stores(turn - 2):
                store.wait()

        if extended:
            weigh(turn)
        else:
            prepare(turn)
        for store in stores(turn):
            store.start()

        @pl.when(turn < 6)
        def _():
            begin_loads(turn + 2)

    def weigh(turn):
        slot = turn % 2
        staged[slot] = jnp.zeros_like(staged[slot])

        @pl.loop(0, blocks // 4)
        def _(i):
            span = pl.ds(i * 4, 4)
            rows = tiles[slot, span].reshape(4 * kept, tiles.shape[3])
            for which, grads in enumerate((gate_grad_ref, up_grad_ref)):
                staged[slot, which] += left_trans(
                    rows, grads[span].reshape(4 * kept, grads.shape[2])
                )

    def prepare(turn):
        blocks, slot = turn_blocks(turn), turn % 2
        mine = number(z, y, x, c)
        parts = [
            jnp.dot(
                select_ref[blocks[group]],
                grads_in[slot, group],
                preferred_element_type=jnp.float32,
            )
            for group in range(4)
        ]
        share = jnp.concatenate([share_ref[block] for block in blocks], axis=0)[:, :1]
        picked = jnp.concatenate(parts, axis=0)
        rows_staged[slot] = (share * picked).astype(rows_staged.dtype)
        ahead = right_transposed(picked.astype(rows_staged.dtype), down_ref[...])
        gate, up = pre_in[slot, 0], pre_in[slot, 1]
        active = jnp.concatenate([active_ref[block] for block in blocks], axis=0)
        grad = jnp.sum(active.astype(jnp.float32) * ahead, axis=1, keepdims=True)
        active_grad = share * ahead
        sigma = 1.0 / (1.0 + jnp.exp(-gate))
        gate_grad = active_grad * up * (sigma * (1.0 + gate * (1.0 - sigma)))
        staged[slot, 0] = gate_grad.astype(staged.dtype)
        staged[slot, 1] = (active_grad * (gate * sigma)).astype(staged.dtype)
        lanes = lax.broadcasted_iota(jnp.int32, (4 * kept, 128), 1)
        high = grad.astype(extra_ref.dtype).astype(jnp.float32)
        both = jnp.where(lanes == mine, high, jnp.where(lanes == 32 + mine, grad - high, 0.0))
        both = both.astype(extra_ref.dtype)
        for group, block in enumerate(blocks):
            extra_ref[block] = both[group * kept : (group + 1) * kept]

    def part(block, group):
        rows = jnp.dot(
            spread_ref[block],
            back[group * kept : (group + 1) * kept],
            preferred_element_type=jnp.float32,
        )
        if not extended:
            return rows
        more = jnp.dot(spread_ref[block], extra_ref[block], preferred_element_type=jnp.float32)
        return jnp.concatenate([rows, more], axis=1)

    def across(group, q):
        return remote(
            outgoing.at[q, group],
            core_in.at[q, group],
            core_sent.at[q, group],
            core_got.at[q, group],
            core_peer,
        )

    def view(group, q, side):
        return total.at[q, group, pl.ds(side * half, half)]

    def x_copy(group, q, side, slot):
        return remote(
            view(group, q, side), x_in.at[slot, q], x_sent.at[slot, q], x_got.at[slot, q], x_peer
        )

    def y_copy(group, q, side, slot):
        return remote(
            view(group, q, side), y_in.at[slot, q], y_sent.at[slot, q], y_got.at[slot, q], y_peer
        )

    def z_copy(q):
        return remote(
            total.at[q, 3, pl.ds(0, wide)],
            z_in.at[q - 1],
            z_sent.at[q - 1],
            z_got.at[q - 1],
            where_is(along_z(z, 2 - q % 2), y, x, c),
        )

    def deep_copy(q):
        return remote(
            total.at[q, :, pl.ds(wide, 2 * thin)],
            deep_in.at[q - 1],
            deep_sent.at[q - 1],
            deep_got.at[q - 1],
            far_z if q == 2 else near_z,
        )

    def corner_copy(over_x, group, side, slot):
        place, peer = (deep_x, x_peer) if over_x else (deep_y, y_peer)
        return remote(
            total.at[0, group, pl.ds(wide + side * thin, thin)],
            place.at[slot],
            corner_sent.at[over_x, slot],
            corner_got.at[over_x, slot],
            peer,
        )

    y_corners = [corner_copy(0, 0, 0, 0), corner_copy(0, 2, 0, 1), corner_copy(0, 2, 1, 2)]
    x_corners = [corner_copy(1, 0, 1, 0), corner_copy(1, 1, 1, 1), corner_copy(1, 1, 0, 2)]

    def add_deep(q, *arrivals):
        rows = pl.ds(wide, 2 * thin)
        sums = total[q, :, rows].astype(jnp.float32)
        for arrival in arrivals:
            deep_copy(arrival).wait_recv()
            sums = sums + deep_in[arrival - 1].astype(jnp.float32)
        total[q, :, rows] = sums.astype(total.dtype)

    def add_corner(group, side, source):
        rows = pl.ds(wide + side * thin, thin)
        total[0, group, rows] = (
            total[0, group, rows].astype(jnp.float32) + source.astype(jnp.float32)
        ).astype(total.dtype)

    def deep_step(i):
        @pl.when(i == 0)
        def _():
            deep_copy(3).start()

        @pl.when(i == 1)
        def _():
            add_deep(2, 3)
            deep_copy(2).start()

        @pl.when(i == 2)
        def _():
            deep_copy(1).start()

        @pl.when(i == 3)
        def _():
            add_deep(0, 1, 2)
            for corner in (*y_corners[:2], *x_corners[:2]):
                corner.start()

        @pl.when(i == 4)
        def _():
            y_corners[0].wait_recv()
            add_corner(1, 0, deep_y[0])
            x_corners[2].start()
            x_corners[0].wait_recv()
            add_corner(2, 1, deep_x[0])
            y_corners[2].start()

    def add(group, q, side, source):
        rows = pl.ds(side * half, half)
        total[q, group, rows] = (
            total[q, group, rows].astype(jnp.float32) + source.astype(jnp.float32)
        ).astype(total.dtype)

    def begin(q):
        rows_back(q, 1 - c)
        for group in range(4):
            outgoing[q, group] = part(block_of(group, q, 1 - c), group).astype(total.dtype)
            across(group, q).start()
        rows_back(q, c)
        for group in range(4):
            sums = part(block_of(group, q, c), group)
            across(group, q).wait_recv()
            total[q, group] = (sums + core_in[q, group].astype(jnp.float32)).astype(total.dtype)
            if group == 0:
                x_copy(0, q, 0, 0).start()
                y_copy(0, q, 1, 0).start()
            if group == 1:
                x_copy(1, q, 0, 1).start()
            if group == 2:
                y_copy(2, q, 1, 1).start()

    def middle(q):
        x_copy(0, q, 0, 0).wait_recv()
        add(2, q, 0, x_in[0, q])
        y_copy(2, q, 0, 2).start()
        y_copy(0, q, 1, 0).wait_recv()
        add(1, q, 1, y_in[0, q])
        x_copy(1, q, 1, 2).start()

    def close(q):
        arrivals = (
            ((x_copy(1, q, 0, 1), x_in, 1), (y_copy(2, q, 0, 2), y_in, 2)),
            ((y_copy(2, q, 1, 1), y_in, 1), (x_copy(1, q, 1, 2), x_in, 2)),
        )
        for side in range(2):
            for arrival, _, _ in arrivals[side]:
                arrival.wait_recv()
            rows = pl.ds(side * half, half)
            sums = total[q, 3, rows].astype(jnp.float32)
            for _, source, slot in arrivals[side]:
                sums = sums + source[slot, q].astype(jnp.float32)
            total[q, 3, rows] = sums.astype(total.dtype)

        @pl.when(q == 2)
        def _():
            z_copy(3).wait_recv()
            rows = pl.ds(0, wide)
            total[2, 3, rows] = (
                total[2, 3, rows].astype(jnp.float32) + z_in[2].astype(jnp.float32)
            ).astype(total.dtype)

        @pl.when(q > 0)
        def _():
            z_copy(q).start()

    def done(i):
        return jnp.maximum(i, 0) + jnp.maximum(i - 2, 0)

    begin_loads(0)
    begin_loads(1)

    @pl.loop(0, 6)
    def _(i):
        @pl.when(i < 4)
        def _():
            begin(3 - i)

        @pl.loop(done(i - 1), done(i))
        def _(turn):
            fill(turn)

        deep_step(i)

        @pl.when((i > 0) & (i < 5))
        def _():
            middle(4 - i)

        @pl.when(i > 1)
        def _():
            close(5 - i)

    for turn in (6, 7):
        for store in stores(turn):
            store.wait()
    for q in (1, 2):
        z_copy(q).wait_recv()

    def finish(start, size, *more):
        rows = pl.ds(start, size)
        sums = total[0, 3, rows].astype(jnp.float32)
        for source in more:
            sums = sums + source.astype(jnp.float32)
        out_ref[rows] = sums[:, :width]
        if extended:
            extra_out[rows] = sums[:, width:]

    finish(0, wide, z_in[0], z_in[1])
    for slot in (1, 2):
        y_corners[slot].wait_recv()
        x_corners[slot].wait_recv()
    finish(wide, thin, deep_y[1], deep_x[2])
    finish(wide + thin, thin, deep_x[1], deep_y[2])
    for corner in (*y_corners, *x_corners):
        corner.wait_send()
    for q in range(1, 4):
        z_copy(q).wait_send()
        deep_copy(q).wait_send()

    @pl.loop(0, 4)
    def _(q):
        for group in range(4):
            across(group, q).wait_send()
        x_copy(0, q, 0, 0).wait_send()
        x_copy(1, q, 0, 1).wait_send()
        x_copy(1, q, 1, 2).wait_send()
        y_copy(0, q, 1, 0).wait_send()
        y_copy(2, q, 1, 1).wait_send()
        y_copy(2, q, 0, 2).wait_send()


def scatter_rows(spread, *operands):
    blocks, count, kept = spread.shape
    extended = len(operands) == 6
    width = operands[2].shape[0] if extended else operands[1].shape[1]
    wide = width + 128 if extended else width
    low = operands[0].dtype
    anywhere = pl.BlockSpec(memory_space=pl.ANY)
    resident = (spread, *operands[: 5 if extended else 4])
    outs = [jax.ShapeDtypeStruct((count, width), jnp.float32)]
    if extended:
        outs.append(jax.ShapeDtypeStruct((count, 128), jnp.float32))
        hidden = operands[0].shape[2]
        outs += [jax.ShapeDtypeStruct((width, hidden), jnp.float32)] * 2
        out_specs = in_vmem(2) + [anywhere] * 2
        filler = [
            pltpu.VMEM((2, blocks, kept, width // 8), low),
            pltpu.VMEM((2, 2, width // 8, hidden), jnp.float32),
            copies(2, 1),
            copies(2, 2),
        ]
    else:
        hidden = operands[0].shape[2]
        outs += [
            jax.ShapeDtypeStruct((blocks, kept, width), low),
            jax.ShapeDtypeStruct((blocks, kept, hidden), low),
            jax.ShapeDtypeStruct((blocks, kept, hidden), low),
            jax.ShapeDtypeStruct((blocks, kept, 128), low),
        ]
        out_specs = in_vmem(1) + [anywhere] * 3 + in_vmem(1)
        filler = [
            pltpu.VMEM((2, 4, count, width), low),
            pltpu.VMEM((2, 2, 4 * kept, hidden), jnp.float32),
            pltpu.VMEM((2, 4 * kept, width), low),
            pltpu.VMEM((2, 2, 4 * kept, hidden), low),
            copies(2, 12),
            copies(2, 12),
        ]
    return pl.pallas_call(
        functools.partial(scatter_kernel, extended),
        out_shape=outs,
        in_specs=[anywhere] * (1 + len(operands)),
        out_specs=out_specs,
        scratch_shapes=filler
        + [pltpu.VMEM(operand.shape, operand.dtype) for operand in resident]
        + [
            copies(len(resident)),
            pltpu.VMEM((4, 4, count, wide), low),
            pltpu.VMEM((4, 4, count, wide), low),
            pltpu.VMEM((4, 4, count, wide), low),
            pltpu.VMEM((4 * kept, width), low),
            pltpu.VMEM((3, 4, count * 3 // 8, wide), low),
            pltpu.VMEM((3, 4, count * 3 // 8, wide), low),
            pltpu.VMEM((3, count * 3 // 4, wide), low),
            pltpu.VMEM((3, 4, count // 4, wide), low),
            pltpu.VMEM((3, count // 8, wide), low),
            pltpu.VMEM((3, count // 8, wide), low),
            copies(4, 4),
            copies(4, 4),
            copies(3, 4),
            copies(3, 4),
            copies(3, 4),
            copies(3, 4),
            copies(3),
            copies(3),
            copies(3),
            copies(3),
            copies(2, 3),
            copies(2, 3),
        ],
        compiler_params=settings(2 if extended else 8),
    )(spread, *operands)


def reduce_kernel(
    cuts,
    parts_ref,
    own_ref,
    vector_ref,
    query_out,
    key_out,
    value_out,
    every_out,
    vector_out,
    sums_out,
    own_sent,
    own_got,
    own_side_sent,
    own_side_got,
    stored,
    *refs,
):
    z, y, x, c = spot()
    member, shard = lax.axis_index("exp"), lax.axis_index("fsdp")
    y_peer = where_is(z, 1 - y, x, c)
    near_z, far_z = where_is(along_z(z, 1), y, x, c), where_is(along_z(z, 2), y, x, c)
    members = [((member + j) % 8, shard) for j in range(8)]
    shards = [(member, (shard + j) % 4) for j in range(4)]
    greet(members[1:] + shards[1:])
    pieces = len(cuts)
    first_got, first_held, first_z = refs[:3]
    y_got_in, y_held, y_z = refs[3:5], refs[5:7], refs[7:9]
    shard_in, member_own, member_in = refs[3 * pieces : 3 * pieces + 3]
    (
        y_sent,
        y_got,
        z_sent,
        z_got,
        back_sent,
        back_got,
        side_sent,
        side_got,
        shard_sent,
        shard_got,
        member_sent,
        member_got,
    ) = refs[3 * pieces + 3 :]

    def shard_copy(j):
        return remote(
            vector_ref.at[(shard + j) % 4],
            shard_in.at[(4 - j) % 4],
            shard_sent.at[j],
            shard_got.at[(4 - j) % 4],
            shards[j],
        )

    def member_copy(j):
        return remote(
            member_own,
            member_in.at[(8 - j) % 8],
            member_sent.at[j],
            member_got.at[(8 - j) % 8],
            members[j],
        )

    def rows(which):
        return pl.ds(*cuts[which])

    def z_peer(q):
        return far_z if q == 2 else near_z

    def y_copy(which, q):
        return remote(
            parts_ref.at[1 - y, along_z(z, q), rows(which)],
            y_got_in[which - 1].at[q],
            y_sent.at[which, q],
            y_got.at[which, q],
            y_peer,
        )

    def z_copy(which, q):
        if which:
            source, target = y_held[which - 1].at[q], y_z[which - 1].at[q]
        elif q == 2:
            source, target = first_held, first_z.at[2]
        else:
            source, target = parts_ref.at[:, along_z(z, q), rows(0)], first_z.at[q]
        return remote(source, target, z_sent.at[which, q], z_got.at[which, q], z_peer(q))

    def first_y():
        return remote(
            first_z.at[0, 1 - y], first_got, y_sent.at[0, 0], y_got.at[0, 0], y_peer
        )

    def place(side, q, which):
        return sums_out.at[side, along_z(z, q), rows(which)]

    def back_copy(which, q):
        held = along_z(z, 2) if q == 3 else z
        if which:
            view = sums_out.at[y, held, rows(which)]
        else:
            view = sums_out.at[:, held, rows(0)]
        return remote(view, view, back_sent.at[which, q], back_got.at[which, q], z_peer(q))

    def side_copy(which, q):
        view = place(y, q, which)
        return remote(view, view, side_sent.at[which, q], side_got.at[which, q], y_peer)

    def own_copy(q):
        view = every_out.at[along_z(z, 2) if q == 3 else z, y]
        return remote(view, view, own_sent.at[q], own_got.at[q], z_peer(q))

    def own_side(q):
        view = every_out.at[along_z(z, q), y]
        return remote(view, view, own_side_sent.at[q], own_side_got.at[q], y_peer)

    def pass_on(q):
        own_copy(q).wait_recv()
        if q == 2:
            own_copy(3).start()
        own_side(q).start()

    def exports(side, q):
        zone = along_z(z, q)
        head, rows = side * 2 + zone // 2, zone % 2
        made, start = [], 0
        for i, out in enumerate((query_out, key_out, value_out)):
            size, depth = out.shape[1] // 4, parts_ref.shape[2]
            source = sums_out.at[side, zone, :, pl.ds(start, size)]
            target = out.at[
                pl.ds(pl.multiple_of(rows * depth, depth), depth),
                pl.ds(pl.multiple_of(head * size, size), size),
            ]
            made.append(pltpu.make_async_copy(source, target, stored.at[side, q, i]))
            start += size
        return made

    later = range(1, pieces)
    every_out[z, y] = own_ref[...]
    for j in range(1, 4):
        shard_copy(j).start()
    z_copy(0, 3).start()
    own_copy(1).start()
    own_copy(2).start()
    for q in (3, 2, 1, 0):
        for which in later:
            y_copy(which, q).start()
    z_copy(0, 1).start()
    own_side(0).start()

    for j in range(1, 4):
        shard_copy(j).wait_recv()
    sums = vector_ref[shard]
    for j in range(1, 4):
        sums = sums + shard_in[j]
    member_own[...] = sums
    for j in range(1, 8):
        member_copy(j).start()

    def add_y(which, q):
        y_copy(which, q).wait_recv()
        sums = parts_ref[y, along_z(z, q), rows(which)].astype(jnp.float32)
        sums = sums + y_got_in[which - 1][q].astype(jnp.float32)
        held, z_in = y_held[which - 1], y_z[which - 1]
        if q == 2:
            z_copy(which, 3).wait_recv()
            sums = sums + z_in[3].astype(jnp.float32)
        if q:
            held[q] = sums.astype(held.dtype)
            z_copy(which, q).start()
            return
        for turn in (1, 2):
            z_copy(which, turn).wait_recv()
            sums = sums + z_in[turn].astype(jnp.float32)
        sums_out[y, z, rows(which)] = sums.astype(sums_out.dtype)
        side_copy(which, 0).start()
        back_copy(which, 2).start()
        back_copy(which, 1).start()

    for which in later:
        add_y(which, 3)
    z_copy(0, 3).wait_recv()
    first_held[...] = (
        parts_ref[:, along_z(z, 2), rows(0)].astype(jnp.float32) + first_z[3].astype(jnp.float32)
    ).astype(first_held.dtype)
    z_copy(0, 2).start()
    pass_on(1)
    for which in later:
        add_y(which, 2)
    pass_on(2)
    z_copy(0, 1).wait_recv()
    z_copy(0, 2).wait_recv()
    first_z[0] = (
        parts_ref[:, z, rows(0)].astype(jnp.float32)
        + first_z[1].astype(jnp.float32)
        + first_z[2].astype(jnp.float32)
    ).astype(first_z.dtype)
    first_y().start()
    for which in later:
        add_y(which, 1)
    pass_on(3)
    first_y().wait_recv()
    sums = first_z[0, y].astype(jnp.float32) + first_got[...].astype(jnp.float32)
    sums_out[y, z, rows(0)] = sums.astype(sums_out.dtype)
    side_copy(0, 0).start()
    for which in later:
        add_y(which, 0)
    side_copy(0, 0).wait_recv()
    back_copy(0, 2).start()
    back_copy(0, 1).start()

    for j in range(1, 8):
        member_copy(j).wait_recv()
    sums = member_own[...]
    for j in range(1, 8):
        sums = sums + member_in[j]
    vector_out[...] = sums

    for q in (1, 2, 3):
        for which in later:
            back_copy(which, q).wait_recv()
            if q == 2:
                back_copy(which, 3).start()
            side_copy(which, q).start()
        back_copy(0, q).wait_recv()
        if q == 2:
            back_copy(0, 3).start()

    for q in range(4):
        for export in exports(y, q):
            export.start()
    for q in range(4):
        for which in later:
            side_copy(which, q).wait_recv()
        for export in exports(1 - y, q):
            export.start()
    for q in range(4):
        own_side(q).wait_recv()
    for q in range(4):
        for side in (y, 1 - y):
            for export in exports(side, q):
                export.wait()
    for q in range(4):
        own_side(q).wait_send()
        if q:
            own_copy(q).wait_send()
    for which in range(pieces):
        for q in range(4):
            if which:
                y_copy(which, q).wait_send()
                side_copy(which, q).wait_send()
            if q:
                z_copy(which, q).wait_send()
                back_copy(which, q).wait_send()
    side_copy(0, 0).wait_send()
    first_y().wait_send()
    for j in range(1, 4):
        shard_copy(j).wait_send()
    for j in range(1, 8):
        member_copy(j).wait_send()


def reduce_over_members(parts, own, vectors, widths):
    low = parts.dtype
    depth, width = parts.shape[2:]
    early = depth // 4 // 16 * 16
    half = (depth - early) // 2 // 16 * 16
    cuts = ((0, early), (early, half), (early + half, depth - early - half))
    anywhere = pl.BlockSpec(memory_space=pl.ANY)

    def quarters(*lead):
        return [pltpu.VMEM((*lead, size, width), low) for _, size in cuts[1:]]

    return pl.pallas_call(
        functools.partial(reduce_kernel, cuts),
        out_shape=[jax.ShapeDtypeStruct((2 * depth, size), low) for size in widths]
        + [
            jax.ShapeDtypeStruct((4, 2, *own.shape), low),
            jax.ShapeDtypeStruct(vectors.shape[1:], vectors.dtype),
        ],
        in_specs=in_vmem(3),
        out_specs=[anywhere] * 3 + in_vmem(2),
        scratch_shapes=[
            pltpu.VMEM(parts.shape, low),
            copies(4),
            copies(4),
            copies(4),
            copies(4),
            copies(2, 4, 3),
            pltpu.VMEM((early, width), low),
            pltpu.VMEM((2, early, width), low),
            pltpu.VMEM((4, 2, early, width), low),
            *quarters(4),
            *quarters(4),
            *quarters(4),
            pltpu.VMEM(vectors.shape, vectors.dtype),
            pltpu.VMEM(vectors.shape[1:], vectors.dtype),
            pltpu.VMEM((8, *vectors.shape[1:]), vectors.dtype),
        ]
        + [copies(3, 4)] * 8
        + [copies(4)] * 2
        + [copies(8)] * 2,
        compiler_params=settings(3),
    )(parts, own, vectors)


def project_kernel(
    x_ref,
    routes_ref,
    gain_ref,
    query_ref,
    key_ref,
    value_ref,
    raw_out,
    hidden_out,
    routes_out,
    scale,
    x_in,
    scale_in,
    outgoing,
    core_in,
    across_x,
    x_sums,
    slice_sent,
    slice_got,
    scale_sent,
    scale_got,
    core_sent,
    core_got,
    x_sent,
    x_got,
    route_sent,
    route_got,
):
    z, y, x, c = spot()
    member, shard = lax.axis_index("exp"), lax.axis_index("fsdp")
    mine = number(z, y, x, c)
    count, depth = hidden_out.shape[1:]
    wide, narrow = query_ref.shape[1] // 4, key_ref.shape[1] // 4

    def everyone(j):
        other = (mine + j) % 32
        return (other // 4, other % 4)

    barrier = pltpu.get_barrier_semaphore()

    @pl.loop(1, 32)
    def _(j):
        pl.semaphore_signal(barrier, inc=1, device_id=everyone(j), device_id_type=MESH)

    pl.semaphore_wait(barrier, 31)

    def slice_copy(j):
        place = (shard + j) % 4
        return remote(
            x_ref.at[:, pl.ds(pl.multiple_of(place * depth, depth), depth)],
            x_in.at[(4 - j) % 4],
            slice_sent.at[j],
            slice_got.at[(4 - j) % 4],
            (member, place),
        )

    def scale_copy(j):
        return remote(
            scale,
            scale_in.at[(4 - j) % 4],
            scale_sent.at[j],
            scale_got.at[(4 - j) % 4],
            (member, (shard + j) % 4),
        )

    def route_copy(j):
        return remote(
            routes_ref, routes_out.at[mine], route_sent.at[j], route_got.at[(32 - j) % 32], everyone(j)
        )

    for j in range(1, 4):
        slice_copy(j).start()
    values = x_ref[...].astype(jnp.float32)
    scale[...] = jnp.broadcast_to(
        lax.rsqrt(jnp.mean(values * values, axis=1, keepdims=True) + EPSILON), scale.shape
    )
    for j in range(1, 4):
        scale_copy(j).start()
    routes_out[mine] = routes_ref[...]

    @pl.loop(1, 32)
    def _(j):
        route_copy(j).start()

    def hide(owner, piece, factor):
        gain = gain_ref[...].astype(jnp.float32)
        hidden = piece.astype(jnp.float32) * factor[:, :1] * gain
        hidden_out[owner] = hidden.astype(hidden_out.dtype)

    hide(shard, x_ref[:, pl.ds(pl.multiple_of(shard * depth, depth), depth)], scale[...])

    def take(owner):
        slot = (owner - shard + 4) % 4
        remote(x_in.at[slot], x_in.at[slot], slice_sent.at[slot], slice_got.at[slot], (member, owner)).wait_recv()
        remote(scale, scale_in.at[slot], scale_sent.at[slot], scale_got.at[slot], (member, owner)).wait_recv()
        hide(owner, x_in[slot], scale_in[slot])

    def partial(side, target):
        rows = jnp.concatenate([hidden_out[side * 2], hidden_out[side * 2 + 1]], axis=0)
        parts = []
        for weight, size in ((query_ref, wide), (key_ref, narrow), (value_ref, narrow)):
            columns = pl.ds(pl.multiple_of(target * size, size), size)
            parts.append(jnp.dot(rows, weight[:, columns], preferred_element_type=jnp.float32))
        return jnp.concatenate(parts, axis=1)

    core_peer, x_peer = where_is(z, y, x, 1 - c), where_is(z, y, 1 - x, c)

    def core_copy(turn, far):
        return remote(
            outgoing.at[turn, far],
            core_in.at[turn, far],
            core_sent.at[turn, far],
            core_got.at[turn, far],
            core_peer,
        )

    def x_copy(turn):
        return remote(across_x.at[turn], x_sums.at[turn], x_sent.at[turn], x_got.at[turn], x_peer)

    low = outgoing.dtype
    for turn in range(2):
        side = x if turn == 0 else 1 - x
        if turn == 0:
            take(side * 2 + 1 - c)
        else:
            take(side * 2 + c)
            take(side * 2 + 1 - c)
        outgoing[turn, 1] = partial(side, (1 - x) * 2 + 1 - c).astype(low)
        core_copy(turn, 1).start()
        sums = partial(side, (1 - x) * 2 + c)
        core_copy(turn, 1).wait_recv()
        across_x[turn] = (sums + core_in[turn, 1].astype(jnp.float32)).astype(low)
        x_copy(turn).start()
        outgoing[turn, 0] = partial(side, x * 2 + 1 - c).astype(low)
        core_copy(turn, 0).start()

    for turn in range(2):
        side = x if turn == 0 else 1 - x
        sums = partial(side, x * 2 + c)
        core_copy(turn, 0).wait_recv()
        sums = sums + core_in[turn, 0].astype(jnp.float32)
        raw_out[side * 2] = sums[:count]
        raw_out[side * 2 + 1] = sums[count:]

    for turn in range(2):
        side = 1 - x if turn == 0 else x
        x_copy(turn).wait_recv()
        raw_out[side * 2] += x_sums[turn, :count].astype(jnp.float32)
        raw_out[side * 2 + 1] += x_sums[turn, count:].astype(jnp.float32)

    @pl.loop(1, 32)
    def _(j):
        remote(
            routes_ref, routes_out.at[(mine + j) % 32], route_sent.at[j], route_got.at[j], everyone(j)
        ).wait_recv()

    @pl.loop(1, 32)
    def _(j):
        route_copy(j).wait_send()

    for j in range(1, 4):
        slice_copy(j).wait_send()
        scale_copy(j).wait_send()
    for turn in range(2):
        x_copy(turn).wait_send()
        for far in range(2):
            core_copy(turn, far).wait_send()


def project_tokens(tokens, routes, gain, w_query, key_weight, value_weight):
    count = tokens.shape[0]
    depth = w_query.shape[0]
    own = (w_query.shape[1] + key_weight.shape[1] + value_weight.shape[1]) // 4
    low = tokens.dtype
    return pl.pallas_call(
        project_kernel,
        out_shape=[
            jax.ShapeDtypeStruct((4, count, own), jnp.float32),
            jax.ShapeDtypeStruct((4, count, depth), low),
            jax.ShapeDtypeStruct((32, *routes.shape), routes.dtype),
        ],
        in_specs=in_vmem(6),
        out_specs=in_vmem(3),
        scratch_shapes=[
            pltpu.VMEM((count, 128), jnp.float32),
            pltpu.VMEM((4, count, depth), low),
            pltpu.VMEM((4, count, 128), jnp.float32),
            pltpu.VMEM((2, 2, 2 * count, own), low),
            pltpu.VMEM((2, 2, 2 * count, own), low),
            pltpu.VMEM((2, 2 * count, own), low),
            pltpu.VMEM((2, 2 * count, own), low),
            copies(4),
            copies(4),
            copies(4),
            copies(4),
            copies(2, 2),
            copies(2, 2),
            copies(2),
            copies(2),
            copies(32),
            copies(32),
        ],
        compiler_params=settings(4),
    )(tokens, routes, gain, w_query, key_weight, value_weight)


def turned(values):
    return pltpu.roll(values, HEAD_WIDTH // 2, 1)


def signed(sine):
    lanes = lax.broadcasted_iota(jnp.int32, sine.shape, 1)
    return jnp.where(lanes < HEAD_WIDTH // 2, -sine, sine)


def finish_kernel(
    row,
    sequences,
    raw_ref,
    notes_ref,
    query_gain_ref,
    key_gain_ref,
    weight_ref,
    x_ref,
    gain_ref,
    middle_out,
    normed_out,
    attended_out,
    probs_out,
    query_out,
    key_out,
    cosine_out,
    sine_out,
    outgoing,
    core_in,
    across_x,
    x_sums,
    core_sent,
    core_got,
    x_sent,
    x_got,
):
    z, y, x, c = spot()
    count = x_ref.shape[0]
    core_peer, x_peer = where_is(z, y, x, 1 - c), where_is(z, y, 1 - x, c)
    greet([core_peer, x_peer])
    heads = query_out.shape[2] // HEAD_WIDTH
    wide = heads * HEAD_WIDTH

    def place(block):
        down = lax.broadcasted_iota(jnp.int32, (count, count), 0)
        along = lax.broadcasted_iota(jnp.int32, (count, count), 1)
        end = jnp.zeros((1, 1), jnp.int32)
        start = jnp.zeros((count, count), jnp.int32)
        own, other = start, start
        for i in range(sequences - 1):
            length = notes_ref[block, row : row + 1, i : i + 1]
            end = end + length
            own = own + jnp.where(down >= end, 1, 0)
            other = other + jnp.where(along >= end, 1, 0)
            start = start + jnp.where(down >= end, length, 0)
        return down - start, (own == other) & (along <= down)

    def attend(block):
        position, allowed = place(block)
        lanes = lax.broadcasted_iota(jnp.int32, position.shape, 1)
        spin = lanes % (HEAD_WIDTH // 2)
        inverse = jnp.exp(spin.astype(jnp.float32) * (-2.0 * math.log(THETA) / HEAD_WIDTH))
        angles = position.astype(jnp.float32) * inverse
        cosine, sine = jnp.cos(angles), jnp.sin(angles)
        cosine_out[block] = cosine
        sine_out[block] = sine
        flipped = signed(sine)

        def normal(values, gain):
            scale = lax.rsqrt(jnp.mean(values * values, axis=1, keepdims=True) + EPSILON)
            values = values * scale * gain
            return (values * cosine + turned(values) * flipped).astype(query_out.dtype)

        key = normal(raw_ref[block, :, wide : wide + HEAD_WIDTH], key_gain_ref[...])
        key_out[block] = key
        value = raw_ref[block, :, wide + HEAD_WIDTH :].astype(query_out.dtype)
        for head in range(heads):
            columns = slice(head * HEAD_WIDTH, (head + 1) * HEAD_WIDTH)
            query = normal(raw_ref[block, :, columns], query_gain_ref[...])
            query_out[block, :, columns] = query
            scores = right_transposed(query, key) * HEAD_WIDTH ** (-0.5)
            scores = jnp.where(allowed, scores, MASKED)
            raised = jnp.exp(scores - jnp.max(scores, axis=1, keepdims=True))
            probs = raised / jnp.sum(raised, axis=1, keepdims=True)
            probs_out[block, head] = probs
            attended_out[block, :, columns] = jnp.dot(
                probs.astype(value.dtype), value, preferred_element_type=jnp.float32
            ).astype(attended_out.dtype)

    def core_copy(far):
        return remote(
            outgoing.at[far], core_in.at[far], core_sent.at[far], core_got.at[far], core_peer
        )

    def x_copy():
        return remote(across_x, x_sums, x_sent, x_got, x_peer)

    @pl.loop(0, 4)
    def _(i):
        block = (1 - x + i // 2) % 2 * 2 + (1 - c + i) % 2
        far = 1 - i // 2
        attend(block)
        product = jnp.dot(attended_out[block], weight_ref[...], preferred_element_type=jnp.float32)

        @pl.when(i % 2 == 0)
        def _():
            outgoing[far] = product.astype(outgoing.dtype)
            core_copy(far).start()

        @pl.when(i == 1)
        def _():
            core_copy(1).wait_recv()
            across_x[...] = (product + core_in[1].astype(jnp.float32)).astype(across_x.dtype)
            x_copy().start()

        @pl.when(i == 3)
        def _():
            core_copy(0).wait_recv()
            sums = product + x_ref[...].astype(jnp.float32)
            middle_out[...] = sums + core_in[0].astype(jnp.float32)

    x_copy().wait_recv()
    middle = middle_out[...] + x_sums[...].astype(jnp.float32)
    middle_out[...] = middle
    scale = lax.rsqrt(jnp.mean(middle * middle, axis=1, keepdims=True) + EPSILON)
    normed_out[...] = (middle * scale * gain_ref[...]).astype(normed_out.dtype)
    x_copy().wait_send()
    core_copy(0).wait_send()
    core_copy(1).wait_send()


def finish_attention(raw, notes, row, sequences, q_gain, k_gain, w_out, tokens, gain):
    count, width = tokens.shape
    low = tokens.dtype
    wide = w_out.shape[0]
    heads = wide // HEAD_WIDTH
    return pl.pallas_call(
        functools.partial(finish_kernel, row, sequences),
        out_shape=[
            jax.ShapeDtypeStruct((count, width), jnp.float32),
            jax.ShapeDtypeStruct((count, width), low),
            jax.ShapeDtypeStruct((4, count, wide), low),
            jax.ShapeDtypeStruct((4, heads, count, count), jnp.float32),
            jax.ShapeDtypeStruct((4, count, wide), low),
            jax.ShapeDtypeStruct((4, count, HEAD_WIDTH), low),
            jax.ShapeDtypeStruct((4, count, HEAD_WIDTH), jnp.float32),
            jax.ShapeDtypeStruct((4, count, HEAD_WIDTH), jnp.float32),
        ],
        in_specs=in_vmem(7),
        out_specs=in_vmem(8),
        scratch_shapes=[
            pltpu.VMEM((2, count, width), low),
            pltpu.VMEM((2, count, width), low),
            pltpu.VMEM((count, width), low),
            pltpu.VMEM((count, width), low),
            copies(2),
            copies(2),
            copies(),
            copies(),
        ],
        compiler_params=settings(5),
    )(raw, notes, q_gain, k_gain, w_out, tokens, gain)


def branch_kernel(
    branch_ref, weight_ref, grad_out, every_out, x_sent, x_got, core_sent, core_got
):
    z, y, x, c = spot()
    mine = x * 2 + c
    core_peer, x_peer = where_is(z, y, x, 1 - c), where_is(z, y, 1 - x, c)
    half = branch_ref.shape[0] // 2
    greet([core_peer, x_peer])
    every_out[mine] = branch_ref[...]

    def x_copy(part):
        rows = pl.ds(part * half, half)
        return remote(
            branch_ref.at[rows], every_out.at[mine, rows], x_sent.at[part], x_got.at[part], x_peer
        )

    def core_copy(far, part):
        view = every_out.at[(1 - x if far else x) * 2 + c, pl.ds(part * half, half)]
        return remote(view, view, core_sent.at[far, part], core_got.at[far, part], core_peer)

    def back(place):
        grad_out[place] = right_transposed(every_out[place], weight_ref[...]).astype(grad_out.dtype)

    for part in range(2):
        x_copy(part).start()
        core_copy(0, part).start()
    back(mine)
    for part in range(2):
        core_copy(0, part).wait_recv()
    back(x * 2 + 1 - c)
    for part in range(2):
        x_copy(part).wait_recv()
        core_copy(1, part).start()
    back((1 - x) * 2 + c)
    for part in range(2):
        core_copy(1, part).wait_recv()
    back((1 - x) * 2 + 1 - c)
    for part in range(2):
        x_copy(part).wait_send()
        core_copy(0, part).wait_send()
        core_copy(1, part).wait_send()


def branch_back(branch, w_out):
    count, width = branch.shape
    low = branch.dtype
    return pl.pallas_call(
        branch_kernel,
        out_shape=[
            jax.ShapeDtypeStruct((4, count, w_out.shape[0]), low),
            jax.ShapeDtypeStruct((4, count, width), low),
        ],
        in_specs=in_vmem(2),
        out_specs=in_vmem(2),
        scratch_shapes=[copies(2), copies(2), copies(2, 2), copies(2, 2)],
        compiler_params=settings(6),
    )(branch, w_out)


def heads_kernel(
    branch_ref,
    raw_ref,
    probs_ref,
    rotated_ref,
    rotated_key_ref,
    cosine_ref,
    sine_ref,
    query_gain_ref,
    key_gain_ref,
    hidden_ref,
    query_ref,
    key_ref,
    value_ref,
    weight_out,
    first_out,
    gains_out,
    every,
    outgoing,
    total,
    x_sent,
    x_got,
    core_sent,
    core_got,
    back_sent,
    back_got,
):
    z, y, x, c = spot()
    member, shard = lax.axis_index("exp"), lax.axis_index("fsdp")
    core_peer, x_peer = where_is(z, y, x, 1 - c), where_is(z, y, 1 - x, c)
    peers = [(member, (shard + j) % 4) for j in range(1, 4)]
    greet(peers)
    rows = every.shape[1]
    count = rows // 4
    depth = hidden_ref.shape[1]
    wide, narrow = query_ref.shape[1] // 4, key_ref.shape[1] // 4
    low = every.dtype

    def attention_back(block):
        cosine = cosine_ref[block]
        flipped = signed(sine_ref[block])

        def unturn(grads):
            return grads * cosine + turned(grads * flipped)

        def normal_back(grads, values, gain, into):
            scale = lax.rsqrt(jnp.mean(values * values, axis=1, keepdims=True) + EPSILON)
            hat = values * scale
            gains_out[into : into + 1] += jnp.sum(grads * hat, axis=0, keepdims=True)
            grads = grads * gain
            return scale * (grads - hat * jnp.mean(grads * hat, axis=1, keepdims=True))

        rotated_key = rotated_key_ref[block]
        value = raw_ref[block, :, wide + narrow :].astype(low)
        place = pl.ds(block * count, count)
        value_grad = key_grad = None
        for head in range(wide // HEAD_WIDTH):
            columns = slice(head * HEAD_WIDTH, (head + 1) * HEAD_WIDTH)
            grads = branch_ref[block, :, columns]
            probs = probs_ref[block, head]
            prob_grad = right_transposed(grads, value)
            term = left_trans(probs.astype(low), grads)
            value_grad = term if value_grad is None else value_grad + term
            balance = jnp.sum(probs * prob_grad, axis=1, keepdims=True)
            score_grad = (probs * (prob_grad - balance)).astype(low)
            query_grad = jnp.dot(score_grad, rotated_key, preferred_element_type=jnp.float32)
            term = left_trans(score_grad, rotated_ref[block, :, columns])
            key_grad = term if key_grad is None else key_grad + term
            query_grad = unturn(query_grad * HEAD_WIDTH ** (-0.5))
            query_grad = normal_back(
                query_grad, raw_ref[block, :, columns], query_gain_ref[...], 0
            )
            every[shard, place, columns] = query_grad.astype(low)
        key_grad = unturn(key_grad * HEAD_WIDTH ** (-0.5))
        key_grad = normal_back(
            key_grad, raw_ref[block, :, wide : wide + narrow], key_gain_ref[...], 1
        )
        every[shard, place, wide : wide + narrow] = key_grad.astype(low)
        every[shard, place, wide + narrow :] = value_grad.astype(low)

    def x_copy(part):
        view = every.at[shard, pl.ds(part * count, count)]
        return remote(view, view, x_sent.at[part], x_got.at[part], x_peer)

    def core_copy(far, part):
        view = every.at[(1 - x if far else x) * 2 + c, pl.ds(part * count, count)]
        return remote(view, view, core_sent.at[far, part], core_got.at[far, part], core_peer)

    gains_out[...] = jnp.zeros_like(gains_out)

    @pl.loop(0, 4)
    def _(block):
        attention_back(block)
        x_copy(block).start()
        core_copy(0, block).start()

    def weigh(place):
        weight_out[place] = left_trans(hidden_ref[...], every[place]).astype(weight_out.dtype)

    def back(place):
        grads = every[place]
        sums = None
        for weight, size, start in (
            (query_ref, wide, 0),
            (key_ref, narrow, wide),
            (value_ref, narrow, wide + narrow),
        ):
            columns = pl.ds(pl.multiple_of(place * size, size), size)
            term = right_transposed(grads[:, start : start + size], weight[:, columns])
            sums = term if sums is None else sums + term
        return sums

    def place_of(i):
        return (x + i // 2) % 2 * 2 + (c + i) % 2

    @pl.loop(0, 4)
    def _(i):
        @pl.when(i == 1)
        def _():
            for part in range(4):
                core_copy(0, part).wait_recv()

        @pl.when(i == 2)
        def _():
            for part in range(4):
                x_copy(part).wait_recv()
                core_copy(1, part).start()

        @pl.when(i == 3)
        def _():
            for part in range(4):
                core_copy(1, part).wait_recv()

        sums = back(place_of(i))

        @pl.when(i == 0)
        def _():
            total[...] = sums

        @pl.when(i > 0)
        def _():
            total[...] += sums

        @pl.when(i < 2)
        def _():
            weigh(place_of(i))

    for owner in range(4):
        outgoing[owner] = total[owner * count : (owner + 1) * count].astype(outgoing.dtype)

    def back_copy(j):
        place = (shard + j) % 4
        return remote(
            outgoing.at[place],
            first_out.at[shard],
            back_sent.at[j],
            back_got.at[(4 - j) % 4],
            (member, place),
        )

    for j in range(1, 4):
        back_copy(j).start()
    first_out[shard] = outgoing[shard]

    @pl.loop(2, 4)
    def _(i):
        weigh(place_of(i))

    for j in range(1, 4):
        place = (shard + j) % 4
        remote(
            outgoing.at[place], first_out.at[place], back_sent.at[j], back_got.at[j], (member, place)
        ).wait_recv()
    for j in range(1, 4):
        back_copy(j).wait_send()
    for part in range(4):
        x_copy(part).wait_send()
        for far in range(2):
            core_copy(far, part).wait_send()


def heads_back(branch, raw, probs, rotated, tables, gains, hidden, weights):
    rows = 4 * raw.shape[1]
    own = raw.shape[2]
    depth = hidden.shape[1]
    low = hidden.dtype
    operands = (branch, raw, probs, *rotated, *tables, *gains, hidden, *weights)
    return pl.pallas_call(
        heads_kernel,
        out_shape=[
            jax.ShapeDtypeStruct((4, depth, own), low),
            jax.ShapeDtypeStruct((4, rows // 4, depth), low),
            jax.ShapeDtypeStruct((8, HEAD_WIDTH), jnp.float32),
        ],
        in_specs=in_vmem(len(operands)),
        out_specs=in_vmem(3),
        scratch_shapes=[
            pltpu.VMEM((4, rows, own), low),
            pltpu.VMEM((4, rows // 4, depth), low),
            pltpu.VMEM((rows, depth), jnp.float32),
            copies(4),
            copies(4),
            copies(2, 4),
            copies(2, 4),
            copies(4),
            copies(4),
        ],
        compiler_params=settings(7),
    )(*operands)


def moe_gathered(normed, router, routes, capacity, cotangent, weights, notes):
    gate_w, up_w, down_w = weights
    token_count, topk = routes.shape
    experts = router.shape[1]
    all_grads = lax.all_gather(cotangent, BOTH, axis=0, tiled=True)
    padded = jnp.pad(router, ((0, 0), (0, 128 - experts)))
    arrived, active, gate_pre, up_pre, share, select, spread = gather_experts(
        normed, notes, topk, capacity, gate_w, up_w, padded
    )
    mixed, out_rows, gate_pre_grad, up_pre_grad, extra = scatter_rows(
        spread,
        active,
        down_w,
        share,
        select,
        all_grads.reshape(experts, token_count, MODEL_WIDTH),
        gate_pre,
        up_pre,
    )
    summed, back, gate_w_grad, up_w_grad = scatter_rows(
        spread, gate_pre_grad, up_pre_grad, gate_w, up_w, extra, arrived
    )

    def flat(rows):
        return rows.reshape(experts * capacity, rows.shape[2])

    weight_grads = (gate_w_grad, up_w_grad, left_trans(flat(active), flat(out_rows)))
    columns = jnp.arange(experts, dtype=jnp.int32)
    gate_grad = back[:, :experts] + back[:, experts : 2 * experts]
    picks = jnp.any(routes[:, :, None] == columns[None, None, :], axis=1)
    gates = jax.nn.softmax(jnp.where(picks, matrix_product(normed, router), MASKED), axis=1)
    logit_grad = gates * (gate_grad - jnp.sum(gates * gate_grad, axis=1, keepdims=True))
    return mixed, summed, logit_grad.astype(jnp.bfloat16), *weight_grads


def moe_exchanged(normed, router, routes, capacity, cotangent, weights, notes):
    gate_w, up_w, down_w = weights
    token_count, topk = routes.shape
    experts = router.shape[1]
    gates = gates_of(matrix_product(normed, router), routes, experts)
    slots = slot_table(routes, experts, capacity)

    def send(rows):
        packed = jnp.zeros((experts * capacity, MODEL_WIDTH), jnp.bfloat16).at[slots].set(rows)
        return exchange(packed.reshape(experts, capacity, MODEL_WIDTH)).reshape(
            experts * capacity, MODEL_WIDTH
        )

    def bring(rows):
        rows = exchange(rows.reshape(experts, capacity, MODEL_WIDTH))
        return rows.reshape(experts * capacity, MODEL_WIDTH)[slots].reshape(
            token_count, topk, MODEL_WIDTH
        )

    arrived = send(jnp.repeat(normed, topk, axis=0))
    hidden = expert_forward(arrived, gate_w, up_w)
    scaled = (gates[:, :, None] * cotangent.astype(jnp.float32)[:, None, :]).astype(jnp.bfloat16)
    out_rows = send(scaled.reshape(token_count * topk, MODEL_WIDTH))
    rows_back, gate_pre_grad, up_pre_grad = expert_back(out_rows, hidden, gate_w, up_w, down_w)
    gate_w_grad = left_trans(arrived, gate_pre_grad)
    up_w_grad = left_trans(arrived, up_pre_grad)
    down_grad = left_trans(hidden[3], out_rows)
    returned = bring(matrix_product(hidden[3], down_w).astype(jnp.bfloat16))
    mixed = jnp.einsum("tk,tkd->td", gates, returned.astype(jnp.float32))
    gate_grad = jnp.einsum("td,tkd->tk", cotangent, returned, preferred_element_type=jnp.float32)
    summed = jnp.sum(bring(rows_back), axis=1, dtype=jnp.float32)
    picked_grad = gates * (gate_grad - jnp.sum(gates * gate_grad, axis=1, keepdims=True))
    onehot = routes[:, :, None] == jnp.arange(experts, dtype=jnp.int32)[None, None, :]
    logit_grad = jnp.sum(jnp.where(onehot, picked_grad[:, :, None], 0.0), axis=1)
    return mixed, summed, logit_grad.astype(jnp.bfloat16), gate_w_grad, up_w_grad, down_grad


def local(
    tokens,
    lengths,
    routes,
    attn_gain,
    w_query,
    key_weight,
    value_weight,
    q_gain,
    k_gain,
    w_out,
    mlp_gain,
    w_router,
    expert_gate,
    expert_up,
    expert_down,
    cotangent,
):
    shards, members = lax.axis_size("fsdp"), lax.axis_size("exp")
    experts = shards * members
    token_count, topk = routes.shape
    capacity = 2 * token_count * topk // experts
    group = shards * token_count
    depth = w_query.shape[0]
    heads = QUERY_HEADS // shards
    kv_heads = max(1, KEY_VALUE_HEADS // shards)
    copies_of = shards * kv_heads // KEY_VALUE_HEADS
    head_group = heads // kv_heads
    wide, narrow = heads * HEAD_WIDTH, kv_heads * HEAD_WIDTH
    place = lax.axis_index("fsdp")

    gathered = lax.all_gather(
        jnp.concatenate([w_router.reshape(-1), attn_gain, mlp_gain, q_gain, k_gain]), "fsdp"
    )
    cuts, start = [], 0
    for leaf in (w_router, attn_gain, mlp_gain, q_gain, k_gain):
        cuts.append(gathered[:, start : start + leaf.size])
        start += leaf.size
    router = cuts[0].reshape(MODEL_WIDTH, experts)
    gain_attn, gain_mlp, gain_query, gain_key = [
        cut.reshape(-1).astype(jnp.float32) for cut in cuts[1:]
    ]
    dense = (members, shards) == (8, 4) and 2 * capacity >= token_count
    inputs = tokens.astype(jnp.float32)
    scale_one = rms_scale(inputs)
    if dense:
        notes = jnp.pad(
            jnp.concatenate(
                [routes.T, jnp.pad(lengths, ((0, 0), (0, token_count - lengths.shape[1])))], axis=0
            ),
            ((0, 15 - topk), (0, 0)),
        )
        raw, hidden, notes = project_tokens(
            tokens, notes, attn_gain[None], w_query, key_weight, value_weight
        )
        hidden = hidden.reshape(group, depth)
        first = lax.axis_index("exp") * shards
        notes_own = lax.dynamic_slice_in_dim(notes, first, shards)
    else:
        notes = None
        all_lengths = lax.all_gather(lengths[0], "fsdp")

        def by_shard(weight):
            weight = weight.reshape(depth, KEY_VALUE_HEADS, HEAD_WIDTH)
            return jnp.repeat(weight, copies_of, axis=1).reshape(depth, shards, narrow)

        joined = jnp.concatenate(
            [w_query.reshape(depth, shards, wide), by_shard(key_weight), by_shard(value_weight)],
            axis=2,
        ).transpose(1, 0, 2)
        first_normed = (inputs * scale_one * gain_attn).astype(jnp.bfloat16)
        hidden = lax.all_to_all(first_normed, "fsdp", split_axis=1, concat_axis=0, tiled=True)
        partial = contract("gk,nkc->ngc", hidden, joined).astype(jnp.bfloat16)
        raw = lax.psum_scatter(partial, "fsdp", scatter_dimension=0, tiled=True)[0]
        raw = raw.astype(jnp.float32)
    if dense:
        gains = (gain_query[None], gain_key[None])
        middle, normed, attended, probs, *rotated, cosine, sine = finish_attention(
            raw, notes_own, topk, lengths.shape[1], *gains, w_out, tokens, gain_mlp[None]
        )
        attended = attended.reshape(group, wide)
        scale_two = rms_scale(middle)
    else:
        raw = raw.reshape(shards, token_count, wide + 2 * narrow)
        query_raw = raw[:, :, :wide].reshape(shards, token_count, heads, HEAD_WIDTH)
        key_raw = raw[:, :, wide : wide + narrow].reshape(shards, token_count, kv_heads, HEAD_WIDTH)
        value = (
            raw[:, :, wide + narrow :]
            .astype(jnp.bfloat16)
            .reshape(shards, token_count, kv_heads, HEAD_WIDTH)
        )
        position, allowed = jax.vmap(lambda row: seq_layout(row, token_count))(all_lengths)
        cosine, sine = rotary_tables(position, HEAD_WIDTH)
        query_scale = rms_scale(query_raw)
        query_hat = query_raw * query_scale
        key_scale = rms_scale(key_raw)
        key_hat = key_raw * key_scale
        query = (
            rotate(query_hat * gain_query, cosine, sine)
            .astype(jnp.bfloat16)
            .reshape(shards, token_count, kv_heads, head_group, HEAD_WIDTH)
        )
        key = rotate(key_hat * gain_key, cosine, sine).astype(jnp.bfloat16)
        scores = contract("bqkgd,bpkd->bkgqp", query, key) * HEAD_WIDTH ** (-0.5)
        scores = jnp.where(allowed[:, None, None], scores, MASKED)
        top = jnp.max(scores, axis=-1, keepdims=True)
        raised = jnp.exp(scores - top)
        probs = raised / jnp.sum(raised, axis=-1, keepdims=True)
        probs_low = probs.astype(jnp.bfloat16)
        attended = contract("bkgqp,bpkd->bqkgd", probs_low, value).astype(jnp.bfloat16)
        attended = attended.reshape(group, wide)
        mixed_heads = lax.psum_scatter(
            matrix_product(attended, w_out).astype(jnp.bfloat16),
            "fsdp",
            scatter_dimension=0,
            tiled=True,
        )
        middle = inputs + mixed_heads.astype(jnp.float32)
        scale_two = rms_scale(middle)
        normed = (middle * scale_two * gain_mlp).astype(jnp.bfloat16)

    moe = moe_gathered if dense else moe_exchanged
    mixed, summed, logit_grad, gate_w_grad, up_w_grad, down_grad = moe(
        normed,
        router,
        routes,
        capacity,
        cotangent,
        (expert_gate[0], expert_up[0], expert_down[0]),
        notes,
    )
    layer_out = (middle + mixed).astype(jnp.bfloat16)

    upstream = cotangent.astype(jnp.float32)
    normed_grad = summed + right_transposed(logit_grad, router)
    mlp_gain_grad = jnp.sum(normed_grad * middle * scale_two, axis=0)
    router_grad = left_trans(normed, logit_grad)
    middle_grad = upstream + rms_back(normed_grad * gain_mlp, middle, scale_two)
    branch_low = middle_grad.astype(jnp.bfloat16)
    if dense:
        attended_grad, branch_grad = branch_back(branch_low, w_out)
        branch_grad = branch_grad.reshape(group, MODEL_WIDTH)
    else:
        branch_grad = lax.all_gather(branch_low, "fsdp", axis=0, tiled=True)
        attended_grad = right_transposed(branch_grad, w_out).astype(jnp.bfloat16)
    out_w_grad = left_trans(attended, branch_grad).astype(jnp.bfloat16)
    attended_grad, out_w_grad = lax.optimization_barrier((attended_grad, out_w_grad))
    if dense:
        joined_grad, first_grad, gain_grads = heads_back(
            attended_grad,
            raw,
            probs,
            rotated,
            (cosine, sine),
            gains,
            hidden,
            (w_query, key_weight, value_weight),
        )
        first_grad = first_grad.transpose(1, 0, 2).reshape(token_count, MODEL_WIDTH)
        q_gain_grad, k_gain_grad = gain_grads[0], gain_grads[1]
    else:
        attended_grad = attended_grad.reshape(shards, token_count, kv_heads, head_group, HEAD_WIDTH)
        prob_grad = contract("bqkgd,bpkd->bkgqp", attended_grad, value)
        value_grad = contract("bkgqp,bqkgd->bpkd", probs_low, attended_grad)
        balance = jnp.sum(probs * prob_grad, axis=-1, keepdims=True)
        score_grad = (probs * (prob_grad - balance)).astype(jnp.bfloat16)
        query_norm_grad = contract("bkgqp,bpkd->bqkgd", score_grad, key) * HEAD_WIDTH ** (-0.5)
        query_norm_grad = query_norm_grad.reshape(shards, token_count, heads, HEAD_WIDTH)
        key_norm_grad = contract("bkgqp,bqkgd->bpkd", score_grad, query) * HEAD_WIDTH ** (-0.5)
        query_norm_grad = rotate_back(query_norm_grad, cosine, sine)
        key_norm_grad = rotate_back(key_norm_grad, cosine, sine)
        q_gain_grad = jnp.sum(query_norm_grad * query_hat, axis=(0, 1, 2))
        k_gain_grad = jnp.sum(key_norm_grad * key_hat, axis=(0, 1, 2))
        query_grad = rms_back(query_norm_grad * gain_query, query_raw, query_scale)
        key_grad = rms_back(key_norm_grad * gain_key, key_raw, key_scale)
        head_grads = jnp.concatenate(
            [
                query_grad.reshape(group, wide),
                key_grad.reshape(group, narrow),
                value_grad.reshape(group, narrow),
            ],
            axis=1,
        ).astype(jnp.bfloat16)
        head_grads = lax.all_gather(head_grads, "fsdp")
        hidden_grad = contract("ngc,nkc->gk", head_grads, joined).astype(jnp.bfloat16)
        first_grad = lax.all_to_all(
            hidden_grad, "fsdp", split_axis=0, concat_axis=1, tiled=True
        )
        joined_grad = contract("gk,ngc->nkc", hidden, head_grads).astype(jnp.bfloat16)
    first_grad = first_grad.astype(jnp.float32)
    attn_gain_grad = jnp.sum(first_grad * inputs * scale_one, axis=0)
    input_grad = (middle_grad + rms_back(first_grad * gain_attn, inputs, scale_one)).astype(
        jnp.bfloat16
    )

    vectors = jnp.concatenate(
        [
            grad.reshape(shards, -1)
            for grad in (router_grad, attn_gain_grad, mlp_gain_grad, q_gain_grad, k_gain_grad)
        ],
        axis=1,
    )
    if dense:
        rows = -(-vectors.shape[1] // 1024) * 8
        vectors = jnp.pad(vectors, ((0, 0), (0, rows * 128 - vectors.shape[1])))
        started = lengths[0, 0] > 0
        gate_w_grad, up_w_grad = (
            jnp.where(started, grad, 0.0) for grad in (gate_w_grad, up_w_grad)
        )
        out_sum = lax.psum_scatter(out_w_grad, "exp", scatter_dimension=0, tiled=True)
        joined_grad, vectors, out_sum, gate_w_grad, up_w_grad, down_grad = (
            lax.optimization_barrier(
                (joined_grad, vectors, out_sum, gate_w_grad, up_w_grad, down_grad)
            )
        )
        *joined_sum, out_sum, vectors = reduce_over_members(
            joined_grad.reshape(2, 4, -1, wide + 2 * narrow),
            out_sum,
            vectors.reshape(shards, rows, 128),
            (shards * wide, shards * narrow, shards * narrow),
        )
        out_sum, vectors = out_sum.reshape(w_out.shape), vectors.reshape(-1)
    else:
        out_sum = lax.psum(out_w_grad, "exp")
        joined_sum = lax.psum(joined_grad, "exp").astype(jnp.float32)
        vectors = lax.psum(vectors, BOTH)[place]
    if not dense:

        def gather_heads(part):
            part = part.transpose(1, 0, 2).reshape(depth, KEY_VALUE_HEADS, copies_of, HEAD_WIDTH)
            return part.sum(axis=2).reshape(depth, KEY_VALUE_HEADS * HEAD_WIDTH)

        joined_sum = (
            joined_sum[:, :, :wide].transpose(1, 0, 2).reshape(depth, QUERY_HEADS * HEAD_WIDTH),
            gather_heads(joined_sum[:, :, wide : wide + narrow]),
            gather_heads(joined_sum[:, :, wide + narrow :]),
        )
    query_sum, key_sum, value_sum = (part.astype(jnp.float32) for part in joined_sum)
    sums, start = [], 0
    for leaf in (w_router, attn_gain, mlp_gain, q_gain, k_gain):
        sums.append(vectors[start : start + leaf.size].reshape(leaf.shape))
        start += leaf.size

    return (
        layer_out,
        input_grad,
        sums[1],
        query_sum,
        key_sum,
        value_sum,
        sums[3],
        sums[4],
        out_sum.astype(jnp.float32),
        sums[2],
        sums[0],
        gate_w_grad[None],
        up_w_grad[None],
        down_grad[None],
    )


def solution(mesh):
    in_specs = (
        P(("exp", "fsdp"), None),
        P(("exp", "fsdp"), None),
        P(("exp", "fsdp"), None),
        P("fsdp"),
        P("fsdp", None),
        P("fsdp", None),
        P("fsdp", None),
        P("fsdp"),
        P("fsdp"),
        P("fsdp", None),
        P("fsdp"),
        P("fsdp", None),
        P(("exp", "fsdp"), None, None),
        P(("exp", "fsdp"), None, None),
        P(("exp", "fsdp"), None, None),
        P(("exp", "fsdp"), None),
    )
    out_specs = (
        P(("exp", "fsdp"), None),
        P(("exp", "fsdp"), None),
        P("fsdp"),
        P("fsdp", None),
        P("fsdp", None),
        P("fsdp", None),
        P("fsdp"),
        P("fsdp"),
        P("fsdp", None),
        P("fsdp"),
        P("fsdp", None),
        P(("exp", "fsdp"), None, None),
        P(("exp", "fsdp"), None, None),
        P(("exp", "fsdp"), None, None),
    )
    return jax.shard_map(local, mesh=mesh, in_specs=in_specs, out_specs=out_specs, check_vma=False)
```

```python
import functools
import math

import jax
import jax.numpy as jnp
from jax import lax
from jax.experimental import pallas as pl
from jax.experimental.pallas import tpu as pltpu
from jax.sharding import PartitionSpec as P

MODEL_WIDTH = 2048
QUERY_HEADS = 32
KEY_VALUE_HEADS = 4
HEAD_WIDTH = 128


EPSILON = 1e-06
THETA = 1000000.0
MASKED = -1e30
BOTH = ("exp", "fsdp")
MESH = pl.DeviceIdType.MESH


def matrix_product(left, right):
    return jnp.dot(left, right, preferred_element_type=jnp.float32)


def left_trans(left, right):
    return lax.dot_general(
        left, right, (((0,), (0,)), ((), ())), preferred_element_type=jnp.float32
    )


def right_transposed(left, right):
    return lax.dot_general(
        left, right, (((1,), (1,)), ((), ())), preferred_element_type=jnp.float32
    )


def contract(spec, left, right):
    return jnp.einsum(spec, left, right, preferred_element_type=jnp.float32)


def rms_scale(values):
    return lax.rsqrt(jnp.mean(values * values, axis=-1, keepdims=True) + EPSILON)


def rms_back(grad_hat, values, scale):
    normal = values * scale
    return scale * (grad_hat - normal * jnp.mean(grad_hat * normal, axis=-1, keepdims=True))


def seq_layout(length_row, token_count):
    ends = jnp.cumsum(length_row)
    starts = ends - length_row
    places = jnp.arange(token_count, dtype=jnp.int32)
    member = (places[:, None] >= starts[None, :]) & (places[:, None] < ends[None, :])
    numbers = jnp.arange(length_row.shape[0], dtype=jnp.int32)
    segment = jnp.sum(jnp.where(member, numbers[None, :], 0), axis=1)
    position = places - jnp.sum(jnp.where(member, starts[None, :], 0), axis=1)
    allowed = (segment[:, None] == segment[None, :]) & (places[None, :] <= places[:, None])
    return (position, allowed)


def rotary_tables(position, head_size):
    half = head_size // 2
    index = jnp.arange(head_size, dtype=jnp.int32) % half
    inverse = jnp.exp(index.astype(jnp.float32) * (-2.0 * math.log(THETA) / head_size))
    angles = position.astype(jnp.float32)[..., None] * inverse
    return (jnp.cos(angles)[..., None, :], jnp.sin(angles)[..., None, :])


def rotate(values, cosine, sine):
    half = values.shape[-1] // 2
    turned = jnp.concatenate([-values[..., half:], values[..., :half]], axis=-1)
    return values * cosine + turned * sine


def rotate_back(grads, cosine, sine):
    half = grads.shape[-1] // 2
    moved = grads * sine
    return grads * cosine + jnp.concatenate([moved[..., half:], -moved[..., :half]], axis=-1)


def slot_table(route_rows, experts, capacity):
    flat = route_rows.reshape(-1)
    onehot = (flat[:, None] == jnp.arange(experts, dtype=jnp.int32)[None, :]).astype(jnp.int32)
    ranks = jnp.cumsum(onehot, axis=0) - 1
    rank = jnp.sum(ranks * onehot, axis=1)
    return flat * capacity + rank


def exchange(buffer):
    return lax.all_to_all(buffer, BOTH, split_axis=0, concat_axis=0, tiled=True)


def two_halves(values):
    high = values.astype(jnp.bfloat16)
    low = (values - high.astype(jnp.float32)).astype(jnp.bfloat16)
    return high, low


def expert_forward(arrived, gate_w, up_w):
    gate_pre = matrix_product(arrived, gate_w)
    up_pre = matrix_product(arrived, up_w)
    sigma = jax.nn.sigmoid(gate_pre)
    active = (gate_pre * sigma * up_pre).astype(jnp.bfloat16)
    return gate_pre, up_pre, sigma, active


def expert_back(out_rows, hidden, gate_w, up_w, down_w):
    gate_pre, up_pre, sigma, _ = hidden
    active_grad = right_transposed(out_rows, down_w)
    gate_pre_grad = (active_grad * up_pre * (sigma * (1.0 + gate_pre * (1.0 - sigma)))).astype(
        jnp.bfloat16
    )
    up_pre_grad = (active_grad * (gate_pre * sigma)).astype(jnp.bfloat16)
    rows_back = right_transposed(gate_pre_grad, gate_w) + right_transposed(up_pre_grad, up_w)
    return rows_back.astype(jnp.bfloat16), gate_pre_grad, up_pre_grad


def gates_of(logits, routes, experts):
    picked = jnp.take_along_axis(logits, routes, axis=1)
    peak = jnp.max(picked, axis=1, keepdims=True)
    lifted = jnp.exp(picked - peak)
    return lifted / jnp.sum(lifted, axis=1, keepdims=True)


def spot():
    member, shard = lax.axis_index("exp"), lax.axis_index("fsdp")
    return member // 2, member % 2, shard // 2, shard % 2


def where_is(z, y, x, c):
    return (z * 2 + y, x * 2 + c)


def number(z, y, x, c):
    return z * 8 + y * 4 + x * 2 + c


def along_z(z, q):
    return (z // 2 + q // 2) % 2 * 2 + (z % 2 + q % 2) % 2


def greet(peers):
    barrier = pltpu.get_barrier_semaphore()
    for peer in peers:
        pl.semaphore_signal(barrier, inc=1, device_id=peer, device_id_type=MESH)
    pl.semaphore_wait(barrier, len(peers))


def remote(source, target, sent, got, peer):
    return pltpu.make_async_remote_copy(
        src_ref=source,
        dst_ref=target,
        send_sem=sent,
        recv_sem=got,
        device_id=peer,
        device_id_type=MESH,
    )


def in_vmem(count):
    return [pl.BlockSpec(memory_space=pltpu.VMEM)] * count


def copies(*shape):
    return pltpu.SemaphoreType.DMA(shape)


def settings(collective_id):
    return pltpu.CompilerParams(
        collective_id=collective_id, has_side_effects=True, vmem_limit_bytes=60 << 20
    )


def fetching(kernel, count):
    def run(*refs):
        given, refs = refs[:count], refs[count:]
        refs, held, fetched = refs[: -count - 1], refs[-count - 1 : -1], refs[-1]
        fetches = [
            pltpu.make_async_copy(source, target, fetched.at[i])
            for i, (source, target) in enumerate(zip(given, held))
        ]
        for fetch in fetches:
            fetch.start()
        kernel(fetches, *held, *refs)

    return run


def anywhere(count):
    return [pl.BlockSpec(memory_space=pl.ANY)] * count


def room_for(operands):
    held = [pltpu.VMEM(operand.shape, operand.dtype) for operand in operands]
    return held + [copies(len(operands))]


def wait_all(fetches):
    for fetch in fetches:
        fetch.wait()


def gather_kernel(
    topk,
    x_ref,
    notes_ref,
    gate_hbm,
    up_hbm,
    router_ref,
    rows_out,
    active_out,
    gate_out,
    up_out,
    share_out,
    select_out,
    spread_out,
    held,
    gate_ref,
    up_ref,
    picked,
    lively,
    results,
    loaded,
    stored,
    arrive,
    to_z,
    to_y,
    to_x,
    to_core,
    corners,
    deep_z,
    deep_core,
):
    z, y, x, c = spot()
    count = x_ref.shape[0]
    half, thin = count * 3 // 8, count // 8
    cuts = ((0, half), (half, half), (2 * half, thin), (2 * half + thin, thin), (2 * half, 2 * thin))
    kept = select_out.shape[1]
    y_peer, x_peer, core_peer = (
        where_is(z, 1 - y, x, c),
        where_is(z, y, 1 - x, c),
        where_is(z, y, x, 1 - c),
    )
    near_z, far_z = where_is(along_z(z, 1), y, x, c), where_is(along_z(z, 2), y, x, c)
    loads = [
        pltpu.make_async_copy(source, target, loaded.at[i])
        for i, (source, target) in enumerate(
            ((gate_hbm, gate_ref), (up_hbm, up_ref))
        )
    ]
    for load in loads:
        load.start()
    greet([y_peer, x_peer, core_peer, near_z, far_z])
    mine = number(z, y, x, c)

    def copy(block, part, sem, peer):
        view = held.at[block, pl.ds(*cuts[part])]
        return remote(view, view, sem, arrive.at[block, 2 if part == 4 else part], peer)

    def arrived(block, part):
        copy(block, part, to_core.at[0, 0, 0], core_peer).wait_recv()

    def block_of(q, other_y, other_x, core):
        return number(
            along_z(z, q), 1 - y if other_y else y, 1 - x if other_x else x, core
        )

    combos = ((0, 0), (0, 1), (1, 0), (1, 1))

    def stores(slot, blocks):
        made = []
        for k in range(4):
            part = pl.ds(k * kept, kept)
            made.append((picked.at[slot, part], rows_out.at[blocks[k]]))
            made.append((lively.at[slot, part], active_out.at[blocks[k]]))
            for i, out in enumerate((gate_out, up_out)):
                made.append((results.at[slot, i, part], out.at[blocks[k]]))
        return [
            pltpu.make_async_copy(source, target, stored.at[slot, i])
            for i, (source, target) in enumerate(made)
        ]

    def choose(block):
        notes = notes_ref[block]
        own = jnp.zeros((1, count), jnp.float32)
        lines = lax.broadcasted_iota(jnp.int32, (128, count), 0)
        names = jnp.zeros((128, count), jnp.float32)
        for k in range(topk):
            line = notes[k : k + 1]
            own = own + jnp.where(line == mine, 1.0, 0.0)
            names = names + jnp.where(lines == line, 1.0, 0.0)
        before = lax.broadcasted_iota(jnp.int32, (count, count), 0)
        before = before < lax.broadcasted_iota(jnp.int32, (count, count), 1)
        rank = jnp.dot(
            jnp.broadcast_to(own, (8, count)).astype(x_ref.dtype),
            jnp.where(before, 1.0, 0.0).astype(x_ref.dtype),
            preferred_element_type=jnp.float32,
        )[:1]
        places = lax.broadcasted_iota(jnp.int32, (kept, count), 0).astype(jnp.float32)
        chosen = jnp.where((rank == places) & (own > 0), 1.0, 0.0)
        spread_out[block] = jnp.transpose(chosen).astype(spread_out.dtype)
        chosen = chosen.astype(select_out.dtype)
        select_out[block] = chosen
        return chosen, right_transposed(chosen, names.astype(chosen.dtype))

    def work(q, slot):
        core = 1 - c if slot else c
        blocks = [block_of(q, *combo, core) for combo in combos]

        @pl.when(q > 0)
        def _():
            for store in stores(slot, [block_of(q - 1, *combo, core) for combo in combos]):
                store.wait()

        named = []
        for k in range(4):
            chosen, names = choose(blocks[k])
            named.append(names)
            rows = jnp.dot(chosen, held[blocks[k]], preferred_element_type=jnp.float32)
            picked[slot, k * kept : (k + 1) * kept] = rows.astype(picked.dtype)
        rows = picked[slot]
        gate_pre = jnp.dot(rows, gate_ref[...], preferred_element_type=jnp.float32)
        up_pre = jnp.dot(rows, up_ref[...], preferred_element_type=jnp.float32)
        logits = jnp.dot(rows, router_ref[...], preferred_element_type=jnp.float32)
        results[slot, 0] = gate_pre
        results[slot, 1] = up_pre
        active = gate_pre * (1.0 / (1.0 + jnp.exp(-gate_pre))) * up_pre
        lively[slot] = active.astype(lively.dtype)
        for k in range(4):
            part = slice(k * kept, (k + 1) * kept)
            block = blocks[k]
            masked = jnp.where(named[k] > 0, logits[part], MASKED)
            lifted = jnp.exp(masked - jnp.max(masked, axis=1, keepdims=True))
            lanes = lax.broadcasted_iota(jnp.int32, lifted.shape, 1)
            share = jnp.sum(jnp.where(lanes == mine, lifted, 0.0), axis=1, keepdims=True)
            share = share / jnp.sum(lifted, axis=1, keepdims=True)
            share_out[block] = jnp.broadcast_to(share, share_out.shape[1:])
        for store in stores(slot, blocks):
            store.start()

    def forward(q):
        block = block_of(q, 0, 0, c)
        if q:
            arrived(block, 0)
            arrived(block, 1)
        if q == 2:
            copy(block, 0, to_z.at[2, 0], near_z).start()
            copy(block, 1, to_z.at[2, 1], near_z).start()
        copy(block, 0, to_y.at[0, q], y_peer).start()
        copy(block, 1, to_x.at[0, q], x_peer).start()
        copy(block, 0, to_x.at[1, q], x_peer).start()
        copy(block, 1, to_y.at[1, q], y_peer).start()
        copy(block, 0, to_core.at[0, 0, q], core_peer).start()
        copy(block, 1, to_core.at[0, 1, q], core_peer).start()

    def second(q):
        block = block_of(q, 1, 0, c)
        arrived(block, 0)
        copy(block, 0, to_x.at[2, q], x_peer).start()
        copy(block, 0, to_core.at[1, 0, q], core_peer).start()
        block = block_of(q, 0, 1, c)
        arrived(block, 1)
        copy(block, 1, to_y.at[2, q], y_peer).start()
        copy(block, 1, to_core.at[2, 1, q], core_peer).start()

    def last(q):
        block = block_of(q, 0, 1, c)
        arrived(block, 0)
        copy(block, 0, to_core.at[2, 0, q], core_peer).start()
        block = block_of(q, 1, 0, c)
        arrived(block, 1)
        copy(block, 1, to_core.at[1, 1, q], core_peer).start()
        block = block_of(q, 1, 1, c)
        arrived(block, 0)
        copy(block, 0, to_core.at[3, 0, q], core_peer).start()
        arrived(block, 1)
        copy(block, 1, to_core.at[3, 1, q], core_peer).start()

    def others(q):
        for combo in combos:
            block = block_of(q, *combo, 1 - c)
            for part in (0, 1, 4):
                arrived(block, part)

    beside_x, beside_y, across = (block_of(0, *combo, c) for combo in combos[1:])

    def corner(i):
        block = (mine, mine, mine, mine, beside_x, beside_y)[i]
        part, peer = ((2, x_peer), (3, y_peer), (2, y_peer), (3, x_peer), (2, y_peer), (3, x_peer))[i]
        return copy(block, part, corners.at[i], peer)

    def deep_copy(kind, i, block):
        return copy(block, 4, deep_z.at[kind, i], far_z if kind == 1 else near_z)

    def deep_core_copy(q, i, block):
        return copy(block, 4, deep_core.at[q, i], core_peer)

    def deep_first():
        arrived(beside_x, 3)
        arrived(beside_y, 2)
        arrived(across, 2)
        arrived(across, 3)
        for i, combo in enumerate(combos):
            block = block_of(0, *combo, c)
            deep_copy(0, i, block).start()
            deep_copy(1, i, block).start()
            deep_core_copy(0, i, block).start()

    def deep_next(q):
        for i, combo in enumerate(combos):
            block = block_of(q, *combo, c)
            arrived(block, 4)
            if q == 2:
                deep_copy(2, i, block).start()
            deep_core_copy(q, i, block).start()

    held[mine] = x_ref[...]
    for part in range(2):
        copy(mine, part, to_z.at[0, part], near_z).start()
    for part in range(2):
        copy(mine, part, to_z.at[1, part], far_z).start()
    for i in range(4):
        corner(i).start()
    forward(0)
    for load in loads:
        load.wait()
    arrived(beside_x, 2)
    corner(4).start()
    arrived(beside_y, 3)
    corner(5).start()
    forward(1)
    second(0)
    deep_first()
    forward(2)
    second(1)

    @pl.loop(0, 4)
    def _(q):
        last(q)
        work(q, 0)
        others(q)
        work(q, 1)

        @pl.when(q == 0)
        def _():
            forward(3)
            deep_next(1)
            second(2)
            deep_next(2)

        @pl.when(q == 1)
        def _():
            second(3)
            deep_next(3)

    for slot in range(2):
        core = 1 - c if slot else c
        for store in stores(slot, [block_of(3, *combo, core) for combo in combos]):
            store.wait()
    for part in range(2):
        copy(mine, part, to_z.at[0, part], near_z).wait_send()
        copy(mine, part, to_z.at[1, part], far_z).wait_send()
        copy(mine, part, to_z.at[2, part], near_z).wait_send()

    for i in range(6):
        corner(i).wait_send()
    for i in range(4):
        for kind in range(3):
            deep_copy(kind, i, mine).wait_send()

    @pl.loop(0, 4)
    def _(q):
        for i in range(4):
            deep_core_copy(q, i, mine).wait_send()
        for i in range(3):
            copy(mine, 0, to_y.at[i, q], y_peer).wait_send()
            copy(mine, 0, to_x.at[i, q], x_peer).wait_send()
        for i in range(4):
            for part in range(2):
                copy(mine, part, to_core.at[i, part, q], core_peer).wait_send()


def gather_experts(rows, notes, topk, kept, gate_w, up_w, router):
    count, width = rows.shape
    blocks = notes.shape[0]
    hidden = gate_w.shape[1]
    low = rows.dtype
    anywhere = pl.BlockSpec(memory_space=pl.ANY)
    vmem = pl.BlockSpec(memory_space=pltpu.VMEM)
    return pl.pallas_call(
        functools.partial(gather_kernel, topk),
        out_shape=[
            jax.ShapeDtypeStruct((blocks, kept, width), low),
            jax.ShapeDtypeStruct((blocks, kept, hidden), low),
            jax.ShapeDtypeStruct((blocks, kept, hidden), jnp.float32),
            jax.ShapeDtypeStruct((blocks, kept, hidden), jnp.float32),
            jax.ShapeDtypeStruct((blocks, kept, 128), jnp.float32),
            jax.ShapeDtypeStruct((blocks, kept, count), low),
            jax.ShapeDtypeStruct((blocks, count, kept), low),
        ],
        in_specs=[vmem, vmem, anywhere, anywhere, vmem],
        out_specs=[anywhere] * 4 + [vmem] * 3,
        scratch_shapes=[
            pltpu.VMEM((blocks, count, width), low),
            pltpu.VMEM(gate_w.shape, low),
            pltpu.VMEM(up_w.shape, low),
            pltpu.VMEM((2, 4 * kept, width), low),
            pltpu.VMEM((2, 4 * kept, hidden), low),
            pltpu.VMEM((2, 2, 4 * kept, hidden), jnp.float32),
            copies(2),
            copies(2, 16),
            copies(blocks, 4),
            copies(3, 2),
            copies(3, 4),
            copies(3, 4),
            copies(4, 2, 4),
            copies(6),
            copies(3, 4),
            copies(4, 4),
        ],
        compiler_params=settings(1),
    )(rows, notes, gate_w, up_w, router)


def scatter_kernel(
    extended,
    *refs,
):
    resident = 6 if extended else 5
    streamed = 1 if extended else 3
    given, refs = refs[:resident], refs[resident:]
    sources, refs = refs[:streamed], refs[streamed:]
    if extended:
        (rows_hbm,) = sources
        out_ref, extra_out, gate_out, up_out = refs[:4]
        tiles, staged, loaded, stored = refs[4:8]
        refs = refs[8:]
    else:
        grads_hbm, gate_hbm, up_hbm = sources
        out_ref, rows_out, gate_out, up_out, extra_ref = refs[:5]
        grads_in, pre_in, rows_staged, staged, loaded, stored = refs[5:11]
        refs = refs[11:]
    held, (fetched, *refs) = refs[:resident], refs[resident:]
    if extended:
        spread_ref, gate_grad_ref, up_grad_ref, gate_ref, up_ref, extra_ref = held
    else:
        spread_ref, active_ref, down_ref, share_ref, select_ref = held
    outgoing, core_in, total, back, x_in, y_in, z_in, deep_in, deep_x, deep_y = refs[:10]
    core_sent, core_got, x_sent, x_got, y_sent, y_got, z_sent, z_got = refs[10:18]
    deep_sent, deep_got, corner_sent, corner_got = refs[18:]
    fetches = [
        pltpu.make_async_copy(source, target, fetched.at[i])
        for i, (source, target) in enumerate(zip(given, held))
    ]
    for fetch in fetches:
        fetch.start()
    z, y, x, c = spot()
    width = out_ref.shape[1]
    count = out_ref.shape[0]
    half, thin = count * 3 // 8, count // 8
    wide = 2 * half
    blocks, _, kept = spread_ref.shape
    y_peer, x_peer, core_peer = (
        where_is(z, 1 - y, x, c),
        where_is(z, y, 1 - x, c),
        where_is(z, y, x, 1 - c),
    )
    near_z, far_z = where_is(along_z(z, 1), y, x, c), where_is(along_z(z, 2), y, x, c)
    greet([y_peer, x_peer, core_peer, near_z, far_z])
    for fetch in fetches:
        fetch.wait()
    groups = ((1, 1), (0, 1), (1, 0), (0, 0))

    def block_of(group, q, core):
        other_y, other_x = groups[group]
        return number(along_z(z, q), 1 - y if other_y else y, 1 - x if other_x else x, core)

    def rows_of(ref, q, core):
        return jnp.concatenate([ref[block_of(group, q, core)] for group in range(4)], axis=0)

    def rows_back(q, core):
        if extended:
            sums = right_transposed(rows_of(gate_grad_ref, q, core), gate_ref[...])
            sums = sums + right_transposed(rows_of(up_grad_ref, q, core), up_ref[...])
        else:
            sums = jnp.dot(
                rows_of(active_ref, q, core), down_ref[...], preferred_element_type=jnp.float32
            )
            sums = sums.astype(back.dtype).astype(jnp.float32)
            sums = sums * rows_of(share_ref, q, core)[:, :1]
        back[...] = sums.astype(back.dtype)

    def turn_blocks(turn):
        core = (c + turn) % 2
        return [block_of(group, turn // 2, core) for group in range(4)]

    def loads(turn):
        slot, made = turn % 2, []
        if extended:
            columns = pl.ds(pl.multiple_of(turn * tiles.shape[3], tiles.shape[3]), tiles.shape[3])
            made.append((rows_hbm.at[:, :, columns], tiles.at[slot]))
        else:
            for group, block in enumerate(turn_blocks(turn)):
                rows = pl.ds(group * kept, kept)
                made.append((grads_hbm.at[block], grads_in.at[slot, group]))
                made.append((gate_hbm.at[block], pre_in.at[slot, 0, rows]))
                made.append((up_hbm.at[block], pre_in.at[slot, 1, rows]))
        return [
            pltpu.make_async_copy(source, target, loaded.at[slot, i])
            for i, (source, target) in enumerate(made)
        ]

    def stores(turn):
        slot, made = turn % 2, []
        if extended:
            columns = tiles.shape[3]
            rows = pl.ds(pl.multiple_of(turn * columns, columns), columns)
            made.append((staged.at[slot, 0], gate_out.at[rows]))
            made.append((staged.at[slot, 1], up_out.at[rows]))
        else:
            for group, block in enumerate(turn_blocks(turn)):
                rows = pl.ds(group * kept, kept)
                made.append((rows_staged.at[slot, rows], rows_out.at[block]))
                made.append((staged.at[slot, 0, rows], gate_out.at[block]))
                made.append((staged.at[slot, 1, rows], up_out.at[block]))
        return [
            pltpu.make_async_copy(source, target, stored.at[slot, i])
            for i, (source, target) in enumerate(made)
        ]

    def begin_loads(turn):
        for load in loads(turn):
            load.start()

    def fill(turn):
        for load in loads(turn):
            load.wait()

        @pl.when(turn >= 2)
        def _():
            for store in stores(turn - 2):
                store.wait()

        if extended:
            weigh(turn)
        else:
            prepare(turn)
        for store in stores(turn):
            store.start()

        @pl.when(turn < 6)
        def _():
            begin_loads(turn + 2)

    def weigh(turn):
        slot = turn % 2
        staged[slot] = jnp.zeros_like(staged[slot])

        @pl.loop(0, blocks // 4)
        def _(i):
            span = pl.ds(i * 4, 4)
            rows = tiles[slot, span].reshape(4 * kept, tiles.shape[3])
            for which, grads in enumerate((gate_grad_ref, up_grad_ref)):
                staged[slot, which] += left_trans(
                    rows, grads[span].reshape(4 * kept, grads.shape[2])
                )

    def prepare(turn):
        blocks, slot = turn_blocks(turn), turn % 2
        mine = number(z, y, x, c)
        parts = [
            jnp.dot(
                select_ref[blocks[group]],
                grads_in[slot, group],
                preferred_element_type=jnp.float32,
            )
            for group in range(4)
        ]
        share = jnp.concatenate([share_ref[block] for block in blocks], axis=0)[:, :1]
        picked = jnp.concatenate(parts, axis=0)
        rows_staged[slot] = (share * picked).astype(rows_staged.dtype)
        ahead = right_transposed(picked.astype(rows_staged.dtype), down_ref[...])
        gate, up = pre_in[slot, 0], pre_in[slot, 1]
        active = jnp.concatenate([active_ref[block] for block in blocks], axis=0)
        grad = jnp.sum(active.astype(jnp.float32) * ahead, axis=1, keepdims=True)
        active_grad = share * ahead
        sigma = 1.0 / (1.0 + jnp.exp(-gate))
        gate_grad = active_grad * up * (sigma * (1.0 + gate * (1.0 - sigma)))
        staged[slot, 0] = gate_grad.astype(staged.dtype)
        staged[slot, 1] = (active_grad * (gate * sigma)).astype(staged.dtype)
        lanes = lax.broadcasted_iota(jnp.int32, (4 * kept, 128), 1)
        high = grad.astype(extra_ref.dtype).astype(jnp.float32)
        both = jnp.where(lanes == mine, high, jnp.where(lanes == 32 + mine, grad - high, 0.0))
        both = both.astype(extra_ref.dtype)
        for group, block in enumerate(blocks):
            extra_ref[block] = both[group * kept : (group + 1) * kept]

    def part(block, group):
        rows = jnp.dot(
            spread_ref[block],
            back[group * kept : (group + 1) * kept],
            preferred_element_type=jnp.float32,
        )
        if not extended:
            return rows
        more = jnp.dot(spread_ref[block], extra_ref[block], preferred_element_type=jnp.float32)
        return jnp.concatenate([rows, more], axis=1)

    def across(group, q):
        return remote(
            outgoing.at[q, group],
            core_in.at[q, group],
            core_sent.at[q, group],
            core_got.at[q, group],
            core_peer,
        )

    def view(group, q, side):
        return total.at[q, group, pl.ds(side * half, half)]

    def x_copy(group, q, side, slot):
        return remote(
            view(group, q, side), x_in.at[slot, q], x_sent.at[slot, q], x_got.at[slot, q], x_peer
        )

    def y_copy(group, q, side, slot):
        return remote(
            view(group, q, side), y_in.at[slot, q], y_sent.at[slot, q], y_got.at[slot, q], y_peer
        )

    def z_copy(q):
        return remote(
            total.at[q, 3, pl.ds(0, wide)],
            z_in.at[q - 1],
            z_sent.at[q - 1],
            z_got.at[q - 1],
            where_is(along_z(z, 2 - q % 2), y, x, c),
        )

    def deep_copy(q):
        return remote(
            total.at[q, :, pl.ds(wide, 2 * thin)],
            deep_in.at[q - 1],
            deep_sent.at[q - 1],
            deep_got.at[q - 1],
            far_z if q == 2 else near_z,
        )

    def corner_copy(over_x, group, side, slot):
        place, peer = (deep_x, x_peer) if over_x else (deep_y, y_peer)
        return remote(
            total.at[0, group, pl.ds(wide + side * thin, thin)],
            place.at[slot],
            corner_sent.at[over_x, slot],
            corner_got.at[over_x, slot],
            peer,
        )

    y_corners = [corner_copy(0, 0, 0, 0), corner_copy(0, 2, 0, 1), corner_copy(0, 2, 1, 2)]
    x_corners = [corner_copy(1, 0, 1, 0), corner_copy(1, 1, 1, 1), corner_copy(1, 1, 0, 2)]

    def add_deep(q, *arrivals):
        rows = pl.ds(wide, 2 * thin)
        sums = total[q, :, rows].astype(jnp.float32)
        for arrival in arrivals:
            deep_copy(arrival).wait_recv()
            sums = sums + deep_in[arrival - 1].astype(jnp.float32)
        total[q, :, rows] = sums.astype(total.dtype)

    def add_corner(group, side, source):
        rows = pl.ds(wide + side * thin, thin)
        total[0, group, rows] = (
            total[0, group, rows].astype(jnp.float32) + source.astype(jnp.float32)
        ).astype(total.dtype)

    def deep_step(i):
        @pl.when(i == 0)
        def _():
            deep_copy(3).start()

        @pl.when(i == 1)
        def _():
            add_deep(2, 3)
            deep_copy(2).start()

        @pl.when(i == 2)
        def _():
            deep_copy(1).start()

        @pl.when(i == 3)
        def _():
            add_deep(0, 1, 2)
            for corner in (*y_corners[:2], *x_corners[:2]):
                corner.start()

        @pl.when(i == 4)
        def _():
            y_corners[0].wait_recv()
            add_corner(1, 0, deep_y[0])
            x_corners[2].start()
            x_corners[0].wait_recv()
            add_corner(2, 1, deep_x[0])
            y_corners[2].start()

    def add(group, q, side, source):
        rows = pl.ds(side * half, half)
        total[q, group, rows] = (
            total[q, group, rows].astype(jnp.float32) + source.astype(jnp.float32)
        ).astype(total.dtype)

    def begin(q):
        rows_back(q, 1 - c)
        for group in range(4):
            outgoing[q, group] = part(block_of(group, q, 1 - c), group).astype(total.dtype)
            across(group, q).start()
        rows_back(q, c)
        for group in range(4):
            sums = part(block_of(group, q, c), group)
            across(group, q).wait_recv()
            total[q, group] = (sums + core_in[q, group].astype(jnp.float32)).astype(total.dtype)
            if group == 0:
                x_copy(0, q, 0, 0).start()
                y_copy(0, q, 1, 0).start()
            if group == 1:
                x_copy(1, q, 0, 1).start()
            if group == 2:
                y_copy(2, q, 1, 1).start()

    def middle(q):
        x_copy(0, q, 0, 0).wait_recv()
        add(2, q, 0, x_in[0, q])
        y_copy(2, q, 0, 2).start()
        y_copy(0, q, 1, 0).wait_recv()
        add(1, q, 1, y_in[0, q])
        x_copy(1, q, 1, 2).start()

    def close(q):
        arrivals = (
            ((x_copy(1, q, 0, 1), x_in, 1), (y_copy(2, q, 0, 2), y_in, 2)),
            ((y_copy(2, q, 1, 1), y_in, 1), (x_copy(1, q, 1, 2), x_in, 2)),
        )
        for side in range(2):
            for arrival, _, _ in arrivals[side]:
                arrival.wait_recv()
            rows = pl.ds(side * half, half)
            sums = total[q, 3, rows].astype(jnp.float32)
            for _, source, slot in arrivals[side]:
                sums = sums + source[slot, q].astype(jnp.float32)
            total[q, 3, rows] = sums.astype(total.dtype)

        @pl.when(q == 2)
        def _():
            z_copy(3).wait_recv()
            rows = pl.ds(0, wide)
            total[2, 3, rows] = (
                total[2, 3, rows].astype(jnp.float32) + z_in[2].astype(jnp.float32)
            ).astype(total.dtype)

        @pl.when(q > 0)
        def _():
            z_copy(q).start()

    def done(i):
        return jnp.maximum(i, 0) + jnp.maximum(i - 2, 0)

    begin_loads(0)
    begin_loads(1)

    @pl.loop(0, 6)
    def _(i):
        @pl.when(i < 4)
        def _():
            begin(3 - i)

        @pl.loop(done(i - 1), done(i))
        def _(turn):
            fill(turn)

        deep_step(i)

        @pl.when((i > 0) & (i < 5))
        def _():
            middle(4 - i)

        @pl.when(i > 1)
        def _():
            close(5 - i)

    for turn in (6, 7):
        for store in stores(turn):
            store.wait()
    for q in (1, 2):
        z_copy(q).wait_recv()

    def finish(start, size, *more):
        rows = pl.ds(start, size)
        sums = total[0, 3, rows].astype(jnp.float32)
        for source in more:
            sums = sums + source.astype(jnp.float32)
        out_ref[rows] = sums[:, :width]
        if extended:
            extra_out[rows] = sums[:, width:]

    finish(0, wide, z_in[0], z_in[1])
    for slot in (1, 2):
        y_corners[slot].wait_recv()
        x_corners[slot].wait_recv()
    finish(wide, thin, deep_y[1], deep_x[2])
    finish(wide + thin, thin, deep_x[1], deep_y[2])
    for corner in (*y_corners, *x_corners):
        corner.wait_send()
    for q in range(1, 4):
        z_copy(q).wait_send()
        deep_copy(q).wait_send()

    @pl.loop(0, 4)
    def _(q):
        for group in range(4):
            across(group, q).wait_send()
        x_copy(0, q, 0, 0).wait_send()
        x_copy(1, q, 0, 1).wait_send()
        x_copy(1, q, 1, 2).wait_send()
        y_copy(0, q, 1, 0).wait_send()
        y_copy(2, q, 1, 1).wait_send()
        y_copy(2, q, 0, 2).wait_send()


def scatter_rows(spread, *operands):
    blocks, count, kept = spread.shape
    extended = len(operands) == 6
    width = operands[2].shape[0] if extended else operands[1].shape[1]
    wide = width + 128 if extended else width
    low = operands[0].dtype
    anywhere = pl.BlockSpec(memory_space=pl.ANY)
    resident = (spread, *operands[: 5 if extended else 4])
    outs = [jax.ShapeDtypeStruct((count, width), jnp.float32)]
    if extended:
        outs.append(jax.ShapeDtypeStruct((count, 128), jnp.float32))
        hidden = operands[0].shape[2]
        outs += [jax.ShapeDtypeStruct((width, hidden), jnp.float32)] * 2
        out_specs = in_vmem(2) + [anywhere] * 2
        filler = [
            pltpu.VMEM((2, blocks, kept, width // 8), low),
            pltpu.VMEM((2, 2, width // 8, hidden), jnp.float32),
            copies(2, 1),
            copies(2, 2),
        ]
    else:
        hidden = operands[0].shape[2]
        outs += [
            jax.ShapeDtypeStruct((blocks, kept, width), low),
            jax.ShapeDtypeStruct((blocks, kept, hidden), low),
            jax.ShapeDtypeStruct((blocks, kept, hidden), low),
            jax.ShapeDtypeStruct((blocks, kept, 128), low),
        ]
        out_specs = in_vmem(1) + [anywhere] * 3 + in_vmem(1)
        filler = [
            pltpu.VMEM((2, 4, count, width), low),
            pltpu.VMEM((2, 2, 4 * kept, hidden), jnp.float32),
            pltpu.VMEM((2, 4 * kept, width), low),
            pltpu.VMEM((2, 2, 4 * kept, hidden), low),
            copies(2, 12),
            copies(2, 12),
        ]
    return pl.pallas_call(
        functools.partial(scatter_kernel, extended),
        out_shape=outs,
        in_specs=[anywhere] * (1 + len(operands)),
        out_specs=out_specs,
        scratch_shapes=filler
        + [pltpu.VMEM(operand.shape, operand.dtype) for operand in resident]
        + [
            copies(len(resident)),
            pltpu.VMEM((4, 4, count, wide), low),
            pltpu.VMEM((4, 4, count, wide), low),
            pltpu.VMEM((4, 4, count, wide), low),
            pltpu.VMEM((4 * kept, width), low),
            pltpu.VMEM((3, 4, count * 3 // 8, wide), low),
            pltpu.VMEM((3, 4, count * 3 // 8, wide), low),
            pltpu.VMEM((3, count * 3 // 4, wide), low),
            pltpu.VMEM((3, 4, count // 4, wide), low),
            pltpu.VMEM((3, count // 8, wide), low),
            pltpu.VMEM((3, count // 8, wide), low),
            copies(4, 4),
            copies(4, 4),
            copies(3, 4),
            copies(3, 4),
            copies(3, 4),
            copies(3, 4),
            copies(3),
            copies(3),
            copies(3),
            copies(3),
            copies(2, 3),
            copies(2, 3),
        ],
        compiler_params=settings(2 if extended else 8),
    )(spread, *operands)


def reduce_kernel(
    cuts,
    fetches,
    parts_ref,
    own_ref,
    vector_ref,
    query_out,
    key_out,
    value_out,
    every_out,
    vector_out,
    sums_out,
    own_sent,
    own_got,
    own_side_sent,
    own_side_got,
    stored,
    *refs,
):
    z, y, x, c = spot()
    member, shard = lax.axis_index("exp"), lax.axis_index("fsdp")
    y_peer = where_is(z, 1 - y, x, c)
    near_z, far_z = where_is(along_z(z, 1), y, x, c), where_is(along_z(z, 2), y, x, c)
    members = [((member + j) % 8, shard) for j in range(8)]
    shards = [(member, (shard + j) % 4) for j in range(4)]
    greet(members[1:] + shards[1:])
    wait_all(fetches)
    pieces = len(cuts)
    first_got, first_held, first_z = refs[:3]
    y_got_in, y_held, y_z = refs[3:5], refs[5:7], refs[7:9]
    shard_in, member_own, member_in = refs[3 * pieces : 3 * pieces + 3]
    (
        y_sent,
        y_got,
        z_sent,
        z_got,
        back_sent,
        back_got,
        side_sent,
        side_got,
        shard_sent,
        shard_got,
        member_sent,
        member_got,
    ) = refs[3 * pieces + 3 :]

    def shard_copy(j):
        return remote(
            vector_ref.at[(shard + j) % 4],
            shard_in.at[(4 - j) % 4],
            shard_sent.at[j],
            shard_got.at[(4 - j) % 4],
            shards[j],
        )

    def member_copy(j):
        return remote(
            member_own,
            member_in.at[(8 - j) % 8],
            member_sent.at[j],
            member_got.at[(8 - j) % 8],
            members[j],
        )

    def rows(which):
        return pl.ds(*cuts[which])

    def z_peer(q):
        return far_z if q == 2 else near_z

    def y_copy(which, q):
        return remote(
            parts_ref.at[1 - y, along_z(z, q), rows(which)],
            y_got_in[which - 1].at[q],
            y_sent.at[which, q],
            y_got.at[which, q],
            y_peer,
        )

    def z_copy(which, q):
        if which:
            source, target = y_held[which - 1].at[q], y_z[which - 1].at[q]
        elif q == 2:
            source, target = first_held, first_z.at[2]
        else:
            source, target = parts_ref.at[:, along_z(z, q), rows(0)], first_z.at[q]
        return remote(source, target, z_sent.at[which, q], z_got.at[which, q], z_peer(q))

    def first_y():
        return remote(
            first_z.at[0, 1 - y], first_got, y_sent.at[0, 0], y_got.at[0, 0], y_peer
        )

    def place(side, q, which):
        return sums_out.at[side, along_z(z, q), rows(which)]

    def back_copy(which, q):
        held = along_z(z, 2) if q == 3 else z
        if which:
            view = sums_out.at[y, held, rows(which)]
        else:
            view = sums_out.at[:, held, rows(0)]
        return remote(view, view, back_sent.at[which, q], back_got.at[which, q], z_peer(q))

    def side_copy(which, q):
        view = place(y, q, which)
        return remote(view, view, side_sent.at[which, q], side_got.at[which, q], y_peer)

    def own_copy(q):
        view = every_out.at[along_z(z, 2) if q == 3 else z, y]
        return remote(view, view, own_sent.at[q], own_got.at[q], z_peer(q))

    def own_side(q):
        view = every_out.at[along_z(z, q), y]
        return remote(view, view, own_side_sent.at[q], own_side_got.at[q], y_peer)

    def pass_on(q):
        own_copy(q).wait_recv()
        if q == 2:
            own_copy(3).start()
        own_side(q).start()

    def exports(side, q):
        zone = along_z(z, q)
        head, rows = side * 2 + zone // 2, zone % 2
        made, start = [], 0
        for i, out in enumerate((query_out, key_out, value_out)):
            size, depth = out.shape[1] // 4, parts_ref.shape[2]
            source = sums_out.at[side, zone, :, pl.ds(start, size)]
            target = out.at[
                pl.ds(pl.multiple_of(rows * depth, depth), depth),
                pl.ds(pl.multiple_of(head * size, size), size),
            ]
            made.append(pltpu.make_async_copy(source, target, stored.at[side, q, i]))
            start += size
        return made

    later = range(1, pieces)
    every_out[z, y] = own_ref[...]
    for j in range(1, 4):
        shard_copy(j).start()
    z_copy(0, 3).start()
    own_copy(1).start()
    own_copy(2).start()
    for q in (3, 2, 1, 0):
        for which in later:
            y_copy(which, q).start()
    z_copy(0, 1).start()
    own_side(0).start()

    for j in range(1, 4):
        shard_copy(j).wait_recv()
    sums = vector_ref[shard]
    for j in range(1, 4):
        sums = sums + shard_in[j]
    member_own[...] = sums
    for j in range(1, 8):
        member_copy(j).start()

    def add_y(which, q):
        y_copy(which, q).wait_recv()
        sums = parts_ref[y, along_z(z, q), rows(which)].astype(jnp.float32)
        sums = sums + y_got_in[which - 1][q].astype(jnp.float32)
        held, z_in = y_held[which - 1], y_z[which - 1]
        if q == 2:
            z_copy(which, 3).wait_recv()
            sums = sums + z_in[3].astype(jnp.float32)
        if q:
            held[q] = sums.astype(held.dtype)
            z_copy(which, q).start()
            return
        for turn in (1, 2):
            z_copy(which, turn).wait_recv()
            sums = sums + z_in[turn].astype(jnp.float32)
        sums_out[y, z, rows(which)] = sums.astype(sums_out.dtype)
        side_copy(which, 0).start()
        back_copy(which, 2).start()
        back_copy(which, 1).start()

    for which in later:
        add_y(which, 3)
    z_copy(0, 3).wait_recv()
    first_held[...] = (
        parts_ref[:, along_z(z, 2), rows(0)].astype(jnp.float32) + first_z[3].astype(jnp.float32)
    ).astype(first_held.dtype)
    z_copy(0, 2).start()
    pass_on(1)
    for which in later:
        add_y(which, 2)
    pass_on(2)
    z_copy(0, 1).wait_recv()
    z_copy(0, 2).wait_recv()
    first_z[0] = (
        parts_ref[:, z, rows(0)].astype(jnp.float32)
        + first_z[1].astype(jnp.float32)
        + first_z[2].astype(jnp.float32)
    ).astype(first_z.dtype)
    first_y().start()
    for which in later:
        add_y(which, 1)
    pass_on(3)
    first_y().wait_recv()
    sums = first_z[0, y].astype(jnp.float32) + first_got[...].astype(jnp.float32)
    sums_out[y, z, rows(0)] = sums.astype(sums_out.dtype)
    side_copy(0, 0).start()
    for which in later:
        add_y(which, 0)
    side_copy(0, 0).wait_recv()
    back_copy(0, 2).start()
    back_copy(0, 1).start()

    for j in range(1, 8):
        member_copy(j).wait_recv()
    sums = member_own[...]
    for j in range(1, 8):
        sums = sums + member_in[j]
    vector_out[...] = sums

    for q in (1, 2, 3):
        for which in later:
            back_copy(which, q).wait_recv()
            if q == 2:
                back_copy(which, 3).start()
            side_copy(which, q).start()
        back_copy(0, q).wait_recv()
        if q == 2:
            back_copy(0, 3).start()

    for q in range(4):
        for export in exports(y, q):
            export.start()
    for q in range(4):
        for which in later:
            side_copy(which, q).wait_recv()
        for export in exports(1 - y, q):
            export.start()
    for q in range(4):
        own_side(q).wait_recv()
    for q in range(4):
        for side in (y, 1 - y):
            for export in exports(side, q):
                export.wait()
    for q in range(4):
        own_side(q).wait_send()
        if q:
            own_copy(q).wait_send()
    for which in range(pieces):
        for q in range(4):
            if which:
                y_copy(which, q).wait_send()
                side_copy(which, q).wait_send()
            if q:
                z_copy(which, q).wait_send()
                back_copy(which, q).wait_send()
    side_copy(0, 0).wait_send()
    first_y().wait_send()
    for j in range(1, 4):
        shard_copy(j).wait_send()
    for j in range(1, 8):
        member_copy(j).wait_send()


def reduce_over_members(parts, own, vectors, widths):
    low = parts.dtype
    depth, width = parts.shape[2:]
    early = depth // 4 // 16 * 16
    half = (depth - early) // 2 // 16 * 16
    cuts = ((0, early), (early, half), (early + half, depth - early - half))
    anywhere = pl.BlockSpec(memory_space=pl.ANY)

    def quarters(*lead):
        return [pltpu.VMEM((*lead, size, width), low) for _, size in cuts[1:]]

    return pl.pallas_call(
        fetching(functools.partial(reduce_kernel, cuts), 3),
        out_shape=[jax.ShapeDtypeStruct((2 * depth, size), low) for size in widths]
        + [
            jax.ShapeDtypeStruct((4, 2, *own.shape), low),
            jax.ShapeDtypeStruct(vectors.shape[1:], vectors.dtype),
        ],
        in_specs=[anywhere] * 3,
        out_specs=[anywhere] * 3 + in_vmem(2),
        scratch_shapes=[
            pltpu.VMEM(parts.shape, low),
            copies(4),
            copies(4),
            copies(4),
            copies(4),
            copies(2, 4, 3),
            pltpu.VMEM((early, width), low),
            pltpu.VMEM((2, early, width), low),
            pltpu.VMEM((4, 2, early, width), low),
            *quarters(4),
            *quarters(4),
            *quarters(4),
            pltpu.VMEM(vectors.shape, vectors.dtype),
            pltpu.VMEM(vectors.shape[1:], vectors.dtype),
            pltpu.VMEM((8, *vectors.shape[1:]), vectors.dtype),
        ]
        + [copies(3, 4)] * 8
        + [copies(4)] * 2
        + [copies(8)] * 2
        + room_for((parts, own, vectors)),
        compiler_params=settings(3),
    )(parts, own, vectors)


def project_kernel(
    x_ref,
    routes_ref,
    gain_ref,
    query_ref,
    key_ref,
    value_ref,
    raw_out,
    hidden_out,
    routes_out,
    scale,
    x_in,
    scale_in,
    outgoing,
    core_in,
    across_x,
    x_sums,
    slice_sent,
    slice_got,
    scale_sent,
    scale_got,
    core_sent,
    core_got,
    x_sent,
    x_got,
    route_sent,
    route_got,
):
    z, y, x, c = spot()
    member, shard = lax.axis_index("exp"), lax.axis_index("fsdp")
    mine = number(z, y, x, c)
    count, depth = hidden_out.shape[1:]
    wide, narrow = query_ref.shape[1] // 4, key_ref.shape[1] // 4

    def everyone(j):
        other = (mine + j) % 32
        return (other // 4, other % 4)

    barrier = pltpu.get_barrier_semaphore()

    @pl.loop(1, 32)
    def _(j):
        pl.semaphore_signal(barrier, inc=1, device_id=everyone(j), device_id_type=MESH)

    pl.semaphore_wait(barrier, 31)

    def slice_copy(j):
        place = (shard + j) % 4
        return remote(
            x_ref.at[:, pl.ds(pl.multiple_of(place * depth, depth), depth)],
            x_in.at[(4 - j) % 4],
            slice_sent.at[j],
            slice_got.at[(4 - j) % 4],
            (member, place),
        )

    def scale_copy(j):
        return remote(
            scale,
            scale_in.at[(4 - j) % 4],
            scale_sent.at[j],
            scale_got.at[(4 - j) % 4],
            (member, (shard + j) % 4),
        )

    def route_copy(j):
        return remote(
            routes_ref, routes_out.at[mine], route_sent.at[j], route_got.at[(32 - j) % 32], everyone(j)
        )

    for j in range(1, 4):
        slice_copy(j).start()
    values = x_ref[...].astype(jnp.float32)
    scale[...] = jnp.broadcast_to(
        lax.rsqrt(jnp.mean(values * values, axis=1, keepdims=True) + EPSILON), scale.shape
    )
    for j in range(1, 4):
        scale_copy(j).start()
    routes_out[mine] = routes_ref[...]

    @pl.loop(1, 32)
    def _(j):
        route_copy(j).start()

    def hide(owner, piece, factor):
        gain = gain_ref[...].astype(jnp.float32)
        hidden = piece.astype(jnp.float32) * factor[:, :1] * gain
        hidden_out[owner] = hidden.astype(hidden_out.dtype)

    hide(shard, x_ref[:, pl.ds(pl.multiple_of(shard * depth, depth), depth)], scale[...])

    def take(owner):
        slot = (owner - shard + 4) % 4
        remote(x_in.at[slot], x_in.at[slot], slice_sent.at[slot], slice_got.at[slot], (member, owner)).wait_recv()
        remote(scale, scale_in.at[slot], scale_sent.at[slot], scale_got.at[slot], (member, owner)).wait_recv()
        hide(owner, x_in[slot], scale_in[slot])

    def partial(side, target):
        rows = jnp.concatenate([hidden_out[side * 2], hidden_out[side * 2 + 1]], axis=0)
        parts = []
        for weight, size in ((query_ref, wide), (key_ref, narrow), (value_ref, narrow)):
            columns = pl.ds(pl.multiple_of(target * size, size), size)
            parts.append(jnp.dot(rows, weight[:, columns], preferred_element_type=jnp.float32))
        return jnp.concatenate(parts, axis=1)

    core_peer, x_peer = where_is(z, y, x, 1 - c), where_is(z, y, 1 - x, c)

    def core_copy(turn, far):
        return remote(
            outgoing.at[turn, far],
            core_in.at[turn, far],
            core_sent.at[turn, far],
            core_got.at[turn, far],
            core_peer,
        )

    def x_copy(turn):
        return remote(across_x.at[turn], x_sums.at[turn], x_sent.at[turn], x_got.at[turn], x_peer)

    low = outgoing.dtype
    for turn in range(2):
        side = x if turn == 0 else 1 - x
        if turn == 0:
            take(side * 2 + 1 - c)
        else:
            take(side * 2 + c)
            take(side * 2 + 1 - c)
        outgoing[turn, 1] = partial(side, (1 - x) * 2 + 1 - c).astype(low)
        core_copy(turn, 1).start()
        sums = partial(side, (1 - x) * 2 + c)
        core_copy(turn, 1).wait_recv()
        across_x[turn] = (sums + core_in[turn, 1].astype(jnp.float32)).astype(low)
        x_copy(turn).start()
        outgoing[turn, 0] = partial(side, x * 2 + 1 - c).astype(low)
        core_copy(turn, 0).start()

    for turn in range(2):
        side = x if turn == 0 else 1 - x
        sums = partial(side, x * 2 + c)
        core_copy(turn, 0).wait_recv()
        sums = sums + core_in[turn, 0].astype(jnp.float32)
        raw_out[side * 2] = sums[:count]
        raw_out[side * 2 + 1] = sums[count:]

    for turn in range(2):
        side = 1 - x if turn == 0 else x
        x_copy(turn).wait_recv()
        raw_out[side * 2] += x_sums[turn, :count].astype(jnp.float32)
        raw_out[side * 2 + 1] += x_sums[turn, count:].astype(jnp.float32)

    @pl.loop(1, 32)
    def _(j):
        remote(
            routes_ref, routes_out.at[(mine + j) % 32], route_sent.at[j], route_got.at[j], everyone(j)
        ).wait_recv()

    @pl.loop(1, 32)
    def _(j):
        route_copy(j).wait_send()

    for j in range(1, 4):
        slice_copy(j).wait_send()
        scale_copy(j).wait_send()
    for turn in range(2):
        x_copy(turn).wait_send()
        for far in range(2):
            core_copy(turn, far).wait_send()


def project_tokens(tokens, routes, gain, w_query, key_weight, value_weight):
    count = tokens.shape[0]
    depth = w_query.shape[0]
    own = (w_query.shape[1] + key_weight.shape[1] + value_weight.shape[1]) // 4
    low = tokens.dtype
    return pl.pallas_call(
        project_kernel,
        out_shape=[
            jax.ShapeDtypeStruct((4, count, own), jnp.float32),
            jax.ShapeDtypeStruct((4, count, depth), low),
            jax.ShapeDtypeStruct((32, *routes.shape), routes.dtype),
        ],
        in_specs=in_vmem(6),
        out_specs=in_vmem(3),
        scratch_shapes=[
            pltpu.VMEM((count, 128), jnp.float32),
            pltpu.VMEM((4, count, depth), low),
            pltpu.VMEM((4, count, 128), jnp.float32),
            pltpu.VMEM((2, 2, 2 * count, own), low),
            pltpu.VMEM((2, 2, 2 * count, own), low),
            pltpu.VMEM((2, 2 * count, own), low),
            pltpu.VMEM((2, 2 * count, own), low),
            copies(4),
            copies(4),
            copies(4),
            copies(4),
            copies(2, 2),
            copies(2, 2),
            copies(2),
            copies(2),
            copies(32),
            copies(32),
        ],
        compiler_params=settings(4),
    )(tokens, routes, gain, w_query, key_weight, value_weight)


def turned(values):
    return pltpu.roll(values, HEAD_WIDTH // 2, 1)


def signed(sine):
    lanes = lax.broadcasted_iota(jnp.int32, sine.shape, 1)
    return jnp.where(lanes < HEAD_WIDTH // 2, -sine, sine)


def finish_kernel(
    row,
    sequences,
    fetches,
    raw_ref,
    notes_ref,
    query_gain_ref,
    key_gain_ref,
    weight_ref,
    x_ref,
    gain_ref,
    middle_out,
    normed_out,
    attended_out,
    probs_out,
    query_out,
    key_out,
    cosine_out,
    sine_out,
    outgoing,
    core_in,
    across_x,
    x_sums,
    core_sent,
    core_got,
    x_sent,
    x_got,
):
    z, y, x, c = spot()
    count = x_ref.shape[0]
    core_peer, x_peer = where_is(z, y, x, 1 - c), where_is(z, y, 1 - x, c)
    greet([core_peer, x_peer])
    wait_all(fetches)
    heads = query_out.shape[2] // HEAD_WIDTH
    wide = heads * HEAD_WIDTH

    def place(block):
        down = lax.broadcasted_iota(jnp.int32, (count, count), 0)
        along = lax.broadcasted_iota(jnp.int32, (count, count), 1)
        end = jnp.zeros((1, 1), jnp.int32)
        start = jnp.zeros((count, count), jnp.int32)
        own, other = start, start
        for i in range(sequences - 1):
            length = notes_ref[block, row : row + 1, i : i + 1]
            end = end + length
            own = own + jnp.where(down >= end, 1, 0)
            other = other + jnp.where(along >= end, 1, 0)
            start = start + jnp.where(down >= end, length, 0)
        return down - start, (own == other) & (along <= down)

    def attend(block):
        position, allowed = place(block)
        lanes = lax.broadcasted_iota(jnp.int32, position.shape, 1)
        spin = lanes % (HEAD_WIDTH // 2)
        inverse = jnp.exp(spin.astype(jnp.float32) * (-2.0 * math.log(THETA) / HEAD_WIDTH))
        angles = position.astype(jnp.float32) * inverse
        cosine, sine = jnp.cos(angles), jnp.sin(angles)
        cosine_out[block] = cosine
        sine_out[block] = sine
        flipped = signed(sine)

        def normal(values, gain):
            scale = lax.rsqrt(jnp.mean(values * values, axis=1, keepdims=True) + EPSILON)
            values = values * scale * gain
            return (values * cosine + turned(values) * flipped).astype(query_out.dtype)

        key = normal(raw_ref[block, :, wide : wide + HEAD_WIDTH], key_gain_ref[...])
        key_out[block] = key
        value = raw_ref[block, :, wide + HEAD_WIDTH :].astype(query_out.dtype)
        for head in range(heads):
            columns = slice(head * HEAD_WIDTH, (head + 1) * HEAD_WIDTH)
            query = normal(raw_ref[block, :, columns], query_gain_ref[...])
            query_out[block, :, columns] = query
            scores = right_transposed(query, key) * HEAD_WIDTH ** (-0.5)
            scores = jnp.where(allowed, scores, MASKED)
            raised = jnp.exp(scores - jnp.max(scores, axis=1, keepdims=True))
            probs = raised / jnp.sum(raised, axis=1, keepdims=True)
            probs_out[block, head] = probs
            attended_out[block, :, columns] = jnp.dot(
                probs.astype(value.dtype), value, preferred_element_type=jnp.float32
            ).astype(attended_out.dtype)

    def core_copy(far):
        return remote(
            outgoing.at[far], core_in.at[far], core_sent.at[far], core_got.at[far], core_peer
        )

    def x_copy():
        return remote(across_x, x_sums, x_sent, x_got, x_peer)

    @pl.loop(0, 4)
    def _(i):
        block = (1 - x + i // 2) % 2 * 2 + (1 - c + i) % 2
        far = 1 - i // 2
        attend(block)
        product = jnp.dot(attended_out[block], weight_ref[...], preferred_element_type=jnp.float32)

        @pl.when(i % 2 == 0)
        def _():
            outgoing[far] = product.astype(outgoing.dtype)
            core_copy(far).start()

        @pl.when(i == 1)
        def _():
            core_copy(1).wait_recv()
            across_x[...] = (product + core_in[1].astype(jnp.float32)).astype(across_x.dtype)
            x_copy().start()

        @pl.when(i == 3)
        def _():
            core_copy(0).wait_recv()
            sums = product + x_ref[...].astype(jnp.float32)
            middle_out[...] = sums + core_in[0].astype(jnp.float32)

    x_copy().wait_recv()
    middle = middle_out[...] + x_sums[...].astype(jnp.float32)
    middle_out[...] = middle
    scale = lax.rsqrt(jnp.mean(middle * middle, axis=1, keepdims=True) + EPSILON)
    normed_out[...] = (middle * scale * gain_ref[...]).astype(normed_out.dtype)
    x_copy().wait_send()
    core_copy(0).wait_send()
    core_copy(1).wait_send()


def finish_attention(raw, notes, row, sequences, q_gain, k_gain, w_out, tokens, gain):
    count, width = tokens.shape
    low = tokens.dtype
    wide = w_out.shape[0]
    heads = wide // HEAD_WIDTH
    operands = (raw, notes, q_gain, k_gain, w_out, tokens, gain)
    return pl.pallas_call(
        fetching(functools.partial(finish_kernel, row, sequences), len(operands)),
        out_shape=[
            jax.ShapeDtypeStruct((count, width), jnp.float32),
            jax.ShapeDtypeStruct((count, width), low),
            jax.ShapeDtypeStruct((4, count, wide), low),
            jax.ShapeDtypeStruct((4, heads, count, count), jnp.float32),
            jax.ShapeDtypeStruct((4, count, wide), low),
            jax.ShapeDtypeStruct((4, count, HEAD_WIDTH), low),
            jax.ShapeDtypeStruct((4, count, HEAD_WIDTH), jnp.float32),
            jax.ShapeDtypeStruct((4, count, HEAD_WIDTH), jnp.float32),
        ],
        in_specs=anywhere(len(operands)),
        out_specs=in_vmem(8),
        scratch_shapes=[
            pltpu.VMEM((2, count, width), low),
            pltpu.VMEM((2, count, width), low),
            pltpu.VMEM((count, width), low),
            pltpu.VMEM((count, width), low),
            copies(2),
            copies(2),
            copies(),
            copies(),
        ]
        + room_for(operands),
        compiler_params=settings(5),
    )(*operands)


def branch_kernel(
    fetches, branch_ref, weight_ref, grad_out, every_out, x_sent, x_got, core_sent, core_got
):
    z, y, x, c = spot()
    mine = x * 2 + c
    core_peer, x_peer = where_is(z, y, x, 1 - c), where_is(z, y, 1 - x, c)
    half = branch_ref.shape[0] // 2
    greet([core_peer, x_peer])
    wait_all(fetches)
    every_out[mine] = branch_ref[...]

    def x_copy(part):
        rows = pl.ds(part * half, half)
        return remote(
            branch_ref.at[rows], every_out.at[mine, rows], x_sent.at[part], x_got.at[part], x_peer
        )

    def core_copy(far, part):
        view = every_out.at[(1 - x if far else x) * 2 + c, pl.ds(part * half, half)]
        return remote(view, view, core_sent.at[far, part], core_got.at[far, part], core_peer)

    def back(place):
        grad_out[place] = right_transposed(every_out[place], weight_ref[...]).astype(grad_out.dtype)

    for part in range(2):
        x_copy(part).start()
        core_copy(0, part).start()
    back(mine)
    for part in range(2):
        core_copy(0, part).wait_recv()
    back(x * 2 + 1 - c)
    for part in range(2):
        x_copy(part).wait_recv()
        core_copy(1, part).start()
    back((1 - x) * 2 + c)
    for part in range(2):
        core_copy(1, part).wait_recv()
    back((1 - x) * 2 + 1 - c)
    for part in range(2):
        x_copy(part).wait_send()
        core_copy(0, part).wait_send()
        core_copy(1, part).wait_send()


def branch_back(branch, w_out):
    count, width = branch.shape
    low = branch.dtype
    return pl.pallas_call(
        fetching(branch_kernel, 2),
        out_shape=[
            jax.ShapeDtypeStruct((4, count, w_out.shape[0]), low),
            jax.ShapeDtypeStruct((4, count, width), low),
        ],
        in_specs=anywhere(2),
        out_specs=in_vmem(2),
        scratch_shapes=[copies(2), copies(2), copies(2, 2), copies(2, 2)]
        + room_for((branch, w_out)),
        compiler_params=settings(6),
    )(branch, w_out)


def heads_kernel(
    fetches,
    branch_ref,
    raw_ref,
    probs_ref,
    rotated_ref,
    rotated_key_ref,
    cosine_ref,
    sine_ref,
    query_gain_ref,
    key_gain_ref,
    hidden_ref,
    query_ref,
    key_ref,
    value_ref,
    weight_out,
    first_out,
    gains_out,
    every,
    outgoing,
    total,
    x_sent,
    x_got,
    core_sent,
    core_got,
    back_sent,
    back_got,
):
    z, y, x, c = spot()
    member, shard = lax.axis_index("exp"), lax.axis_index("fsdp")
    core_peer, x_peer = where_is(z, y, x, 1 - c), where_is(z, y, 1 - x, c)
    peers = [(member, (shard + j) % 4) for j in range(1, 4)]
    greet(peers)
    wait_all(fetches)
    rows = every.shape[1]
    count = rows // 4
    depth = hidden_ref.shape[1]
    wide, narrow = query_ref.shape[1] // 4, key_ref.shape[1] // 4
    low = every.dtype

    def attention_back(block):
        cosine = cosine_ref[block]
        flipped = signed(sine_ref[block])

        def unturn(grads):
            return grads * cosine + turned(grads * flipped)

        def normal_back(grads, values, gain, into):
            scale = lax.rsqrt(jnp.mean(values * values, axis=1, keepdims=True) + EPSILON)
            hat = values * scale
            gains_out[into : into + 1] += jnp.sum(grads * hat, axis=0, keepdims=True)
            grads = grads * gain
            return scale * (grads - hat * jnp.mean(grads * hat, axis=1, keepdims=True))

        rotated_key = rotated_key_ref[block]
        value = raw_ref[block, :, wide + narrow :].astype(low)
        place = pl.ds(block * count, count)
        value_grad = key_grad = None
        for head in range(wide // HEAD_WIDTH):
            columns = slice(head * HEAD_WIDTH, (head + 1) * HEAD_WIDTH)
            grads = branch_ref[block, :, columns]
            probs = probs_ref[block, head]
            prob_grad = right_transposed(grads, value)
            term = left_trans(probs.astype(low), grads)
            value_grad = term if value_grad is None else value_grad + term
            balance = jnp.sum(probs * prob_grad, axis=1, keepdims=True)
            score_grad = (probs * (prob_grad - balance)).astype(low)
            query_grad = jnp.dot(score_grad, rotated_key, preferred_element_type=jnp.float32)
            term = left_trans(score_grad, rotated_ref[block, :, columns])
            key_grad = term if key_grad is None else key_grad + term
            query_grad = unturn(query_grad * HEAD_WIDTH ** (-0.5))
            query_grad = normal_back(
                query_grad, raw_ref[block, :, columns], query_gain_ref[...], 0
            )
            every[shard, place, columns] = query_grad.astype(low)
        key_grad = unturn(key_grad * HEAD_WIDTH ** (-0.5))
        key_grad = normal_back(
            key_grad, raw_ref[block, :, wide : wide + narrow], key_gain_ref[...], 1
        )
        every[shard, place, wide : wide + narrow] = key_grad.astype(low)
        every[shard, place, wide + narrow :] = value_grad.astype(low)

    def x_copy(part):
        view = every.at[shard, pl.ds(part * count, count)]
        return remote(view, view, x_sent.at[part], x_got.at[part], x_peer)

    def core_copy(far, part):
        view = every.at[(1 - x if far else x) * 2 + c, pl.ds(part * count, count)]
        return remote(view, view, core_sent.at[far, part], core_got.at[far, part], core_peer)

    gains_out[...] = jnp.zeros_like(gains_out)

    @pl.loop(0, 4)
    def _(block):
        attention_back(block)
        x_copy(block).start()
        core_copy(0, block).start()

    def weigh(place):
        weight_out[place] = left_trans(hidden_ref[...], every[place]).astype(weight_out.dtype)

    def back(place):
        grads = every[place]
        sums = None
        for weight, size, start in (
            (query_ref, wide, 0),
            (key_ref, narrow, wide),
            (value_ref, narrow, wide + narrow),
        ):
            columns = pl.ds(pl.multiple_of(place * size, size), size)
            term = right_transposed(grads[:, start : start + size], weight[:, columns])
            sums = term if sums is None else sums + term
        return sums

    def place_of(i):
        return (x + i // 2) % 2 * 2 + (c + i) % 2

    @pl.loop(0, 4)
    def _(i):
        @pl.when(i == 1)
        def _():
            for part in range(4):
                core_copy(0, part).wait_recv()

        @pl.when(i == 2)
        def _():
            for part in range(4):
                x_copy(part).wait_recv()
                core_copy(1, part).start()

        @pl.when(i == 3)
        def _():
            for part in range(4):
                core_copy(1, part).wait_recv()

        sums = back(place_of(i))

        @pl.when(i == 0)
        def _():
            total[...] = sums

        @pl.when(i > 0)
        def _():
            total[...] += sums

        @pl.when(i < 2)
        def _():
            weigh(place_of(i))

    for owner in range(4):
        outgoing[owner] = total[owner * count : (owner + 1) * count].astype(outgoing.dtype)

    def back_copy(j):
        place = (shard + j) % 4
        return remote(
            outgoing.at[place],
            first_out.at[shard],
            back_sent.at[j],
            back_got.at[(4 - j) % 4],
            (member, place),
        )

    for j in range(1, 4):
        back_copy(j).start()
    first_out[shard] = outgoing[shard]

    @pl.loop(2, 4)
    def _(i):
        weigh(place_of(i))

    for j in range(1, 4):
        place = (shard + j) % 4
        remote(
            outgoing.at[place], first_out.at[place], back_sent.at[j], back_got.at[j], (member, place)
        ).wait_recv()
    for j in range(1, 4):
        back_copy(j).wait_send()
    for part in range(4):
        x_copy(part).wait_send()
        for far in range(2):
            core_copy(far, part).wait_send()


def heads_back(branch, raw, probs, rotated, tables, gains, hidden, weights):
    rows = 4 * raw.shape[1]
    own = raw.shape[2]
    depth = hidden.shape[1]
    low = hidden.dtype
    operands = (branch, raw, probs, *rotated, *tables, *gains, hidden, *weights)
    return pl.pallas_call(
        fetching(heads_kernel, len(operands)),
        out_shape=[
            jax.ShapeDtypeStruct((4, depth, own), low),
            jax.ShapeDtypeStruct((4, rows // 4, depth), low),
            jax.ShapeDtypeStruct((8, HEAD_WIDTH), jnp.float32),
        ],
        in_specs=anywhere(len(operands)),
        out_specs=in_vmem(3),
        scratch_shapes=[
            pltpu.VMEM((4, rows, own), low),
            pltpu.VMEM((4, rows // 4, depth), low),
            pltpu.VMEM((rows, depth), jnp.float32),
            copies(4),
            copies(4),
            copies(2, 4),
            copies(2, 4),
            copies(4),
            copies(4),
        ]
        + room_for(operands),
        compiler_params=settings(7),
    )(*operands)


def moe_gathered(normed, router, routes, capacity, cotangent, weights, notes):
    gate_w, up_w, down_w = weights
    token_count, topk = routes.shape
    experts = router.shape[1]
    all_grads = lax.all_gather(cotangent, BOTH, axis=0, tiled=True)
    padded = jnp.pad(router, ((0, 0), (0, 128 - experts)))
    arrived, active, gate_pre, up_pre, share, select, spread = gather_experts(
        normed, notes, topk, capacity, gate_w, up_w, padded
    )
    mixed, out_rows, gate_pre_grad, up_pre_grad, extra = scatter_rows(
        spread,
        active,
        down_w,
        share,
        select,
        all_grads.reshape(experts, token_count, MODEL_WIDTH),
        gate_pre,
        up_pre,
    )
    summed, back, gate_w_grad, up_w_grad = scatter_rows(
        spread, gate_pre_grad, up_pre_grad, gate_w, up_w, extra, arrived
    )

    def flat(rows):
        return rows.reshape(experts * capacity, rows.shape[2])

    weight_grads = (gate_w_grad, up_w_grad, left_trans(flat(active), flat(out_rows)))
    columns = jnp.arange(experts, dtype=jnp.int32)
    gate_grad = back[:, :experts] + back[:, experts : 2 * experts]
    picks = jnp.any(routes[:, :, None] == columns[None, None, :], axis=1)
    gates = jax.nn.softmax(jnp.where(picks, matrix_product(normed, router), MASKED), axis=1)
    logit_grad = gates * (gate_grad - jnp.sum(gates * gate_grad, axis=1, keepdims=True))
    return mixed, summed, logit_grad.astype(jnp.bfloat16), *weight_grads


def moe_exchanged(normed, router, routes, capacity, cotangent, weights, notes):
    gate_w, up_w, down_w = weights
    token_count, topk = routes.shape
    experts = router.shape[1]
    gates = gates_of(matrix_product(normed, router), routes, experts)
    slots = slot_table(routes, experts, capacity)

    def send(rows):
        packed = jnp.zeros((experts * capacity, MODEL_WIDTH), jnp.bfloat16).at[slots].set(rows)
        return exchange(packed.reshape(experts, capacity, MODEL_WIDTH)).reshape(
            experts * capacity, MODEL_WIDTH
        )

    def bring(rows):
        rows = exchange(rows.reshape(experts, capacity, MODEL_WIDTH))
        return rows.reshape(experts * capacity, MODEL_WIDTH)[slots].reshape(
            token_count, topk, MODEL_WIDTH
        )

    arrived = send(jnp.repeat(normed, topk, axis=0))
    hidden = expert_forward(arrived, gate_w, up_w)
    scaled = (gates[:, :, None] * cotangent.astype(jnp.float32)[:, None, :]).astype(jnp.bfloat16)
    out_rows = send(scaled.reshape(token_count * topk, MODEL_WIDTH))
    rows_back, gate_pre_grad, up_pre_grad = expert_back(out_rows, hidden, gate_w, up_w, down_w)
    gate_w_grad = left_trans(arrived, gate_pre_grad)
    up_w_grad = left_trans(arrived, up_pre_grad)
    down_grad = left_trans(hidden[3], out_rows)
    returned = bring(matrix_product(hidden[3], down_w).astype(jnp.bfloat16))
    mixed = jnp.einsum("tk,tkd->td", gates, returned.astype(jnp.float32))
    gate_grad = jnp.einsum("td,tkd->tk", cotangent, returned, preferred_element_type=jnp.float32)
    summed = jnp.sum(bring(rows_back), axis=1, dtype=jnp.float32)
    picked_grad = gates * (gate_grad - jnp.sum(gates * gate_grad, axis=1, keepdims=True))
    onehot = routes[:, :, None] == jnp.arange(experts, dtype=jnp.int32)[None, None, :]
    logit_grad = jnp.sum(jnp.where(onehot, picked_grad[:, :, None], 0.0), axis=1)
    return mixed, summed, logit_grad.astype(jnp.bfloat16), gate_w_grad, up_w_grad, down_grad


def local(
    tokens,
    lengths,
    routes,
    attn_gain,
    w_query,
    key_weight,
    value_weight,
    q_gain,
    k_gain,
    w_out,
    mlp_gain,
    w_router,
    expert_gate,
    expert_up,
    expert_down,
    cotangent,
):
    shards, members = lax.axis_size("fsdp"), lax.axis_size("exp")
    experts = shards * members
    token_count, topk = routes.shape
    capacity = 2 * token_count * topk // experts
    group = shards * token_count
    depth = w_query.shape[0]
    heads = QUERY_HEADS // shards
    kv_heads = max(1, KEY_VALUE_HEADS // shards)
    copies_of = shards * kv_heads // KEY_VALUE_HEADS
    head_group = heads // kv_heads
    wide, narrow = heads * HEAD_WIDTH, kv_heads * HEAD_WIDTH
    place = lax.axis_index("fsdp")

    gathered = lax.all_gather(
        jnp.concatenate([w_router.reshape(-1), attn_gain, mlp_gain, q_gain, k_gain]), "fsdp"
    )
    cuts, start = [], 0
    for leaf in (w_router, attn_gain, mlp_gain, q_gain, k_gain):
        cuts.append(gathered[:, start : start + leaf.size])
        start += leaf.size
    router = cuts[0].reshape(MODEL_WIDTH, experts)
    gain_attn, gain_mlp, gain_query, gain_key = [
        cut.reshape(-1).astype(jnp.float32) for cut in cuts[1:]
    ]
    dense = (members, shards) == (8, 4) and 2 * capacity >= token_count
    inputs = tokens.astype(jnp.float32)
    scale_one = rms_scale(inputs)
    if dense:
        notes = jnp.pad(
            jnp.concatenate(
                [routes.T, jnp.pad(lengths, ((0, 0), (0, token_count - lengths.shape[1])))], axis=0
            ),
            ((0, 15 - topk), (0, 0)),
        )
        raw, hidden, notes = project_tokens(
            tokens, notes, attn_gain[None], w_query, key_weight, value_weight
        )
        hidden = hidden.reshape(group, depth)
        first = lax.axis_index("exp") * shards
        notes_own = lax.dynamic_slice_in_dim(notes, first, shards)
    else:
        notes = None
        all_lengths = lax.all_gather(lengths[0], "fsdp")

        def by_shard(weight):
            weight = weight.reshape(depth, KEY_VALUE_HEADS, HEAD_WIDTH)
            return jnp.repeat(weight, copies_of, axis=1).reshape(depth, shards, narrow)

        joined = jnp.concatenate(
            [w_query.reshape(depth, shards, wide), by_shard(key_weight), by_shard(value_weight)],
            axis=2,
        ).transpose(1, 0, 2)
        first_normed = (inputs * scale_one * gain_attn).astype(jnp.bfloat16)
        hidden = lax.all_to_all(first_normed, "fsdp", split_axis=1, concat_axis=0, tiled=True)
        partial = contract("gk,nkc->ngc", hidden, joined).astype(jnp.bfloat16)
        raw = lax.psum_scatter(partial, "fsdp", scatter_dimension=0, tiled=True)[0]
        raw = raw.astype(jnp.float32)
    if dense:
        gains = (gain_query[None], gain_key[None])
        middle, normed, attended, probs, *rotated, cosine, sine = finish_attention(
            raw, notes_own, topk, lengths.shape[1], *gains, w_out, tokens, gain_mlp[None]
        )
        attended = attended.reshape(group, wide)
        scale_two = rms_scale(middle)
    else:
        raw = raw.reshape(shards, token_count, wide + 2 * narrow)
        query_raw = raw[:, :, :wide].reshape(shards, token_count, heads, HEAD_WIDTH)
        key_raw = raw[:, :, wide : wide + narrow].reshape(shards, token_count, kv_heads, HEAD_WIDTH)
        value = (
            raw[:, :, wide + narrow :]
            .astype(jnp.bfloat16)
            .reshape(shards, token_count, kv_heads, HEAD_WIDTH)
        )
        position, allowed = jax.vmap(lambda row: seq_layout(row, token_count))(all_lengths)
        cosine, sine = rotary_tables(position, HEAD_WIDTH)
        query_scale = rms_scale(query_raw)
        query_hat = query_raw * query_scale
        key_scale = rms_scale(key_raw)
        key_hat = key_raw * key_scale
        query = (
            rotate(query_hat * gain_query, cosine, sine)
            .astype(jnp.bfloat16)
            .reshape(shards, token_count, kv_heads, head_group, HEAD_WIDTH)
        )
        key = rotate(key_hat * gain_key, cosine, sine).astype(jnp.bfloat16)
        scores = contract("bqkgd,bpkd->bkgqp", query, key) * HEAD_WIDTH ** (-0.5)
        scores = jnp.where(allowed[:, None, None], scores, MASKED)
        top = jnp.max(scores, axis=-1, keepdims=True)
        raised = jnp.exp(scores - top)
        probs = raised / jnp.sum(raised, axis=-1, keepdims=True)
        probs_low = probs.astype(jnp.bfloat16)
        attended = contract("bkgqp,bpkd->bqkgd", probs_low, value).astype(jnp.bfloat16)
        attended = attended.reshape(group, wide)
        mixed_heads = lax.psum_scatter(
            matrix_product(attended, w_out).astype(jnp.bfloat16),
            "fsdp",
            scatter_dimension=0,
            tiled=True,
        )
        middle = inputs + mixed_heads.astype(jnp.float32)
        scale_two = rms_scale(middle)
        normed = (middle * scale_two * gain_mlp).astype(jnp.bfloat16)

    moe = moe_gathered if dense else moe_exchanged
    mixed, summed, logit_grad, gate_w_grad, up_w_grad, down_grad = moe(
        normed,
        router,
        routes,
        capacity,
        cotangent,
        (expert_gate[0], expert_up[0], expert_down[0]),
        notes,
    )
    layer_out = (middle + mixed).astype(jnp.bfloat16)

    upstream = cotangent.astype(jnp.float32)
    normed_grad = summed + right_transposed(logit_grad, router)
    mlp_gain_grad = jnp.sum(normed_grad * middle * scale_two, axis=0)
    router_grad = left_trans(normed, logit_grad)
    middle_grad = upstream + rms_back(normed_grad * gain_mlp, middle, scale_two)
    branch_low = middle_grad.astype(jnp.bfloat16)
    if dense:
        attended_grad, branch_grad = branch_back(branch_low, w_out)
        branch_grad = branch_grad.reshape(group, MODEL_WIDTH)
    else:
        branch_grad = lax.all_gather(branch_low, "fsdp", axis=0, tiled=True)
        attended_grad = right_transposed(branch_grad, w_out).astype(jnp.bfloat16)
    out_w_grad = left_trans(attended, branch_grad).astype(jnp.bfloat16)
    attended_grad, out_w_grad = lax.optimization_barrier((attended_grad, out_w_grad))
    if dense:
        joined_grad, first_grad, gain_grads = heads_back(
            attended_grad,
            raw,
            probs,
            rotated,
            (cosine, sine),
            gains,
            hidden,
            (w_query, key_weight, value_weight),
        )
        first_grad = first_grad.transpose(1, 0, 2).reshape(token_count, MODEL_WIDTH)
        q_gain_grad, k_gain_grad = gain_grads[0], gain_grads[1]
    else:
        attended_grad = attended_grad.reshape(shards, token_count, kv_heads, head_group, HEAD_WIDTH)
        prob_grad = contract("bqkgd,bpkd->bkgqp", attended_grad, value)
        value_grad = contract("bkgqp,bqkgd->bpkd", probs_low, attended_grad)
        balance = jnp.sum(probs * prob_grad, axis=-1, keepdims=True)
        score_grad = (probs * (prob_grad - balance)).astype(jnp.bfloat16)
        query_norm_grad = contract("bkgqp,bpkd->bqkgd", score_grad, key) * HEAD_WIDTH ** (-0.5)
        query_norm_grad = query_norm_grad.reshape(shards, token_count, heads, HEAD_WIDTH)
        key_norm_grad = contract("bkgqp,bqkgd->bpkd", score_grad, query) * HEAD_WIDTH ** (-0.5)
        query_norm_grad = rotate_back(query_norm_grad, cosine, sine)
        key_norm_grad = rotate_back(key_norm_grad, cosine, sine)
        q_gain_grad = jnp.sum(query_norm_grad * query_hat, axis=(0, 1, 2))
        k_gain_grad = jnp.sum(key_norm_grad * key_hat, axis=(0, 1, 2))
        query_grad = rms_back(query_norm_grad * gain_query, query_raw, query_scale)
        key_grad = rms_back(key_norm_grad * gain_key, key_raw, key_scale)
        head_grads = jnp.concatenate(
            [
                query_grad.reshape(group, wide),
                key_grad.reshape(group, narrow),
                value_grad.reshape(group, narrow),
            ],
            axis=1,
        ).astype(jnp.bfloat16)
        head_grads = lax.all_gather(head_grads, "fsdp")
        hidden_grad = contract("ngc,nkc->gk", head_grads, joined).astype(jnp.bfloat16)
        first_grad = lax.all_to_all(
            hidden_grad, "fsdp", split_axis=0, concat_axis=1, tiled=True
        )
        joined_grad = contract("gk,ngc->nkc", hidden, head_grads).astype(jnp.bfloat16)
    first_grad = first_grad.astype(jnp.float32)
    attn_gain_grad = jnp.sum(first_grad * inputs * scale_one, axis=0)
    input_grad = (middle_grad + rms_back(first_grad * gain_attn, inputs, scale_one)).astype(
        jnp.bfloat16
    )

    vectors = jnp.concatenate(
        [
            grad.reshape(shards, -1)
            for grad in (router_grad, attn_gain_grad, mlp_gain_grad, q_gain_grad, k_gain_grad)
        ],
        axis=1,
    )
    if dense:
        rows = -(-vectors.shape[1] // 1024) * 8
        vectors = jnp.pad(vectors, ((0, 0), (0, rows * 128 - vectors.shape[1])))
        started = lengths[0, 0] > 0
        gate_w_grad, up_w_grad = (
            jnp.where(started, grad, 0.0) for grad in (gate_w_grad, up_w_grad)
        )
        out_sum = lax.psum_scatter(out_w_grad, "exp", scatter_dimension=0, tiled=True)
        joined_grad, vectors, out_sum, gate_w_grad, up_w_grad, down_grad = (
            lax.optimization_barrier(
                (joined_grad, vectors, out_sum, gate_w_grad, up_w_grad, down_grad)
            )
        )
        *joined_sum, out_sum, vectors = reduce_over_members(
            joined_grad.reshape(2, 4, -1, wide + 2 * narrow),
            out_sum,
            vectors.reshape(shards, rows, 128),
            (shards * wide, shards * narrow, shards * narrow),
        )
        out_sum, vectors = out_sum.reshape(w_out.shape), vectors.reshape(-1)
    else:
        out_sum = lax.psum(out_w_grad, "exp")
        joined_sum = lax.psum(joined_grad, "exp").astype(jnp.float32)
        vectors = lax.psum(vectors, BOTH)[place]
    if not dense:

        def gather_heads(part):
            part = part.transpose(1, 0, 2).reshape(depth, KEY_VALUE_HEADS, copies_of, HEAD_WIDTH)
            return part.sum(axis=2).reshape(depth, KEY_VALUE_HEADS * HEAD_WIDTH)

        joined_sum = (
            joined_sum[:, :, :wide].transpose(1, 0, 2).reshape(depth, QUERY_HEADS * HEAD_WIDTH),
            gather_heads(joined_sum[:, :, wide : wide + narrow]),
            gather_heads(joined_sum[:, :, wide + narrow :]),
        )
    query_sum, key_sum, value_sum = (part.astype(jnp.float32) for part in joined_sum)
    sums, start = [], 0
    for leaf in (w_router, attn_gain, mlp_gain, q_gain, k_gain):
        sums.append(vectors[start : start + leaf.size].reshape(leaf.shape))
        start += leaf.size

    return (
        layer_out,
        input_grad,
        sums[1],
        query_sum,
        key_sum,
        value_sum,
        sums[3],
        sums[4],
        out_sum.astype(jnp.float32),
        sums[2],
        sums[0],
        gate_w_grad[None],
        up_w_grad[None],
        down_grad[None],
    )


def solution(mesh):
    in_specs = (
        P(("exp", "fsdp"), None),
        P(("exp", "fsdp"), None),
        P(("exp", "fsdp"), None),
        P("fsdp"),
        P("fsdp", None),
        P("fsdp", None),
        P("fsdp", None),
        P("fsdp"),
        P("fsdp"),
        P("fsdp", None),
        P("fsdp"),
        P("fsdp", None),
        P(("exp", "fsdp"), None, None),
        P(("exp", "fsdp"), None, None),
        P(("exp", "fsdp"), None, None),
        P(("exp", "fsdp"), None),
    )
    out_specs = (
        P(("exp", "fsdp"), None),
        P(("exp", "fsdp"), None),
        P("fsdp"),
        P("fsdp", None),
        P("fsdp", None),
        P("fsdp", None),
        P("fsdp"),
        P("fsdp"),
        P("fsdp", None),
        P("fsdp"),
        P("fsdp", None),
        P(("exp", "fsdp"), None, None),
        P(("exp", "fsdp"), None, None),
        P(("exp", "fsdp"), None, None),
    )
    return jax.shard_map(local, mesh=mesh, in_specs=in_specs, out_specs=out_specs, check_vma=False)
```

```python
import functools
import math

import jax
import jax.numpy as jnp
from jax import lax
from jax.experimental import pallas as pl
from jax.experimental.pallas import tpu as pltpu
from jax.sharding import PartitionSpec as P

MODEL_WIDTH = 2048
QUERY_HEADS = 32
KEY_VALUE_HEADS = 4
HEAD_WIDTH = 128


EPSILON = 1e-06
THETA = 1000000.0
MASKED = -1e30
BOTH = ("exp", "fsdp")
MESH = pl.DeviceIdType.MESH


def matrix_product(left, right):
    return jnp.dot(left, right, preferred_element_type=jnp.float32)


def left_trans(left, right):
    return lax.dot_general(
        left, right, (((0,), (0,)), ((), ())), preferred_element_type=jnp.float32
    )


def right_transposed(left, right):
    return lax.dot_general(
        left, right, (((1,), (1,)), ((), ())), preferred_element_type=jnp.float32
    )


def contract(spec, left, right):
    return jnp.einsum(spec, left, right, preferred_element_type=jnp.float32)


def rms_scale(values):
    return lax.rsqrt(jnp.mean(values * values, axis=-1, keepdims=True) + EPSILON)


def rms_back(grad_hat, values, scale):
    normal = values * scale
    return scale * (grad_hat - normal * jnp.mean(grad_hat * normal, axis=-1, keepdims=True))


def seq_layout(length_row, token_count):
    ends = jnp.cumsum(length_row)
    starts = ends - length_row
    places = jnp.arange(token_count, dtype=jnp.int32)
    member = (places[:, None] >= starts[None, :]) & (places[:, None] < ends[None, :])
    numbers = jnp.arange(length_row.shape[0], dtype=jnp.int32)
    segment = jnp.sum(jnp.where(member, numbers[None, :], 0), axis=1)
    position = places - jnp.sum(jnp.where(member, starts[None, :], 0), axis=1)
    allowed = (segment[:, None] == segment[None, :]) & (places[None, :] <= places[:, None])
    return (position, allowed)


def rotary_tables(position, head_size):
    half = head_size // 2
    index = jnp.arange(head_size, dtype=jnp.int32) % half
    inverse = jnp.exp(index.astype(jnp.float32) * (-2.0 * math.log(THETA) / head_size))
    angles = position.astype(jnp.float32)[..., None] * inverse
    return (jnp.cos(angles)[..., None, :], jnp.sin(angles)[..., None, :])


def rotate(values, cosine, sine):
    half = values.shape[-1] // 2
    turned = jnp.concatenate([-values[..., half:], values[..., :half]], axis=-1)
    return values * cosine + turned * sine


def rotate_back(grads, cosine, sine):
    half = grads.shape[-1] // 2
    moved = grads * sine
    return grads * cosine + jnp.concatenate([moved[..., half:], -moved[..., :half]], axis=-1)


def slot_table(route_rows, experts, capacity):
    flat = route_rows.reshape(-1)
    onehot = (flat[:, None] == jnp.arange(experts, dtype=jnp.int32)[None, :]).astype(jnp.int32)
    ranks = jnp.cumsum(onehot, axis=0) - 1
    rank = jnp.sum(ranks * onehot, axis=1)
    return flat * capacity + rank


def exchange(buffer):
    return lax.all_to_all(buffer, BOTH, split_axis=0, concat_axis=0, tiled=True)


def two_halves(values):
    high = values.astype(jnp.bfloat16)
    low = (values - high.astype(jnp.float32)).astype(jnp.bfloat16)
    return high, low


def expert_forward(arrived, gate_w, up_w):
    gate_pre = matrix_product(arrived, gate_w)
    up_pre = matrix_product(arrived, up_w)
    sigma = jax.nn.sigmoid(gate_pre)
    active = (gate_pre * sigma * up_pre).astype(jnp.bfloat16)
    return gate_pre, up_pre, sigma, active


def expert_back(out_rows, hidden, gate_w, up_w, down_w):
    gate_pre, up_pre, sigma, _ = hidden
    active_grad = right_transposed(out_rows, down_w)
    gate_pre_grad = (active_grad * up_pre * (sigma * (1.0 + gate_pre * (1.0 - sigma)))).astype(
        jnp.bfloat16
    )
    up_pre_grad = (active_grad * (gate_pre * sigma)).astype(jnp.bfloat16)
    rows_back = right_transposed(gate_pre_grad, gate_w) + right_transposed(up_pre_grad, up_w)
    return rows_back.astype(jnp.bfloat16), gate_pre_grad, up_pre_grad


def gates_of(logits, routes, experts):
    picked = jnp.take_along_axis(logits, routes, axis=1)
    peak = jnp.max(picked, axis=1, keepdims=True)
    lifted = jnp.exp(picked - peak)
    return lifted / jnp.sum(lifted, axis=1, keepdims=True)


def spot():
    member, shard = lax.axis_index("exp"), lax.axis_index("fsdp")
    return member // 2, member % 2, shard // 2, shard % 2


def where_is(z, y, x, c):
    return (z * 2 + y, x * 2 + c)


def number(z, y, x, c):
    return z * 8 + y * 4 + x * 2 + c


def along_z(z, q):
    return (z // 2 + q // 2) % 2 * 2 + (z % 2 + q % 2) % 2


def greet(peers):
    barrier = pltpu.get_barrier_semaphore()
    for peer in peers:
        pl.semaphore_signal(barrier, inc=1, device_id=peer, device_id_type=MESH)
    pl.semaphore_wait(barrier, len(peers))


def remote(source, target, sent, got, peer):
    return pltpu.make_async_remote_copy(
        src_ref=source,
        dst_ref=target,
        send_sem=sent,
        recv_sem=got,
        device_id=peer,
        device_id_type=MESH,
    )


def in_vmem(count):
    return [pl.BlockSpec(memory_space=pltpu.VMEM)] * count


def copies(*shape):
    return pltpu.SemaphoreType.DMA(shape)


def settings(collective_id):
    return pltpu.CompilerParams(
        collective_id=collective_id, has_side_effects=True, vmem_limit_bytes=60 << 20
    )


def fetching(kernel, count):
    def run(*refs):
        given, refs = refs[:count], refs[count:]
        refs, held, fetched = refs[: -count - 1], refs[-count - 1 : -1], refs[-1]
        fetches = [
            pltpu.make_async_copy(source, target, fetched.at[i])
            for i, (source, target) in enumerate(zip(given, held))
        ]
        for fetch in fetches:
            fetch.start()
        kernel(fetches, *held, *refs)

    return run


def anywhere(count):
    return [pl.BlockSpec(memory_space=pl.ANY)] * count


def room_for(operands):
    held = [pltpu.VMEM(operand.shape, operand.dtype) for operand in operands]
    return held + [copies(len(operands))]


def wait_all(fetches):
    for fetch in fetches:
        fetch.wait()


def gather_kernel(
    topk,
    x_ref,
    notes_ref,
    gate_hbm,
    up_hbm,
    router_ref,
    rows_out,
    active_out,
    gate_out,
    up_out,
    share_out,
    select_out,
    spread_out,
    held,
    gate_ref,
    up_ref,
    picked,
    lively,
    results,
    loaded,
    stored,
    arrive,
    to_z,
    to_y,
    to_x,
    to_core,
    corners,
    deep_z,
    deep_core,
):
    z, y, x, c = spot()
    count = x_ref.shape[0]
    half, thin = count * 3 // 8, count // 8
    cuts = ((0, half), (half, half), (2 * half, thin), (2 * half + thin, thin), (2 * half, 2 * thin))
    kept = select_out.shape[1]
    y_peer, x_peer, core_peer = (
        where_is(z, 1 - y, x, c),
        where_is(z, y, 1 - x, c),
        where_is(z, y, x, 1 - c),
    )
    near_z, far_z = where_is(along_z(z, 1), y, x, c), where_is(along_z(z, 2), y, x, c)
    loads = [
        pltpu.make_async_copy(source, target, loaded.at[i])
        for i, (source, target) in enumerate(
            ((gate_hbm, gate_ref), (up_hbm, up_ref))
        )
    ]
    for load in loads:
        load.start()
    greet([y_peer, x_peer, core_peer, near_z, far_z])
    mine = number(z, y, x, c)

    def copy(block, part, sem, peer):
        view = held.at[block, pl.ds(*cuts[part])]
        return remote(view, view, sem, arrive.at[block, 2 if part == 4 else part], peer)

    def arrived(block, part):
        copy(block, part, to_core.at[0, 0, 0], core_peer).wait_recv()

    def block_of(q, other_y, other_x, core):
        return number(
            along_z(z, q), 1 - y if other_y else y, 1 - x if other_x else x, core
        )

    combos = ((0, 0), (0, 1), (1, 0), (1, 1))

    def stores(slot, blocks):
        made = []
        for k in range(4):
            part = pl.ds(k * kept, kept)
            made.append((picked.at[slot, part], rows_out.at[blocks[k]]))
            made.append((lively.at[slot, part], active_out.at[blocks[k]]))
            for i, out in enumerate((gate_out, up_out)):
                made.append((results.at[slot, i, part], out.at[blocks[k]]))
        return [
            pltpu.make_async_copy(source, target, stored.at[slot, i])
            for i, (source, target) in enumerate(made)
        ]

    def choose(block):
        notes = notes_ref[block]
        own = jnp.zeros((1, count), jnp.float32)
        lines = lax.broadcasted_iota(jnp.int32, (128, count), 0)
        names = jnp.zeros((128, count), jnp.float32)
        for k in range(topk):
            line = notes[k : k + 1]
            own = own + jnp.where(line == mine, 1.0, 0.0)
            names = names + jnp.where(lines == line, 1.0, 0.0)
        before = lax.broadcasted_iota(jnp.int32, (count, count), 0)
        before = before < lax.broadcasted_iota(jnp.int32, (count, count), 1)
        rank = jnp.dot(
            jnp.broadcast_to(own, (8, count)).astype(x_ref.dtype),
            jnp.where(before, 1.0, 0.0).astype(x_ref.dtype),
            preferred_element_type=jnp.float32,
        )[:1]
        places = lax.broadcasted_iota(jnp.int32, (kept, count), 0).astype(jnp.float32)
        chosen = jnp.where((rank == places) & (own > 0), 1.0, 0.0)
        spread_out[block] = jnp.transpose(chosen).astype(spread_out.dtype)
        chosen = chosen.astype(select_out.dtype)
        select_out[block] = chosen
        return chosen, right_transposed(chosen, names.astype(chosen.dtype))

    def work(q, slot):
        core = 1 - c if slot else c
        blocks = [block_of(q, *combo, core) for combo in combos]

        @pl.when(q > 0)
        def _():
            for store in stores(slot, [block_of(q - 1, *combo, core) for combo in combos]):
                store.wait()

        named = []
        for k in range(4):
            chosen, names = choose(blocks[k])
            named.append(names)
            rows = jnp.dot(chosen, held[blocks[k]], preferred_element_type=jnp.float32)
            picked[slot, k * kept : (k + 1) * kept] = rows.astype(picked.dtype)
        rows = picked[slot]
        gate_pre = jnp.dot(rows, gate_ref[...], preferred_element_type=jnp.float32)
        up_pre = jnp.dot(rows, up_ref[...], preferred_element_type=jnp.float32)
        logits = jnp.dot(rows, router_ref[...], preferred_element_type=jnp.float32)
        results[slot, 0] = gate_pre
        results[slot, 1] = up_pre
        active = gate_pre * (1.0 / (1.0 + jnp.exp(-gate_pre))) * up_pre
        lively[slot] = active.astype(lively.dtype)
        for k in range(4):
            part = slice(k * kept, (k + 1) * kept)
            block = blocks[k]
            masked = jnp.where(named[k] > 0, logits[part], MASKED)
            lifted = jnp.exp(masked - jnp.max(masked, axis=1, keepdims=True))
            lanes = lax.broadcasted_iota(jnp.int32, lifted.shape, 1)
            share = jnp.sum(jnp.where(lanes == mine, lifted, 0.0), axis=1, keepdims=True)
            share = share / jnp.sum(lifted, axis=1, keepdims=True)
            share_out[block] = jnp.broadcast_to(share, share_out.shape[1:])
        for store in stores(slot, blocks):
            store.start()

    def forward(q):
        block = block_of(q, 0, 0, c)
        if q:
            arrived(block, 0)
            arrived(block, 1)
        if q == 2:
            copy(block, 0, to_z.at[2, 0], near_z).start()
            copy(block, 1, to_z.at[2, 1], near_z).start()
        copy(block, 0, to_y.at[0, q], y_peer).start()
        copy(block, 1, to_x.at[0, q], x_peer).start()
        copy(block, 0, to_x.at[1, q], x_peer).start()
        copy(block, 1, to_y.at[1, q], y_peer).start()
        copy(block, 0, to_core.at[0, 0, q], core_peer).start()
        copy(block, 1, to_core.at[0, 1, q], core_peer).start()

    def second(q):
        block = block_of(q, 1, 0, c)
        arrived(block, 0)
        copy(block, 0, to_x.at[2, q], x_peer).start()
        copy(block, 0, to_core.at[1, 0, q], core_peer).start()
        block = block_of(q, 0, 1, c)
        arrived(block, 1)
        copy(block, 1, to_y.at[2, q], y_peer).start()
        copy(block, 1, to_core.at[2, 1, q], core_peer).start()

    def last(q):
        block = block_of(q, 0, 1, c)
        arrived(block, 0)
        copy(block, 0, to_core.at[2, 0, q], core_peer).start()
        block = block_of(q, 1, 0, c)
        arrived(block, 1)
        copy(block, 1, to_core.at[1, 1, q], core_peer).start()
        block = block_of(q, 1, 1, c)
        arrived(block, 0)
        copy(block, 0, to_core.at[3, 0, q], core_peer).start()
        arrived(block, 1)
        copy(block, 1, to_core.at[3, 1, q], core_peer).start()

    def others(q):
        for combo in combos:
            block = block_of(q, *combo, 1 - c)
            for part in (0, 1, 4):
                arrived(block, part)

    beside_x, beside_y, across = (block_of(0, *combo, c) for combo in combos[1:])

    def corner(i):
        block = (mine, mine, mine, mine, beside_x, beside_y)[i]
        part, peer = ((2, x_peer), (3, y_peer), (2, y_peer), (3, x_peer), (2, y_peer), (3, x_peer))[i]
        return copy(block, part, corners.at[i], peer)

    def deep_copy(kind, i, block):
        return copy(block, 4, deep_z.at[kind, i], far_z if kind == 1 else near_z)

    def deep_core_copy(q, i, block):
        return copy(block, 4, deep_core.at[q, i], core_peer)

    def deep_first():
        arrived(beside_x, 3)
        arrived(beside_y, 2)
        arrived(across, 2)
        arrived(across, 3)
        for i, combo in enumerate(combos):
            block = block_of(0, *combo, c)
            deep_copy(0, i, block).start()
            deep_copy(1, i, block).start()
            deep_core_copy(0, i, block).start()

    def deep_next(q):
        for i, combo in enumerate(combos):
            block = block_of(q, *combo, c)
            arrived(block, 4)
            if q == 2:
                deep_copy(2, i, block).start()
            deep_core_copy(q, i, block).start()

    held[mine] = x_ref[...]
    for part in range(2):
        copy(mine, part, to_z.at[0, part], near_z).start()
    for part in range(2):
        copy(mine, part, to_z.at[1, part], far_z).start()
    for i in range(4):
        corner(i).start()
    forward(0)
    for load in loads:
        load.wait()
    arrived(beside_x, 2)
    corner(4).start()
    arrived(beside_y, 3)
    corner(5).start()
    forward(1)
    second(0)
    deep_first()
    forward(2)
    second(1)

    @pl.loop(0, 4)
    def _(q):
        last(q)
        work(q, 0)
        others(q)
        work(q, 1)

        @pl.when(q == 0)
        def _():
            forward(3)
            deep_next(1)
            second(2)
            deep_next(2)

        @pl.when(q == 1)
        def _():
            second(3)
            deep_next(3)

    for slot in range(2):
        core = 1 - c if slot else c
        for store in stores(slot, [block_of(3, *combo, core) for combo in combos]):
            store.wait()
    for part in range(2):
        copy(mine, part, to_z.at[0, part], near_z).wait_send()
        copy(mine, part, to_z.at[1, part], far_z).wait_send()
        copy(mine, part, to_z.at[2, part], near_z).wait_send()

    for i in range(6):
        corner(i).wait_send()
    for i in range(4):
        for kind in range(3):
            deep_copy(kind, i, mine).wait_send()

    @pl.loop(0, 4)
    def _(q):
        for i in range(4):
            deep_core_copy(q, i, mine).wait_send()
        for i in range(3):
            copy(mine, 0, to_y.at[i, q], y_peer).wait_send()
            copy(mine, 0, to_x.at[i, q], x_peer).wait_send()
        for i in range(4):
            for part in range(2):
                copy(mine, part, to_core.at[i, part, q], core_peer).wait_send()


def gather_experts(rows, notes, topk, kept, gate_w, up_w, router):
    count, width = rows.shape
    blocks = notes.shape[0]
    hidden = gate_w.shape[1]
    low = rows.dtype
    anywhere = pl.BlockSpec(memory_space=pl.ANY)
    vmem = pl.BlockSpec(memory_space=pltpu.VMEM)
    return pl.pallas_call(
        functools.partial(gather_kernel, topk),
        out_shape=[
            jax.ShapeDtypeStruct((blocks, kept, width), low),
            jax.ShapeDtypeStruct((blocks, kept, hidden), low),
            jax.ShapeDtypeStruct((blocks, kept, hidden), jnp.float32),
            jax.ShapeDtypeStruct((blocks, kept, hidden), jnp.float32),
            jax.ShapeDtypeStruct((blocks, kept, 128), jnp.float32),
            jax.ShapeDtypeStruct((blocks, kept, count), low),
            jax.ShapeDtypeStruct((blocks, count, kept), low),
        ],
        in_specs=[vmem, vmem, anywhere, anywhere, vmem],
        out_specs=[anywhere] * 4 + [vmem] * 3,
        scratch_shapes=[
            pltpu.VMEM((blocks, count, width), low),
            pltpu.VMEM(gate_w.shape, low),
            pltpu.VMEM(up_w.shape, low),
            pltpu.VMEM((2, 4 * kept, width), low),
            pltpu.VMEM((2, 4 * kept, hidden), low),
            pltpu.VMEM((2, 2, 4 * kept, hidden), jnp.float32),
            copies(2),
            copies(2, 16),
            copies(blocks, 4),
            copies(3, 2),
            copies(3, 4),
            copies(3, 4),
            copies(4, 2, 4),
            copies(6),
            copies(3, 4),
            copies(4, 4),
        ],
        compiler_params=settings(1),
    )(rows, notes, gate_w, up_w, router)


def scatter_kernel(
    extended,
    *refs,
):
    resident = 6 if extended else 5
    streamed = 1 if extended else 3
    given, refs = refs[:resident], refs[resident:]
    sources, refs = refs[:streamed], refs[streamed:]
    if extended:
        (rows_hbm,) = sources
        out_ref, extra_out, gate_out, up_out = refs[:4]
        tiles, staged, loaded, stored = refs[4:8]
        refs = refs[8:]
    else:
        grads_hbm, gate_hbm, up_hbm = sources
        out_ref, rows_out, gate_out, up_out, extra_ref = refs[:5]
        grads_in, pre_in, rows_staged, staged, loaded, stored = refs[5:11]
        refs = refs[11:]
    held, (fetched, *refs) = refs[:resident], refs[resident:]
    if extended:
        spread_ref, gate_grad_ref, up_grad_ref, gate_ref, up_ref, extra_ref = held
    else:
        spread_ref, active_ref, down_ref, share_ref, select_ref = held
    outgoing, core_in, total, back, x_in, y_in, z_in, deep_in, deep_x, deep_y = refs[:10]
    core_sent, core_got, x_sent, x_got, y_sent, y_got, z_sent, z_got = refs[10:18]
    deep_sent, deep_got, corner_sent, corner_got = refs[18:]
    fetches = [
        pltpu.make_async_copy(source, target, fetched.at[i])
        for i, (source, target) in enumerate(zip(given, held))
    ]
    for fetch in fetches:
        fetch.start()
    z, y, x, c = spot()
    width = out_ref.shape[1]
    count = out_ref.shape[0]
    half, thin = count * 3 // 8, count // 8
    wide = 2 * half
    blocks, _, kept = spread_ref.shape
    y_peer, x_peer, core_peer = (
        where_is(z, 1 - y, x, c),
        where_is(z, y, 1 - x, c),
        where_is(z, y, x, 1 - c),
    )
    near_z, far_z = where_is(along_z(z, 1), y, x, c), where_is(along_z(z, 2), y, x, c)
    greet([y_peer, x_peer, core_peer, near_z, far_z])
    for fetch in fetches:
        fetch.wait()
    groups = ((1, 1), (0, 1), (1, 0), (0, 0))

    def block_of(group, q, core):
        other_y, other_x = groups[group]
        return number(along_z(z, q), 1 - y if other_y else y, 1 - x if other_x else x, core)

    def rows_of(ref, q, core):
        return jnp.concatenate([ref[block_of(group, q, core)] for group in range(4)], axis=0)

    def rows_back(q, core):
        if extended:
            sums = right_transposed(rows_of(gate_grad_ref, q, core), gate_ref[...])
            sums = sums + right_transposed(rows_of(up_grad_ref, q, core), up_ref[...])
        else:
            sums = jnp.dot(
                rows_of(active_ref, q, core), down_ref[...], preferred_element_type=jnp.float32
            )
            sums = sums.astype(back.dtype).astype(jnp.float32)
            sums = sums * rows_of(share_ref, q, core)[:, :1]
        back[...] = sums.astype(back.dtype)

    def turn_blocks(turn):
        core = (c + turn) % 2
        return [block_of(group, turn // 2, core) for group in range(4)]

    def loads(turn):
        slot, made = turn % 2, []
        if extended:
            columns = pl.ds(pl.multiple_of(turn * tiles.shape[3], tiles.shape[3]), tiles.shape[3])
            made.append((rows_hbm.at[:, :, columns], tiles.at[slot]))
        else:
            for group, block in enumerate(turn_blocks(turn)):
                rows = pl.ds(group * kept, kept)
                made.append((grads_hbm.at[block], grads_in.at[slot, group]))
                made.append((gate_hbm.at[block], pre_in.at[slot, 0, rows]))
                made.append((up_hbm.at[block], pre_in.at[slot, 1, rows]))
        return [
            pltpu.make_async_copy(source, target, loaded.at[slot, i])
            for i, (source, target) in enumerate(made)
        ]

    def stores(turn):
        slot, made = turn % 2, []
        if extended:
            columns = tiles.shape[3]
            rows = pl.ds(pl.multiple_of(turn * columns, columns), columns)
            made.append((staged.at[slot, 0], gate_out.at[rows]))
            made.append((staged.at[slot, 1], up_out.at[rows]))
        else:
            for group, block in enumerate(turn_blocks(turn)):
                rows = pl.ds(group * kept, kept)
                made.append((rows_staged.at[slot, rows], rows_out.at[block]))
                made.append((staged.at[slot, 0, rows], gate_out.at[block]))
                made.append((staged.at[slot, 1, rows], up_out.at[block]))
        return [
            pltpu.make_async_copy(source, target, stored.at[slot, i])
            for i, (source, target) in enumerate(made)
        ]

    def begin_loads(turn):
        for load in loads(turn):
            load.start()

    def fill(turn):
        for load in loads(turn):
            load.wait()

        @pl.when(turn >= 2)
        def _():
            for store in stores(turn - 2):
                store.wait()

        if extended:
            weigh(turn)
        else:
            prepare(turn)
        for store in stores(turn):
            store.start()

        @pl.when(turn < 6)
        def _():
            begin_loads(turn + 2)

    def weigh(turn):
        slot = turn % 2
        staged[slot] = jnp.zeros_like(staged[slot])

        @pl.loop(0, blocks // 4)
        def _(i):
            span = pl.ds(i * 4, 4)
            rows = tiles[slot, span].reshape(4 * kept, tiles.shape[3])
            for which, grads in enumerate((gate_grad_ref, up_grad_ref)):
                staged[slot, which] += left_trans(
                    rows, grads[span].reshape(4 * kept, grads.shape[2])
                )

    def prepare(turn):
        blocks, slot = turn_blocks(turn), turn % 2
        mine = number(z, y, x, c)
        parts = [
            jnp.dot(
                select_ref[blocks[group]],
                grads_in[slot, group],
                preferred_element_type=jnp.float32,
            )
            for group in range(4)
        ]
        share = jnp.concatenate([share_ref[block] for block in blocks], axis=0)[:, :1]
        picked = jnp.concatenate(parts, axis=0)
        rows_staged[slot] = (share * picked).astype(rows_staged.dtype)
        ahead = right_transposed(picked.astype(rows_staged.dtype), down_ref[...])
        gate, up = pre_in[slot, 0], pre_in[slot, 1]
        active = jnp.concatenate([active_ref[block] for block in blocks], axis=0)
        grad = jnp.sum(active.astype(jnp.float32) * ahead, axis=1, keepdims=True)
        active_grad = share * ahead
        sigma = 1.0 / (1.0 + jnp.exp(-gate))
        gate_grad = active_grad * up * (sigma * (1.0 + gate * (1.0 - sigma)))
        staged[slot, 0] = gate_grad.astype(staged.dtype)
        staged[slot, 1] = (active_grad * (gate * sigma)).astype(staged.dtype)
        lanes = lax.broadcasted_iota(jnp.int32, (4 * kept, 128), 1)
        high = grad.astype(extra_ref.dtype).astype(jnp.float32)
        both = jnp.where(lanes == mine, high, jnp.where(lanes == 32 + mine, grad - high, 0.0))
        both = both.astype(extra_ref.dtype)
        for group, block in enumerate(blocks):
            extra_ref[block] = both[group * kept : (group + 1) * kept]

    def part(block, group):
        rows = jnp.dot(
            spread_ref[block],
            back[group * kept : (group + 1) * kept],
            preferred_element_type=jnp.float32,
        )
        if not extended:
            return rows
        more = jnp.dot(spread_ref[block], extra_ref[block], preferred_element_type=jnp.float32)
        return jnp.concatenate([rows, more], axis=1)

    def across(group, q):
        return remote(
            outgoing.at[q, group],
            core_in.at[q, group],
            core_sent.at[q, group],
            core_got.at[q, group],
            core_peer,
        )

    def view(group, q, side):
        return total.at[q, group, pl.ds(side * half, half)]

    def x_copy(group, q, side, slot):
        return remote(
            view(group, q, side), x_in.at[slot, q], x_sent.at[slot, q], x_got.at[slot, q], x_peer
        )

    def y_copy(group, q, side, slot):
        return remote(
            view(group, q, side), y_in.at[slot, q], y_sent.at[slot, q], y_got.at[slot, q], y_peer
        )

    def z_copy(q):
        return remote(
            total.at[q, 3, pl.ds(0, wide)],
            z_in.at[q - 1],
            z_sent.at[q - 1],
            z_got.at[q - 1],
            where_is(along_z(z, 2 - q % 2), y, x, c),
        )

    def deep_copy(q):
        return remote(
            total.at[q, :, pl.ds(wide, 2 * thin)],
            deep_in.at[q - 1],
            deep_sent.at[q - 1],
            deep_got.at[q - 1],
            far_z if q == 2 else near_z,
        )

    def corner_copy(over_x, group, side, slot):
        place, peer = (deep_x, x_peer) if over_x else (deep_y, y_peer)
        return remote(
            total.at[0, group, pl.ds(wide + side * thin, thin)],
            place.at[slot],
            corner_sent.at[over_x, slot],
            corner_got.at[over_x, slot],
            peer,
        )

    y_corners = [corner_copy(0, 0, 0, 0), corner_copy(0, 2, 0, 1), corner_copy(0, 2, 1, 2)]
    x_corners = [corner_copy(1, 0, 1, 0), corner_copy(1, 1, 1, 1), corner_copy(1, 1, 0, 2)]

    def add_deep(q, *arrivals):
        rows = pl.ds(wide, 2 * thin)
        sums = total[q, :, rows].astype(jnp.float32)
        for arrival in arrivals:
            deep_copy(arrival).wait_recv()
            sums = sums + deep_in[arrival - 1].astype(jnp.float32)
        total[q, :, rows] = sums.astype(total.dtype)

    def add_corner(group, side, source):
        rows = pl.ds(wide + side * thin, thin)
        total[0, group, rows] = (
            total[0, group, rows].astype(jnp.float32) + source.astype(jnp.float32)
        ).astype(total.dtype)

    def deep_step(i):
        @pl.when(i == 0)
        def _():
            deep_copy(3).start()

        @pl.when(i == 1)
        def _():
            add_deep(2, 3)
            deep_copy(2).start()

        @pl.when(i == 2)
        def _():
            deep_copy(1).start()

        @pl.when(i == 3)
        def _():
            add_deep(0, 1, 2)
            for corner in (*y_corners[:2], *x_corners[:2]):
                corner.start()

        @pl.when(i == 4)
        def _():
            y_corners[0].wait_recv()
            add_corner(1, 0, deep_y[0])
            x_corners[2].start()
            x_corners[0].wait_recv()
            add_corner(2, 1, deep_x[0])
            y_corners[2].start()

    def add(group, q, side, source):
        rows = pl.ds(side * half, half)
        total[q, group, rows] = (
            total[q, group, rows].astype(jnp.float32) + source.astype(jnp.float32)
        ).astype(total.dtype)

    def begin(q):
        rows_back(q, 1 - c)
        for group in range(4):
            outgoing[q, group] = part(block_of(group, q, 1 - c), group).astype(total.dtype)
            across(group, q).start()
        rows_back(q, c)
        for group in range(4):
            sums = part(block_of(group, q, c), group)
            across(group, q).wait_recv()
            total[q, group] = (sums + core_in[q, group].astype(jnp.float32)).astype(total.dtype)
            if group == 0:
                x_copy(0, q, 0, 0).start()
                y_copy(0, q, 1, 0).start()
            if group == 1:
                x_copy(1, q, 0, 1).start()
            if group == 2:
                y_copy(2, q, 1, 1).start()

    def middle(q):
        x_copy(0, q, 0, 0).wait_recv()
        add(2, q, 0, x_in[0, q])
        y_copy(2, q, 0, 2).start()
        y_copy(0, q, 1, 0).wait_recv()
        add(1, q, 1, y_in[0, q])
        x_copy(1, q, 1, 2).start()

    def close(q):
        arrivals = (
            ((x_copy(1, q, 0, 1), x_in, 1), (y_copy(2, q, 0, 2), y_in, 2)),
            ((y_copy(2, q, 1, 1), y_in, 1), (x_copy(1, q, 1, 2), x_in, 2)),
        )
        for side in range(2):
            for arrival, _, _ in arrivals[side]:
                arrival.wait_recv()
            rows = pl.ds(side * half, half)
            sums = total[q, 3, rows].astype(jnp.float32)
            for _, source, slot in arrivals[side]:
                sums = sums + source[slot, q].astype(jnp.float32)
            total[q, 3, rows] = sums.astype(total.dtype)

        @pl.when(q == 2)
        def _():
            z_copy(3).wait_recv()
            rows = pl.ds(0, wide)
            total[2, 3, rows] = (
                total[2, 3, rows].astype(jnp.float32) + z_in[2].astype(jnp.float32)
            ).astype(total.dtype)

        @pl.when(q > 0)
        def _():
            z_copy(q).start()

    def done(i):
        return jnp.maximum(i, 0) + jnp.maximum(i - 2, 0)

    begin_loads(0)
    begin_loads(1)

    @pl.loop(0, 6)
    def _(i):
        @pl.when(i < 4)
        def _():
            begin(3 - i)

        @pl.loop(done(i - 1), done(i))
        def _(turn):
            fill(turn)

        deep_step(i)

        @pl.when((i > 0) & (i < 5))
        def _():
            middle(4 - i)

        @pl.when(i > 1)
        def _():
            close(5 - i)

    for turn in (6, 7):
        for store in stores(turn):
            store.wait()
    for q in (1, 2):
        z_copy(q).wait_recv()

    def finish(start, size, *more):
        rows = pl.ds(start, size)
        sums = total[0, 3, rows].astype(jnp.float32)
        for source in more:
            sums = sums + source.astype(jnp.float32)
        out_ref[rows] = sums[:, :width]
        if extended:
            extra_out[rows] = sums[:, width:]

    finish(0, wide, z_in[0], z_in[1])
    for slot in (1, 2):
        y_corners[slot].wait_recv()
        x_corners[slot].wait_recv()
    finish(wide, thin, deep_y[1], deep_x[2])
    finish(wide + thin, thin, deep_x[1], deep_y[2])
    for corner in (*y_corners, *x_corners):
        corner.wait_send()
    for q in range(1, 4):
        z_copy(q).wait_send()
        deep_copy(q).wait_send()

    @pl.loop(0, 4)
    def _(q):
        for group in range(4):
            across(group, q).wait_send()
        x_copy(0, q, 0, 0).wait_send()
        x_copy(1, q, 0, 1).wait_send()
        x_copy(1, q, 1, 2).wait_send()
        y_copy(0, q, 1, 0).wait_send()
        y_copy(2, q, 1, 1).wait_send()
        y_copy(2, q, 0, 2).wait_send()


def scatter_rows(spread, *operands):
    blocks, count, kept = spread.shape
    extended = len(operands) == 6
    width = operands[2].shape[0] if extended else operands[1].shape[1]
    wide = width + 128 if extended else width
    low = operands[0].dtype
    anywhere = pl.BlockSpec(memory_space=pl.ANY)
    resident = (spread, *operands[: 5 if extended else 4])
    outs = [jax.ShapeDtypeStruct((count, width), jnp.float32)]
    if extended:
        outs.append(jax.ShapeDtypeStruct((count, 128), jnp.float32))
        hidden = operands[0].shape[2]
        outs += [jax.ShapeDtypeStruct((width, hidden), jnp.float32)] * 2
        out_specs = in_vmem(2) + [anywhere] * 2
        filler = [
            pltpu.VMEM((2, blocks, kept, width // 8), low),
            pltpu.VMEM((2, 2, width // 8, hidden), jnp.float32),
            copies(2, 1),
            copies(2, 2),
        ]
    else:
        hidden = operands[0].shape[2]
        outs += [
            jax.ShapeDtypeStruct((blocks, kept, width), low),
            jax.ShapeDtypeStruct((blocks, kept, hidden), low),
            jax.ShapeDtypeStruct((blocks, kept, hidden), low),
            jax.ShapeDtypeStruct((blocks, kept, 128), low),
        ]
        out_specs = in_vmem(1) + [anywhere] * 3 + in_vmem(1)
        filler = [
            pltpu.VMEM((2, 4, count, width), low),
            pltpu.VMEM((2, 2, 4 * kept, hidden), jnp.float32),
            pltpu.VMEM((2, 4 * kept, width), low),
            pltpu.VMEM((2, 2, 4 * kept, hidden), low),
            copies(2, 12),
            copies(2, 12),
        ]
    return pl.pallas_call(
        functools.partial(scatter_kernel, extended),
        out_shape=outs,
        in_specs=[anywhere] * (1 + len(operands)),
        out_specs=out_specs,
        scratch_shapes=filler
        + [pltpu.VMEM(operand.shape, operand.dtype) for operand in resident]
        + [
            copies(len(resident)),
            pltpu.VMEM((4, 4, count, wide), low),
            pltpu.VMEM((4, 4, count, wide), low),
            pltpu.VMEM((4, 4, count, wide), low),
            pltpu.VMEM((4 * kept, width), low),
            pltpu.VMEM((3, 4, count * 3 // 8, wide), low),
            pltpu.VMEM((3, 4, count * 3 // 8, wide), low),
            pltpu.VMEM((3, count * 3 // 4, wide), low),
            pltpu.VMEM((3, 4, count // 4, wide), low),
            pltpu.VMEM((3, count // 8, wide), low),
            pltpu.VMEM((3, count // 8, wide), low),
            copies(4, 4),
            copies(4, 4),
            copies(3, 4),
            copies(3, 4),
            copies(3, 4),
            copies(3, 4),
            copies(3),
            copies(3),
            copies(3),
            copies(3),
            copies(2, 3),
            copies(2, 3),
        ],
        compiler_params=settings(2 if extended else 8),
    )(spread, *operands)


def reduce_kernel(
    cuts,
    fetches,
    parts_ref,
    own_ref,
    vector_ref,
    query_out,
    key_out,
    value_out,
    every_out,
    vector_out,
    sums_out,
    own_sent,
    own_got,
    own_side_sent,
    own_side_got,
    stored,
    *refs,
):
    z, y, x, c = spot()
    member, shard = lax.axis_index("exp"), lax.axis_index("fsdp")
    y_peer = where_is(z, 1 - y, x, c)
    near_z, far_z = where_is(along_z(z, 1), y, x, c), where_is(along_z(z, 2), y, x, c)
    members = [((member + j) % 8, shard) for j in range(8)]
    shards = [(member, (shard + j) % 4) for j in range(4)]
    greet(members[1:] + shards[1:])
    wait_all(fetches)
    pieces = len(cuts)
    first_got, first_held, first_z = refs[:3]
    y_got_in, y_held, y_z = refs[3:5], refs[5:7], refs[7:9]
    shard_in, member_own, member_in = refs[3 * pieces : 3 * pieces + 3]
    (
        y_sent,
        y_got,
        z_sent,
        z_got,
        back_sent,
        back_got,
        side_sent,
        side_got,
        shard_sent,
        shard_got,
        member_sent,
        member_got,
    ) = refs[3 * pieces + 3 :]

    def shard_copy(j):
        return remote(
            vector_ref.at[(shard + j) % 4],
            shard_in.at[(4 - j) % 4],
            shard_sent.at[j],
            shard_got.at[(4 - j) % 4],
            shards[j],
        )

    def member_copy(j):
        return remote(
            member_own,
            member_in.at[(8 - j) % 8],
            member_sent.at[j],
            member_got.at[(8 - j) % 8],
            members[j],
        )

    def rows(which):
        return pl.ds(*cuts[which])

    def z_peer(q):
        return far_z if q == 2 else near_z

    def y_copy(which, q):
        return remote(
            parts_ref.at[1 - y, along_z(z, q), rows(which)],
            y_got_in[which - 1].at[q],
            y_sent.at[which, q],
            y_got.at[which, q],
            y_peer,
        )

    def z_copy(which, q):
        if which:
            source, target = y_held[which - 1].at[q], y_z[which - 1].at[q]
        elif q == 2:
            source, target = first_held, first_z.at[2]
        else:
            source, target = parts_ref.at[:, along_z(z, q), rows(0)], first_z.at[q]
        return remote(source, target, z_sent.at[which, q], z_got.at[which, q], z_peer(q))

    def first_y():
        return remote(
            first_z.at[0, 1 - y], first_got, y_sent.at[0, 0], y_got.at[0, 0], y_peer
        )

    def place(side, q, which):
        return sums_out.at[side, along_z(z, q), rows(which)]

    def back_copy(which, q):
        held = along_z(z, 2) if q == 3 else z
        if which:
            view = sums_out.at[y, held, rows(which)]
        else:
            view = sums_out.at[:, held, rows(0)]
        return remote(view, view, back_sent.at[which, q], back_got.at[which, q], z_peer(q))

    def side_copy(which, q):
        view = place(y, q, which)
        return remote(view, view, side_sent.at[which, q], side_got.at[which, q], y_peer)

    def own_copy(q):
        view = every_out.at[along_z(z, 2) if q == 3 else z, y]
        return remote(view, view, own_sent.at[q], own_got.at[q], z_peer(q))

    def own_side(q):
        view = every_out.at[along_z(z, q), y]
        return remote(view, view, own_side_sent.at[q], own_side_got.at[q], y_peer)

    def pass_on(q):
        own_copy(q).wait_recv()
        if q == 2:
            own_copy(3).start()
        own_side(q).start()

    def exports(side, q):
        zone = along_z(z, q)
        head, rows = side * 2 + zone // 2, zone % 2
        made, start = [], 0
        for i, out in enumerate((query_out, key_out, value_out)):
            size, depth = out.shape[1] // 4, parts_ref.shape[2]
            source = sums_out.at[side, zone, :, pl.ds(start, size)]
            target = out.at[
                pl.ds(pl.multiple_of(rows * depth, depth), depth),
                pl.ds(pl.multiple_of(head * size, size), size),
            ]
            made.append(pltpu.make_async_copy(source, target, stored.at[side, q, i]))
            start += size
        return made

    later = range(1, pieces)
    every_out[z, y] = own_ref[...]
    for j in range(1, 4):
        shard_copy(j).start()
    z_copy(0, 3).start()
    own_copy(1).start()
    own_copy(2).start()
    for q in (3, 2, 1, 0):
        for which in later:
            y_copy(which, q).start()
    z_copy(0, 1).start()
    own_side(0).start()

    for j in range(1, 4):
        shard_copy(j).wait_recv()
    sums = vector_ref[shard]
    for j in range(1, 4):
        sums = sums + shard_in[j]
    member_own[...] = sums
    for j in range(1, 8):
        member_copy(j).start()

    def add_y(which, q):
        y_copy(which, q).wait_recv()
        sums = parts_ref[y, along_z(z, q), rows(which)].astype(jnp.float32)
        sums = sums + y_got_in[which - 1][q].astype(jnp.float32)
        held, z_in = y_held[which - 1], y_z[which - 1]
        if q == 2:
            z_copy(which, 3).wait_recv()
            sums = sums + z_in[3].astype(jnp.float32)
        if q:
            held[q] = sums.astype(held.dtype)
            z_copy(which, q).start()
            return
        for turn in (1, 2):
            z_copy(which, turn).wait_recv()
            sums = sums + z_in[turn].astype(jnp.float32)
        sums_out[y, z, rows(which)] = sums.astype(sums_out.dtype)
        side_copy(which, 0).start()
        back_copy(which, 2).start()
        back_copy(which, 1).start()

    for which in later:
        add_y(which, 3)
    z_copy(0, 3).wait_recv()
    first_held[...] = (
        parts_ref[:, along_z(z, 2), rows(0)].astype(jnp.float32) + first_z[3].astype(jnp.float32)
    ).astype(first_held.dtype)
    z_copy(0, 2).start()
    pass_on(1)
    for which in later:
        add_y(which, 2)
    pass_on(2)
    z_copy(0, 1).wait_recv()
    z_copy(0, 2).wait_recv()
    first_z[0] = (
        parts_ref[:, z, rows(0)].astype(jnp.float32)
        + first_z[1].astype(jnp.float32)
        + first_z[2].astype(jnp.float32)
    ).astype(first_z.dtype)
    first_y().start()
    for which in later:
        add_y(which, 1)
    pass_on(3)
    first_y().wait_recv()
    sums = first_z[0, y].astype(jnp.float32) + first_got[...].astype(jnp.float32)
    sums_out[y, z, rows(0)] = sums.astype(sums_out.dtype)
    side_copy(0, 0).start()
    for which in later:
        add_y(which, 0)
    side_copy(0, 0).wait_recv()
    back_copy(0, 2).start()
    back_copy(0, 1).start()

    for j in range(1, 8):
        member_copy(j).wait_recv()
    sums = member_own[...]
    for j in range(1, 8):
        sums = sums + member_in[j]
    vector_out[...] = sums

    for q in (1, 2, 3):
        for which in later:
            back_copy(which, q).wait_recv()
            if q == 2:
                back_copy(which, 3).start()
            side_copy(which, q).start()
        back_copy(0, q).wait_recv()
        if q == 2:
            back_copy(0, 3).start()

    for q in range(4):
        for export in exports(y, q):
            export.start()
    for q in range(4):
        for which in later:
            side_copy(which, q).wait_recv()
        for export in exports(1 - y, q):
            export.start()
    for q in range(4):
        own_side(q).wait_recv()
    for q in range(4):
        for side in (y, 1 - y):
            for export in exports(side, q):
                export.wait()
    for q in range(4):
        own_side(q).wait_send()
        if q:
            own_copy(q).wait_send()
    for which in range(pieces):
        for q in range(4):
            if which:
                y_copy(which, q).wait_send()
                side_copy(which, q).wait_send()
            if q:
                z_copy(which, q).wait_send()
                back_copy(which, q).wait_send()
    side_copy(0, 0).wait_send()
    first_y().wait_send()
    for j in range(1, 4):
        shard_copy(j).wait_send()
    for j in range(1, 8):
        member_copy(j).wait_send()


def reduce_over_members(parts, own, vectors, widths):
    low = parts.dtype
    depth, width = parts.shape[2:]
    early = depth // 4 // 16 * 16
    half = (depth - early) // 2 // 16 * 16
    cuts = ((0, early), (early, half), (early + half, depth - early - half))
    anywhere = pl.BlockSpec(memory_space=pl.ANY)

    def quarters(*lead):
        return [pltpu.VMEM((*lead, size, width), low) for _, size in cuts[1:]]

    return pl.pallas_call(
        fetching(functools.partial(reduce_kernel, cuts), 3),
        out_shape=[jax.ShapeDtypeStruct((2 * depth, size), low) for size in widths]
        + [
            jax.ShapeDtypeStruct((4, 2, *own.shape), low),
            jax.ShapeDtypeStruct(vectors.shape[1:], vectors.dtype),
        ],
        in_specs=[anywhere] * 3,
        out_specs=[anywhere] * 3 + in_vmem(2),
        scratch_shapes=[
            pltpu.VMEM(parts.shape, low),
            copies(4),
            copies(4),
            copies(4),
            copies(4),
            copies(2, 4, 3),
            pltpu.VMEM((early, width), low),
            pltpu.VMEM((2, early, width), low),
            pltpu.VMEM((4, 2, early, width), low),
            *quarters(4),
            *quarters(4),
            *quarters(4),
            pltpu.VMEM(vectors.shape, vectors.dtype),
            pltpu.VMEM(vectors.shape[1:], vectors.dtype),
            pltpu.VMEM((8, *vectors.shape[1:]), vectors.dtype),
        ]
        + [copies(3, 4)] * 8
        + [copies(4)] * 2
        + [copies(8)] * 2
        + room_for((parts, own, vectors)),
        compiler_params=settings(3),
    )(parts, own, vectors)


def project_kernel(
    fetches,
    x_ref,
    routes_ref,
    gain_ref,
    query_ref,
    key_ref,
    value_ref,
    raw_out,
    hidden_out,
    routes_out,
    scale,
    x_in,
    scale_in,
    outgoing,
    core_in,
    across_x,
    x_sums,
    slice_sent,
    slice_got,
    scale_sent,
    scale_got,
    core_sent,
    core_got,
    x_sent,
    x_got,
    route_sent,
    route_got,
):
    z, y, x, c = spot()
    member, shard = lax.axis_index("exp"), lax.axis_index("fsdp")
    mine = number(z, y, x, c)
    count, depth = hidden_out.shape[1:]
    wide, narrow = query_ref.shape[1] // 4, key_ref.shape[1] // 4

    def everyone(j):
        other = (mine + j) % 32
        return (other // 4, other % 4)

    barrier = pltpu.get_barrier_semaphore()

    @pl.loop(1, 32)
    def _(j):
        pl.semaphore_signal(barrier, inc=1, device_id=everyone(j), device_id_type=MESH)

    pl.semaphore_wait(barrier, 31)
    wait_all(fetches)

    def slice_copy(j):
        place = (shard + j) % 4
        return remote(
            x_ref.at[:, pl.ds(pl.multiple_of(place * depth, depth), depth)],
            x_in.at[(4 - j) % 4],
            slice_sent.at[j],
            slice_got.at[(4 - j) % 4],
            (member, place),
        )

    def scale_copy(j):
        return remote(
            scale,
            scale_in.at[(4 - j) % 4],
            scale_sent.at[j],
            scale_got.at[(4 - j) % 4],
            (member, (shard + j) % 4),
        )

    def route_copy(j):
        return remote(
            routes_ref, routes_out.at[mine], route_sent.at[j], route_got.at[(32 - j) % 32], everyone(j)
        )

    for j in range(1, 4):
        slice_copy(j).start()
    values = x_ref[...].astype(jnp.float32)
    scale[...] = jnp.broadcast_to(
        lax.rsqrt(jnp.mean(values * values, axis=1, keepdims=True) + EPSILON), scale.shape
    )
    for j in range(1, 4):
        scale_copy(j).start()
    routes_out[mine] = routes_ref[...]

    @pl.loop(1, 32)
    def _(j):
        route_copy(j).start()

    def hide(owner, piece, factor):
        gain = gain_ref[...].astype(jnp.float32)
        hidden = piece.astype(jnp.float32) * factor[:, :1] * gain
        hidden_out[owner] = hidden.astype(hidden_out.dtype)

    hide(shard, x_ref[:, pl.ds(pl.multiple_of(shard * depth, depth), depth)], scale[...])

    def take(owner):
        slot = (owner - shard + 4) % 4
        remote(x_in.at[slot], x_in.at[slot], slice_sent.at[slot], slice_got.at[slot], (member, owner)).wait_recv()
        remote(scale, scale_in.at[slot], scale_sent.at[slot], scale_got.at[slot], (member, owner)).wait_recv()
        hide(owner, x_in[slot], scale_in[slot])

    def partial(side, target):
        rows = jnp.concatenate([hidden_out[side * 2], hidden_out[side * 2 + 1]], axis=0)
        parts = []
        for weight, size in ((query_ref, wide), (key_ref, narrow), (value_ref, narrow)):
            columns = pl.ds(pl.multiple_of(target * size, size), size)
            parts.append(jnp.dot(rows, weight[:, columns], preferred_element_type=jnp.float32))
        return jnp.concatenate(parts, axis=1)

    core_peer, x_peer = where_is(z, y, x, 1 - c), where_is(z, y, 1 - x, c)

    def core_copy(turn, far):
        return remote(
            outgoing.at[turn, far],
            core_in.at[turn, far],
            core_sent.at[turn, far],
            core_got.at[turn, far],
            core_peer,
        )

    def x_copy(turn):
        return remote(across_x.at[turn], x_sums.at[turn], x_sent.at[turn], x_got.at[turn], x_peer)

    low = outgoing.dtype
    for turn in range(2):
        side = x if turn == 0 else 1 - x
        if turn == 0:
            take(side * 2 + 1 - c)
        else:
            take(side * 2 + c)
            take(side * 2 + 1 - c)
        outgoing[turn, 1] = partial(side, (1 - x) * 2 + 1 - c).astype(low)
        core_copy(turn, 1).start()
        sums = partial(side, (1 - x) * 2 + c)
        core_copy(turn, 1).wait_recv()
        across_x[turn] = (sums + core_in[turn, 1].astype(jnp.float32)).astype(low)
        x_copy(turn).start()
        outgoing[turn, 0] = partial(side, x * 2 + 1 - c).astype(low)
        core_copy(turn, 0).start()

    for turn in range(2):
        side = x if turn == 0 else 1 - x
        sums = partial(side, x * 2 + c)
        core_copy(turn, 0).wait_recv()
        sums = sums + core_in[turn, 0].astype(jnp.float32)
        raw_out[side * 2] = sums[:count]
        raw_out[side * 2 + 1] = sums[count:]

    for turn in range(2):
        side = 1 - x if turn == 0 else x
        x_copy(turn).wait_recv()
        raw_out[side * 2] += x_sums[turn, :count].astype(jnp.float32)
        raw_out[side * 2 + 1] += x_sums[turn, count:].astype(jnp.float32)

    @pl.loop(1, 32)
    def _(j):
        remote(
            routes_ref, routes_out.at[(mine + j) % 32], route_sent.at[j], route_got.at[j], everyone(j)
        ).wait_recv()

    @pl.loop(1, 32)
    def _(j):
        route_copy(j).wait_send()

    for j in range(1, 4):
        slice_copy(j).wait_send()
        scale_copy(j).wait_send()
    for turn in range(2):
        x_copy(turn).wait_send()
        for far in range(2):
            core_copy(turn, far).wait_send()


def project_tokens(tokens, routes, gain, w_query, key_weight, value_weight):
    count = tokens.shape[0]
    depth = w_query.shape[0]
    own = (w_query.shape[1] + key_weight.shape[1] + value_weight.shape[1]) // 4
    low = tokens.dtype
    return pl.pallas_call(
        fetching(project_kernel, 6),
        out_shape=[
            jax.ShapeDtypeStruct((4, count, own), jnp.float32),
            jax.ShapeDtypeStruct((4, count, depth), low),
            jax.ShapeDtypeStruct((32, *routes.shape), routes.dtype),
        ],
        in_specs=anywhere(6),
        out_specs=in_vmem(3),
        scratch_shapes=[
            pltpu.VMEM((count, 128), jnp.float32),
            pltpu.VMEM((4, count, depth), low),
            pltpu.VMEM((4, count, 128), jnp.float32),
            pltpu.VMEM((2, 2, 2 * count, own), low),
            pltpu.VMEM((2, 2, 2 * count, own), low),
            pltpu.VMEM((2, 2 * count, own), low),
            pltpu.VMEM((2, 2 * count, own), low),
            copies(4),
            copies(4),
            copies(4),
            copies(4),
            copies(2, 2),
            copies(2, 2),
            copies(2),
            copies(2),
            copies(32),
            copies(32),
        ]
        + room_for((tokens, routes, gain, w_query, key_weight, value_weight)),
        compiler_params=settings(4),
    )(tokens, routes, gain, w_query, key_weight, value_weight)


def turned(values):
    return pltpu.roll(values, HEAD_WIDTH // 2, 1)


def signed(sine):
    lanes = lax.broadcasted_iota(jnp.int32, sine.shape, 1)
    return jnp.where(lanes < HEAD_WIDTH // 2, -sine, sine)


def finish_kernel(
    row,
    sequences,
    fetches,
    raw_ref,
    notes_ref,
    query_gain_ref,
    key_gain_ref,
    weight_ref,
    x_ref,
    gain_ref,
    middle_out,
    normed_out,
    attended_out,
    probs_out,
    query_out,
    key_out,
    cosine_out,
    sine_out,
    outgoing,
    core_in,
    across_x,
    x_sums,
    core_sent,
    core_got,
    x_sent,
    x_got,
):
    z, y, x, c = spot()
    count = x_ref.shape[0]
    core_peer, x_peer = where_is(z, y, x, 1 - c), where_is(z, y, 1 - x, c)
    greet([core_peer, x_peer])
    wait_all(fetches)
    heads = query_out.shape[2] // HEAD_WIDTH
    wide = heads * HEAD_WIDTH

    def place(block):
        down = lax.broadcasted_iota(jnp.int32, (count, count), 0)
        along = lax.broadcasted_iota(jnp.int32, (count, count), 1)
        end = jnp.zeros((1, 1), jnp.int32)
        start = jnp.zeros((count, count), jnp.int32)
        own, other = start, start
        for i in range(sequences - 1):
            length = notes_ref[block, row : row + 1, i : i + 1]
            end = end + length
            own = own + jnp.where(down >= end, 1, 0)
            other = other + jnp.where(along >= end, 1, 0)
            start = start + jnp.where(down >= end, length, 0)
        return down - start, (own == other) & (along <= down)

    def attend(block):
        position, allowed = place(block)
        lanes = lax.broadcasted_iota(jnp.int32, position.shape, 1)
        spin = lanes % (HEAD_WIDTH // 2)
        inverse = jnp.exp(spin.astype(jnp.float32) * (-2.0 * math.log(THETA) / HEAD_WIDTH))
        angles = position.astype(jnp.float32) * inverse
        cosine, sine = jnp.cos(angles), jnp.sin(angles)
        cosine_out[block] = cosine
        sine_out[block] = sine
        flipped = signed(sine)

        def normal(values, gain):
            scale = lax.rsqrt(jnp.mean(values * values, axis=1, keepdims=True) + EPSILON)
            values = values * scale * gain
            return (values * cosine + turned(values) * flipped).astype(query_out.dtype)

        key = normal(raw_ref[block, :, wide : wide + HEAD_WIDTH], key_gain_ref[...])
        key_out[block] = key
        value = raw_ref[block, :, wide + HEAD_WIDTH :].astype(query_out.dtype)
        for head in range(heads):
            columns = slice(head * HEAD_WIDTH, (head + 1) * HEAD_WIDTH)
            query = normal(raw_ref[block, :, columns], query_gain_ref[...])
            query_out[block, :, columns] = query
            scores = right_transposed(query, key) * HEAD_WIDTH ** (-0.5)
            scores = jnp.where(allowed, scores, MASKED)
            raised = jnp.exp(scores - jnp.max(scores, axis=1, keepdims=True))
            probs = raised / jnp.sum(raised, axis=1, keepdims=True)
            probs_out[block, head] = probs
            attended_out[block, :, columns] = jnp.dot(
                probs.astype(value.dtype), value, preferred_element_type=jnp.float32
            ).astype(attended_out.dtype)

    def core_copy(far):
        return remote(
            outgoing.at[far], core_in.at[far], core_sent.at[far], core_got.at[far], core_peer
        )

    def x_copy():
        return remote(across_x, x_sums, x_sent, x_got, x_peer)

    @pl.loop(0, 4)
    def _(i):
        block = (1 - x + i // 2) % 2 * 2 + (1 - c + i) % 2
        far = 1 - i // 2
        attend(block)
        product = jnp.dot(attended_out[block], weight_ref[...], preferred_element_type=jnp.float32)

        @pl.when(i % 2 == 0)
        def _():
            outgoing[far] = product.astype(outgoing.dtype)
            core_copy(far).start()

        @pl.when(i == 1)
        def _():
            core_copy(1).wait_recv()
            across_x[...] = (product + core_in[1].astype(jnp.float32)).astype(across_x.dtype)
            x_copy().start()

        @pl.when(i == 3)
        def _():
            core_copy(0).wait_recv()
            sums = product + x_ref[...].astype(jnp.float32)
            middle_out[...] = sums + core_in[0].astype(jnp.float32)

    x_copy().wait_recv()
    middle = middle_out[...] + x_sums[...].astype(jnp.float32)
    middle_out[...] = middle
    scale = lax.rsqrt(jnp.mean(middle * middle, axis=1, keepdims=True) + EPSILON)
    normed_out[...] = (middle * scale * gain_ref[...]).astype(normed_out.dtype)
    x_copy().wait_send()
    core_copy(0).wait_send()
    core_copy(1).wait_send()


def finish_attention(raw, notes, row, sequences, q_gain, k_gain, w_out, tokens, gain):
    count, width = tokens.shape
    low = tokens.dtype
    wide = w_out.shape[0]
    heads = wide // HEAD_WIDTH
    operands = (raw, notes, q_gain, k_gain, w_out, tokens, gain)
    return pl.pallas_call(
        fetching(functools.partial(finish_kernel, row, sequences), len(operands)),
        out_shape=[
            jax.ShapeDtypeStruct((count, width), jnp.float32),
            jax.ShapeDtypeStruct((count, width), low),
            jax.ShapeDtypeStruct((4, count, wide), low),
            jax.ShapeDtypeStruct((4, heads, count, count), jnp.float32),
            jax.ShapeDtypeStruct((4, count, wide), low),
            jax.ShapeDtypeStruct((4, count, HEAD_WIDTH), low),
            jax.ShapeDtypeStruct((4, count, HEAD_WIDTH), jnp.float32),
            jax.ShapeDtypeStruct((4, count, HEAD_WIDTH), jnp.float32),
        ],
        in_specs=anywhere(len(operands)),
        out_specs=in_vmem(8),
        scratch_shapes=[
            pltpu.VMEM((2, count, width), low),
            pltpu.VMEM((2, count, width), low),
            pltpu.VMEM((count, width), low),
            pltpu.VMEM((count, width), low),
            copies(2),
            copies(2),
            copies(),
            copies(),
        ]
        + room_for(operands),
        compiler_params=settings(5),
    )(*operands)


def branch_kernel(
    fetches, branch_ref, weight_ref, grad_out, every_out, x_sent, x_got, core_sent, core_got
):
    z, y, x, c = spot()
    mine = x * 2 + c
    core_peer, x_peer = where_is(z, y, x, 1 - c), where_is(z, y, 1 - x, c)
    half = branch_ref.shape[0] // 2
    greet([core_peer, x_peer])
    wait_all(fetches)
    every_out[mine] = branch_ref[...]

    def x_copy(part):
        rows = pl.ds(part * half, half)
        return remote(
            branch_ref.at[rows], every_out.at[mine, rows], x_sent.at[part], x_got.at[part], x_peer
        )

    def core_copy(far, part):
        view = every_out.at[(1 - x if far else x) * 2 + c, pl.ds(part * half, half)]
        return remote(view, view, core_sent.at[far, part], core_got.at[far, part], core_peer)

    def back(place):
        grad_out[place] = right_transposed(every_out[place], weight_ref[...]).astype(grad_out.dtype)

    for part in range(2):
        x_copy(part).start()
        core_copy(0, part).start()
    back(mine)
    for part in range(2):
        core_copy(0, part).wait_recv()
    back(x * 2 + 1 - c)
    for part in range(2):
        x_copy(part).wait_recv()
        core_copy(1, part).start()
    back((1 - x) * 2 + c)
    for part in range(2):
        core_copy(1, part).wait_recv()
    back((1 - x) * 2 + 1 - c)
    for part in range(2):
        x_copy(part).wait_send()
        core_copy(0, part).wait_send()
        core_copy(1, part).wait_send()


def branch_back(branch, w_out):
    count, width = branch.shape
    low = branch.dtype
    return pl.pallas_call(
        fetching(branch_kernel, 2),
        out_shape=[
            jax.ShapeDtypeStruct((4, count, w_out.shape[0]), low),
            jax.ShapeDtypeStruct((4, count, width), low),
        ],
        in_specs=anywhere(2),
        out_specs=in_vmem(2),
        scratch_shapes=[copies(2), copies(2), copies(2, 2), copies(2, 2)]
        + room_for((branch, w_out)),
        compiler_params=settings(6),
    )(branch, w_out)


def heads_kernel(
    fetches,
    branch_ref,
    raw_ref,
    probs_ref,
    rotated_ref,
    rotated_key_ref,
    cosine_ref,
    sine_ref,
    query_gain_ref,
    key_gain_ref,
    hidden_ref,
    query_ref,
    key_ref,
    value_ref,
    weight_out,
    first_out,
    gains_out,
    every,
    outgoing,
    total,
    x_sent,
    x_got,
    core_sent,
    core_got,
    back_sent,
    back_got,
):
    z, y, x, c = spot()
    member, shard = lax.axis_index("exp"), lax.axis_index("fsdp")
    core_peer, x_peer = where_is(z, y, x, 1 - c), where_is(z, y, 1 - x, c)
    peers = [(member, (shard + j) % 4) for j in range(1, 4)]
    greet(peers)
    wait_all(fetches)
    rows = every.shape[1]
    count = rows // 4
    depth = hidden_ref.shape[1]
    wide, narrow = query_ref.shape[1] // 4, key_ref.shape[1] // 4
    low = every.dtype

    def attention_back(block):
        cosine = cosine_ref[block]
        flipped = signed(sine_ref[block])

        def unturn(grads):
            return grads * cosine + turned(grads * flipped)

        def normal_back(grads, values, gain, into):
            scale = lax.rsqrt(jnp.mean(values * values, axis=1, keepdims=True) + EPSILON)
            hat = values * scale
            gains_out[into : into + 1] += jnp.sum(grads * hat, axis=0, keepdims=True)
            grads = grads * gain
            return scale * (grads - hat * jnp.mean(grads * hat, axis=1, keepdims=True))

        rotated_key = rotated_key_ref[block]
        value = raw_ref[block, :, wide + narrow :].astype(low)
        place = pl.ds(block * count, count)
        value_grad = key_grad = None
        for head in range(wide // HEAD_WIDTH):
            columns = slice(head * HEAD_WIDTH, (head + 1) * HEAD_WIDTH)
            grads = branch_ref[block, :, columns]
            probs = probs_ref[block, head]
            prob_grad = right_transposed(grads, value)
            term = left_trans(probs.astype(low), grads)
            value_grad = term if value_grad is None else value_grad + term
            balance = jnp.sum(probs * prob_grad, axis=1, keepdims=True)
            score_grad = (probs * (prob_grad - balance)).astype(low)
            query_grad = jnp.dot(score_grad, rotated_key, preferred_element_type=jnp.float32)
            term = left_trans(score_grad, rotated_ref[block, :, columns])
            key_grad = term if key_grad is None else key_grad + term
            query_grad = unturn(query_grad * HEAD_WIDTH ** (-0.5))
            query_grad = normal_back(
                query_grad, raw_ref[block, :, columns], query_gain_ref[...], 0
            )
            every[shard, place, columns] = query_grad.astype(low)
        key_grad = unturn(key_grad * HEAD_WIDTH ** (-0.5))
        key_grad = normal_back(
            key_grad, raw_ref[block, :, wide : wide + narrow], key_gain_ref[...], 1
        )
        every[shard, place, wide : wide + narrow] = key_grad.astype(low)
        every[shard, place, wide + narrow :] = value_grad.astype(low)

    def x_copy(part):
        view = every.at[shard, pl.ds(part * count, count)]
        return remote(view, view, x_sent.at[part], x_got.at[part], x_peer)

    def core_copy(far, part):
        view = every.at[(1 - x if far else x) * 2 + c, pl.ds(part * count, count)]
        return remote(view, view, core_sent.at[far, part], core_got.at[far, part], core_peer)

    gains_out[...] = jnp.zeros_like(gains_out)

    @pl.loop(0, 4)
    def _(block):
        attention_back(block)
        x_copy(block).start()
        core_copy(0, block).start()

    def weigh(place):
        weight_out[place] = left_trans(hidden_ref[...], every[place]).astype(weight_out.dtype)

    def back(place):
        grads = every[place]
        sums = None
        for weight, size, start in (
            (query_ref, wide, 0),
            (key_ref, narrow, wide),
            (value_ref, narrow, wide + narrow),
        ):
            columns = pl.ds(pl.multiple_of(place * size, size), size)
            term = right_transposed(grads[:, start : start + size], weight[:, columns])
            sums = term if sums is None else sums + term
        return sums

    def place_of(i):
        return (x + i // 2) % 2 * 2 + (c + i) % 2

    @pl.loop(0, 4)
    def _(i):
        @pl.when(i == 1)
        def _():
            for part in range(4):
                core_copy(0, part).wait_recv()

        @pl.when(i == 2)
        def _():
            for part in range(4):
                x_copy(part).wait_recv()
                core_copy(1, part).start()

        @pl.when(i == 3)
        def _():
            for part in range(4):
                core_copy(1, part).wait_recv()

        sums = back(place_of(i))

        @pl.when(i == 0)
        def _():
            total[...] = sums

        @pl.when(i > 0)
        def _():
            total[...] += sums

        @pl.when(i < 2)
        def _():
            weigh(place_of(i))

    for owner in range(4):
        outgoing[owner] = total[owner * count : (owner + 1) * count].astype(outgoing.dtype)

    def back_copy(j):
        place = (shard + j) % 4
        return remote(
            outgoing.at[place],
            first_out.at[shard],
            back_sent.at[j],
            back_got.at[(4 - j) % 4],
            (member, place),
        )

    for j in range(1, 4):
        back_copy(j).start()
    first_out[shard] = outgoing[shard]

    @pl.loop(2, 4)
    def _(i):
        weigh(place_of(i))

    for j in range(1, 4):
        place = (shard + j) % 4
        remote(
            outgoing.at[place], first_out.at[place], back_sent.at[j], back_got.at[j], (member, place)
        ).wait_recv()
    for j in range(1, 4):
        back_copy(j).wait_send()
    for part in range(4):
        x_copy(part).wait_send()
        for far in range(2):
            core_copy(far, part).wait_send()


def heads_back(branch, raw, probs, rotated, tables, gains, hidden, weights):
    rows = 4 * raw.shape[1]
    own = raw.shape[2]
    depth = hidden.shape[1]
    low = hidden.dtype
    operands = (branch, raw, probs, *rotated, *tables, *gains, hidden, *weights)
    return pl.pallas_call(
        fetching(heads_kernel, len(operands)),
        out_shape=[
            jax.ShapeDtypeStruct((4, depth, own), low),
            jax.ShapeDtypeStruct((4, rows // 4, depth), low),
            jax.ShapeDtypeStruct((8, HEAD_WIDTH), jnp.float32),
        ],
        in_specs=anywhere(len(operands)),
        out_specs=in_vmem(3),
        scratch_shapes=[
            pltpu.VMEM((4, rows, own), low),
            pltpu.VMEM((4, rows // 4, depth), low),
            pltpu.VMEM((rows, depth), jnp.float32),
            copies(4),
            copies(4),
            copies(2, 4),
            copies(2, 4),
            copies(4),
            copies(4),
        ]
        + room_for(operands),
        compiler_params=settings(7),
    )(*operands)


def moe_gathered(normed, router, routes, capacity, cotangent, weights, notes):
    gate_w, up_w, down_w = weights
    token_count, topk = routes.shape
    experts = router.shape[1]
    all_grads = lax.all_gather(cotangent, BOTH, axis=0, tiled=True)
    padded = jnp.pad(router, ((0, 0), (0, 128 - experts)))
    arrived, active, gate_pre, up_pre, share, select, spread = gather_experts(
        normed, notes, topk, capacity, gate_w, up_w, padded
    )
    mixed, out_rows, gate_pre_grad, up_pre_grad, extra = scatter_rows(
        spread,
        active,
        down_w,
        share,
        select,
        all_grads.reshape(experts, token_count, MODEL_WIDTH),
        gate_pre,
        up_pre,
    )
    summed, back, gate_w_grad, up_w_grad = scatter_rows(
        spread, gate_pre_grad, up_pre_grad, gate_w, up_w, extra, arrived
    )

    def flat(rows):
        return rows.reshape(experts * capacity, rows.shape[2])

    weight_grads = (gate_w_grad, up_w_grad, left_trans(flat(active), flat(out_rows)))
    columns = jnp.arange(experts, dtype=jnp.int32)
    gate_grad = back[:, :experts] + back[:, experts : 2 * experts]
    picks = jnp.any(routes[:, :, None] == columns[None, None, :], axis=1)
    gates = jax.nn.softmax(jnp.where(picks, matrix_product(normed, router), MASKED), axis=1)
    logit_grad = gates * (gate_grad - jnp.sum(gates * gate_grad, axis=1, keepdims=True))
    return mixed, summed, logit_grad.astype(jnp.bfloat16), *weight_grads


def moe_exchanged(normed, router, routes, capacity, cotangent, weights, notes):
    gate_w, up_w, down_w = weights
    token_count, topk = routes.shape
    experts = router.shape[1]
    gates = gates_of(matrix_product(normed, router), routes, experts)
    slots = slot_table(routes, experts, capacity)

    def send(rows):
        packed = jnp.zeros((experts * capacity, MODEL_WIDTH), jnp.bfloat16).at[slots].set(rows)
        return exchange(packed.reshape(experts, capacity, MODEL_WIDTH)).reshape(
            experts * capacity, MODEL_WIDTH
        )

    def bring(rows):
        rows = exchange(rows.reshape(experts, capacity, MODEL_WIDTH))
        return rows.reshape(experts * capacity, MODEL_WIDTH)[slots].reshape(
            token_count, topk, MODEL_WIDTH
        )

    arrived = send(jnp.repeat(normed, topk, axis=0))
    hidden = expert_forward(arrived, gate_w, up_w)
    scaled = (gates[:, :, None] * cotangent.astype(jnp.float32)[:, None, :]).astype(jnp.bfloat16)
    out_rows = send(scaled.reshape(token_count * topk, MODEL_WIDTH))
    rows_back, gate_pre_grad, up_pre_grad = expert_back(out_rows, hidden, gate_w, up_w, down_w)
    gate_w_grad = left_trans(arrived, gate_pre_grad)
    up_w_grad = left_trans(arrived, up_pre_grad)
    down_grad = left_trans(hidden[3], out_rows)
    returned = bring(matrix_product(hidden[3], down_w).astype(jnp.bfloat16))
    mixed = jnp.einsum("tk,tkd->td", gates, returned.astype(jnp.float32))
    gate_grad = jnp.einsum("td,tkd->tk", cotangent, returned, preferred_element_type=jnp.float32)
    summed = jnp.sum(bring(rows_back), axis=1, dtype=jnp.float32)
    picked_grad = gates * (gate_grad - jnp.sum(gates * gate_grad, axis=1, keepdims=True))
    onehot = routes[:, :, None] == jnp.arange(experts, dtype=jnp.int32)[None, None, :]
    logit_grad = jnp.sum(jnp.where(onehot, picked_grad[:, :, None], 0.0), axis=1)
    return mixed, summed, logit_grad.astype(jnp.bfloat16), gate_w_grad, up_w_grad, down_grad


def local(
    tokens,
    lengths,
    routes,
    attn_gain,
    w_query,
    key_weight,
    value_weight,
    q_gain,
    k_gain,
    w_out,
    mlp_gain,
    w_router,
    expert_gate,
    expert_up,
    expert_down,
    cotangent,
):
    shards, members = lax.axis_size("fsdp"), lax.axis_size("exp")
    experts = shards * members
    token_count, topk = routes.shape
    capacity = 2 * token_count * topk // experts
    group = shards * token_count
    depth = w_query.shape[0]
    heads = QUERY_HEADS // shards
    kv_heads = max(1, KEY_VALUE_HEADS // shards)
    copies_of = shards * kv_heads // KEY_VALUE_HEADS
    head_group = heads // kv_heads
    wide, narrow = heads * HEAD_WIDTH, kv_heads * HEAD_WIDTH
    place = lax.axis_index("fsdp")

    gathered = lax.all_gather(
        jnp.concatenate([w_router.reshape(-1), attn_gain, mlp_gain, q_gain, k_gain]), "fsdp"
    )
    cuts, start = [], 0
    for leaf in (w_router, attn_gain, mlp_gain, q_gain, k_gain):
        cuts.append(gathered[:, start : start + leaf.size])
        start += leaf.size
    router = cuts[0].reshape(MODEL_WIDTH, experts)
    gain_attn, gain_mlp, gain_query, gain_key = [
        cut.reshape(-1).astype(jnp.float32) for cut in cuts[1:]
    ]
    dense = (members, shards) == (8, 4) and 2 * capacity >= token_count
    inputs = tokens.astype(jnp.float32)
    scale_one = rms_scale(inputs)
    if dense:
        notes = jnp.pad(
            jnp.concatenate(
                [routes.T, jnp.pad(lengths, ((0, 0), (0, token_count - lengths.shape[1])))], axis=0
            ),
            ((0, 15 - topk), (0, 0)),
        )
        raw, hidden, notes = project_tokens(
            tokens, notes, attn_gain[None], w_query, key_weight, value_weight
        )
        hidden = hidden.reshape(group, depth)
        first = lax.axis_index("exp") * shards
        notes_own = lax.dynamic_slice_in_dim(notes, first, shards)
    else:
        notes = None
        all_lengths = lax.all_gather(lengths[0], "fsdp")

        def by_shard(weight):
            weight = weight.reshape(depth, KEY_VALUE_HEADS, HEAD_WIDTH)
            return jnp.repeat(weight, copies_of, axis=1).reshape(depth, shards, narrow)

        joined = jnp.concatenate(
            [w_query.reshape(depth, shards, wide), by_shard(key_weight), by_shard(value_weight)],
            axis=2,
        ).transpose(1, 0, 2)
        first_normed = (inputs * scale_one * gain_attn).astype(jnp.bfloat16)
        hidden = lax.all_to_all(first_normed, "fsdp", split_axis=1, concat_axis=0, tiled=True)
        partial = contract("gk,nkc->ngc", hidden, joined).astype(jnp.bfloat16)
        raw = lax.psum_scatter(partial, "fsdp", scatter_dimension=0, tiled=True)[0]
        raw = raw.astype(jnp.float32)
    if dense:
        gains = (gain_query[None], gain_key[None])
        middle, normed, attended, probs, *rotated, cosine, sine = finish_attention(
            raw, notes_own, topk, lengths.shape[1], *gains, w_out, tokens, gain_mlp[None]
        )
        attended = attended.reshape(group, wide)
        scale_two = rms_scale(middle)
    else:
        raw = raw.reshape(shards, token_count, wide + 2 * narrow)
        query_raw = raw[:, :, :wide].reshape(shards, token_count, heads, HEAD_WIDTH)
        key_raw = raw[:, :, wide : wide + narrow].reshape(shards, token_count, kv_heads, HEAD_WIDTH)
        value = (
            raw[:, :, wide + narrow :]
            .astype(jnp.bfloat16)
            .reshape(shards, token_count, kv_heads, HEAD_WIDTH)
        )
        position, allowed = jax.vmap(lambda row: seq_layout(row, token_count))(all_lengths)
        cosine, sine = rotary_tables(position, HEAD_WIDTH)
        query_scale = rms_scale(query_raw)
        query_hat = query_raw * query_scale
        key_scale = rms_scale(key_raw)
        key_hat = key_raw * key_scale
        query = (
            rotate(query_hat * gain_query, cosine, sine)
            .astype(jnp.bfloat16)
            .reshape(shards, token_count, kv_heads, head_group, HEAD_WIDTH)
        )
        key = rotate(key_hat * gain_key, cosine, sine).astype(jnp.bfloat16)
        scores = contract("bqkgd,bpkd->bkgqp", query, key) * HEAD_WIDTH ** (-0.5)
        scores = jnp.where(allowed[:, None, None], scores, MASKED)
        top = jnp.max(scores, axis=-1, keepdims=True)
        raised = jnp.exp(scores - top)
        probs = raised / jnp.sum(raised, axis=-1, keepdims=True)
        probs_low = probs.astype(jnp.bfloat16)
        attended = contract("bkgqp,bpkd->bqkgd", probs_low, value).astype(jnp.bfloat16)
        attended = attended.reshape(group, wide)
        mixed_heads = lax.psum_scatter(
            matrix_product(attended, w_out).astype(jnp.bfloat16),
            "fsdp",
            scatter_dimension=0,
            tiled=True,
        )
        middle = inputs + mixed_heads.astype(jnp.float32)
        scale_two = rms_scale(middle)
        normed = (middle * scale_two * gain_mlp).astype(jnp.bfloat16)

    moe = moe_gathered if dense else moe_exchanged
    mixed, summed, logit_grad, gate_w_grad, up_w_grad, down_grad = moe(
        normed,
        router,
        routes,
        capacity,
        cotangent,
        (expert_gate[0], expert_up[0], expert_down[0]),
        notes,
    )
    layer_out = (middle + mixed).astype(jnp.bfloat16)

    upstream = cotangent.astype(jnp.float32)
    normed_grad = summed + right_transposed(logit_grad, router)
    mlp_gain_grad = jnp.sum(normed_grad * middle * scale_two, axis=0)
    router_grad = left_trans(normed, logit_grad)
    middle_grad = upstream + rms_back(normed_grad * gain_mlp, middle, scale_two)
    branch_low = middle_grad.astype(jnp.bfloat16)
    if dense:
        attended_grad, branch_grad = branch_back(branch_low, w_out)
        branch_grad = branch_grad.reshape(group, MODEL_WIDTH)
    else:
        branch_grad = lax.all_gather(branch_low, "fsdp", axis=0, tiled=True)
        attended_grad = right_transposed(branch_grad, w_out).astype(jnp.bfloat16)
    out_w_grad = left_trans(attended, branch_grad).astype(jnp.bfloat16)
    attended_grad, out_w_grad = lax.optimization_barrier((attended_grad, out_w_grad))
    if dense:
        joined_grad, first_grad, gain_grads = heads_back(
            attended_grad,
            raw,
            probs,
            rotated,
            (cosine, sine),
            gains,
            hidden,
            (w_query, key_weight, value_weight),
        )
        first_grad = first_grad.transpose(1, 0, 2).reshape(token_count, MODEL_WIDTH)
        q_gain_grad, k_gain_grad = gain_grads[0], gain_grads[1]
    else:
        attended_grad = attended_grad.reshape(shards, token_count, kv_heads, head_group, HEAD_WIDTH)
        prob_grad = contract("bqkgd,bpkd->bkgqp", attended_grad, value)
        value_grad = contract("bkgqp,bqkgd->bpkd", probs_low, attended_grad)
        balance = jnp.sum(probs * prob_grad, axis=-1, keepdims=True)
        score_grad = (probs * (prob_grad - balance)).astype(jnp.bfloat16)
        query_norm_grad = contract("bkgqp,bpkd->bqkgd", score_grad, key) * HEAD_WIDTH ** (-0.5)
        query_norm_grad = query_norm_grad.reshape(shards, token_count, heads, HEAD_WIDTH)
        key_norm_grad = contract("bkgqp,bqkgd->bpkd", score_grad, query) * HEAD_WIDTH ** (-0.5)
        query_norm_grad = rotate_back(query_norm_grad, cosine, sine)
        key_norm_grad = rotate_back(key_norm_grad, cosine, sine)
        q_gain_grad = jnp.sum(query_norm_grad * query_hat, axis=(0, 1, 2))
        k_gain_grad = jnp.sum(key_norm_grad * key_hat, axis=(0, 1, 2))
        query_grad = rms_back(query_norm_grad * gain_query, query_raw, query_scale)
        key_grad = rms_back(key_norm_grad * gain_key, key_raw, key_scale)
        head_grads = jnp.concatenate(
            [
                query_grad.reshape(group, wide),
                key_grad.reshape(group, narrow),
                value_grad.reshape(group, narrow),
            ],
            axis=1,
        ).astype(jnp.bfloat16)
        head_grads = lax.all_gather(head_grads, "fsdp")
        hidden_grad = contract("ngc,nkc->gk", head_grads, joined).astype(jnp.bfloat16)
        first_grad = lax.all_to_all(
            hidden_grad, "fsdp", split_axis=0, concat_axis=1, tiled=True
        )
        joined_grad = contract("gk,ngc->nkc", hidden, head_grads).astype(jnp.bfloat16)
    first_grad = first_grad.astype(jnp.float32)
    attn_gain_grad = jnp.sum(first_grad * inputs * scale_one, axis=0)
    input_grad = (middle_grad + rms_back(first_grad * gain_attn, inputs, scale_one)).astype(
        jnp.bfloat16
    )

    vectors = jnp.concatenate(
        [
            grad.reshape(shards, -1)
            for grad in (router_grad, attn_gain_grad, mlp_gain_grad, q_gain_grad, k_gain_grad)
        ],
        axis=1,
    )
    if dense:
        rows = -(-vectors.shape[1] // 1024) * 8
        vectors = jnp.pad(vectors, ((0, 0), (0, rows * 128 - vectors.shape[1])))
        started = lengths[0, 0] > 0
        gate_w_grad, up_w_grad = (
            jnp.where(started, grad, 0.0) for grad in (gate_w_grad, up_w_grad)
        )
        out_sum = lax.psum_scatter(out_w_grad, "exp", scatter_dimension=0, tiled=True)
        joined_grad, vectors, out_sum, gate_w_grad, up_w_grad, down_grad = (
            lax.optimization_barrier(
                (joined_grad, vectors, out_sum, gate_w_grad, up_w_grad, down_grad)
            )
        )
        *joined_sum, out_sum, vectors = reduce_over_members(
            joined_grad.reshape(2, 4, -1, wide + 2 * narrow),
            out_sum,
            vectors.reshape(shards, rows, 128),
            (shards * wide, shards * narrow, shards * narrow),
        )
        out_sum, vectors = out_sum.reshape(w_out.shape), vectors.reshape(-1)
    else:
        out_sum = lax.psum(out_w_grad, "exp")
        joined_sum = lax.psum(joined_grad, "exp").astype(jnp.float32)
        vectors = lax.psum(vectors, BOTH)[place]
    if not dense:

        def gather_heads(part):
            part = part.transpose(1, 0, 2).reshape(depth, KEY_VALUE_HEADS, copies_of, HEAD_WIDTH)
            return part.sum(axis=2).reshape(depth, KEY_VALUE_HEADS * HEAD_WIDTH)

        joined_sum = (
            joined_sum[:, :, :wide].transpose(1, 0, 2).reshape(depth, QUERY_HEADS * HEAD_WIDTH),
            gather_heads(joined_sum[:, :, wide : wide + narrow]),
            gather_heads(joined_sum[:, :, wide + narrow :]),
        )
    query_sum, key_sum, value_sum = (part.astype(jnp.float32) for part in joined_sum)
    sums, start = [], 0
    for leaf in (w_router, attn_gain, mlp_gain, q_gain, k_gain):
        sums.append(vectors[start : start + leaf.size].reshape(leaf.shape))
        start += leaf.size

    return (
        layer_out,
        input_grad,
        sums[1],
        query_sum,
        key_sum,
        value_sum,
        sums[3],
        sums[4],
        out_sum.astype(jnp.float32),
        sums[2],
        sums[0],
        gate_w_grad[None],
        up_w_grad[None],
        down_grad[None],
    )


def solution(mesh):
    in_specs = (
        P(("exp", "fsdp"), None),
        P(("exp", "fsdp"), None),
        P(("exp", "fsdp"), None),
        P("fsdp"),
        P("fsdp", None),
        P("fsdp", None),
        P("fsdp", None),
        P("fsdp"),
        P("fsdp"),
        P("fsdp", None),
        P("fsdp"),
        P("fsdp", None),
        P(("exp", "fsdp"), None, None),
        P(("exp", "fsdp"), None, None),
        P(("exp", "fsdp"), None, None),
        P(("exp", "fsdp"), None),
    )
    out_specs = (
        P(("exp", "fsdp"), None),
        P(("exp", "fsdp"), None),
        P("fsdp"),
        P("fsdp", None),
        P("fsdp", None),
        P("fsdp", None),
        P("fsdp"),
        P("fsdp"),
        P("fsdp", None),
        P("fsdp"),
        P("fsdp", None),
        P(("exp", "fsdp"), None, None),
        P(("exp", "fsdp"), None, None),
        P(("exp", "fsdp"), None, None),
    )
    return jax.shard_map(local, mesh=mesh, in_specs=in_specs, out_specs=out_specs, check_vma=False)
```
